32 devices in a mesh: wide: 16 (over z, y, x), narrow: 2 (over core).
Axes of the slice: x: 2, y: 2, z: 4, core: 2. Of those that a mesh axis runs over, the one named last changes fastest.
Arguments:
- tokens: bfloat16 [4096, 1280], P(('wide', 'narrow')), may hold values from -6 to 6
- cotangent: bfloat16 [4096, 1280], P(('wide', 'narrow')), may hold values from -6 to 6
- lengths: int32 [16, 3], P('wide'), may hold values from 1 to 170, 256 in all within a row
- routes: int32 [4096, 7], P(('wide', 'narrow')), may hold values from 0 to 15, all different within a row; in each aligned block of 128 rows (0 to 127, 128 to 255, ...) at most 88 rows name the same one
- keep: int32 [4096, 7], P(('wide', 'narrow')), may hold values 0 or 1
- attn_gain: bfloat16 [1280], P('narrow'), may hold values from 0.099609375 to 1.8984375
- w_query: bfloat16 [1280, 1280], P('narrow'), may hold values from -0.15625 to 0.15625
- w_key: bfloat16 [1280, 1280], P('narrow'), may hold values from -0.15625 to 0.15625
- w_value: bfloat16 [1280, 1280], P('narrow'), may hold values from -0.15625 to 0.15625
- w_out: bfloat16 [1280, 1280], P('narrow'), may hold values from -1 to 1
- ffn_gain: bfloat16 [1280], P('narrow'), may hold values from 0.099609375 to 1.8984375
- w_router: bfloat16 [1280, 16], P('narrow'), may hold values from -0.078125 to 0.078125
- shared_gate: bfloat16 [1280, 896], P('narrow'), may hold values from -0.15625 to 0.15625
- shared_up: bfloat16 [1280, 896], P('narrow'), may hold values from -0.15625 to 0.15625
- shared_down: bfloat16 [896, 1280], P('narrow'), may hold values from -0.25 to 0.25
- expert_gate: bfloat16 [16, 1280, 896], P('wide', None, 'narrow'), may hold values from -0.15625 to 0.15625
- expert_up: bfloat16 [16, 1280, 896], P('wide', None, 'narrow'), may hold values from -0.15625 to 0.15625
- expert_down: bfloat16 [16, 896, 1280], P('wide', 'narrow'), may hold values from -0.5 to 0.5
Outputs:
- out: bfloat16 [4096, 1280], P(('wide', 'narrow'))
- grad_tokens: float32 [4096, 1280], P(('wide', 'narrow'))
- grad_attn_gain: float32 [1280], P('narrow')
- grad_w_query: float32 [1280, 1280], P('narrow')
- grad_w_key: float32 [1280, 1280], P('narrow')
- grad_w_value: float32 [1280, 1280], P('narrow')
- grad_w_out: float32 [1280, 1280], P('narrow')
- grad_ffn_gain: float32 [1280], P('narrow')
- grad_w_router: float32 [1280, 16], P('narrow')
- grad_shared_gate: float32 [1280, 896], P('narrow')
- grad_shared_up: float32 [1280, 896], P('narrow')
- grad_shared_down: float32 [896, 1280], P('narrow')
- grad_expert_gate: float32 [16, 1280, 896], P('wide', None, 'narrow')
- grad_expert_up: float32 [16, 1280, 896], P('wide', None, 'narrow')
- grad_expert_down: float32 [16, 896, 1280], P('wide', 'narrow')
The draws below stay inside these ranges and needn't reach their ends.
Inputs may be any that keep to these rules, and one draw needn't show every extreme that they name: `lengths`: each row sums to 256; the longest document of every row has exactly 170 tokens. `routes`: each token names 7 different experts. Among the 128 tokens of one device no expert is named more than 88 times, and in every draw some device names some expert exactly 88 times.
All inputs are finite; a program needn't handle non-finite values. No bound on the sum of `keep` on one device may be relied on, other than what follows from the above.
Results may differ from the reference program's by a relative error of at most 0.018.
Values may be sent and summed in bfloat16 or wider, within the bound.
A program may use at most 256 MiB of HBM per device.

```python
import math
import jax
import jax.numpy as jnp
import numpy as np
from jax import lax

D = 1280
HEADS = 10
HEAD_DIM = 128
FF = 896
TOPK = 7
DOCS = 3
TOK_DEV = 128
EXPERTS = 16
ROW = 256
TOKENS = 4096
DOC_MOST = 170
CAP = 88
N_WIDE = 16
N_NARROW = 2


def plant(entries, rng, least, largest):
    extent = entries.shape
    spot = [jax.random.randint(jax.random.fold_in(rng, axis), (), 0, extent[axis]) for axis in range(len(extent))]
    entries = entries.at[tuple(spot)].set(least)
    longest = extent.index(max(extent))
    spot[longest] = (spot[longest] + 1) % extent[longest]
    return entries.at[tuple(spot)].set(largest)


def shard_levels(rng, dims, split, smallest, largest):
    factor_of = 1.0
    for axis_at, shards_of in split:
        steps = jax.random.uniform(jax.random.fold_in(jax.random.fold_in(rng, 6), axis_at), (shards_of,), jnp.float32, smallest / len(split), largest / len(split))
        factor_of = factor_of * jnp.repeat(jnp.exp(steps), dims[axis_at] // shards_of).reshape((-1,) + (1,) * (len(dims) - 1 - axis_at))
    return factor_of


def length_profile(count, total, most, skew):
    loads = [(1 << 20) // math.isqrt(standing ** skew) + 1 for standing in range(2, count + 1)]
    surplus, holding = total - most - (count - 1), [1] * (count - 1)
    while surplus > 0:
        movable = [i for i in range(count - 1) if holding[i] < most]
        whole, left = sum([loads[i] for i in movable]), surplus
        for i in movable:
            extra = min(most - holding[i], max(1, left * loads[i] // whole), surplus)
            holding[i] = holding[i] + extra
            surplus = surplus - extra
    return np.array([most] + holding)


def uneven(key, count, total, most, slope):
    if count == 2:
        one = jax.random.randint(key, (), max(1, total - most), min(most, total - 1) + 1)
        return jnp.stack([one, total - one])
    tallies = jnp.asarray(length_profile(count, total, most, slope), jnp.int32)
    twos = (count - 1) // 2
    donor, taker = tallies[1:1 + 2 * twos:2], tallies[2:2 + 2 * twos:2]
    margin = jnp.minimum(donor - 1, most - taker)
    moved = jax.random.randint(jax.random.fold_in(key, 1), (twos,), 0, 1 << 20) % (margin + 1)
    tallies = tallies.at[1:1 + 2 * twos:2].set(donor - moved).at[2:2 + 2 * twos:2].set(taker + moved)
    return tallies[jax.random.permutation(jax.random.fold_in(key, 2), count)]


def shared_out(key, own, number, rows, count, top, most, slope):
    sequence = jax.random.permutation(key, count)
    crowded, common = portions_of(count, rows * top, most, slope, True), portions_of(count, rows * top, most, slope, False)
    places = jnp.arange(count)

    def named(sizes, rotation):
        used = int((sizes > 0).sum())
        fixed = max(1, used // 4)
        moved = fixed + (places - fixed + rotation * (used - fixed)) % max(1, count - fixed)
        return jnp.zeros((count,), jnp.int32).at[sequence[jnp.where(places < fixed, places, moved)]].set(jnp.asarray(sizes, jnp.int32))

    sizes = jnp.where(number % 4 == 0, named(crowded, number // 4), named(common, number - number // 4 - 1))
    mixed = jax.random.permutation(jax.random.fold_in(own, 3), count)
    giver, taker = mixed[0:count // 2 * 2:2], mixed[1:count // 2 * 2:2]
    margin = jnp.minimum(sizes[giver] - 1, most - sizes[taker]) // 2
    margin = jnp.where((giver == sequence[0]) | (taker == sequence[0]) | (sizes[taker] == 0), 0, jnp.maximum(margin, 0))
    moved = jax.random.randint(jax.random.fold_in(own, 4), (count // 2,), 0, 1 << 20) % (margin + 1)
    sizes = sizes.at[giver].add(-moved).at[taker].add(moved)
    labels = jnp.searchsorted(jnp.cumsum(sizes), jnp.arange(rows * top), side="right").astype(jnp.int32)
    listing = labels.reshape(top, rows).T
    listing = listing[jax.random.permutation(jax.random.fold_in(own, 1), rows)]
    rotation = jax.random.randint(jax.random.fold_in(own, 2), (rows, 1), 0, top)
    return jnp.take_along_axis(listing, (jnp.arange(top)[None, :] + rotation) % top, axis=1)


def portions_of(number_of, total, reach, skew, full):
    loads = [(1 << 20) // math.isqrt(rank ** skew) + 1 for rank in range(1, number_of + 1)]
    largest = reach if full else min(reach, max(-(-total // number_of), total * loads[0] // sum(loads)))
    least = 1 if total - largest >= number_of - 1 else 0
    holding, spare = [largest] + [least] * (number_of - 1), total - largest - least * (number_of - 1)
    while spare > 0:
        movable = [i for i in range(1, number_of) if holding[i] < largest] or [i for i in range(1, number_of) if holding[i] < reach]
        mass, remaining = sum([loads[i] for i in movable]), spare
        for i in movable:
            extra = min(reach - holding[i], max(1, remaining * loads[i] // mass), spare)
            holding[i] = holding[i] + extra
            spare = spare - extra
    return np.array(holding)


def bell_draw(stream_key, dims, deviation, most, shards=(), held_as=jnp.bfloat16):
    factor_of = shard_levels(stream_key, dims, shards, -0.22, 0.18) if shards else 1.0
    values = jax.random.normal(stream_key, dims, jnp.float32) * deviation * factor_of
    return jnp.minimum(jnp.maximum(values, -most), most).astype(held_as)


def setup_inputs(seed: int = 0) -> dict:
    streams_of = jax.random.split(jax.random.key(seed), 19)
    tokens = bell_draw(streams_of[0], (TOKENS, D), 1.0, 6.0, ((0, 32),))
    cotangent = bell_draw(streams_of[1], (TOKENS, D), 1.0, 6.0, ((0, 32),))
    lengths = jax.vmap(lambda own: uneven(own, DOCS, ROW, DOC_MOST, 1))(jax.random.split(streams_of[2], N_WIDE)).reshape((N_WIDE, DOCS)).astype(jnp.int32)
    routes_keys = jax.random.split(jax.random.fold_in(streams_of[3], 1), TOKENS // TOK_DEV)
    routes_turns = jax.random.permutation(jax.random.fold_in(streams_of[3], 3), TOKENS // TOK_DEV)
    routes = jax.vmap(lambda own, number: shared_out(jax.random.fold_in(streams_of[3], 2), own, number, TOK_DEV, EXPERTS, TOPK, CAP, 2))(routes_keys, routes_turns).reshape((TOKENS, TOPK))
    keep = plant((jax.random.randint(streams_of[4], (TOKENS, TOPK), 0, 8) < 7).astype(jnp.int32), jax.random.fold_in(streams_of[4], 1), 0, 1)
    attn_gain = jnp.clip(1.0 + 0.18 * jax.random.normal(streams_of[5], (D,), jnp.float32), 0.099609375, 1.8984375).astype(jnp.bfloat16)
    w_query = bell_draw(streams_of[6], (D, D), D ** -0.5, 0.15625, ((0, 2),))
    w_key = bell_draw(streams_of[7], (D, D), D ** -0.5, 0.15625, ((0, 2),))
    w_value = bell_draw(streams_of[8], (D, D), D ** -0.5, 0.15625, ((0, 2),))
    w_out = bell_draw(streams_of[9], (D, D), (max(D // 32, 8)) ** -0.5, 1.0, ((0, 2),))
    ffn_gain = jnp.clip(1.0 + 0.18 * jax.random.normal(streams_of[10], (D,), jnp.float32), 0.099609375, 1.8984375).astype(jnp.bfloat16)
    w_router = bell_draw(streams_of[11], (D, EXPERTS), (4 * D) ** -0.5, 0.078125, ((0, 2),))
    shared_gate = bell_draw(streams_of[12], (D, FF), D ** -0.5, 0.15625, ((0, 2),))
    shared_up = bell_draw(streams_of[13], (D, FF), D ** -0.5, 0.15625, ((0, 2),))
    shared_down = bell_draw(streams_of[14], (FF, D), (FF // 2) ** -0.5, 0.25, ((0, 2),))
    expert_gate = bell_draw(streams_of[15], (EXPERTS, D, FF), D ** -0.5, 0.15625, ((0, 16), (2, 2)))
    expert_up = bell_draw(streams_of[16], (EXPERTS, D, FF), D ** -0.5, 0.15625, ((0, 16), (2, 2)))
    expert_down = bell_draw(streams_of[17], (EXPERTS, FF, D), (FF // 8) ** -0.5, 0.5, ((0, 16), (1, 2)))
    return dict(tokens=tokens, cotangent=cotangent, lengths=lengths, routes=routes, keep=keep, attn_gain=attn_gain, w_query=w_query, w_key=w_key, w_value=w_value, w_out=w_out, ffn_gain=ffn_gain, w_router=w_router, shared_gate=shared_gate, shared_up=shared_up, shared_down=shared_down, expert_gate=expert_gate, expert_up=expert_up, expert_down=expert_down)


@jax.custom_vjp
def low(v):
    return lax.optimization_barrier(v.astype(jnp.bfloat16)).astype(jnp.float32)

@jax.custom_vjp
def low_back(v):
    return v

def low_keep(v):
    return (low(v), None)

def low_pass(kept, grad):
    return (grad,)

def back_keep(v):
    return (v, None)

def back_low(kept, grad):
    return (low(grad),)
low.defvjp(low_keep, low_pass)
low_back.defvjp(back_keep, back_low)
EPS = 1e-06
MASKED = -1e+30

def matmul(left, right):
    return jnp.dot(left, right, precision=lax.Precision.HIGHEST, preferred_element_type=jnp.float32)

def doc_layout(positions, doc_lens):
    doc_ends = jnp.cumsum(doc_lens).astype(jnp.int32)
    passed = (positions[:, None] >= doc_ends[None, :]).astype(jnp.int32)
    doc_ids = lax.optimization_barrier(jnp.sum(passed, axis=1)).astype(jnp.int32)
    return (doc_ids, positions - lax.optimization_barrier(jnp.sum(passed * doc_lens[None, :], axis=1)).astype(jnp.int32))

def rotary_angles(positions):
    half_dim = HEAD_DIM // 2
    inverse = jnp.exp(jnp.arange(half_dim, dtype=jnp.float32) * (-2.0 * math.log(10000.0) / HEAD_DIM))
    angles = positions.astype(jnp.float32)[:, None] * inverse[None, :]
    return (jnp.cos(angles), jnp.sin(angles))

def rotate(values, cosine, sine_table):
    half_dim = values.shape[-1] // 2
    lower_half = values[..., :half_dim]
    upper_half = values[..., half_dim:]
    cos_b = cosine[:, None, :]
    sin_b = sine_table[:, None, :]
    return jnp.concatenate([lower_half * cos_b - upper_half * sin_b, upper_half * cos_b + lower_half * sin_b], axis=-1)

def norm_rows(values, gain_vec):
    row_scale = lax.rsqrt(lax.optimization_barrier(jnp.mean(values * values, axis=-1, keepdims=True)) + EPS)
    return values * row_scale * gain_vec

def silu_product(gate_vals, upper):
    return jax.nn.silu(gate_vals) * upper

def row_attention(queries, keys_all, values_all, doc_lens):
    positions = jnp.arange(ROW, dtype=jnp.int32)
    doc_ids, unused = doc_layout(positions, doc_lens)
    allowed = (doc_ids[:, None] == doc_ids[None, :]) & (positions[None, :] <= positions[:, None])
    scores = low_back(jnp.einsum('qhd,khd->hqk', queries, keys_all, precision=lax.Precision.HIGHEST))
    masked = jnp.where(allowed[None], scores, MASKED)
    prob_rows = jax.nn.softmax(masked, axis=-1)
    return jnp.einsum('hqk,khd->qhd', low(prob_rows), values_all, precision=lax.Precision.HIGHEST)

def expert_rows(in_rows, gate_mat, upper_mat, down_mat):
    gate_vals = low_back(matmul(in_rows, gate_mat))
    upper = low_back(matmul(in_rows, upper_mat))
    return matmul(low(silu_product(gate_vals, upper)), down_mat)

def layer_forward(tokens, attn_gain, w_query, w_key, w_value, w_out, ffn_gain, w_router, shared_gate, shared_up, shared_down, expert_gate, expert_up, expert_down, lengths, routes, keep):
    n_one = low(norm_rows(tokens, attn_gain))
    positions = jnp.arange(ROW, dtype=jnp.int32)
    doc_pos = jax.vmap(lambda doc_lens: doc_layout(positions, doc_lens)[1])(lengths)
    cosine, sine_table = rotary_angles(doc_pos.reshape(-1))
    shape_heads = (TOKENS, HEADS, HEAD_DIM)
    queries = low_back(matmul(n_one, w_query)).reshape(shape_heads)
    keys_all = low_back(matmul(n_one, w_key)).reshape(shape_heads)
    values_all = low(low_back(matmul(n_one, w_value))).reshape(shape_heads)
    queries = low(rotate(queries, cosine, sine_table) * HEAD_DIM ** (-0.5))
    keys_all = low(rotate(keys_all, cosine, sine_table))
    shape_rows = (N_WIDE, ROW, HEADS, HEAD_DIM)
    checked = jax.checkpoint(row_attention)
    attended = lax.map(lambda map_item: checked(map_item[0], map_item[1], map_item[2], map_item[3]), (queries.reshape(shape_rows), keys_all.reshape(shape_rows), values_all.reshape(shape_rows), lengths))
    attended = low(low_back(attended.reshape(TOKENS, D)))
    hidden = tokens + low_back(matmul(attended, w_out))
    n_two = low(norm_rows(hidden, ffn_gain))
    logits = low_back(matmul(n_two, w_router))
    selected = jnp.take_along_axis(logits, routes, axis=1)
    mixing = jax.nn.softmax(selected, axis=1) * keep.astype(jnp.float32)
    shared = expert_rows(n_two, shared_gate, shared_up, shared_down)
    devices = N_WIDE * N_NARROW
    per_device = routes.reshape(devices, TOK_DEV * TOPK)
    onehot = (per_device[:, :, None] == jnp.arange(EXPERTS, dtype=jnp.int32)[None, None, :]).astype(jnp.int32)
    earlier = (jnp.cumsum(onehot, axis=1) - onehot).astype(jnp.int32)
    slot_place = lax.optimization_barrier(jnp.sum(earlier * onehot, axis=2)).astype(jnp.int32)
    owner_ids = jnp.arange(devices, dtype=jnp.int32)[:, None]
    slot_index = (per_device * (devices * CAP) + owner_ids * CAP + slot_place).reshape(TOKENS, TOPK).astype(jnp.int32)
    slot_total = EXPERTS * devices * CAP
    token_ids = jnp.broadcast_to(jnp.arange(TOKENS, dtype=jnp.int32)[:, None], (TOKENS, TOPK))
    source = jnp.full((slot_total,), -1, jnp.int32).at[slot_index.reshape(-1)].set(token_ids.reshape(-1))

    def run_expert(map_item):
        filled = map_item[0] >= 0
        in_rows = low_back(jnp.where(filled[:, None], n_two[jnp.maximum(map_item[0], 0)], 0.0))
        return expert_rows(in_rows, map_item[1], map_item[2], map_item[3])
    outputs = lax.map(jax.checkpoint(run_expert), (source.reshape(EXPERTS, devices * CAP), expert_gate, expert_up, expert_down))
    outputs = low(low_back(outputs)).reshape(slot_total, D)
    routed = jnp.zeros((TOKENS, D), jnp.float32)
    for member in range(TOPK):
        routed = routed + mixing[:, member:member + 1] * outputs[slot_index[:, member]]
    return hidden + shared + routed

def reference(tokens, cotangent, lengths, routes, keep, attn_gain, w_query, w_key, w_value, w_out, ffn_gain, w_router, shared_gate, shared_up, shared_down, expert_gate, expert_up, expert_down):
    floats = tuple((array.astype(jnp.float32) for array in (tokens, attn_gain, w_query, w_key, w_value, w_out, ffn_gain, w_router, shared_gate, shared_up, shared_down, expert_gate, expert_up, expert_down)))

    def closed(*values):
        return layer_forward(*values, lengths, routes, keep)
    result, pullback = jax.vjp(closed, *floats)
    gradients = pullback(cotangent.astype(jnp.float32))
    return (result.astype(jnp.bfloat16), gradients[0], gradients[1], gradients[2], gradients[3], gradients[4], gradients[5], gradients[6], gradients[7], gradients[8], gradients[9], gradients[10], gradients[11], gradients[12], gradients[13])
```

```python
import functools
import math

import jax
import jax.numpy as jnp
from jax import lax
from jax.experimental import pallas as pl
from jax.experimental.pallas import tpu as pltpu
from jax.sharding import PartitionSpec as P

HEAD_DIM = 128
TOPK = 7


EPS = 1e-06
MASKED = -1e30


def matmul(left, right):
    return jnp.dot(left, right, preferred_element_type=jnp.float32)


def matmul_left(left, right):
    return lax.dot_general(
        left, right, (((0,), (0,)), ((), ())), preferred_element_type=jnp.float32
    )


def matmul_right(left, right):
    return lax.dot_general(
        left, right, (((1,), (1,)), ((), ())), preferred_element_type=jnp.float32
    )


def doc_layout(positions, doc_lens):
    doc_ends = jnp.cumsum(doc_lens)
    passed = (positions[:, None] >= doc_ends[None, :]).astype(jnp.int32)
    doc_ids = jnp.sum(passed, axis=1)
    return (doc_ids, positions - jnp.sum(passed * doc_lens[None, :], axis=1))


def rotary_angles(positions):
    half_dim = HEAD_DIM // 2
    inverse = jnp.exp(
        jnp.arange(half_dim, dtype=jnp.float32) * (-2.0 * math.log(10000.0) / HEAD_DIM)
    )
    angles = positions.astype(jnp.float32)[:, None] * inverse[None, :]
    return (jnp.cos(angles), jnp.sin(angles))


def rotate(values, cosine, sine_table):
    half_dim = values.shape[-1] // 2
    lower_half = values[..., :half_dim]
    upper_half = values[..., half_dim:]
    cos_b = cosine[:, None, :]
    sin_b = sine_table[:, None, :]
    return jnp.concatenate(
        [lower_half * cos_b - upper_half * sin_b, upper_half * cos_b + lower_half * sin_b], axis=-1
    )


def norm_forward(values, gain_vec):
    row_scale = lax.rsqrt(jnp.mean(values * values, axis=-1, keepdims=True) + EPS)
    unit_rows = values * row_scale
    return (unit_rows * gain_vec, unit_rows, row_scale)


def norm_backward(grad_rows, unit_rows, row_scale, gain_vec):
    scaled = grad_rows * gain_vec
    grad_gain = jnp.sum(grad_rows * unit_rows, axis=0)
    grad_input = row_scale * (
        scaled - unit_rows * jnp.mean(scaled * unit_rows, axis=-1, keepdims=True)
    )
    return (grad_input, grad_gain)


def silu_parts(gate_vals):
    sigmoid_vals = jax.nn.sigmoid(gate_vals)
    return (gate_vals * sigmoid_vals, sigmoid_vals * (1.0 + gate_vals * (1.0 - sigmoid_vals)))


def expert_forward(in_rows, gate_mat, upper_mat):
    gate_vals = matmul(in_rows, gate_mat)
    upper = matmul(in_rows, upper_mat)
    act_vals, unused = silu_parts(gate_vals)
    return (gate_vals, upper, (act_vals * upper).astype(jnp.bfloat16))


def expert_backward(in_rows, grad_rows, gate_vals, upper, active, gate_mat, upper_mat, down_mat):
    grad_act = matmul_right(grad_rows, down_mat)
    act_vals, slope_vals = silu_parts(gate_vals)
    grad_gate = (grad_act * upper * slope_vals).astype(jnp.bfloat16)
    grad_upper = (grad_act * act_vals).astype(jnp.bfloat16)
    grad_down_mat = matmul_left(active, grad_rows)
    grad_gate_mat = matmul_left(in_rows, grad_gate)
    grad_upper_mat = matmul_left(in_rows, grad_upper)
    grad_input = matmul_right(grad_gate, gate_mat) + matmul_right(grad_upper, upper_mat)
    return (grad_input, grad_gate_mat, grad_upper_mat, grad_down_mat)


def attend_block(queries, keys_all, values_all, allowed):
    scores = jnp.einsum("qhd,khd->hqk", queries, keys_all, preferred_element_type=jnp.float32)
    masked = jnp.where(allowed[None], scores, MASKED)
    row_max = jnp.max(masked, axis=-1, keepdims=True)
    weights = jnp.exp(masked - row_max)
    row_total = jnp.sum(weights, axis=-1, keepdims=True)
    prob_rows = (weights / row_total).astype(jnp.bfloat16)
    attended = jnp.einsum("hqk,khd->qhd", prob_rows, values_all, preferred_element_type=jnp.float32)
    return (attended.astype(jnp.bfloat16), (row_max + jnp.log(row_total))[..., 0])


def attend_back(queries, keys_all, values_all, allowed, logsum, grad_attended):
    scores = jnp.einsum("qhd,khd->hqk", queries, keys_all, preferred_element_type=jnp.float32)
    masked = jnp.where(allowed[None], scores, MASKED)
    prob_rows = jnp.exp(masked - logsum[..., None])
    grad_probs = jnp.einsum(
        "qhd,khd->hqk", grad_attended, values_all, preferred_element_type=jnp.float32
    )
    row_delta = jnp.sum(prob_rows * grad_probs, axis=-1, keepdims=True)
    grad_scores = (prob_rows * (grad_probs - row_delta)).astype(jnp.bfloat16)
    grad_queries = jnp.einsum(
        "hqk,khd->qhd", grad_scores, keys_all, preferred_element_type=jnp.float32
    )
    grad_keys = jnp.einsum("hqk,qhd->khd", grad_scores, queries, preferred_element_type=jnp.float32)
    grad_values = jnp.einsum(
        "hqk,qhd->khd",
        prob_rows.astype(jnp.bfloat16),
        grad_attended,
        preferred_element_type=jnp.float32,
    )
    return (grad_queries, grad_keys, grad_values)


MESH_ID = pl.DeviceIdType.MESH
BF16 = jnp.bfloat16
F32 = jnp.float32


class Place:
    def __init__(self, levels):
        self.levels = levels
        wide = lax.axis_index("wide")
        self.core = lax.axis_index("narrow")
        self.level = wide // 4
        self.spot = lax.rem(wide, 4)
        self.across = self.spot + 1 - 2 * lax.rem(self.spot, 2)
        self.along = lax.rem(self.spot + 2, 4)
        self.corner = 3 - self.spot
        self.has_up = self.level < levels - 1
        self.has_down = self.level > 0

    def device(self, level, spot, core=None):
        return {"wide": level * 4 + spot, "narrow": self.core if core is None else core}

    def enter(self, sibling):
        barrier = pltpu.get_barrier_semaphore()

        def greet(device):
            pl.semaphore_signal(barrier, inc=1, device_id=device, device_id_type=MESH_ID)

        greet(self.device(self.level, self.across))
        greet(self.device(self.level, self.along))
        if sibling:
            greet(self.device(self.level, self.spot, 1 - self.core))

        @pl.when(self.has_up)
        def _():
            greet(self.device(self.level + 1, self.spot))

        @pl.when(self.has_down)
        def _():
            greet(self.device(self.level - 1, self.spot))

        both = jnp.where(self.has_up, 1, 0) + jnp.where(self.has_down, 1, 0)
        pl.semaphore_wait(barrier, both + (3 if sibling else 2))


def remote(src, dst, send, recv, device):
    return pltpu.make_async_remote_copy(
        src_ref=src,
        dst_ref=dst,
        send_sem=send,
        recv_sem=recv,
        device_id=device,
        device_id_type=MESH_ID,
    )


def gather_kernel(levels, sibling, x_ref, out_ref, own_sem, *sems):
    send_up, send_dn, send_x, send_y, send_cx, send_cy, send_n = sems[:7]
    recv_z, recv_x, recv_y, recv_cx, recv_cy, recv_n = sems[7:]
    at = Place(levels)
    level, spot, core = at.level, at.spot, at.core
    across, along, corner = at.across, at.along, at.corner
    half = x_ref.shape[0] // 2
    first, second = pl.ds(0, half), pl.ds(half, half)
    at.enter(sibling)

    def block(lev, sp, co=None):
        if sibling:
            return out_ref.at[(lev * 4 + sp) * 2 + (core if co is None else co)]
        return out_ref.at[lev * 4 + sp]

    own = pltpu.make_async_copy(x_ref, block(level, spot), own_sem)
    own.start()

    def go_up(lev, src=None):
        dst = block(lev, spot)
        src = dst if src is None else src
        return remote(src, dst, send_up.at[lev], recv_z.at[lev], at.device(level + 1, spot))

    def go_down(lev, src=None):
        dst = block(lev, spot)
        src = dst if src is None else src
        return remote(src, dst, send_dn.at[lev], recv_z.at[lev], at.device(level - 1, spot))

    def go_x(lev, sp, src=None):
        dst = block(lev, sp)
        src = dst if src is None else src
        return remote(src, dst, send_x.at[lev], recv_x.at[lev], at.device(level, across))

    def go_y(lev, sp, src=None):
        dst = block(lev, sp)
        src = dst if src is None else src
        return remote(src, dst, send_y.at[lev], recv_y.at[lev], at.device(level, along))

    def corner_y(lev, sp):
        ref = block(lev, sp).at[first]
        return remote(ref, ref, send_cy.at[lev], recv_cy.at[lev], at.device(level, along))

    def corner_x(lev, sp):
        ref = block(lev, sp).at[second]
        return remote(ref, ref, send_cx.at[lev], recv_cx.at[lev], at.device(level, across))

    def to_sibling(lev, sp, src=None):
        dst = block(lev, sp)
        src = dst if src is None else src
        sems = send_n.at[lev * 4 + sp], recv_n.at[lev * 4 + sp]
        return remote(src, dst, *sems, at.device(level, spot, 1 - core))

    def from_sibling(lev, sp):
        ref = block(lev, sp, 1 - core)
        sems = send_n.at[lev * 4 + sp], recv_n.at[lev * 4 + sp]
        return remote(ref, ref, *sems, at.device(level, spot, 1 - core))

    @pl.when(at.has_up)
    def _():
        go_up(level, x_ref).start()

    @pl.when(at.has_down)
    def _():
        go_down(level, x_ref).start()

    go_x(level, spot, x_ref).start()
    go_y(level, spot, x_ref).start()
    if sibling:
        to_sibling(level, spot, x_ref).start()

    def when(cond, run):
        if cond is None:
            run()
        else:
            pl.when(cond)(run)

    def at_distance(s):
        if s == 0:
            return [(level, None)]
        return [(level - s, level - s >= 0), (level + s, level + s < levels)]

    def column(s):
        for sign, (lev, cond) in zip((-1, 1), at_distance(s)):

            def run(lev=lev, sign=sign):
                go_up(lev).wait_recv()
                if sign < 0:
                    pl.when(at.has_up)(lambda: go_up(lev).start())
                else:
                    pl.when(at.has_down)(lambda: go_down(lev).start())
                go_x(lev, spot).start()
                go_y(lev, spot).start()
                if sibling:
                    to_sibling(lev, spot).start()

            when(cond, run)

    def square(s):
        for lev, cond in at_distance(s):

            def run(lev=lev):
                go_x(lev, across).wait_recv()
                corner_y(lev, across).start()
                if sibling:
                    to_sibling(lev, across).start()
                go_y(lev, along).wait_recv()
                corner_x(lev, along).start()
                if sibling:
                    to_sibling(lev, along).start()

            when(cond, run)

    def corners(s):
        for lev, cond in at_distance(s):

            def run(lev=lev):
                corner_y(lev, corner).wait_recv()
                corner_x(lev, corner).wait_recv()
                if sibling:
                    to_sibling(lev, corner).start()

            when(cond, run)

    for s in range(1, levels + 2):
        if s < levels:
            column(s)
        if s - 1 < levels:
            square(s - 1)
        if s >= 2:
            corners(s - 2)
    own.wait()
    for lev in range(levels):

        @pl.when(at.has_up & (lev <= level))
        def _():
            go_up(lev).wait_send()

        @pl.when(at.has_down & (lev >= level))
        def _():
            go_down(lev).wait_send()

        go_x(lev, spot).wait_send()
        go_y(lev, spot).wait_send()
        corner_y(lev, across).wait_send()
        corner_x(lev, along).wait_send()
        if sibling:
            for sp in range(4):
                to_sibling(lev, sp).wait_send()
                from_sibling(lev, sp).wait_recv()


def gather_wide(x, levels, sibling, collective_id):
    dma = pltpu.SemaphoreType.DMA
    blocks = levels * 4
    anywhere = pl.BlockSpec(memory_space=pl.ANY)
    return pl.pallas_call(
        functools.partial(gather_kernel, levels, sibling),
        out_shape=jax.ShapeDtypeStruct((blocks * (2 if sibling else 1), *x.shape), x.dtype),
        in_specs=[anywhere],
        out_specs=anywhere,
        scratch_shapes=[dma]
        + [dma((levels,))] * 6
        + [dma((blocks,))]
        + [dma((levels,))] * 5
        + [dma((blocks,))],
        compiler_params=pltpu.CompilerParams(
            collective_id=collective_id, has_side_effects=True
        ),
    )(x)


def destinations(levels):
    return [
        sorted(range(levels), key=lambda to: (-abs(to - here), -to)) for here in range(levels)
    ]


def add_rows(write, sources, rows):
    step = 16

    def body(k, carry):
        r = pl.ds(pl.multiple_of(k * step, step), step)
        total = sources[0](r)
        for source in sources[1:]:
            total = total + source(r)
        write(r, total)
        return carry

    lax.fori_loop(0, rows // step, body, 0)


def reads(ref):
    return lambda r: ref[r, :].astype(F32)


def writes(ref):
    def write(r, total):
        ref[r, :] = total.astype(ref.dtype)

    return write


def scatter_kernel(levels, sibling, x_ref, out_ref, acc, near, hx, hy, fx, fy, out_buf, za, zb, *sems):
    send_n, recv_n = sems[:2]
    send_hx, send_hy, send_fx, send_fy, send_up, send_dn = sems[2:8]
    recv_hx, recv_hy, recv_fx, recv_fy, recv_za, recv_zb = sems[8:]
    at = Place(levels)
    level, spot, core = at.level, at.spot, at.core
    across, along, corner = at.across, at.along, at.corner
    rows = out_ref.shape[0]
    half = rows // 2
    first, second = pl.ds(0, half), pl.ds(half, half)
    at.enter(sibling)
    table = destinations(levels)

    def destination(s):
        lev = jnp.int32(table[0][s])
        for k in range(1, levels):
            lev = jnp.where(level == k, table[k][s], lev)
        return lev

    order = [destination(s) for s in range(levels)]

    def to_sibling(lev, sp):
        b = lev * 4 + sp
        src = x_ref.at[b * 2 + 1 - core]
        return remote(
            src, near.at[b], send_n.at[b], recv_n.at[b], at.device(level, spot, 1 - core)
        )

    def half_y(lev):
        src = acc.at[lev * 4 + corner].at[first]
        return remote(
            src, hy.at[lev], send_hy.at[lev], recv_hy.at[lev], at.device(level, along)
        )

    def half_x(lev):
        src = acc.at[lev * 4 + corner].at[second]
        return remote(
            src, hx.at[lev], send_hx.at[lev], recv_hx.at[lev], at.device(level, across)
        )

    def full_x(lev):
        src = acc.at[lev * 4 + across]
        return remote(
            src, fx.at[lev], send_fx.at[lev], recv_fx.at[lev], at.device(level, across)
        )

    def full_y(lev):
        src = acc.at[lev * 4 + along]
        return remote(
            src, fy.at[lev], send_fy.at[lev], recv_fy.at[lev], at.device(level, along)
        )

    def go_up(lev):
        sems = send_up.at[lev], recv_zb.at[lev]
        return remote(out_buf.at[lev], zb.at[lev], *sems, at.device(level + 1, spot))

    def go_down(lev):
        sems = send_dn.at[lev], recv_za.at[lev]
        return remote(out_buf.at[lev], za.at[lev], *sems, at.device(level - 1, spot))

    if sibling:
        for lev in order:
            for sp in (corner, across, along, spot):
                to_sibling(lev, sp).start()

    def local(lev):
        for n, sp in enumerate((corner, across, along, spot)):
            b = lev * 4 + sp
            if sibling:
                to_sibling(lev, sp).wait_recv()
                add_rows(writes(acc.at[b]), [reads(x_ref.at[b * 2 + core]), reads(near.at[b])], rows)
            else:
                add_rows(writes(acc.at[b]), [reads(x_ref.at[b])], rows)
            if n == 0:
                half_y(lev).start()
                half_x(lev).start()

    def halves(lev):
        half_y(lev).wait_recv()
        ref = acc.at[lev * 4 + across].at[first]
        add_rows(writes(ref), [reads(ref), reads(hy.at[lev])], half)
        full_x(lev).start()
        half_x(lev).wait_recv()
        ref = acc.at[lev * 4 + along].at[second]
        add_rows(writes(ref), [reads(ref), reads(hx.at[lev])], half)
        full_y(lev).start()

    def column(lev):
        full_x(lev).wait_recv()
        full_y(lev).wait_recv()
        own = [reads(acc.at[lev * 4 + spot]), reads(fx.at[lev]), reads(fy.at[lev])]
        above, below = reads(za.at[lev]), reads(zb.at[lev])

        @pl.when(lev < level)
        def _():
            @pl.when(at.has_up)
            def _():
                go_down(lev).wait_recv()
                add_rows(writes(out_buf.at[lev]), [*own, above], rows)

            @pl.when(jnp.logical_not(at.has_up))
            def _():
                add_rows(writes(out_buf.at[lev]), own, rows)

            go_down(lev).start()

        @pl.when(lev > level)
        def _():
            @pl.when(at.has_down)
            def _():
                go_up(lev).wait_recv()
                add_rows(writes(out_buf.at[lev]), [*own, below], rows)

            @pl.when(jnp.logical_not(at.has_down))
            def _():
                add_rows(writes(out_buf.at[lev]), own, rows)

            go_up(lev).start()

        @pl.when(lev == level)
        def _():
            pl.when(at.has_up)(lambda: go_down(lev).wait_recv())
            pl.when(at.has_down)(lambda: go_up(lev).wait_recv())

            @pl.when(at.has_up & at.has_down)
            def _():
                add_rows(writes(out_ref), [*own, above, below], rows)

            @pl.when(jnp.logical_not(at.has_down))
            def _():
                add_rows(writes(out_ref), [*own, above], rows)

            @pl.when(jnp.logical_not(at.has_up))
            def _():
                add_rows(writes(out_ref), [*own, below], rows)

    for s in range(levels + 2):
        if s < levels:
            local(order[s])
        if 0 <= s - 1 < levels:
            halves(order[s - 1])
        if s >= 2:
            column(order[s - 2])
    for lev in range(levels):
        if sibling:
            for sp in range(4):
                to_sibling(lev, sp).wait_send()
        half_y(lev).wait_send()
        half_x(lev).wait_send()
        full_x(lev).wait_send()
        full_y(lev).wait_send()

        @pl.when(lev < level)
        def _():
            go_down(lev).wait_send()

        @pl.when(lev > level)
        def _():
            go_up(lev).wait_send()


def scatter_wide(x, levels, sibling, collective_id):
    dma = pltpu.SemaphoreType.DMA
    blocks = levels * 4
    rows, width = x.shape[1:]
    vmem = pltpu.VMEM
    inside = pl.BlockSpec(memory_space=vmem)
    return pl.pallas_call(
        functools.partial(scatter_kernel, levels, sibling),
        out_shape=jax.ShapeDtypeStruct((rows, width), BF16),
        in_specs=[inside],
        out_specs=inside,
        scratch_shapes=[
            vmem((blocks, rows, width), BF16),
            vmem((blocks if sibling else 1, rows, width), BF16),
            vmem((levels, rows // 2, width), BF16),
            vmem((levels, rows // 2, width), BF16),
        ]
        + [vmem((levels, rows, width), BF16)] * 5
        + [dma((blocks,))] * 2
        + [dma((levels,))] * 12,
        compiler_params=pltpu.CompilerParams(
            collective_id=collective_id,
            has_side_effects=True,
            vmem_limit_bytes=60 * 1024 * 1024,
        ),
    )(x)


def slots_path(
    tokens,
    cotangent,
    lengths,
    routes,
    keep,
    attn_gain,
    w_query,
    w_key,
    w_value,
    w_out,
    ffn_gain,
    w_router,
    shared_gate,
    shared_up,
    shared_down,
    expert_gate,
    expert_up,
    expert_down,
):
    narrow_size = lax.axis_size("narrow")
    narrow_index = lax.axis_index("narrow")
    wide_size = lax.axis_size("wide")
    local_rows = tokens.shape[0]
    model_width = tokens.shape[1]
    head_count = model_width // HEAD_DIM
    row_length = local_rows * narrow_size
    capacity = 8 * (3 * local_rows * TOPK // (16 * wide_size) + 1)
    gathered = (
        lax.all_gather(attn_gain, "narrow", axis=0, tiled=True),
        lax.all_gather(w_query, "narrow", axis=0, tiled=True),
        lax.all_gather(w_key, "narrow", axis=0, tiled=True),
        lax.all_gather(w_value, "narrow", axis=0, tiled=True),
        lax.all_gather(w_out, "narrow", axis=0, tiled=True),
        lax.all_gather(ffn_gain, "narrow", axis=0, tiled=True),
        lax.all_gather(w_router, "narrow", axis=0, tiled=True),
        lax.all_gather(shared_gate, "narrow", axis=0, tiled=True),
        lax.all_gather(shared_up, "narrow", axis=0, tiled=True),
        lax.all_gather(shared_down, "narrow", axis=0, tiled=True),
    )
    attn_scale = gathered[0].astype(jnp.float32)
    query_proj = gathered[1]
    key_proj = gathered[2]
    value_proj = gathered[3]
    output_proj = gathered[4]
    ffn_scale = gathered[5].astype(jnp.float32)
    router_proj = gathered[6]
    common_gate = gathered[7]
    common_upper = gathered[8]
    common_down = gathered[9]
    expert_mats = (expert_gate, expert_up, expert_down)
    routed_gate = expert_mats[0][0]
    routed_upper = expert_mats[1][0]
    routed_down = expert_mats[2][0]
    doc_lens = lengths[0]
    key_index = jnp.arange(row_length, dtype=jnp.int32)
    key_doc, unused = doc_layout(key_index, doc_lens)
    query_index = narrow_index * local_rows + jnp.arange(local_rows, dtype=jnp.int32)
    query_doc, query_pos = doc_layout(query_index, doc_lens)
    cosine, sine_table = rotary_angles(query_pos)
    inputs = tokens.astype(jnp.float32)
    normed, unit_one, scale_one = norm_forward(inputs, attn_scale)
    normed_one = normed.astype(jnp.bfloat16)
    head_shape = (local_rows, head_count, HEAD_DIM)
    query_rows = rotate(matmul(normed_one, query_proj).reshape(head_shape), cosine, sine_table)
    query_rows = (query_rows * HEAD_DIM ** (-0.5)).astype(jnp.bfloat16)
    key_rows = rotate(matmul(normed_one, key_proj).reshape(head_shape), cosine, sine_table).astype(
        jnp.bfloat16
    )
    valued = matmul(normed_one, value_proj).astype(jnp.bfloat16)
    all_keys, all_values = (
        lax.all_gather(key_rows.reshape(local_rows, model_width), "narrow", axis=0, tiled=True),
        lax.all_gather(valued, "narrow", axis=0, tiled=True),
    )
    all_keys = all_keys.reshape(row_length, head_count, HEAD_DIM)
    all_values = all_values.reshape(row_length, head_count, HEAD_DIM)
    block_rows = min(local_rows, 512)
    blocks = local_rows // block_rows
    query_blocks = query_rows.reshape(blocks, block_rows, head_count, HEAD_DIM)
    doc_blocks = query_doc.reshape(blocks, block_rows)
    index_blocks = query_index.reshape(blocks, block_rows)

    def allowed_for(doc_rows, index_rows):
        return (doc_rows[:, None] == key_doc[None, :]) & (key_index[None, :] <= index_rows[:, None])

    def forward_block(map_item):
        return attend_block(
            map_item[0], all_keys, all_values, allowed_for(map_item[1], map_item[2])
        )

    attended, logsum = lax.map(forward_block, (query_blocks, doc_blocks, index_blocks))
    attended = attended.reshape(local_rows, model_width)
    hidden = inputs + matmul(attended, output_proj)
    normed, unit_two, scale_two = norm_forward(hidden, ffn_scale)
    normed_two = normed.astype(jnp.bfloat16)
    logits = matmul(normed_two, router_proj)
    experts = router_proj.shape[1]
    pick_table = (routes[:, :, None] == jnp.arange(experts, dtype=jnp.int32)[None, None, :]).astype(
        jnp.float32
    )
    chosen = jnp.sum(pick_table * logits[:, None, :], axis=2)
    gate_probs = jax.nn.softmax(chosen, axis=1)
    keep_float = keep.astype(jnp.float32)
    mixing = gate_probs * keep_float
    common_gate_vals, common_upper_vals, common_act = expert_forward(
        normed_two, common_gate, common_upper
    )
    shared_out = matmul(common_act, common_down)
    pair_expert = routes.reshape(-1)
    pair_total = pair_expert.shape[0]
    onehot = (pair_expert[:, None] == jnp.arange(experts, dtype=jnp.int32)[None, :]).astype(
        jnp.int32
    )
    earlier = jnp.cumsum(onehot, axis=0) - onehot
    slot_place = jnp.sum(earlier * onehot, axis=1)
    slot_index = pair_expert * capacity + slot_place
    slot_total = experts * capacity
    source = (
        jnp.full((slot_total,), -1, jnp.int32)
        .at[slot_index]
        .set(jnp.arange(pair_total, dtype=jnp.int32))
    )
    filled = source >= 0
    pair_index = jnp.maximum(source, 0)

    def fill_slots(in_rows, row_index):
        taken = jnp.take(in_rows, row_index, axis=0)
        return jnp.where(filled[:, None], taken, jnp.zeros((), in_rows.dtype)).reshape(
            experts, capacity, model_width
        )

    received = lax.all_to_all(
        fill_slots(normed_two, pair_index // TOPK), "wide", split_axis=0, concat_axis=0, tiled=True
    )
    expert_in = lax.all_gather(received, "narrow", axis=0, tiled=True).reshape(-1, model_width)
    routed_gate_vals, routed_upper_vals, routed_act = expert_forward(
        expert_in, routed_gate, routed_upper
    )
    partial_value = matmul(routed_act, routed_down)
    expert_out = lax.psum_scatter(partial_value, "narrow", scatter_dimension=0, tiled=True)
    returned = lax.all_to_all(
        expert_out.astype(jnp.bfloat16).reshape(wide_size, capacity, model_width),
        "wide",
        split_axis=0,
        concat_axis=0,
        tiled=True,
    )
    pair_out = (
        jnp.take(returned.reshape(slot_total, model_width), slot_index, axis=0)
        .astype(jnp.float32)
        .reshape(local_rows, TOPK, model_width)
    )
    routed = jnp.sum(mixing[:, :, None] * pair_out, axis=1)
    output = (hidden + shared_out + routed).astype(jnp.bfloat16)
    grad_output = cotangent.astype(jnp.float32)
    grad_pairs = (
        (mixing[:, :, None] * grad_output[:, None, :])
        .astype(jnp.bfloat16)
        .reshape(pair_total, model_width)
    )
    grad_mixing = jnp.sum(pair_out * grad_output[:, None, :], axis=2)
    grad_received = lax.all_to_all(
        fill_slots(grad_pairs, pair_index), "wide", split_axis=0, concat_axis=0, tiled=True
    )
    grad_expert_out = lax.all_gather(grad_received, "narrow", axis=0, tiled=True).reshape(
        -1, model_width
    )
    grad_expert_in, grad_rgate, grad_rupper, grad_rdown = expert_backward(
        expert_in,
        grad_expert_out,
        routed_gate_vals,
        routed_upper_vals,
        routed_act,
        routed_gate,
        routed_upper,
        routed_down,
    )
    grad_slot_rows = lax.psum_scatter(grad_expert_in, "narrow", scatter_dimension=0, tiled=True)
    expert_grads = (grad_rgate, grad_rupper, grad_rdown)
    grad_back = lax.all_to_all(
        grad_slot_rows.astype(jnp.bfloat16).reshape(wide_size, capacity, model_width),
        "wide",
        split_axis=0,
        concat_axis=0,
        tiled=True,
    )
    grad_pair_rows = jnp.take(
        grad_back.reshape(slot_total, model_width), slot_index, axis=0
    ).astype(jnp.float32)
    grad_normed = jnp.sum(grad_pair_rows.reshape(local_rows, TOPK, model_width), axis=1)
    grad_gates = grad_mixing * keep_float
    grad_chosen = gate_probs * (
        grad_gates - jnp.sum(gate_probs * grad_gates, axis=1, keepdims=True)
    )
    grad_logits = jnp.sum(pick_table * grad_chosen[:, :, None], axis=1).astype(jnp.bfloat16)
    grad_router = matmul_left(normed_two, grad_logits)
    grad_normed = grad_normed + matmul_right(grad_logits, router_proj)
    grad_common_in, grad_cgate, grad_cupper, grad_cdown = expert_backward(
        normed_two,
        cotangent,
        common_gate_vals,
        common_upper_vals,
        common_act,
        common_gate,
        common_upper,
        common_down,
    )
    grad_normed = grad_normed + grad_common_in
    grad_hidden_norm, grad_ffn = norm_backward(grad_normed, unit_two, scale_two, ffn_scale)
    grad_hidden = grad_output + grad_hidden_norm
    grad_branch = grad_hidden.astype(jnp.bfloat16)
    grad_output_proj = matmul_left(attended, grad_branch)
    grad_attended = (
        matmul_right(grad_branch, output_proj)
        .astype(jnp.bfloat16)
        .reshape(blocks, block_rows, head_count, HEAD_DIM)
    )

    def backward_block(running, map_item):
        grad_queries, grad_keys, grad_values = attend_back(
            map_item[0],
            all_keys,
            all_values,
            allowed_for(map_item[1], map_item[2]),
            map_item[3],
            map_item[4],
        )
        return ((running[0] + grad_keys, running[1] + grad_values), grad_queries)

    empty_keys = jnp.zeros((row_length, head_count, HEAD_DIM), jnp.float32)
    sums_kv, grad_query_rows = lax.scan(
        backward_block,
        (empty_keys, empty_keys),
        (query_blocks, doc_blocks, index_blocks, logsum, grad_attended),
    )
    grad_key_own, grad_value_own = (
        lax.psum_scatter(
            sums_kv[0].reshape(row_length, model_width).astype(jnp.bfloat16),
            "narrow",
            scatter_dimension=0,
            tiled=True,
        ).astype(jnp.float32),
        lax.psum_scatter(
            sums_kv[1].reshape(row_length, model_width).astype(jnp.bfloat16),
            "narrow",
            scatter_dimension=0,
            tiled=True,
        ).astype(jnp.float32),
    )
    grad_query_rows = rotate(
        grad_query_rows.reshape(head_shape) * HEAD_DIM ** (-0.5), cosine, -sine_table
    )
    grad_query_rows = grad_query_rows.reshape(local_rows, model_width).astype(jnp.bfloat16)
    grad_key_rows = (
        rotate(grad_key_own.reshape(head_shape), cosine, -sine_table)
        .reshape(local_rows, model_width)
        .astype(jnp.bfloat16)
    )
    grad_value_rows = grad_value_own.astype(jnp.bfloat16)
    grad_query_proj = matmul_left(normed_one, grad_query_rows)
    grad_key_proj = matmul_left(normed_one, grad_key_rows)
    grad_value_proj = matmul_left(normed_one, grad_value_rows)
    grad_normed_one = (
        matmul_right(grad_query_rows, query_proj)
        + matmul_right(grad_key_rows, key_proj)
        + matmul_right(grad_value_rows, value_proj)
    )
    grad_input_norm, grad_attn = norm_backward(grad_normed_one, unit_one, scale_one, attn_scale)
    grad_tokens = grad_hidden + grad_input_norm
    halves = (
        lax.psum_scatter(
            grad_attn.astype(jnp.bfloat16), "narrow", scatter_dimension=0, tiled=True
        ).astype(jnp.float32),
        lax.psum_scatter(
            grad_query_proj.astype(jnp.bfloat16), "narrow", scatter_dimension=0, tiled=True
        ).astype(jnp.float32),
        lax.psum_scatter(
            grad_key_proj.astype(jnp.bfloat16), "narrow", scatter_dimension=0, tiled=True
        ).astype(jnp.float32),
        lax.psum_scatter(
            grad_value_proj.astype(jnp.bfloat16), "narrow", scatter_dimension=0, tiled=True
        ).astype(jnp.float32),
        lax.psum_scatter(
            grad_output_proj.astype(jnp.bfloat16), "narrow", scatter_dimension=0, tiled=True
        ).astype(jnp.float32),
        lax.psum_scatter(
            grad_ffn.astype(jnp.bfloat16), "narrow", scatter_dimension=0, tiled=True
        ).astype(jnp.float32),
        lax.psum_scatter(
            grad_router.astype(jnp.bfloat16), "narrow", scatter_dimension=0, tiled=True
        ).astype(jnp.float32),
        lax.psum_scatter(
            grad_cgate.astype(jnp.bfloat16), "narrow", scatter_dimension=0, tiled=True
        ).astype(jnp.float32),
        lax.psum_scatter(
            grad_cupper.astype(jnp.bfloat16), "narrow", scatter_dimension=0, tiled=True
        ).astype(jnp.float32),
        lax.psum_scatter(
            grad_cdown.astype(jnp.bfloat16), "narrow", scatter_dimension=0, tiled=True
        ).astype(jnp.float32),
    )
    owned = lax.psum(
        (
            halves[0],
            halves[1],
            halves[2],
            halves[3],
            halves[4],
            halves[5],
            halves[6],
            halves[7],
            halves[8],
            halves[9],
        ),
        "wide",
    )
    return (
        output,
        grad_tokens,
        owned[0],
        owned[1],
        owned[2],
        owned[3],
        owned[4],
        owned[5],
        owned[6],
        owned[7],
        owned[8],
        owned[9],
        expert_grads[0][None],
        expert_grads[1][None],
        expert_grads[2][None],
    )


def tokens_path(
    tokens,
    cotangent,
    lengths,
    routes,
    keep,
    attn_gain,
    w_query,
    w_key,
    w_value,
    w_out,
    ffn_gain,
    w_router,
    shared_gate,
    shared_up,
    shared_down,
    expert_gate,
    expert_up,
    expert_down,
):
    core = lax.axis_index("narrow")
    place = lax.axis_index("wide")
    wide_size = lax.axis_size("wide")
    levels = wide_size // 4
    local_rows, width = tokens.shape
    row_length = 2 * local_rows
    part = width // 2
    heads = part // HEAD_DIM
    hidden_part = expert_gate.shape[2]
    slice_width = shared_gate.shape[1] // (2 * wide_size)
    experts = w_router.shape[1]

    def swap(value):
        return lax.ppermute(value, "narrow", [(0, 1), (1, 0)])

    def other_rows(value):
        return jnp.concatenate([value[local_rows:], value[:local_rows]], axis=0)

    def in_order(mine, theirs, axis):
        return jnp.where(
            core == 0,
            jnp.concatenate([mine, theirs], axis=axis),
            jnp.concatenate([theirs, mine], axis=axis),
        )

    def columns(value, which, size):
        return lax.dynamic_slice_in_dim(value, which * size, size, axis=1)

    picks = (routes[:, :, None] == jnp.arange(experts, dtype=jnp.int32)[None, None, :]).astype(
        jnp.int32
    )
    marks = jnp.sum(picks * (1 + keep)[:, :, None], axis=1).astype(BF16)
    all_marks = lax.all_gather(marks, ("wide", "narrow"), axis=0, tiled=True).astype(F32)
    all_grads = gather_wide(cotangent, levels, True, 0).reshape(-1, width)

    first_unit = place * slice_width
    stored = shared_gate.shape[1] // 2
    gate_mine = lax.dynamic_slice_in_dim(shared_gate, core * stored + first_unit, slice_width, 1)
    up_mine = lax.dynamic_slice_in_dim(shared_up, core * stored + first_unit, slice_width, 1)
    gate_send = lax.dynamic_slice_in_dim(
        shared_gate, (1 - core) * stored + first_unit, slice_width, 1
    )
    up_send = lax.dynamic_slice_in_dim(shared_up, (1 - core) * stored + first_unit, slice_width, 1)
    down_slice = lax.dynamic_slice_in_dim(shared_down, first_unit, slice_width, 0)
    gains = jnp.stack([attn_gain, ffn_gain])
    sent = swap(jnp.concatenate([gate_send, up_send, w_router], axis=1))
    gains = in_order(gains, swap(gains), 1).astype(F32)
    attn_scale, ffn_scale = gains[0], gains[1]
    dense = in_order(jnp.concatenate([gate_mine, up_mine, w_router], axis=1), sent, 0)
    gate_slice = dense[:, :slice_width]
    up_slice = dense[:, slice_width : 2 * slice_width]
    router = dense[:, 2 * slice_width :]

    row_tokens = jnp.concatenate([tokens, swap(tokens)], axis=0).astype(F32)
    normed, unit_one, scale_one = norm_forward(row_tokens, attn_scale)
    normed_one = columns(normed.astype(BF16), core, part)
    projections = [w_query, w_key, w_value]
    keep_side = jnp.concatenate([columns(w, core, part) for w in projections], axis=1)
    send_side = jnp.concatenate([columns(w, 1 - core, part) for w in projections], axis=1)
    arrived = swap(matmul(normed_one, send_side).astype(BF16))
    qkv = matmul(normed_one, keep_side) + other_rows(arrived).astype(F32)
    index = jnp.arange(local_rows, dtype=jnp.int32)
    index = jnp.concatenate([core * local_rows + index, (1 - core) * local_rows + index])
    docs, positions = doc_layout(index, lengths[0])
    allowed = (docs[:, None] == docs[None, :]) & (index[None, :] <= index[:, None])
    cosine, sine_table = rotary_angles(positions)
    head_shape = (row_length, heads, HEAD_DIM)
    query_rows = rotate(qkv[:, :part].reshape(head_shape), cosine, sine_table)
    query_rows = (query_rows * HEAD_DIM ** (-0.5)).astype(BF16)
    key_rows = rotate(qkv[:, part : 2 * part].reshape(head_shape), cosine, sine_table).astype(BF16)
    value_rows = qkv[:, 2 * part :].astype(BF16).reshape(head_shape)
    attended, logsum = attend_block(query_rows, key_rows, value_rows, allowed)
    attended = attended.reshape(row_length, part)
    branch = matmul(attended, w_out)
    arrived = swap(branch[local_rows:].astype(BF16))
    inputs = row_tokens[:local_rows]
    hidden = inputs + branch[:local_rows] + arrived.astype(F32)
    normed, unit_two, scale_two = norm_forward(hidden, ffn_scale)
    normed_two = normed.astype(BF16)
    all_rows = gather_wide(normed_two, levels, True, 1).reshape(-1, width)

    used = hidden_part + slice_width
    full = -(-(used + experts) // 128) * 128

    def pad(value, size, axis):
        extra = list(value.shape)
        extra[axis] = size - value.shape[axis]
        return jnp.concatenate([value, jnp.zeros(extra, value.dtype)], axis=axis)

    gate_all = pad(jnp.concatenate([expert_gate[0], gate_slice, router], axis=1), full, 1)
    up_all = pad(jnp.concatenate([expert_up[0], up_slice], axis=1), full, 1)
    down_all = pad(jnp.concatenate([expert_down[0], down_slice], axis=0), full, 0)
    gate_vals = matmul(all_rows, gate_all)
    upper = matmul(all_rows, up_all)
    back = matmul_right(all_grads, down_all)
    logits = gate_vals[:, used : used + experts]
    routed = all_marks > 0.0
    masked = jnp.where(routed, logits, MASKED)
    weights = jnp.where(routed, jnp.exp(masked - jnp.max(masked, axis=1, keepdims=True)), 0.0)
    gates = weights / jnp.sum(weights, axis=1, keepdims=True)
    mix_all = gates * (all_marks > 1.5)
    mix = jnp.sum(
        jnp.where(jnp.arange(experts)[None, :] == place, mix_all, 0.0), axis=1, keepdims=True
    )
    unit = jnp.arange(full)[None, :]
    scale = jnp.where(unit < hidden_part, mix, jnp.where(unit < used, 1.0, 0.0))
    act_vals, slope_vals = silu_parts(gate_vals)
    active = act_vals * upper
    grad_act = scale * back
    grad_gate = (grad_act * upper * slope_vals).astype(BF16)
    grad_upper = (grad_act * act_vals).astype(BF16)
    mixed = (scale * active).astype(BF16)
    grad_mix = jnp.sum(jnp.where(unit < hidden_part, active * back, 0.0), axis=1)
    grad_mix = lax.all_to_all(
        grad_mix.reshape(wide_size, 2, local_rows), "wide", split_axis=0, concat_axis=0, tiled=True
    )
    pick_core = jnp.where(core == 0, grad_mix[:, 0], grad_mix[:, 1])
    send_core = jnp.where(core == 0, grad_mix[:, 1], grad_mix[:, 0])
    grad_mix = (pick_core + swap(send_core)).T
    block_shape = (2 * wide_size, local_rows, width)
    grad_rows = matmul_right(grad_gate, gate_all) + matmul_right(grad_upper, up_all)
    grad_rows = scatter_wide(grad_rows.astype(BF16).reshape(block_shape), levels, True, 2)
    expert_out = scatter_wide(matmul(mixed, down_all).astype(BF16).reshape(block_shape), levels, True, 3)
    output = (hidden + expert_out.astype(F32)).astype(BF16)
    grad_gate_all = matmul_left(all_rows, grad_gate)
    grad_up_all = matmul_left(all_rows, grad_upper)
    grad_down_all = matmul_left(mixed, all_grads)

    marks = marks.astype(F32)
    routed = marks > 0.0
    logits = matmul(normed_two, router)
    masked = jnp.where(routed, logits, MASKED)
    weights = jnp.where(routed, jnp.exp(masked - jnp.max(masked, axis=1, keepdims=True)), 0.0)
    gates = weights / jnp.sum(weights, axis=1, keepdims=True)
    grad_gates = jnp.where(marks > 1.5, grad_mix, 0.0)
    grad_logits = gates * (grad_gates - jnp.sum(gates * grad_gates, axis=1, keepdims=True))
    grad_logits = grad_logits.astype(BF16)
    grad_router = matmul_left(normed_two, grad_logits)
    grad_normed = grad_rows.astype(F32) + matmul_right(grad_logits, router)
    grad_hidden_norm, grad_ffn = norm_backward(grad_normed, unit_two, scale_two, ffn_scale)
    grad_hidden = cotangent.astype(F32) + grad_hidden_norm
    grad_branch = grad_hidden.astype(BF16)
    row_branch = jnp.concatenate([grad_branch, swap(grad_branch)], axis=0)

    grad_w_out = matmul_left(attended, row_branch)
    grad_attended = matmul_right(row_branch, w_out).astype(BF16).reshape(head_shape)
    grad_queries, grad_keys, grad_values = attend_back(
        query_rows, key_rows, value_rows, allowed, logsum, grad_attended
    )
    grad_queries = rotate(grad_queries * HEAD_DIM ** (-0.5), cosine, -sine_table)
    grad_keys = rotate(grad_keys, cosine, -sine_table)
    mine = jnp.stack([grad_queries, grad_keys, grad_values]).reshape(3, row_length, part)
    mine = mine.astype(BF16)
    theirs = swap(mine)
    theirs = jnp.concatenate([theirs[:, local_rows:], theirs[:, :local_rows]], axis=1)
    grad_qkv = in_order(mine, theirs, 2)
    grad_dense = jnp.stack(
        [matmul_left(normed_one, grad_qkv[k]) for k in range(3)] + [grad_w_out]
    ).astype(BF16)
    grad_part = sum(matmul_right(grad_qkv[k], projections[k]) for k in range(3))
    grad_normed_one = in_order(
        grad_part[:local_rows], swap(grad_part[local_rows:].astype(BF16)).astype(F32), 1
    )
    grad_input_norm, grad_attn = norm_backward(
        grad_normed_one, unit_one[:local_rows], scale_one[:local_rows], attn_scale
    )
    grad_tokens = grad_hidden + grad_input_norm

    small = jnp.concatenate([grad_attn[:, None], grad_ffn[:, None], grad_router], axis=1)
    small_mine = lax.dynamic_slice_in_dim(small, core * part, part, 0)
    small_send = lax.dynamic_slice_in_dim(small, (1 - core) * part, part, 0)
    small = (small_mine + swap(small_send)).astype(BF16)
    shared_t = jnp.concatenate(
        [
            grad_gate_all[:, hidden_part:used].astype(BF16),
            grad_up_all[:, hidden_part:used].astype(BF16),
        ],
        axis=1,
    )
    shared_mine = lax.dynamic_slice_in_dim(shared_t, core * part, part, 0)
    shared_send = lax.dynamic_slice_in_dim(shared_t, (1 - core) * part, part, 0)
    shared_pair = in_order(shared_mine[None], swap(shared_send)[None], 0)
    shared_down_grad = grad_down_all[hidden_part:used].astype(BF16)
    flat = jnp.concatenate(
        [shared_pair.reshape(-1), shared_down_grad.reshape(-1), small.reshape(-1)]
    )
    unit_rows = 32
    extra_rows = -(-flat.shape[0] // (width * unit_rows)) * unit_rows
    flat = jnp.concatenate([flat, jnp.zeros((extra_rows * width - flat.shape[0],), BF16)])
    sum_rows = 4 * part // wide_size
    summed = scatter_wide(grad_dense.reshape(wide_size, sum_rows, width), levels, False, 4)
    everything = gather_wide(
        jnp.concatenate([summed, flat.reshape(extra_rows, width)], axis=0), levels, False, 5
    ).astype(F32)
    owned = everything[:, :sum_rows].reshape(4, part, width)
    flat = everything[:, sum_rows:].reshape(wide_size, -1)
    size = 2 * part * 2 * slice_width
    pair = flat[:, :size].reshape(wide_size, 2, part, 2, slice_width)
    pair = pair.transpose(3, 2, 1, 0, 4).reshape(2, part, 2 * wide_size * slice_width)
    down_size = slice_width * width
    own_down = flat[:, size : size + down_size].reshape(wide_size * slice_width, width)
    small = jnp.sum(flat[:, size + down_size : size + down_size + small.size], axis=0)
    small = small.reshape(part, 2 + experts)
    return (
        output,
        grad_tokens,
        small[:, 0],
        owned[0],
        owned[1],
        owned[2],
        owned[3],
        small[:, 1],
        small[:, 2:],
        pair[0],
        pair[1],
        own_down,
        grad_gate_all[None, :, :hidden_part],
        grad_up_all[None, :, :hidden_part],
        grad_down_all[None, :hidden_part],
    )


def per_device(*arrays):
    tokens = arrays[0]
    gathered = lax.axis_size("wide") * lax.axis_size("narrow") * tokens.size * 2
    fits = gathered <= 12 * 1024 * 1024
    return (tokens_path if fits else slots_path)(*arrays)


def solution(mesh):
    in_specs = (
        P(("wide", "narrow"), None),
        P(("wide", "narrow"), None),
        P("wide", None),
        P(("wide", "narrow"), None),
        P(("wide", "narrow"), None),
        P("narrow"),
        P("narrow", None),
        P("narrow", None),
        P("narrow", None),
        P("narrow", None),
        P("narrow"),
        P("narrow", None),
        P("narrow", None),
        P("narrow", None),
        P("narrow", None),
        P("wide", None, "narrow"),
        P("wide", None, "narrow"),
        P("wide", "narrow", None),
    )
    out_specs = (
        P(("wide", "narrow"), None),
        P(("wide", "narrow"), None),
        P("narrow"),
        P("narrow", None),
        P("narrow", None),
        P("narrow", None),
        P("narrow", None),
        P("narrow"),
        P("narrow", None),
        P("narrow", None),
        P("narrow", None),
        P("narrow", None),
        P("wide", None, "narrow"),
        P("wide", None, "narrow"),
        P("wide", "narrow", None),
    )
    return jax.shard_map(
        per_device, mesh=mesh, in_specs=in_specs, out_specs=out_specs, check_vma=False
    )
```

```python
import functools
import math

import jax
import jax.numpy as jnp
from jax import lax
from jax.experimental import pallas as pl
from jax.experimental.pallas import tpu as pltpu
from jax.sharding import PartitionSpec as P

HEAD_DIM = 128
TOPK = 7


EPS = 1e-06
MASKED = -1e30


def matmul(left, right):
    return jnp.dot(left, right, preferred_element_type=jnp.float32)


def matmul_left(left, right):
    return lax.dot_general(
        left, right, (((0,), (0,)), ((), ())), preferred_element_type=jnp.float32
    )


def matmul_right(left, right):
    return lax.dot_general(
        left, right, (((1,), (1,)), ((), ())), preferred_element_type=jnp.float32
    )


def doc_layout(positions, doc_lens):
    doc_ends = jnp.cumsum(doc_lens)
    passed = (positions[:, None] >= doc_ends[None, :]).astype(jnp.int32)
    doc_ids = jnp.sum(passed, axis=1)
    return (doc_ids, positions - jnp.sum(passed * doc_lens[None, :], axis=1))


def rotary_angles(positions):
    half_dim = HEAD_DIM // 2
    inverse = jnp.exp(
        jnp.arange(half_dim, dtype=jnp.float32) * (-2.0 * math.log(10000.0) / HEAD_DIM)
    )
    angles = positions.astype(jnp.float32)[:, None] * inverse[None, :]
    return (jnp.cos(angles), jnp.sin(angles))


def rotate(values, cosine, sine_table):
    half_dim = values.shape[-1] // 2
    lower_half = values[..., :half_dim]
    upper_half = values[..., half_dim:]
    cos_b = cosine[:, None, :]
    sin_b = sine_table[:, None, :]
    return jnp.concatenate(
        [lower_half * cos_b - upper_half * sin_b, upper_half * cos_b + lower_half * sin_b], axis=-1
    )


def norm_forward(values, gain_vec):
    row_scale = lax.rsqrt(jnp.mean(values * values, axis=-1, keepdims=True) + EPS)
    unit_rows = values * row_scale
    return (unit_rows * gain_vec, unit_rows, row_scale)


def norm_backward(grad_rows, unit_rows, row_scale, gain_vec):
    scaled = grad_rows * gain_vec
    grad_gain = jnp.sum(grad_rows * unit_rows, axis=0)
    grad_input = row_scale * (
        scaled - unit_rows * jnp.mean(scaled * unit_rows, axis=-1, keepdims=True)
    )
    return (grad_input, grad_gain)


def silu_parts(gate_vals):
    sigmoid_vals = jax.nn.sigmoid(gate_vals)
    return (gate_vals * sigmoid_vals, sigmoid_vals * (1.0 + gate_vals * (1.0 - sigmoid_vals)))


def expert_forward(in_rows, gate_mat, upper_mat):
    gate_vals = matmul(in_rows, gate_mat)
    upper = matmul(in_rows, upper_mat)
    act_vals, unused = silu_parts(gate_vals)
    return (gate_vals, upper, (act_vals * upper).astype(jnp.bfloat16))


def expert_backward(in_rows, grad_rows, gate_vals, upper, active, gate_mat, upper_mat, down_mat):
    grad_act = matmul_right(grad_rows, down_mat)
    act_vals, slope_vals = silu_parts(gate_vals)
    grad_gate = (grad_act * upper * slope_vals).astype(jnp.bfloat16)
    grad_upper = (grad_act * act_vals).astype(jnp.bfloat16)
    grad_down_mat = matmul_left(active, grad_rows)
    grad_gate_mat = matmul_left(in_rows, grad_gate)
    grad_upper_mat = matmul_left(in_rows, grad_upper)
    grad_input = matmul_right(grad_gate, gate_mat) + matmul_right(grad_upper, upper_mat)
    return (grad_input, grad_gate_mat, grad_upper_mat, grad_down_mat)


def attend_block(queries, keys_all, values_all, allowed):
    scores = jnp.einsum("qhd,khd->hqk", queries, keys_all, preferred_element_type=jnp.float32)
    masked = jnp.where(allowed[None], scores, MASKED)
    row_max = jnp.max(masked, axis=-1, keepdims=True)
    weights = jnp.exp(masked - row_max)
    row_total = jnp.sum(weights, axis=-1, keepdims=True)
    prob_rows = (weights / row_total).astype(jnp.bfloat16)
    attended = jnp.einsum("hqk,khd->qhd", prob_rows, values_all, preferred_element_type=jnp.float32)
    return (attended.astype(jnp.bfloat16), (row_max + jnp.log(row_total))[..., 0])


def attend_back(queries, keys_all, values_all, allowed, logsum, grad_attended):
    scores = jnp.einsum("qhd,khd->hqk", queries, keys_all, preferred_element_type=jnp.float32)
    masked = jnp.where(allowed[None], scores, MASKED)
    prob_rows = jnp.exp(masked - logsum[..., None])
    grad_probs = jnp.einsum(
        "qhd,khd->hqk", grad_attended, values_all, preferred_element_type=jnp.float32
    )
    row_delta = jnp.sum(prob_rows * grad_probs, axis=-1, keepdims=True)
    grad_scores = (prob_rows * (grad_probs - row_delta)).astype(jnp.bfloat16)
    grad_queries = jnp.einsum(
        "hqk,khd->qhd", grad_scores, keys_all, preferred_element_type=jnp.float32
    )
    grad_keys = jnp.einsum("hqk,qhd->khd", grad_scores, queries, preferred_element_type=jnp.float32)
    grad_values = jnp.einsum(
        "hqk,qhd->khd",
        prob_rows.astype(jnp.bfloat16),
        grad_attended,
        preferred_element_type=jnp.float32,
    )
    return (grad_queries, grad_keys, grad_values)


MESH_ID = pl.DeviceIdType.MESH
BF16 = jnp.bfloat16
F32 = jnp.float32


class Place:
    def __init__(self, levels):
        self.levels = levels
        wide = lax.axis_index("wide")
        self.core = lax.axis_index("narrow")
        self.level = wide // 4
        self.spot = lax.rem(wide, 4)
        self.across = self.spot + 1 - 2 * lax.rem(self.spot, 2)
        self.along = lax.rem(self.spot + 2, 4)
        self.corner = 3 - self.spot
        self.has_up = self.level < levels - 1
        self.has_down = self.level > 0

    def choose(self, values):
        result = jnp.int32(values[0])
        for k in range(1, self.levels):
            result = jnp.where(self.level == k, values[k], result)
        return result

    def device(self, level, spot, core=None):
        return {"wide": level * 4 + spot, "narrow": self.core if core is None else core}

    def enter(self, sibling):
        barrier = pltpu.get_barrier_semaphore()

        def greet(device):
            pl.semaphore_signal(barrier, inc=1, device_id=device, device_id_type=MESH_ID)

        greet(self.device(self.level, self.across))
        greet(self.device(self.level, self.along))
        if sibling:
            greet(self.device(self.level, self.spot, 1 - self.core))

        @pl.when(self.has_up)
        def _():
            greet(self.device(self.level + 1, self.spot))

        @pl.when(self.has_down)
        def _():
            greet(self.device(self.level - 1, self.spot))

        both = jnp.where(self.has_up, 1, 0) + jnp.where(self.has_down, 1, 0)
        pl.semaphore_wait(barrier, both + (3 if sibling else 2))


def remote(src, dst, send, recv, device):
    return pltpu.make_async_remote_copy(
        src_ref=src,
        dst_ref=dst,
        send_sem=send,
        recv_sem=recv,
        device_id=device,
        device_id_type=MESH_ID,
    )


class Gather:
    NAMES = ("up", "dn", "x", "y", "cx", "cy", "rz", "rx", "ry", "rcx", "rcy")

    def __init__(self, at, sibling, pairs, sems):
        self.at, self.sibling, self.pairs = at, sibling, pairs
        self.own_sem = sems[0]
        self.sems = dict(zip(self.NAMES, sems[1:12]))
        self.send_n, self.recv_n = sems[12:]
        self.order = self.visits()

    @staticmethod
    def scratch(levels, arrays):
        dma = pltpu.SemaphoreType.DMA
        return (
            [dma((arrays,))]
            + [dma((arrays, levels))] * 11
            + [dma((arrays, levels * 4))] * 2
        )

    def visits(self):
        at = self.at
        table = [
            sorted(range(at.levels), key=lambda lev: (abs(lev - here), lev))
            for here in range(at.levels)
        ]
        return [at.choose([row[k] for row in table]) for k in range(at.levels)]

    def block(self, n, lev, sp, core=None):
        ref = self.pairs[n][1]
        if self.sibling:
            return ref.at[(lev * 4 + sp) * 2 + (self.at.core if core is None else core)]
        return ref.at[lev * 4 + sp]

    def each(self, send, recv, lev, sp, device, part=None, own=False):
        copies = []
        for n, (x_ref, _) in enumerate(self.pairs):
            dst = self.block(n, lev, sp)
            src = x_ref if own else dst
            if part is not None:
                half = x_ref.shape[0] // 2
                src = src.at[pl.ds(part * half, half)]
                dst = dst.at[pl.ds(part * half, half)]
            copies.append(
                remote(src, dst, self.sems[send].at[n, lev], self.sems[recv].at[n, lev], device)
            )
        return copies

    def up(self, lev, own=False):
        at = self.at
        return self.each("up", "rz", lev, at.spot, at.device(at.level + 1, at.spot), own=own)

    def down(self, lev, own=False):
        at = self.at
        return self.each("dn", "rz", lev, at.spot, at.device(at.level - 1, at.spot), own=own)

    def over_x(self, lev, sp, own=False):
        at = self.at
        return self.each("x", "rx", lev, sp, at.device(at.level, at.across), own=own)

    def over_y(self, lev, sp, own=False):
        at = self.at
        return self.each("y", "ry", lev, sp, at.device(at.level, at.along), own=own)

    def corner_y(self, lev, sp):
        at = self.at
        return self.each("cy", "rcy", lev, sp, at.device(at.level, at.along), part=0)

    def corner_x(self, lev, sp):
        at = self.at
        return self.each("cx", "rcx", lev, sp, at.device(at.level, at.across), part=1)

    def near(self, lev, sp, core=None, own=False):
        at = self.at
        copies = []
        for n, (x_ref, _) in enumerate(self.pairs):
            dst = self.block(n, lev, sp, core)
            sems = self.send_n.at[n, lev * 4 + sp], self.recv_n.at[n, lev * 4 + sp]
            device = at.device(at.level, at.spot, 1 - at.core)
            copies.append(remote(x_ref if own else dst, dst, *sems, device))
        return copies

    def own_copies(self):
        at = self.at
        return [
            pltpu.make_async_copy(x_ref, self.block(n, at.level, at.spot), self.own_sem.at[n])
            for n, (x_ref, _) in enumerate(self.pairs)
        ]

    def take_own(self):
        for copy in self.own_copies():
            copy.wait()

    def begin(self):
        at = self.at
        pl.when(at.has_up)(lambda: start(self.up(at.level, own=True)))
        pl.when(at.has_down)(lambda: start(self.down(at.level, own=True)))
        start(self.over_x(at.level, at.spot, own=True))
        start(self.over_y(at.level, at.spot, own=True))
        if self.sibling:
            start(self.near(at.level, at.spot, own=True))
        start(self.own_copies())

    def take_column(self, lev):
        at = self.at
        arrived(self.up(lev))
        pl.when((lev < at.level) & at.has_up)(lambda: start(self.up(lev)))
        pl.when((lev > at.level) & at.has_down)(lambda: start(self.down(lev)))
        start(self.over_x(lev, at.spot))
        start(self.over_y(lev, at.spot))
        if self.sibling:
            start(self.near(lev, at.spot))

    def take_x(self, lev):
        at = self.at
        arrived(self.over_x(lev, at.across))
        start(self.corner_y(lev, at.across))
        if self.sibling:
            start(self.near(lev, at.across))

    def take_y(self, lev):
        at = self.at
        arrived(self.over_y(lev, at.along))
        start(self.corner_x(lev, at.along))
        if self.sibling:
            start(self.near(lev, at.along))

    def take_corner(self, lev):
        at = self.at
        arrived(self.corner_y(lev, at.corner))
        arrived(self.corner_x(lev, at.corner))
        if self.sibling:
            start(self.near(lev, at.corner))

    def take_near(self, lev, sp):
        arrived(self.near(lev, sp, 1 - self.at.core))

    def steps(self):
        levels, steps = self.at.levels, []
        for s in range(1, levels + 2):
            if s < levels:
                steps.append(lambda lev=self.order[s]: self.take_column(lev))
            if s - 1 < levels:
                steps.append(lambda lev=self.order[s - 1]: self.take_x(lev))
                steps.append(lambda lev=self.order[s - 1]: self.take_y(lev))
            if s >= 2:
                steps.append(lambda lev=self.order[s - 2]: self.take_corner(lev))
        return steps

    def finish(self, near=True):
        at = self.at
        if near:
            self.take_own()
        for lev in range(at.levels):
            pl.when(at.has_up & (lev <= at.level))(lambda lev=lev: sent(self.up(lev)))
            pl.when(at.has_down & (lev >= at.level))(lambda lev=lev: sent(self.down(lev)))
            sent(self.over_x(lev, at.spot))
            sent(self.over_y(lev, at.spot))
            sent(self.corner_y(lev, at.across))
            sent(self.corner_x(lev, at.along))
            if self.sibling:
                for sp in range(4):
                    sent(self.near(lev, sp))
                    if near:
                        self.take_near(lev, sp)


def start(copies):
    for copy in copies:
        copy.start()


def arrived(copies):
    for copy in copies:
        copy.wait_recv()


def sent(copies):
    for copy in copies:
        copy.wait_send()


def gather_kernel(levels, sibling, arrays, *refs):
    x_refs, out_refs, sems = refs[:arrays], refs[arrays : 2 * arrays], refs[2 * arrays :]
    at = Place(levels)
    at.enter(sibling)
    gather = Gather(at, sibling, list(zip(x_refs, out_refs)), sems)
    gather.begin()
    for step in gather.steps():
        step()
    gather.finish()


def gather_wide(arrays, levels, sibling, collective_id):
    blocks = levels * 4 * (2 if sibling else 1)
    anywhere = pl.BlockSpec(memory_space=pl.ANY)
    return pl.pallas_call(
        functools.partial(gather_kernel, levels, sibling, len(arrays)),
        out_shape=[jax.ShapeDtypeStruct((blocks, *x.shape), x.dtype) for x in arrays],
        in_specs=[anywhere] * len(arrays),
        out_specs=[anywhere] * len(arrays),
        scratch_shapes=Gather.scratch(levels, len(arrays)),
        compiler_params=pltpu.CompilerParams(
            collective_id=collective_id, has_side_effects=True
        ),
    )(*arrays)


def dot_nn(left, right):
    return lax.dot_general(left, right, (((1,), (0,)), ((), ())), preferred_element_type=F32)


def dot_nt(left, right):
    return lax.dot_general(left, right, (((1,), (1,)), ((), ())), preferred_element_type=F32)


def experts_kernel(
    levels, sizes, x_ref, grads_ref, marks_ref, gate_ref, down_ref,
    rows_ref, mixed_ref, act_ref, back_ref, out_ref, gm_ref,
    x_buf, g_buf, mark_buf, cu_buf, g_val, mixed_buf, act_buf, back_buf, out_buf, gm_buf, mark_t,
    in_sem, out_sem, gm_val, *sems,
):
    hidden, used, full = sizes
    at = Place(levels)
    at.enter(True)
    gather = Gather(at, True, [(x_ref, rows_ref)], sems)
    gather.begin()
    place = at.level * 4 + at.spot
    units = 4 * levels
    plan = [(0, 0)]
    for s in range(1, levels + 2):
        if s < levels:
            plan.append((s, 0))
        if s - 1 < levels:
            plan += [(s - 1, 1), (s - 1, 2)]
        if s >= 2:
            plan.append((s - 2, 3))
    rows = x_ref.shape[0]
    batch = 2 * rows

    def pick(k, values):
        result = jnp.int32(0) + values[0]
        for j in range(1, len(values)):
            result = jnp.where(k == j, values[j], result)
        return result

    def unit(k):
        visit = pick(k, [v for v, _ in plan])
        kind = pick(k, [t for _, t in plan])
        lev = pick(visit, gather.order)
        sp = pick(kind, [at.spot, at.across, at.along, at.corner])
        return lev, sp, kind

    def loads(k, first):
        slot = lax.rem(k, 2)
        blocks = pl.ds(first, 2)
        return [
            pltpu.make_async_copy(rows_ref.at[blocks], x_buf.at[slot], in_sem.at[slot, 0]),
            pltpu.make_async_copy(grads_ref.at[blocks], g_buf.at[slot], in_sem.at[slot, 1]),
            pltpu.make_async_copy(marks_ref.at[blocks], mark_buf.at[slot], in_sem.at[slot, 2]),
        ]

    def stores(k, first):
        slot = lax.rem(k, 2)
        rng = pl.ds(pl.multiple_of(first * rows, batch), batch)
        pairs = [(mixed_buf, mixed_ref), (act_buf, act_ref), (back_buf, back_ref), (out_buf, out_ref)]
        return [
            pltpu.make_async_copy(buf.at[slot], ref.at[rng], out_sem.at[slot, n])
            for n, (buf, ref) in enumerate(pairs)
        ]

    def serve(k):
        lev, sp, kind = unit(k)
        pl.when(kind == 0)(lambda: gather.take_column(lev))
        pl.when(kind == 1)(lambda: gather.take_x(lev))
        pl.when(kind == 2)(lambda: gather.take_y(lev))
        pl.when(kind == 3)(lambda: gather.take_corner(lev))

    def fetch(k):
        lev, sp, _ = unit(k)
        gather.take_near(lev, sp)
        start(loads(k, (lev * 4 + sp) * 2))

    def lanes(n):
        return lax.broadcasted_iota(jnp.int32, (batch, 128), 1) + n * 128

    def mixing():
        tail = full // 128 - 1
        mark = mark_t[...]
        masked = jnp.where(mark > 0.5, cu_buf[:, full - 128 : full], MASKED)
        top = jnp.max(masked, axis=1, keepdims=True)
        weight = jnp.where(mark > 0.5, jnp.exp(masked - top), 0.0)
        mine = jnp.where((lanes(tail) == used + place) & (mark > 1.5), weight, 0.0)
        return jnp.sum(mine, axis=1, keepdims=True) / jnp.sum(weight, axis=1, keepdims=True)

    def elementwise(slot):
        mix = jnp.broadcast_to(mixing(), (batch, 128))
        total = jnp.zeros((batch, 128), F32)
        for n in range(full // 128):
            cols = slice(n * 128, (n + 1) * 128)
            up_cols = slice(full + n * 128, full + (n + 1) * 128)
            gate, upper, back = cu_buf[:, cols], cu_buf[:, up_cols], g_val[:, cols]
            whole = (n + 1) * 128 <= hidden
            scale = mix
            if not whole:
                scale = jnp.where(lanes(n) < hidden, mix, jnp.where(lanes(n) < used, 1.0, 0.0))
            sig = jax.nn.sigmoid(gate)
            act = gate * sig
            active = act * upper
            grad_act = scale * back
            slope = sig * (1.0 + gate * (1.0 - sig))
            mixed_buf[slot, :, cols] = (scale * active).astype(BF16)
            act_buf[slot, :, cols] = (grad_act * upper * slope).astype(BF16)
            act_buf[slot, :, up_cols] = (grad_act * act).astype(BF16)
            term = active * back
            total = total + (term if whole else jnp.where(lanes(n) < hidden, term, 0.0))
        gm_buf[...] = total

    def compute(k):
        lev, sp, _ = unit(k)
        first = (lev * 4 + sp) * 2
        slot = lax.rem(k, 2)
        for copy in loads(k, first):
            copy.wait()
        x = x_buf[slot].reshape(batch, -1)
        cu_buf[...] = dot_nn(x, gate_ref[...])
        g_val[...] = dot_nt(g_buf[slot].reshape(batch, -1), down_ref[...])
        for n in range(2):
            marks = mark_buf[slot, n]
            above = jnp.zeros((used - (full - 128), 128), F32)
            below = jnp.zeros((full - used - marks.shape[0], 128), F32)
            mark_t[pl.ds(n * rows, rows), :] = jnp.transpose(jnp.concatenate([above, marks, below], axis=0))

        @pl.when(k >= 2)
        def _():
            for copy in stores(k, 0):
                copy.wait()

        elementwise(slot)
        back_buf[slot] = dot_nt(act_buf[slot], gate_ref[...]).astype(BF16)
        out_buf[slot] = dot_nn(mixed_buf[slot], down_ref[...]).astype(BF16)
        for n in range(2):
            gm = jnp.transpose(gm_buf[pl.ds(n * rows, rows), :])
            gm_val[pl.ds(first + n, 1), :] = jnp.sum(gm, axis=0, keepdims=True)
        start(stores(k, first))

    gather.take_own()
    fetch(0)

    def loop(k, carry):
        @pl.when((k > 0) & (k + 1 < units))
        def _():
            serve(k + 1)
            fetch(k + 1)

        compute(k)

        @pl.when(k == 0)
        def _():
            serve(1)
            fetch(1)

        return carry

    lax.fori_loop(0, units, loop, 0)
    gm_ref[...] = gm_val[...]
    for k in (0, 1):
        for copy in stores(k, 0):
            copy.wait()
    gather.finish(near=False)


def experts_rows(x, grads, marks, gate_up, down, hidden, used, levels, collective_id):
    rows, width = x.shape
    full = down.shape[0]
    blocks = 8 * levels
    total = blocks * rows
    dma = pltpu.SemaphoreType.DMA
    vmem = pltpu.VMEM
    anywhere = pl.BlockSpec(memory_space=pl.ANY)
    inside = pl.BlockSpec(memory_space=vmem)
    shape = jax.ShapeDtypeStruct
    batch = 2 * rows
    return pl.pallas_call(
        functools.partial(experts_kernel, levels, (hidden, used, full)),
        out_shape=[
            shape((blocks, rows, width), BF16),
            shape((total, full), BF16),
            shape((total, 2 * full), BF16),
            shape((total, width), BF16),
            shape((total, width), BF16),
            shape((blocks, rows), F32),
        ],
        in_specs=[anywhere, anywhere, anywhere, inside, inside],
        out_specs=[anywhere] * 5 + [inside],
        scratch_shapes=[
            vmem((2, 2, rows, width), BF16),
            vmem((2, 2, rows, width), BF16),
            vmem((2, 2, *marks.shape[1:]), F32),
            vmem((batch, 2 * full), F32),
            vmem((batch, full), F32),
            vmem((2, batch, full), BF16),
            vmem((2, batch, 2 * full), BF16),
            vmem((2, batch, width), BF16),
            vmem((2, batch, width), BF16),
            vmem((batch, 128), F32),
            vmem((batch, 128), F32),
            dma((2, 3)),
            dma((2, 4)),
            vmem((blocks, rows), F32),
        ]
        + Gather.scratch(levels, 1),
        compiler_params=pltpu.CompilerParams(
            collective_id=collective_id,
            has_side_effects=True,
            vmem_limit_bytes=56 * 1024 * 1024,
        ),
    )(x, grads, marks, gate_up, down)


def destinations(levels):
    return [
        sorted(range(levels), key=lambda to: (-abs(to - here), -to)) for here in range(levels)
    ]


def add_rows(write, sources, rows):
    step = 16

    def body(k, carry):
        r = pl.ds(pl.multiple_of(k * step, step), step)
        total = sources[0](r)
        for source in sources[1:]:
            total = total + source(r)
        write(r, total)
        return carry

    lax.fori_loop(0, rows // step, body, 0)


def reads(ref):
    return lambda r: ref[r, :].astype(F32)


def writes(ref):
    def write(r, total):
        ref[r, :] = total.astype(ref.dtype)

    return write


def scatter_kernel(levels, sibling, x_ref, out_ref, acc, near, hx, hy, fx, fy, out_buf, za, zb, *sems):
    send_n, recv_n = sems[:2]
    send_hx, send_hy, send_fx, send_fy, send_up, send_dn = sems[2:8]
    recv_hx, recv_hy, recv_fx, recv_fy, recv_za, recv_zb = sems[8:]
    at = Place(levels)
    level, spot, core = at.level, at.spot, at.core
    across, along, corner = at.across, at.along, at.corner
    rows = out_ref.shape[0]
    half = rows // 2
    first, second = pl.ds(0, half), pl.ds(half, half)
    at.enter(sibling)
    table = destinations(levels)

    order = [at.choose([row[s] for row in table]) for s in range(levels)]

    def to_sibling(lev, sp):
        b = lev * 4 + sp
        src = x_ref.at[b * 2 + 1 - core]
        return remote(
            src, near.at[b], send_n.at[b], recv_n.at[b], at.device(level, spot, 1 - core)
        )

    def half_y(lev):
        src = acc.at[lev * 4 + corner].at[first]
        return remote(
            src, hy.at[lev], send_hy.at[lev], recv_hy.at[lev], at.device(level, along)
        )

    def half_x(lev):
        src = acc.at[lev * 4 + corner].at[second]
        return remote(
            src, hx.at[lev], send_hx.at[lev], recv_hx.at[lev], at.device(level, across)
        )

    def full_x(lev):
        src = acc.at[lev * 4 + across]
        return remote(
            src, fx.at[lev], send_fx.at[lev], recv_fx.at[lev], at.device(level, across)
        )

    def full_y(lev):
        src = acc.at[lev * 4 + along]
        return remote(
            src, fy.at[lev], send_fy.at[lev], recv_fy.at[lev], at.device(level, along)
        )

    def go_up(lev):
        sems = send_up.at[lev], recv_zb.at[lev]
        return remote(out_buf.at[lev], zb.at[lev], *sems, at.device(level + 1, spot))

    def go_down(lev):
        sems = send_dn.at[lev], recv_za.at[lev]
        return remote(out_buf.at[lev], za.at[lev], *sems, at.device(level - 1, spot))

    if sibling:
        for lev in order:
            for sp in (corner, across, along, spot):
                to_sibling(lev, sp).start()

    def local(lev):
        for n, sp in enumerate((corner, across, along, spot)):
            b = lev * 4 + sp
            if sibling:
                to_sibling(lev, sp).wait_recv()
                add_rows(writes(acc.at[b]), [reads(x_ref.at[b * 2 + core]), reads(near.at[b])], rows)
            else:
                add_rows(writes(acc.at[b]), [reads(x_ref.at[b])], rows)
            if n == 0:
                half_y(lev).start()
                half_x(lev).start()

    def halves(lev):
        half_y(lev).wait_recv()
        ref = acc.at[lev * 4 + across].at[first]
        add_rows(writes(ref), [reads(ref), reads(hy.at[lev])], half)
        full_x(lev).start()
        half_x(lev).wait_recv()
        ref = acc.at[lev * 4 + along].at[second]
        add_rows(writes(ref), [reads(ref), reads(hx.at[lev])], half)
        full_y(lev).start()

    def column(lev):
        full_x(lev).wait_recv()
        full_y(lev).wait_recv()
        own = [reads(acc.at[lev * 4 + spot]), reads(fx.at[lev]), reads(fy.at[lev])]
        above, below = reads(za.at[lev]), reads(zb.at[lev])

        @pl.when(lev < level)
        def _():
            @pl.when(at.has_up)
            def _():
                go_down(lev).wait_recv()
                add_rows(writes(out_buf.at[lev]), [*own, above], rows)

            @pl.when(jnp.logical_not(at.has_up))
            def _():
                add_rows(writes(out_buf.at[lev]), own, rows)

            go_down(lev).start()

        @pl.when(lev > level)
        def _():
            @pl.when(at.has_down)
            def _():
                go_up(lev).wait_recv()
                add_rows(writes(out_buf.at[lev]), [*own, below], rows)

            @pl.when(jnp.logical_not(at.has_down))
            def _():
                add_rows(writes(out_buf.at[lev]), own, rows)

            go_up(lev).start()

        @pl.when(lev == level)
        def _():
            pl.when(at.has_up)(lambda: go_down(lev).wait_recv())
            pl.when(at.has_down)(lambda: go_up(lev).wait_recv())

            @pl.when(at.has_up & at.has_down)
            def _():
                add_rows(writes(out_ref), [*own, above, below], rows)

            @pl.when(jnp.logical_not(at.has_down))
            def _():
                add_rows(writes(out_ref), [*own, above], rows)

            @pl.when(jnp.logical_not(at.has_up))
            def _():
                add_rows(writes(out_ref), [*own, below], rows)

    for s in range(levels + 2):
        if s < levels:
            local(order[s])
        if 0 <= s - 1 < levels:
            halves(order[s - 1])
        if s >= 2:
            column(order[s - 2])
    for lev in range(levels):
        if sibling:
            for sp in range(4):
                to_sibling(lev, sp).wait_send()
        half_y(lev).wait_send()
        half_x(lev).wait_send()
        full_x(lev).wait_send()
        full_y(lev).wait_send()

        @pl.when(lev < level)
        def _():
            go_down(lev).wait_send()

        @pl.when(lev > level)
        def _():
            go_up(lev).wait_send()


def scatter_wide(x, levels, sibling, collective_id):
    dma = pltpu.SemaphoreType.DMA
    blocks = levels * 4
    rows, width = x.shape[1:]
    vmem = pltpu.VMEM
    inside = pl.BlockSpec(memory_space=vmem)
    return pl.pallas_call(
        functools.partial(scatter_kernel, levels, sibling),
        out_shape=jax.ShapeDtypeStruct((rows, width), BF16),
        in_specs=[inside],
        out_specs=inside,
        scratch_shapes=[
            vmem((blocks, rows, width), BF16),
            vmem((blocks if sibling else 1, rows, width), BF16),
            vmem((levels, rows // 2, width), BF16),
            vmem((levels, rows // 2, width), BF16),
        ]
        + [vmem((levels, rows, width), BF16)] * 5
        + [dma((blocks,))] * 2
        + [dma((levels,))] * 12,
        compiler_params=pltpu.CompilerParams(
            collective_id=collective_id,
            has_side_effects=True,
            vmem_limit_bytes=60 * 1024 * 1024,
        ),
    )(x)


def slots_path(
    tokens,
    cotangent,
    lengths,
    routes,
    keep,
    attn_gain,
    w_query,
    w_key,
    w_value,
    w_out,
    ffn_gain,
    w_router,
    shared_gate,
    shared_up,
    shared_down,
    expert_gate,
    expert_up,
    expert_down,
):
    narrow_size = lax.axis_size("narrow")
    narrow_index = lax.axis_index("narrow")
    wide_size = lax.axis_size("wide")
    local_rows = tokens.shape[0]
    model_width = tokens.shape[1]
    head_count = model_width // HEAD_DIM
    row_length = local_rows * narrow_size
    capacity = 8 * (3 * local_rows * TOPK // (16 * wide_size) + 1)
    gathered = (
        lax.all_gather(attn_gain, "narrow", axis=0, tiled=True),
        lax.all_gather(w_query, "narrow", axis=0, tiled=True),
        lax.all_gather(w_key, "narrow", axis=0, tiled=True),
        lax.all_gather(w_value, "narrow", axis=0, tiled=True),
        lax.all_gather(w_out, "narrow", axis=0, tiled=True),
        lax.all_gather(ffn_gain, "narrow", axis=0, tiled=True),
        lax.all_gather(w_router, "narrow", axis=0, tiled=True),
        lax.all_gather(shared_gate, "narrow", axis=0, tiled=True),
        lax.all_gather(shared_up, "narrow", axis=0, tiled=True),
        lax.all_gather(shared_down, "narrow", axis=0, tiled=True),
    )
    attn_scale = gathered[0].astype(jnp.float32)
    query_proj = gathered[1]
    key_proj = gathered[2]
    value_proj = gathered[3]
    output_proj = gathered[4]
    ffn_scale = gathered[5].astype(jnp.float32)
    router_proj = gathered[6]
    common_gate = gathered[7]
    common_upper = gathered[8]
    common_down = gathered[9]
    expert_mats = (expert_gate, expert_up, expert_down)
    routed_gate = expert_mats[0][0]
    routed_upper = expert_mats[1][0]
    routed_down = expert_mats[2][0]
    doc_lens = lengths[0]
    key_index = jnp.arange(row_length, dtype=jnp.int32)
    key_doc, unused = doc_layout(key_index, doc_lens)
    query_index = narrow_index * local_rows + jnp.arange(local_rows, dtype=jnp.int32)
    query_doc, query_pos = doc_layout(query_index, doc_lens)
    cosine, sine_table = rotary_angles(query_pos)
    inputs = tokens.astype(jnp.float32)
    normed, unit_one, scale_one = norm_forward(inputs, attn_scale)
    normed_one = normed.astype(jnp.bfloat16)
    head_shape = (local_rows, head_count, HEAD_DIM)
    query_rows = rotate(matmul(normed_one, query_proj).reshape(head_shape), cosine, sine_table)
    query_rows = (query_rows * HEAD_DIM ** (-0.5)).astype(jnp.bfloat16)
    key_rows = rotate(matmul(normed_one, key_proj).reshape(head_shape), cosine, sine_table).astype(
        jnp.bfloat16
    )
    valued = matmul(normed_one, value_proj).astype(jnp.bfloat16)
    all_keys, all_values = (
        lax.all_gather(key_rows.reshape(local_rows, model_width), "narrow", axis=0, tiled=True),
        lax.all_gather(valued, "narrow", axis=0, tiled=True),
    )
    all_keys = all_keys.reshape(row_length, head_count, HEAD_DIM)
    all_values = all_values.reshape(row_length, head_count, HEAD_DIM)
    block_rows = min(local_rows, 512)
    blocks = local_rows // block_rows
    query_blocks = query_rows.reshape(blocks, block_rows, head_count, HEAD_DIM)
    doc_blocks = query_doc.reshape(blocks, block_rows)
    index_blocks = query_index.reshape(blocks, block_rows)

    def allowed_for(doc_rows, index_rows):
        return (doc_rows[:, None] == key_doc[None, :]) & (key_index[None, :] <= index_rows[:, None])

    def forward_block(map_item):
        return attend_block(
            map_item[0], all_keys, all_values, allowed_for(map_item[1], map_item[2])
        )

    attended, logsum = lax.map(forward_block, (query_blocks, doc_blocks, index_blocks))
    attended = attended.reshape(local_rows, model_width)
    hidden = inputs + matmul(attended, output_proj)
    normed, unit_two, scale_two = norm_forward(hidden, ffn_scale)
    normed_two = normed.astype(jnp.bfloat16)
    logits = matmul(normed_two, router_proj)
    experts = router_proj.shape[1]
    pick_table = (routes[:, :, None] == jnp.arange(experts, dtype=jnp.int32)[None, None, :]).astype(
        jnp.float32
    )
    chosen = jnp.sum(pick_table * logits[:, None, :], axis=2)
    gate_probs = jax.nn.softmax(chosen, axis=1)
    keep_float = keep.astype(jnp.float32)
    mixing = gate_probs * keep_float
    common_gate_vals, common_upper_vals, common_act = expert_forward(
        normed_two, common_gate, common_upper
    )
    shared_out = matmul(common_act, common_down)
    pair_expert = routes.reshape(-1)
    pair_total = pair_expert.shape[0]
    onehot = (pair_expert[:, None] == jnp.arange(experts, dtype=jnp.int32)[None, :]).astype(
        jnp.int32
    )
    earlier = jnp.cumsum(onehot, axis=0) - onehot
    slot_place = jnp.sum(earlier * onehot, axis=1)
    slot_index = pair_expert * capacity + slot_place
    slot_total = experts * capacity
    source = (
        jnp.full((slot_total,), -1, jnp.int32)
        .at[slot_index]
        .set(jnp.arange(pair_total, dtype=jnp.int32))
    )
    filled = source >= 0
    pair_index = jnp.maximum(source, 0)

    def fill_slots(in_rows, row_index):
        taken = jnp.take(in_rows, row_index, axis=0)
        return jnp.where(filled[:, None], taken, jnp.zeros((), in_rows.dtype)).reshape(
            experts, capacity, model_width
        )

    received = lax.all_to_all(
        fill_slots(normed_two, pair_index // TOPK), "wide", split_axis=0, concat_axis=0, tiled=True
    )
    expert_in = lax.all_gather(received, "narrow", axis=0, tiled=True).reshape(-1, model_width)
    routed_gate_vals, routed_upper_vals, routed_act = expert_forward(
        expert_in, routed_gate, routed_upper
    )
    partial_value = matmul(routed_act, routed_down)
    expert_out = lax.psum_scatter(partial_value, "narrow", scatter_dimension=0, tiled=True)
    returned = lax.all_to_all(
        expert_out.astype(jnp.bfloat16).reshape(wide_size, capacity, model_width),
        "wide",
        split_axis=0,
        concat_axis=0,
        tiled=True,
    )
    pair_out = (
        jnp.take(returned.reshape(slot_total, model_width), slot_index, axis=0)
        .astype(jnp.float32)
        .reshape(local_rows, TOPK, model_width)
    )
    routed = jnp.sum(mixing[:, :, None] * pair_out, axis=1)
    output = (hidden + shared_out + routed).astype(jnp.bfloat16)
    grad_output = cotangent.astype(jnp.float32)
    grad_pairs = (
        (mixing[:, :, None] * grad_output[:, None, :])
        .astype(jnp.bfloat16)
        .reshape(pair_total, model_width)
    )
    grad_mixing = jnp.sum(pair_out * grad_output[:, None, :], axis=2)
    grad_received = lax.all_to_all(
        fill_slots(grad_pairs, pair_index), "wide", split_axis=0, concat_axis=0, tiled=True
    )
    grad_expert_out = lax.all_gather(grad_received, "narrow", axis=0, tiled=True).reshape(
        -1, model_width
    )
    grad_expert_in, grad_rgate, grad_rupper, grad_rdown = expert_backward(
        expert_in,
        grad_expert_out,
        routed_gate_vals,
        routed_upper_vals,
        routed_act,
        routed_gate,
        routed_upper,
        routed_down,
    )
    grad_slot_rows = lax.psum_scatter(grad_expert_in, "narrow", scatter_dimension=0, tiled=True)
    expert_grads = (grad_rgate, grad_rupper, grad_rdown)
    grad_back = lax.all_to_all(
        grad_slot_rows.astype(jnp.bfloat16).reshape(wide_size, capacity, model_width),
        "wide",
        split_axis=0,
        concat_axis=0,
        tiled=True,
    )
    grad_pair_rows = jnp.take(
        grad_back.reshape(slot_total, model_width), slot_index, axis=0
    ).astype(jnp.float32)
    grad_normed = jnp.sum(grad_pair_rows.reshape(local_rows, TOPK, model_width), axis=1)
    grad_gates = grad_mixing * keep_float
    grad_chosen = gate_probs * (
        grad_gates - jnp.sum(gate_probs * grad_gates, axis=1, keepdims=True)
    )
    grad_logits = jnp.sum(pick_table * grad_chosen[:, :, None], axis=1).astype(jnp.bfloat16)
    grad_router = matmul_left(normed_two, grad_logits)
    grad_normed = grad_normed + matmul_right(grad_logits, router_proj)
    grad_common_in, grad_cgate, grad_cupper, grad_cdown = expert_backward(
        normed_two,
        cotangent,
        common_gate_vals,
        common_upper_vals,
        common_act,
        common_gate,
        common_upper,
        common_down,
    )
    grad_normed = grad_normed + grad_common_in
    grad_hidden_norm, grad_ffn = norm_backward(grad_normed, unit_two, scale_two, ffn_scale)
    grad_hidden = grad_output + grad_hidden_norm
    grad_branch = grad_hidden.astype(jnp.bfloat16)
    grad_output_proj = matmul_left(attended, grad_branch)
    grad_attended = (
        matmul_right(grad_branch, output_proj)
        .astype(jnp.bfloat16)
        .reshape(blocks, block_rows, head_count, HEAD_DIM)
    )

    def backward_block(running, map_item):
        grad_queries, grad_keys, grad_values = attend_back(
            map_item[0],
            all_keys,
            all_values,
            allowed_for(map_item[1], map_item[2]),
            map_item[3],
            map_item[4],
        )
        return ((running[0] + grad_keys, running[1] + grad_values), grad_queries)

    empty_keys = jnp.zeros((row_length, head_count, HEAD_DIM), jnp.float32)
    sums_kv, grad_query_rows = lax.scan(
        backward_block,
        (empty_keys, empty_keys),
        (query_blocks, doc_blocks, index_blocks, logsum, grad_attended),
    )
    grad_key_own, grad_value_own = (
        lax.psum_scatter(
            sums_kv[0].reshape(row_length, model_width).astype(jnp.bfloat16),
            "narrow",
            scatter_dimension=0,
            tiled=True,
        ).astype(jnp.float32),
        lax.psum_scatter(
            sums_kv[1].reshape(row_length, model_width).astype(jnp.bfloat16),
            "narrow",
            scatter_dimension=0,
            tiled=True,
        ).astype(jnp.float32),
    )
    grad_query_rows = rotate(
        grad_query_rows.reshape(head_shape) * HEAD_DIM ** (-0.5), cosine, -sine_table
    )
    grad_query_rows = grad_query_rows.reshape(local_rows, model_width).astype(jnp.bfloat16)
    grad_key_rows = (
        rotate(grad_key_own.reshape(head_shape), cosine, -sine_table)
        .reshape(local_rows, model_width)
        .astype(jnp.bfloat16)
    )
    grad_value_rows = grad_value_own.astype(jnp.bfloat16)
    grad_query_proj = matmul_left(normed_one, grad_query_rows)
    grad_key_proj = matmul_left(normed_one, grad_key_rows)
    grad_value_proj = matmul_left(normed_one, grad_value_rows)
    grad_normed_one = (
        matmul_right(grad_query_rows, query_proj)
        + matmul_right(grad_key_rows, key_proj)
        + matmul_right(grad_value_rows, value_proj)
    )
    grad_input_norm, grad_attn = norm_backward(grad_normed_one, unit_one, scale_one, attn_scale)
    grad_tokens = grad_hidden + grad_input_norm
    halves = (
        lax.psum_scatter(
            grad_attn.astype(jnp.bfloat16), "narrow", scatter_dimension=0, tiled=True
        ).astype(jnp.float32),
        lax.psum_scatter(
            grad_query_proj.astype(jnp.bfloat16), "narrow", scatter_dimension=0, tiled=True
        ).astype(jnp.float32),
        lax.psum_scatter(
            grad_key_proj.astype(jnp.bfloat16), "narrow", scatter_dimension=0, tiled=True
        ).astype(jnp.float32),
        lax.psum_scatter(
            grad_value_proj.astype(jnp.bfloat16), "narrow", scatter_dimension=0, tiled=True
        ).astype(jnp.float32),
        lax.psum_scatter(
            grad_output_proj.astype(jnp.bfloat16), "narrow", scatter_dimension=0, tiled=True
        ).astype(jnp.float32),
        lax.psum_scatter(
            grad_ffn.astype(jnp.bfloat16), "narrow", scatter_dimension=0, tiled=True
        ).astype(jnp.float32),
        lax.psum_scatter(
            grad_router.astype(jnp.bfloat16), "narrow", scatter_dimension=0, tiled=True
        ).astype(jnp.float32),
        lax.psum_scatter(
            grad_cgate.astype(jnp.bfloat16), "narrow", scatter_dimension=0, tiled=True
        ).astype(jnp.float32),
        lax.psum_scatter(
            grad_cupper.astype(jnp.bfloat16), "narrow", scatter_dimension=0, tiled=True
        ).astype(jnp.float32),
        lax.psum_scatter(
            grad_cdown.astype(jnp.bfloat16), "narrow", scatter_dimension=0, tiled=True
        ).astype(jnp.float32),
    )
    owned = lax.psum(
        (
            halves[0],
            halves[1],
            halves[2],
            halves[3],
            halves[4],
            halves[5],
            halves[6],
            halves[7],
            halves[8],
            halves[9],
        ),
        "wide",
    )
    return (
        output,
        grad_tokens,
        owned[0],
        owned[1],
        owned[2],
        owned[3],
        owned[4],
        owned[5],
        owned[6],
        owned[7],
        owned[8],
        owned[9],
        expert_grads[0][None],
        expert_grads[1][None],
        expert_grads[2][None],
    )


def tokens_path(
    tokens,
    cotangent,
    lengths,
    routes,
    keep,
    attn_gain,
    w_query,
    w_key,
    w_value,
    w_out,
    ffn_gain,
    w_router,
    shared_gate,
    shared_up,
    shared_down,
    expert_gate,
    expert_up,
    expert_down,
):
    core = lax.axis_index("narrow")
    place = lax.axis_index("wide")
    wide_size = lax.axis_size("wide")
    levels = wide_size // 4
    local_rows, width = tokens.shape
    row_length = 2 * local_rows
    part = width // 2
    heads = part // HEAD_DIM
    hidden_part = expert_gate.shape[2]
    stored = shared_gate.shape[1] // 2
    slice_width = -(-stored // (16 * wide_size)) * 16
    slices = stored // slice_width
    experts = w_router.shape[1]

    def swap(value):
        return lax.ppermute(value, "narrow", [(0, 1), (1, 0)])

    def other_rows(value):
        return jnp.concatenate([value[local_rows:], value[:local_rows]], axis=0)

    def in_order(mine, theirs, axis):
        return jnp.where(
            core == 0,
            jnp.concatenate([mine, theirs], axis=axis),
            jnp.concatenate([theirs, mine], axis=axis),
        )

    def columns(value, which, size):
        return lax.dynamic_slice_in_dim(value, which * size, size, axis=1)

    picks = (routes[:, :, None] == jnp.arange(experts, dtype=jnp.int32)[None, None, :]).astype(
        jnp.int32
    )
    marks = jnp.sum(picks * (1 + keep)[:, :, None], axis=1).astype(F32)
    all_grads, all_marks = gather_wide([cotangent, marks.T], levels, True, 0)

    first_unit = place * slice_width
    holds = place < slices

    def shared_slice(value, which, axis):
        begin = which * stored + first_unit
        taken = lax.dynamic_slice_in_dim(value, begin, slice_width, axis)
        return jnp.where(holds, taken, jnp.zeros((), value.dtype))

    gate_mine, up_mine = shared_slice(shared_gate, core, 1), shared_slice(shared_up, core, 1)
    gate_send, up_send = shared_slice(shared_gate, 1 - core, 1), shared_slice(shared_up, 1 - core, 1)
    down_slice = shared_slice(shared_down, 0, 0)
    gains = jnp.stack([attn_gain, ffn_gain])
    sent = swap(jnp.concatenate([gate_send, up_send, w_router], axis=1))
    gains = in_order(gains, swap(gains), 1).astype(F32)
    attn_scale, ffn_scale = gains[0], gains[1]
    dense = in_order(jnp.concatenate([gate_mine, up_mine, w_router], axis=1), sent, 0)
    gate_slice = dense[:, :slice_width]
    up_slice = dense[:, slice_width : 2 * slice_width]
    router = dense[:, 2 * slice_width :]

    row_tokens = jnp.concatenate([tokens, swap(tokens)], axis=0).astype(F32)
    normed, unit_one, scale_one = norm_forward(row_tokens, attn_scale)
    normed_one = columns(normed.astype(BF16), core, part)
    projections = [w_query, w_key, w_value]
    keep_side = jnp.concatenate([columns(w, core, part) for w in projections], axis=1)
    send_side = jnp.concatenate([columns(w, 1 - core, part) for w in projections], axis=1)
    arrived = swap(matmul(normed_one, send_side).astype(BF16))
    qkv = matmul(normed_one, keep_side) + other_rows(arrived).astype(F32)
    index = jnp.arange(local_rows, dtype=jnp.int32)
    index = jnp.concatenate([core * local_rows + index, (1 - core) * local_rows + index])
    docs, positions = doc_layout(index, lengths[0])
    allowed = (docs[:, None] == docs[None, :]) & (index[None, :] <= index[:, None])
    cosine, sine_table = rotary_angles(positions)
    head_shape = (row_length, heads, HEAD_DIM)
    query_rows = rotate(qkv[:, :part].reshape(head_shape), cosine, sine_table)
    query_rows = (query_rows * HEAD_DIM ** (-0.5)).astype(BF16)
    key_rows = rotate(qkv[:, part : 2 * part].reshape(head_shape), cosine, sine_table).astype(BF16)
    value_rows = qkv[:, 2 * part :].astype(BF16).reshape(head_shape)
    attended, logsum = attend_block(query_rows, key_rows, value_rows, allowed)
    attended = attended.reshape(row_length, part)
    branch = matmul(attended, w_out)
    arrived = swap(branch[local_rows:].astype(BF16))
    inputs = row_tokens[:local_rows]
    hidden = inputs + branch[:local_rows] + arrived.astype(F32)
    normed, unit_two, scale_two = norm_forward(hidden, ffn_scale)
    normed_two = normed.astype(BF16)

    used = hidden_part + slice_width
    full = -(-(used + experts) // 128) * 128

    def pad(value, size, axis):
        extra = list(value.shape)
        extra[axis] = size - value.shape[axis]
        return jnp.concatenate([value, jnp.zeros(extra, value.dtype)], axis=axis)

    gate_all = pad(jnp.concatenate([expert_gate[0], gate_slice, router], axis=1), full, 1)
    up_all = pad(jnp.concatenate([expert_up[0], up_slice], axis=1), full, 1)
    down_all = pad(jnp.concatenate([expert_down[0], down_slice], axis=0), full, 0)
    all_rows, mixed, act, grad_rows, expert_out, grad_mix = experts_rows(
        normed_two,
        all_grads,
        all_marks,
        jnp.concatenate([gate_all, up_all], axis=1),
        down_all,
        hidden_part,
        used,
        levels,
        1,
    )
    all_rows = all_rows.reshape(-1, width)
    all_grads = all_grads.reshape(-1, width)
    grad_mix = lax.all_to_all(
        grad_mix.reshape(wide_size, 2, local_rows), "wide", split_axis=0, concat_axis=0, tiled=True
    )
    pick_core = jnp.where(core == 0, grad_mix[:, 0], grad_mix[:, 1])
    send_core = jnp.where(core == 0, grad_mix[:, 1], grad_mix[:, 0])
    grad_mix = (pick_core + swap(send_core)).T
    block_shape = (2 * wide_size, local_rows, width)
    grad_rows = scatter_wide(grad_rows.reshape(block_shape), levels, True, 2)
    expert_out = scatter_wide(expert_out.reshape(block_shape), levels, True, 3)
    output = (hidden + expert_out.astype(F32)).astype(BF16)
    grad_expert_gate = matmul_left(all_rows, act[:, :hidden_part])
    grad_expert_up = matmul_left(all_rows, act[:, full : full + hidden_part])
    grad_expert_down = matmul_left(mixed[:, :hidden_part], all_grads)
    shared_act = jnp.concatenate([act[:, hidden_part:used], act[:, full + hidden_part : full + used]], 1)
    shared_t = matmul_left(shared_act, all_rows).astype(BF16)
    shared_down_grad = matmul_left(mixed[:, hidden_part:used], all_grads).astype(BF16)
    theirs = swap(columns(shared_t, 1 - core, part))
    shared_t = columns(shared_t, core, part)

    def side_by_side(value):
        return jnp.concatenate([value[:slice_width], value[slice_width:]], axis=1)

    shared_block = jnp.concatenate(
        [in_order(side_by_side(shared_t), side_by_side(theirs), 0), shared_down_grad], axis=0
    )
    (shared_all,) = gather_wide([shared_block], levels, False, 4)
    shared_all = shared_all[:slices].astype(F32)
    pair = shared_all[:, : 2 * slice_width].reshape(slices, 2, slice_width, 2, part)
    grad_shared_gate = pair[:, :, :, 0].transpose(3, 1, 0, 2).reshape(part, 2 * stored)
    grad_shared_up = pair[:, :, :, 1].transpose(3, 1, 0, 2).reshape(part, 2 * stored)
    grad_shared_down = shared_all[:, 2 * slice_width :].reshape(stored, width)

    marks = marks.astype(F32)
    routed = marks > 0.0
    logits = matmul(normed_two, router)
    masked = jnp.where(routed, logits, MASKED)
    weights = jnp.where(routed, jnp.exp(masked - jnp.max(masked, axis=1, keepdims=True)), 0.0)
    gates = weights / jnp.sum(weights, axis=1, keepdims=True)
    grad_gates = jnp.where(marks > 1.5, grad_mix, 0.0)
    grad_logits = gates * (grad_gates - jnp.sum(gates * grad_gates, axis=1, keepdims=True))
    grad_logits = grad_logits.astype(BF16)
    grad_router = matmul_left(normed_two, grad_logits)
    grad_normed = grad_rows.astype(F32) + matmul_right(grad_logits, router)
    grad_hidden_norm, grad_ffn = norm_backward(grad_normed, unit_two, scale_two, ffn_scale)
    grad_hidden = cotangent.astype(F32) + grad_hidden_norm
    grad_branch = grad_hidden.astype(BF16)
    row_branch = jnp.concatenate([grad_branch, swap(grad_branch)], axis=0)

    grad_w_out = matmul_left(attended, row_branch)
    grad_attended = matmul_right(row_branch, w_out).astype(BF16).reshape(head_shape)
    grad_queries, grad_keys, grad_values = attend_back(
        query_rows, key_rows, value_rows, allowed, logsum, grad_attended
    )
    grad_queries = rotate(grad_queries * HEAD_DIM ** (-0.5), cosine, -sine_table)
    grad_keys = rotate(grad_keys, cosine, -sine_table)
    mine = jnp.stack([grad_queries, grad_keys, grad_values]).reshape(3, row_length, part)
    mine = mine.astype(BF16)
    theirs = swap(mine)
    theirs = jnp.concatenate([theirs[:, local_rows:], theirs[:, :local_rows]], axis=1)
    grad_qkv = in_order(mine, theirs, 2)
    grad_dense = jnp.stack(
        [matmul_left(normed_one, grad_qkv[k]) for k in range(3)] + [grad_w_out]
    ).astype(BF16)
    grad_part = sum(matmul_right(grad_qkv[k], projections[k]) for k in range(3))
    grad_normed_one = in_order(
        grad_part[:local_rows], swap(grad_part[local_rows:].astype(BF16)).astype(F32), 1
    )
    grad_input_norm, grad_attn = norm_backward(
        grad_normed_one, unit_one[:local_rows], scale_one[:local_rows], attn_scale
    )
    grad_tokens = grad_hidden + grad_input_norm

    small = jnp.concatenate([grad_attn[:, None], grad_ffn[:, None], grad_router], axis=1)
    small_mine = lax.dynamic_slice_in_dim(small, core * part, part, 0)
    small_send = lax.dynamic_slice_in_dim(small, (1 - core) * part, part, 0)
    small = (small_mine + swap(small_send)).astype(BF16)
    size = small.size
    extra_rows = -(-size // (width * 16)) * 16
    flat = jnp.concatenate([small.reshape(-1), jnp.zeros((extra_rows * width - size,), BF16)])
    sum_rows = 4 * part // wide_size
    summed = scatter_wide(grad_dense.reshape(wide_size, sum_rows, width), levels, False, 5)
    (everything,) = gather_wide(
        [jnp.concatenate([summed, flat.reshape(extra_rows, width)], axis=0)], levels, False, 6
    )
    owned = everything[:, :sum_rows].reshape(4, part, width)
    flat = everything[:, sum_rows:].astype(F32).reshape(wide_size, -1)
    small = jnp.sum(flat[:, :size], axis=0).reshape(part, 2 + experts)
    return (
        output,
        grad_tokens,
        small[:, 0],
        owned[0].astype(F32),
        owned[1].astype(F32),
        owned[2].astype(F32),
        owned[3].astype(F32),
        small[:, 1],
        small[:, 2:],
        grad_shared_gate,
        grad_shared_up,
        grad_shared_down,
        grad_expert_gate[None],
        grad_expert_up[None],
        grad_expert_down[None],
    )


def per_device(*arrays):
    tokens = arrays[0]
    gathered = lax.axis_size("wide") * lax.axis_size("narrow") * tokens.size * 2
    fits = gathered <= 12 * 1024 * 1024
    return (tokens_path if fits else slots_path)(*arrays)


def solution(mesh):
    in_specs = (
        P(("wide", "narrow"), None),
        P(("wide", "narrow"), None),
        P("wide", None),
        P(("wide", "narrow"), None),
        P(("wide", "narrow"), None),
        P("narrow"),
        P("narrow", None),
        P("narrow", None),
        P("narrow", None),
        P("narrow", None),
        P("narrow"),
        P("narrow", None),
        P("narrow", None),
        P("narrow", None),
        P("narrow", None),
        P("wide", None, "narrow"),
        P("wide", None, "narrow"),
        P("wide", "narrow", None),
    )
    out_specs = (
        P(("wide", "narrow"), None),
        P(("wide", "narrow"), None),
        P("narrow"),
        P("narrow", None),
        P("narrow", None),
        P("narrow", None),
        P("narrow", None),
        P("narrow"),
        P("narrow", None),
        P("narrow", None),
        P("narrow", None),
        P("narrow", None),
        P("wide", None, "narrow"),
        P("wide", None, "narrow"),
        P("wide", "narrow", None),
    )
    return jax.shard_map(
        per_device, mesh=mesh, in_specs=in_specs, out_specs=out_specs, check_vma=False
    )
```

```python
import functools
import math

import jax
import jax.numpy as jnp
from jax import lax
from jax.experimental import pallas as pl
from jax.experimental.pallas import tpu as pltpu
from jax.sharding import PartitionSpec as P

HEAD_DIM = 128
TOPK = 7


EPS = 1e-06
MASKED = -1e30


def matmul(left, right):
    return jnp.dot(left, right, preferred_element_type=jnp.float32)


def matmul_left(left, right):
    return lax.dot_general(
        left, right, (((0,), (0,)), ((), ())), preferred_element_type=jnp.float32
    )


def matmul_right(left, right):
    return lax.dot_general(
        left, right, (((1,), (1,)), ((), ())), preferred_element_type=jnp.float32
    )


def doc_layout(positions, doc_lens):
    doc_ends = jnp.cumsum(doc_lens)
    passed = (positions[:, None] >= doc_ends[None, :]).astype(jnp.int32)
    doc_ids = jnp.sum(passed, axis=1)
    return (doc_ids, positions - jnp.sum(passed * doc_lens[None, :], axis=1))


def rotary_angles(positions):
    half_dim = HEAD_DIM // 2
    inverse = jnp.exp(
        jnp.arange(half_dim, dtype=jnp.float32) * (-2.0 * math.log(10000.0) / HEAD_DIM)
    )
    angles = positions.astype(jnp.float32)[:, None] * inverse[None, :]
    return (jnp.cos(angles), jnp.sin(angles))


def rotate(values, cosine, sine_table):
    half_dim = values.shape[-1] // 2
    lower_half = values[..., :half_dim]
    upper_half = values[..., half_dim:]
    cos_b = cosine[:, None, :]
    sin_b = sine_table[:, None, :]
    return jnp.concatenate(
        [lower_half * cos_b - upper_half * sin_b, upper_half * cos_b + lower_half * sin_b], axis=-1
    )


def norm_forward(values, gain_vec):
    row_scale = lax.rsqrt(jnp.mean(values * values, axis=-1, keepdims=True) + EPS)
    unit_rows = values * row_scale
    return (unit_rows * gain_vec, unit_rows, row_scale)


def norm_backward(grad_rows, unit_rows, row_scale, gain_vec):
    scaled = grad_rows * gain_vec
    grad_gain = jnp.sum(grad_rows * unit_rows, axis=0)
    grad_input = row_scale * (
        scaled - unit_rows * jnp.mean(scaled * unit_rows, axis=-1, keepdims=True)
    )
    return (grad_input, grad_gain)


def silu_parts(gate_vals):
    sigmoid_vals = jax.nn.sigmoid(gate_vals)
    return (gate_vals * sigmoid_vals, sigmoid_vals * (1.0 + gate_vals * (1.0 - sigmoid_vals)))


def expert_forward(in_rows, gate_mat, upper_mat):
    gate_vals = matmul(in_rows, gate_mat)
    upper = matmul(in_rows, upper_mat)
    act_vals, unused = silu_parts(gate_vals)
    return (gate_vals, upper, (act_vals * upper).astype(jnp.bfloat16))


def expert_backward(in_rows, grad_rows, gate_vals, upper, active, gate_mat, upper_mat, down_mat):
    grad_act = matmul_right(grad_rows, down_mat)
    act_vals, slope_vals = silu_parts(gate_vals)
    grad_gate = (grad_act * upper * slope_vals).astype(jnp.bfloat16)
    grad_upper = (grad_act * act_vals).astype(jnp.bfloat16)
    grad_down_mat = matmul_left(active, grad_rows)
    grad_gate_mat = matmul_left(in_rows, grad_gate)
    grad_upper_mat = matmul_left(in_rows, grad_upper)
    grad_input = matmul_right(grad_gate, gate_mat) + matmul_right(grad_upper, upper_mat)
    return (grad_input, grad_gate_mat, grad_upper_mat, grad_down_mat)


def attend_block(queries, keys_all, values_all, allowed):
    scores = jnp.einsum("qhd,khd->hqk", queries, keys_all, preferred_element_type=jnp.float32)
    masked = jnp.where(allowed[None], scores, MASKED)
    row_max = jnp.max(masked, axis=-1, keepdims=True)
    weights = jnp.exp(masked - row_max)
    row_total = jnp.sum(weights, axis=-1, keepdims=True)
    prob_rows = (weights / row_total).astype(jnp.bfloat16)
    attended = jnp.einsum("hqk,khd->qhd", prob_rows, values_all, preferred_element_type=jnp.float32)
    return (attended.astype(jnp.bfloat16), (row_max + jnp.log(row_total))[..., 0])


def attend_back(queries, keys_all, values_all, allowed, logsum, grad_attended):
    scores = jnp.einsum("qhd,khd->hqk", queries, keys_all, preferred_element_type=jnp.float32)
    masked = jnp.where(allowed[None], scores, MASKED)
    prob_rows = jnp.exp(masked - logsum[..., None])
    grad_probs = jnp.einsum(
        "qhd,khd->hqk", grad_attended, values_all, preferred_element_type=jnp.float32
    )
    row_delta = jnp.sum(prob_rows * grad_probs, axis=-1, keepdims=True)
    grad_scores = (prob_rows * (grad_probs - row_delta)).astype(jnp.bfloat16)
    grad_queries = jnp.einsum(
        "hqk,khd->qhd", grad_scores, keys_all, preferred_element_type=jnp.float32
    )
    grad_keys = jnp.einsum("hqk,qhd->khd", grad_scores, queries, preferred_element_type=jnp.float32)
    grad_values = jnp.einsum(
        "hqk,qhd->khd",
        prob_rows.astype(jnp.bfloat16),
        grad_attended,
        preferred_element_type=jnp.float32,
    )
    return (grad_queries, grad_keys, grad_values)


MESH_ID = pl.DeviceIdType.MESH
BF16 = jnp.bfloat16
F32 = jnp.float32


class Place:
    def __init__(self, levels):
        self.levels = levels
        wide = lax.axis_index("wide")
        self.core = lax.axis_index("narrow")
        self.level = wide // 4
        self.spot = lax.rem(wide, 4)
        self.across = self.spot + 1 - 2 * lax.rem(self.spot, 2)
        self.along = lax.rem(self.spot + 2, 4)
        self.corner = 3 - self.spot
        self.has_up = self.level < levels - 1
        self.has_down = self.level > 0

    def choose(self, values):
        result = jnp.int32(values[0])
        for k in range(1, self.levels):
            result = jnp.where(self.level == k, values[k], result)
        return result

    def device(self, level, spot, core=None):
        return {"wide": level * 4 + spot, "narrow": self.core if core is None else core}

    def enter(self, sibling):
        barrier = pltpu.get_barrier_semaphore()

        def greet(device):
            pl.semaphore_signal(barrier, inc=1, device_id=device, device_id_type=MESH_ID)

        greet(self.device(self.level, self.across))
        greet(self.device(self.level, self.along))
        if sibling:
            greet(self.device(self.level, self.spot, 1 - self.core))

        @pl.when(self.has_up)
        def _():
            greet(self.device(self.level + 1, self.spot))

        @pl.when(self.has_down)
        def _():
            greet(self.device(self.level - 1, self.spot))

        both = jnp.where(self.has_up, 1, 0) + jnp.where(self.has_down, 1, 0)
        pl.semaphore_wait(barrier, both + (3 if sibling else 2))


def remote(src, dst, send, recv, device):
    return pltpu.make_async_remote_copy(
        src_ref=src,
        dst_ref=dst,
        send_sem=send,
        recv_sem=recv,
        device_id=device,
        device_id_type=MESH_ID,
    )


class Gather:
    NAMES = ("up", "dn", "x", "y", "cx", "cy", "rz", "rx", "ry", "rcx", "rcy")

    def __init__(self, at, sibling, pairs, sems, keeps_own=True):
        self.at, self.sibling, self.pairs, self.keeps_own = at, sibling, pairs, keeps_own
        self.own_sem = sems[0]
        self.sems = dict(zip(self.NAMES, sems[1:12]))
        self.send_n, self.recv_n = sems[12:]
        self.order = self.visits()

    @staticmethod
    def scratch(levels, arrays):
        dma = pltpu.SemaphoreType.DMA
        return (
            [dma((arrays,))]
            + [dma((arrays, levels))] * 11
            + [dma((arrays, levels * 4))] * 2
        )

    def visits(self):
        at = self.at
        table = [
            sorted(range(at.levels), key=lambda lev: (abs(lev - here), lev))
            for here in range(at.levels)
        ]
        return [at.choose([row[k] for row in table]) for k in range(at.levels)]

    def block(self, n, lev, sp, core=None):
        ref = self.pairs[n][1]
        if self.sibling:
            return ref.at[(lev * 4 + sp) * 2 + (self.at.core if core is None else core)]
        return ref.at[lev * 4 + sp]

    def each(self, send, recv, lev, sp, device, part=None, own=False):
        copies = []
        for n, (x_ref, _) in enumerate(self.pairs):
            dst = self.block(n, lev, sp)
            src = x_ref if own else dst
            if part is not None:
                half = x_ref.shape[0] // 2
                src = src.at[pl.ds(part * half, half)]
                dst = dst.at[pl.ds(part * half, half)]
            copies.append(
                remote(src, dst, self.sems[send].at[n, lev], self.sems[recv].at[n, lev], device)
            )
        return copies

    def up(self, lev, own=False):
        at = self.at
        return self.each("up", "rz", lev, at.spot, at.device(at.level + 1, at.spot), own=own)

    def down(self, lev, own=False):
        at = self.at
        return self.each("dn", "rz", lev, at.spot, at.device(at.level - 1, at.spot), own=own)

    def over_x(self, lev, sp, own=False):
        at = self.at
        return self.each("x", "rx", lev, sp, at.device(at.level, at.across), own=own)

    def over_y(self, lev, sp, own=False):
        at = self.at
        return self.each("y", "ry", lev, sp, at.device(at.level, at.along), own=own)

    def corner_y(self, lev, sp):
        at = self.at
        return self.each("cy", "rcy", lev, sp, at.device(at.level, at.along), part=0)

    def corner_x(self, lev, sp):
        at = self.at
        return self.each("cx", "rcx", lev, sp, at.device(at.level, at.across), part=1)

    def near(self, lev, sp, core=None, own=False):
        at = self.at
        copies = []
        for n, (x_ref, _) in enumerate(self.pairs):
            dst = self.block(n, lev, sp, core)
            sems = self.send_n.at[n, lev * 4 + sp], self.recv_n.at[n, lev * 4 + sp]
            device = at.device(at.level, at.spot, 1 - at.core)
            copies.append(remote(x_ref if own else dst, dst, *sems, device))
        return copies

    def own_copies(self):
        at = self.at
        return [
            pltpu.make_async_copy(x_ref, self.block(n, at.level, at.spot), self.own_sem.at[n])
            for n, (x_ref, _) in enumerate(self.pairs)
        ]

    def take_own(self):
        for copy in self.own_copies():
            copy.wait()

    def begin(self):
        at = self.at
        pl.when(at.has_up)(lambda: start(self.up(at.level, own=True)))
        pl.when(at.has_down)(lambda: start(self.down(at.level, own=True)))
        start(self.over_x(at.level, at.spot, own=True))
        start(self.over_y(at.level, at.spot, own=True))
        if self.sibling:
            start(self.near(at.level, at.spot, own=True))
        if self.keeps_own:
            start(self.own_copies())

    def take_column(self, lev):
        at = self.at
        arrived(self.up(lev))
        pl.when((lev < at.level) & at.has_up)(lambda: start(self.up(lev)))
        pl.when((lev > at.level) & at.has_down)(lambda: start(self.down(lev)))
        start(self.over_x(lev, at.spot))
        start(self.over_y(lev, at.spot))
        if self.sibling:
            start(self.near(lev, at.spot))

    def take_x(self, lev):
        at = self.at
        arrived(self.over_x(lev, at.across))
        start(self.corner_y(lev, at.across))
        if self.sibling:
            start(self.near(lev, at.across))

    def take_y(self, lev):
        at = self.at
        arrived(self.over_y(lev, at.along))
        start(self.corner_x(lev, at.along))
        if self.sibling:
            start(self.near(lev, at.along))

    def take_corner(self, lev):
        at = self.at
        arrived(self.corner_y(lev, at.corner))
        arrived(self.corner_x(lev, at.corner))
        if self.sibling:
            start(self.near(lev, at.corner))

    def take_near(self, lev, sp):
        arrived(self.near(lev, sp, 1 - self.at.core))

    def steps(self):
        levels, steps = self.at.levels, []
        for s in range(1, levels + 2):
            if s < levels:
                steps.append(lambda lev=self.order[s]: self.take_column(lev))
            if s - 1 < levels:
                steps.append(lambda lev=self.order[s - 1]: self.take_x(lev))
                steps.append(lambda lev=self.order[s - 1]: self.take_y(lev))
            if s >= 2:
                steps.append(lambda lev=self.order[s - 2]: self.take_corner(lev))
        return steps

    def finish(self, near=True):
        at = self.at
        if near:
            self.take_own()
        for lev in range(at.levels):
            pl.when(at.has_up & (lev <= at.level))(lambda lev=lev: sent(self.up(lev)))
            pl.when(at.has_down & (lev >= at.level))(lambda lev=lev: sent(self.down(lev)))
            sent(self.over_x(lev, at.spot))
            sent(self.over_y(lev, at.spot))
            sent(self.corner_y(lev, at.across))
            sent(self.corner_x(lev, at.along))
            if self.sibling:
                for sp in range(4):
                    sent(self.near(lev, sp))
                    if near:
                        self.take_near(lev, sp)


def start(copies):
    for copy in copies:
        copy.start()


def arrived(copies):
    for copy in copies:
        copy.wait_recv()


def sent(copies):
    for copy in copies:
        copy.wait_send()


def gather_kernel(levels, sibling, arrays, *refs):
    x_refs, out_refs, sems = refs[:arrays], refs[arrays : 2 * arrays], refs[2 * arrays :]
    at = Place(levels)
    at.enter(sibling)
    gather = Gather(at, sibling, list(zip(x_refs, out_refs)), sems)
    gather.begin()
    for step in gather.steps():
        step()
    gather.finish()


def gather_wide(arrays, levels, sibling, collective_id):
    blocks = levels * 4 * (2 if sibling else 1)
    anywhere = pl.BlockSpec(memory_space=pl.ANY)
    return pl.pallas_call(
        functools.partial(gather_kernel, levels, sibling, len(arrays)),
        out_shape=[jax.ShapeDtypeStruct((blocks, *x.shape), x.dtype) for x in arrays],
        in_specs=[anywhere] * len(arrays),
        out_specs=[anywhere] * len(arrays),
        scratch_shapes=Gather.scratch(levels, len(arrays)),
        compiler_params=pltpu.CompilerParams(
            collective_id=collective_id, has_side_effects=True
        ),
    )(*arrays)


def dot_nn(left, right):
    return lax.dot_general(left, right, (((1,), (0,)), ((), ())), preferred_element_type=F32)


def dot_tn(left, right):
    return lax.dot_general(left, right, (((0,), (0,)), ((), ())), preferred_element_type=F32)


def dot_nt(left, right):
    return lax.dot_general(left, right, (((1,), (1,)), ((), ())), preferred_element_type=F32)


def experts_kernel(
    levels, sizes, x_ref, g_ref, m_ref, gate_ref, down_ref,
    rows_ref, grads_ref, marks_ref, back_ref, out_ref, gm_ref, dgate_ref, dup_ref, ddown_ref, shared_ref,
    x_buf, g_buf, mark_buf, cu_buf, g_val, mixed_buf, act_buf, back_buf, out_buf, gm_buf, mark_t,
    in_sem, out_sem, gm_val, gw_ref, gd_ref, *sems,
):
    hidden, used, full = sizes
    at = Place(levels)
    at.enter(True)
    gather = Gather(at, True, [(x_ref, rows_ref), (g_ref, grads_ref), (m_ref, marks_ref)], sems, False)
    gather.begin()
    place = at.level * 4 + at.spot
    units = 4 * levels
    plan = [(0, 0)]
    for s in range(1, levels + 2):
        if s < levels:
            plan.append((s, 0))
        if s - 1 < levels:
            plan += [(s - 1, 1), (s - 1, 2)]
        if s >= 2:
            plan.append((s - 2, 3))
    rows = x_ref.shape[0]
    batch = 2 * rows

    def pick(k, values):
        result = jnp.int32(0) + values[0]
        for j in range(1, len(values)):
            result = jnp.where(k == j, values[j], result)
        return result

    def unit(k):
        visit = pick(k, [v for v, _ in plan])
        kind = pick(k, [t for _, t in plan])
        lev = pick(visit, gather.order)
        sp = pick(kind, [at.spot, at.across, at.along, at.corner])
        return lev, sp, kind

    def loads(k, first):
        slot = lax.rem(k, 2)
        blocks = pl.ds(first, 2)
        return [
            pltpu.make_async_copy(rows_ref.at[blocks], x_buf.at[slot], in_sem.at[slot, 0]),
            pltpu.make_async_copy(grads_ref.at[blocks], g_buf.at[slot], in_sem.at[slot, 1]),
            pltpu.make_async_copy(marks_ref.at[blocks], mark_buf.at[slot], in_sem.at[slot, 2]),
        ]

    def stores(k, first):
        slot = lax.rem(k, 2)
        rng = pl.ds(pl.multiple_of(first * rows, batch), batch)
        pairs = [(back_buf, back_ref), (out_buf, out_ref)]
        return [
            pltpu.make_async_copy(buf.at[slot], ref.at[rng], out_sem.at[slot, n])
            for n, (buf, ref) in enumerate(pairs)
        ]

    def serve(k):
        lev, sp, kind = unit(k)
        pl.when(kind == 0)(lambda: gather.take_column(lev))
        pl.when(kind == 1)(lambda: gather.take_x(lev))
        pl.when(kind == 2)(lambda: gather.take_y(lev))
        pl.when(kind == 3)(lambda: gather.take_corner(lev))

    def fetch(k):
        lev, sp, _ = unit(k)
        gather.take_near(lev, sp)
        start(loads(k, (lev * 4 + sp) * 2))

    def fetch_own():
        gather.take_near(at.level, at.spot)
        theirs = 1 - at.core
        triples = [(x_ref, rows_ref, x_buf), (g_ref, grads_ref, g_buf), (m_ref, marks_ref, mark_buf)]
        for n, (own, gathered, buf) in enumerate(triples):
            sem = in_sem.at[0, n]
            other = gathered.at[place * 2 + theirs]
            pltpu.make_async_copy(own, buf.at[0, at.core], sem).start()
            pltpu.make_async_copy(other, buf.at[0, theirs], sem).start()

    def lanes(n):
        return lax.broadcasted_iota(jnp.int32, (batch, 128), 1) + n * 128

    def mixing():
        tail = full // 128 - 1
        mark = mark_t[...]
        masked = jnp.where(mark > 0.5, cu_buf[:, full - 128 : full], MASKED)
        top = jnp.max(masked, axis=1, keepdims=True)
        weight = jnp.where(mark > 0.5, jnp.exp(masked - top), 0.0)
        mine = jnp.where((lanes(tail) == used + place) & (mark > 1.5), weight, 0.0)
        return jnp.sum(mine, axis=1, keepdims=True) / jnp.sum(weight, axis=1, keepdims=True)

    def elementwise():
        mix = jnp.broadcast_to(mixing(), (batch, 128))
        total = jnp.zeros((batch, 128), F32)
        for n in range(full // 128):
            cols = slice(n * 128, (n + 1) * 128)
            up_cols = slice(full + n * 128, full + (n + 1) * 128)
            gate, upper, back = cu_buf[:, cols], cu_buf[:, up_cols], g_val[:, cols]
            whole = (n + 1) * 128 <= hidden
            scale = mix
            if not whole:
                scale = jnp.where(lanes(n) < hidden, mix, jnp.where(lanes(n) < used, 1.0, 0.0))
            sig = jax.nn.sigmoid(gate)
            act = gate * sig
            active = act * upper
            grad_act = scale * back
            slope = sig * (1.0 + gate * (1.0 - sig))
            mixed_buf[:, cols] = (scale * active).astype(BF16)
            act_buf[:, cols] = (grad_act * upper * slope).astype(BF16)
            act_buf[:, up_cols] = (grad_act * act).astype(BF16)
            term = active * back
            total = total + (term if whole else jnp.where(lanes(n) < hidden, term, 0.0))
        gm_buf[...] = total

    def forward(k):
        lev, sp, _ = unit(k)
        first = (lev * 4 + sp) * 2
        slot = lax.rem(k, 2)
        for copy in loads(k, first):
            copy.wait()
        x = x_buf[slot].reshape(batch, -1)
        cu_buf[...] = dot_nn(x, gate_ref[...])
        g_val[...] = dot_nt(g_buf[slot].reshape(batch, -1), down_ref[...])
        for n in range(2):
            marks = mark_buf[slot, n]
            above = jnp.zeros((used - (full - 128), 128), F32)
            below = jnp.zeros((full - used - marks.shape[0], 128), F32)
            mark_t[pl.ds(n * rows, rows), :] = jnp.transpose(jnp.concatenate([above, marks, below], axis=0))
        elementwise()

    def backward(k):
        lev, sp, _ = unit(k)
        first = (lev * 4 + sp) * 2
        slot = lax.rem(k, 2)

        @pl.when(k >= 2)
        def _():
            for copy in stores(k, 0):
                copy.wait()

        back_buf[slot] = dot_nt(act_buf[...], gate_ref[...]).astype(BF16)
        out_buf[slot] = dot_nn(mixed_buf[...], down_ref[...]).astype(BF16)
        for n in range(2):
            gm = jnp.transpose(gm_buf[pl.ds(n * rows, rows), :])
            gm_val[pl.ds(first + n, 1), :] = jnp.sum(gm, axis=0, keepdims=True)
        start(stores(k, first))

        def gate_grad(m, carry):
            part = pl.ds(pl.multiple_of(m * 256, 256), 256)
            x = x_buf[slot, :, :, part].reshape(batch, 256)
            gw_ref[part, :] += dot_tn(x, act_buf[...])
            return carry

        def down_grad(m, carry):
            part = pl.ds(pl.multiple_of(m * 256, 256), 256)
            gd_ref[part, :] += dot_tn(mixed_buf[:, part], g_buf[slot].reshape(batch, -1))
            return carry

        lax.fori_loop(0, gw_ref.shape[0] // 256, gate_grad, 0)
        lax.fori_loop(0, full // 256, down_grad, 0)

    gw_ref[...] = jnp.zeros_like(gw_ref)
    gd_ref[...] = jnp.zeros_like(gd_ref)
    fetch_own()

    def loop(k, carry):
        pl.when((k > 0) & (k + 1 < units))(lambda: serve(k + 1))
        forward(k)
        pl.when(k == 0)(lambda: serve(1))
        pl.when(k + 1 < units)(lambda: fetch(k + 1))
        backward(k)
        return carry

    lax.fori_loop(0, units, loop, 0)
    gm_ref[...] = gm_val[...]
    dgate_ref[...] = gw_ref[:, :hidden]
    dup_ref[...] = gw_ref[:, full : full + hidden]
    ddown_ref[...] = gd_ref[:hidden, :]
    size, skip = used - hidden, hidden - (full - 128)
    for n in range(2):
        turned = jnp.transpose(gw_ref[:, (n + 1) * full - 128 : (n + 1) * full])
        shared_ref[n * size : (n + 1) * size, :] = turned[skip : skip + size, :].astype(BF16)
    shared_ref[2 * size :, :] = gd_ref[hidden:used, :].astype(BF16)
    for k in (0, 1):
        for copy in stores(k, 0):
            copy.wait()
    gather.finish(near=False)


def experts_rows(x, grads, marks, gate_up, down, hidden, used, levels, collective_id):
    rows, width = x.shape
    full = down.shape[0]
    blocks = 8 * levels
    total = blocks * rows
    dma = pltpu.SemaphoreType.DMA
    vmem = pltpu.VMEM
    anywhere = pl.BlockSpec(memory_space=pl.ANY)
    inside = pl.BlockSpec(memory_space=vmem)
    shape = jax.ShapeDtypeStruct
    batch = 2 * rows
    return pl.pallas_call(
        functools.partial(experts_kernel, levels, (hidden, used, full)),
        out_shape=[
            shape((blocks, rows, width), BF16),
            shape((blocks, rows, width), BF16),
            shape((blocks, *marks.shape), F32),
            shape((total, width), BF16),
            shape((total, width), BF16),
            shape((blocks, rows), F32),
            shape((width, hidden), F32),
            shape((width, hidden), F32),
            shape((hidden, width), F32),
            shape((3 * (used - hidden), width), BF16),
        ],
        in_specs=[anywhere, anywhere, anywhere, inside, inside],
        out_specs=[anywhere] * 5 + [inside] * 5,
        scratch_shapes=[
            vmem((2, 2, rows, width), BF16),
            vmem((2, 2, rows, width), BF16),
            vmem((2, 2, *marks.shape), F32),
            vmem((batch, 2 * full), F32),
            vmem((batch, full), F32),
            vmem((batch, full), BF16),
            vmem((batch, 2 * full), BF16),
            vmem((2, batch, width), BF16),
            vmem((2, batch, width), BF16),
            vmem((batch, 128), F32),
            vmem((batch, 128), F32),
            dma((2, 3)),
            dma((2, 2)),
            vmem((blocks, rows), F32),
            vmem((width, 2 * full), F32),
            vmem((full, width), F32),
        ]
        + Gather.scratch(levels, 3),
        compiler_params=pltpu.CompilerParams(
            collective_id=collective_id,
            has_side_effects=True,
            vmem_limit_bytes=56 * 1024 * 1024,
        ),
    )(x, grads, marks, gate_up, down)


def shared_kernel(slices, x_ref, gate_ref, up_ref, down_ref, gate_buf, up_buf, down_buf, sem):
    part, units = gate_ref.shape
    stored = units // 2
    size = stored // slices
    copies = []
    for n in range(slices):
        for c in range(2):
            rows = pl.ds(c * stored + n * size, size)
            src = x_ref.at[n, pl.ds(c * size, size)]
            for buf, lanes in ((gate_buf, pl.ds(0, part)), (up_buf, pl.ds(part, part))):
                copies.append(pltpu.make_async_copy(src.at[:, lanes], buf.at[rows], sem.at[len(copies)]))
        src, dst = x_ref.at[n, pl.ds(2 * size, size)], down_buf.at[pl.ds(n * size, size)]
        copies.append(pltpu.make_async_copy(src, dst, sem.at[len(copies)]))
    start(copies)
    for copy in copies:
        copy.wait()
    down_ref[...] = down_buf[...].astype(F32)
    for buf, ref in ((gate_buf, gate_ref), (up_buf, up_ref)):
        for n in range(units // 128):
            rows = pl.ds(n * 128, 128)
            ref[:, rows] = jnp.transpose(buf[rows, :].astype(F32))


def shared_grads(gathered, slices, part, stored):
    width = gathered.shape[2]
    vmem = pltpu.VMEM
    inside = pl.BlockSpec(memory_space=vmem)
    shape = jax.ShapeDtypeStruct
    return pl.pallas_call(
        functools.partial(shared_kernel, slices),
        out_shape=[
            shape((part, 2 * stored), F32),
            shape((part, 2 * stored), F32),
            shape((stored, width), F32),
        ],
        in_specs=[pl.BlockSpec(memory_space=pl.ANY)],
        out_specs=[inside] * 3,
        scratch_shapes=[
            vmem((2 * stored, part), BF16),
            vmem((2 * stored, part), BF16),
            vmem((stored, width), BF16),
            pltpu.SemaphoreType.DMA((5 * slices,)),
        ],
        compiler_params=pltpu.CompilerParams(vmem_limit_bytes=32 * 1024 * 1024),
    )(gathered)


def destinations(levels):
    return [
        sorted(range(levels), key=lambda to: (-abs(to - here), -to)) for here in range(levels)
    ]


def add_rows(write, sources, rows):
    step = 16

    def body(k, carry):
        r = pl.ds(pl.multiple_of(k * step, step), step)
        total = sources[0](r)
        for source in sources[1:]:
            total = total + source(r)
        write(r, total)
        return carry

    lax.fori_loop(0, rows // step, body, 0)


def reads(ref):
    return lambda r: ref[r, :].astype(F32)


def writes(ref):
    def write(r, total):
        ref[r, :] = total.astype(ref.dtype)

    return write


class Scatter:
    def __init__(self, at, sibling, x_ref, out_ref, refs):
        self.at, self.sibling, self.x_ref, self.out_ref = at, sibling, x_ref, out_ref
        self.acc, self.near, self.hx, self.hy, self.fx, self.fy = refs[:6]
        self.out_buf, self.za, self.zb = refs[6:9]
        self.own_sem, self.send_n, self.recv_n = refs[9:12]
        self.send = dict(zip(("hx", "hy", "fx", "fy", "up", "dn"), refs[12:18]))
        self.recv = dict(zip(("hx", "hy", "fx", "fy", "za", "zb"), refs[18:24]))
        self.rows = out_ref.shape[0]
        table = destinations(at.levels)
        self.order = [at.choose([row[s] for row in table]) for s in range(at.levels)]

    SCRATCH = 24

    @staticmethod
    def scratch(levels, sibling, rows, width):
        dma, vmem = pltpu.SemaphoreType.DMA, pltpu.VMEM
        blocks = levels * 4
        return (
            [
                vmem((blocks, rows, width), BF16),
                vmem((blocks if sibling else 1, rows, width), BF16),
                vmem((levels, rows // 2, width), BF16),
                vmem((levels, rows // 2, width), BF16),
            ]
            + [vmem((levels, rows, width), BF16)] * 5
            + [dma((blocks,))] * 3
            + [dma((levels,))] * 12
        )

    def own(self, lev, sp):
        b = lev * 4 + sp
        src = self.x_ref.at[b * 2 + self.at.core if self.sibling else b]
        return pltpu.make_async_copy(src, self.acc.at[b], self.own_sem.at[b])

    def to_sibling(self, lev, sp):
        at, b = self.at, lev * 4 + sp
        sems = self.send_n.at[b], self.recv_n.at[b]
        src = self.x_ref.at[b * 2 + 1 - at.core]
        return remote(src, self.near.at[b], *sems, at.device(at.level, at.spot, 1 - at.core))

    def side(self, name, src, dst, lev, spot):
        sems = self.send[name].at[lev], self.recv[name].at[lev]
        return remote(src, dst, *sems, self.at.device(self.at.level, spot))

    def half_y(self, lev):
        src = self.acc.at[lev * 4 + self.at.corner].at[pl.ds(0, self.rows // 2)]
        return self.side("hy", src, self.hy.at[lev], lev, self.at.along)

    def half_x(self, lev):
        src = self.acc.at[lev * 4 + self.at.corner].at[pl.ds(self.rows // 2, self.rows // 2)]
        return self.side("hx", src, self.hx.at[lev], lev, self.at.across)

    def full_x(self, lev):
        return self.side("fx", self.acc.at[lev * 4 + self.at.across], self.fx.at[lev], lev, self.at.across)

    def full_y(self, lev):
        return self.side("fy", self.acc.at[lev * 4 + self.at.along], self.fy.at[lev], lev, self.at.along)

    def go_up(self, lev):
        sems = self.send["up"].at[lev], self.recv["zb"].at[lev]
        device = self.at.device(self.at.level + 1, self.at.spot)
        return remote(self.out_buf.at[lev], self.zb.at[lev], *sems, device)

    def go_down(self, lev):
        sems = self.send["dn"].at[lev], self.recv["za"].at[lev]
        device = self.at.device(self.at.level - 1, self.at.spot)
        return remote(self.out_buf.at[lev], self.za.at[lev], *sems, device)

    def spots(self):
        return self.at.corner, self.at.across, self.at.along, self.at.spot

    def begin(self):
        for lev in self.order:
            for sp in self.spots():
                if self.sibling:
                    self.to_sibling(lev, sp).start()
                self.own(lev, sp).start()

    def local(self, lev):
        for n, sp in enumerate(self.spots()):
            ref = self.acc.at[lev * 4 + sp]
            self.own(lev, sp).wait()
            if self.sibling:
                self.to_sibling(lev, sp).wait_recv()
                add_rows(writes(ref), [reads(ref), reads(self.near.at[lev * 4 + sp])], self.rows)
            if n == 0:
                self.half_y(lev).start()
                self.half_x(lev).start()

    def halves(self, lev):
        half = self.rows // 2
        self.half_y(lev).wait_recv()
        ref = self.acc.at[lev * 4 + self.at.across].at[pl.ds(0, half)]
        add_rows(writes(ref), [reads(ref), reads(self.hy.at[lev])], half)
        self.full_x(lev).start()
        self.half_x(lev).wait_recv()
        ref = self.acc.at[lev * 4 + self.at.along].at[pl.ds(half, half)]
        add_rows(writes(ref), [reads(ref), reads(self.hx.at[lev])], half)
        self.full_y(lev).start()

    def column(self, lev):
        at, rows, level = self.at, self.rows, self.at.level
        self.full_x(lev).wait_recv()
        self.full_y(lev).wait_recv()
        own = [reads(self.acc.at[lev * 4 + at.spot]), reads(self.fx.at[lev]), reads(self.fy.at[lev])]
        above, below = reads(self.za.at[lev]), reads(self.zb.at[lev])
        passed = writes(self.out_buf.at[lev])
        final = writes(self.out_ref)

        def send(has, arrival, term, departure):
            @pl.when(has)
            def _():
                arrival(lev).wait_recv()
                add_rows(passed, [*own, term], rows)

            pl.when(jnp.logical_not(has))(lambda: add_rows(passed, own, rows))
            departure(lev).start()

        pl.when(lev < level)(lambda: send(at.has_up, self.go_down, above, self.go_down))
        pl.when(lev > level)(lambda: send(at.has_down, self.go_up, below, self.go_up))

        @pl.when(lev == level)
        def _():
            pl.when(at.has_up)(lambda: self.go_down(lev).wait_recv())
            pl.when(at.has_down)(lambda: self.go_up(lev).wait_recv())
            both = at.has_up & at.has_down
            pl.when(both)(lambda: add_rows(final, [*own, above, below], rows))
            pl.when(jnp.logical_not(at.has_down))(lambda: add_rows(final, [*own, above], rows))
            pl.when(jnp.logical_not(at.has_up))(lambda: add_rows(final, [*own, below], rows))

    def steps(self):
        levels, steps = self.at.levels, []
        for s in range(levels + 2):
            if s < levels:
                steps.append(lambda lev=self.order[s]: self.local(lev))
            if 0 <= s - 1 < levels:
                steps.append(lambda lev=self.order[s - 1]: self.halves(lev))
            if s >= 2:
                steps.append(lambda lev=self.order[s - 2]: self.column(lev))
        return steps

    def finish(self):
        for lev in range(self.at.levels):
            if self.sibling:
                for sp in range(4):
                    self.to_sibling(lev, sp).wait_send()
            sent([self.half_y(lev), self.half_x(lev), self.full_x(lev), self.full_y(lev)])
            pl.when(lev < self.at.level)(lambda lev=lev: self.go_down(lev).wait_send())
            pl.when(lev > self.at.level)(lambda lev=lev: self.go_up(lev).wait_send())


def scatter_kernel(levels, sibling, lag, count, *refs):
    x_refs, refs = refs[:count], refs[count:]
    out_refs, refs = refs[:count], refs[count:]
    at = Place(levels)
    at.enter(sibling)
    size = Scatter.SCRATCH
    tasks = [
        Scatter(at, sibling, x_refs[n], out_refs[n], refs[n * size : (n + 1) * size])
        for n in range(count)
    ]
    for task in tasks:
        task.begin()
    order = [
        (s + n * lag, n, step) for n, task in enumerate(tasks) for s, step in enumerate(task.steps())
    ]
    for _, _, step in sorted(order, key=lambda entry: entry[:2]):
        step()
    for task in tasks:
        task.finish()


def scatter_wide(arrays, levels, sibling, collective_id):
    rows, width = arrays[0].shape[1:]
    anywhere, inside = pl.BlockSpec(memory_space=pl.ANY), pl.BlockSpec(memory_space=pltpu.VMEM)
    count = len(arrays)
    return pl.pallas_call(
        functools.partial(scatter_kernel, levels, sibling, 7, count),
        out_shape=[jax.ShapeDtypeStruct((rows, width), BF16)] * count,
        in_specs=[anywhere] * count,
        out_specs=[inside] * count,
        scratch_shapes=Scatter.scratch(levels, sibling, rows, width) * count,
        compiler_params=pltpu.CompilerParams(
            collective_id=collective_id,
            has_side_effects=True,
            vmem_limit_bytes=60 * 1024 * 1024,
        ),
    )(*arrays)


def slots_path(
    tokens,
    cotangent,
    lengths,
    routes,
    keep,
    attn_gain,
    w_query,
    w_key,
    w_value,
    w_out,
    ffn_gain,
    w_router,
    shared_gate,
    shared_up,
    shared_down,
    expert_gate,
    expert_up,
    expert_down,
):
    narrow_size = lax.axis_size("narrow")
    narrow_index = lax.axis_index("narrow")
    wide_size = lax.axis_size("wide")
    local_rows = tokens.shape[0]
    model_width = tokens.shape[1]
    head_count = model_width // HEAD_DIM
    row_length = local_rows * narrow_size
    capacity = 8 * (3 * local_rows * TOPK // (16 * wide_size) + 1)
    gathered = (
        lax.all_gather(attn_gain, "narrow", axis=0, tiled=True),
        lax.all_gather(w_query, "narrow", axis=0, tiled=True),
        lax.all_gather(w_key, "narrow", axis=0, tiled=True),
        lax.all_gather(w_value, "narrow", axis=0, tiled=True),
        lax.all_gather(w_out, "narrow", axis=0, tiled=True),
        lax.all_gather(ffn_gain, "narrow", axis=0, tiled=True),
        lax.all_gather(w_router, "narrow", axis=0, tiled=True),
        lax.all_gather(shared_gate, "narrow", axis=0, tiled=True),
        lax.all_gather(shared_up, "narrow", axis=0, tiled=True),
        lax.all_gather(shared_down, "narrow", axis=0, tiled=True),
    )
    attn_scale = gathered[0].astype(jnp.float32)
    query_proj = gathered[1]
    key_proj = gathered[2]
    value_proj = gathered[3]
    output_proj = gathered[4]
    ffn_scale = gathered[5].astype(jnp.float32)
    router_proj = gathered[6]
    common_gate = gathered[7]
    common_upper = gathered[8]
    common_down = gathered[9]
    expert_mats = (expert_gate, expert_up, expert_down)
    routed_gate = expert_mats[0][0]
    routed_upper = expert_mats[1][0]
    routed_down = expert_mats[2][0]
    doc_lens = lengths[0]
    key_index = jnp.arange(row_length, dtype=jnp.int32)
    key_doc, unused = doc_layout(key_index, doc_lens)
    query_index = narrow_index * local_rows + jnp.arange(local_rows, dtype=jnp.int32)
    query_doc, query_pos = doc_layout(query_index, doc_lens)
    cosine, sine_table = rotary_angles(query_pos)
    inputs = tokens.astype(jnp.float32)
    normed, unit_one, scale_one = norm_forward(inputs, attn_scale)
    normed_one = normed.astype(jnp.bfloat16)
    head_shape = (local_rows, head_count, HEAD_DIM)
    query_rows = rotate(matmul(normed_one, query_proj).reshape(head_shape), cosine, sine_table)
    query_rows = (query_rows * HEAD_DIM ** (-0.5)).astype(jnp.bfloat16)
    key_rows = rotate(matmul(normed_one, key_proj).reshape(head_shape), cosine, sine_table).astype(
        jnp.bfloat16
    )
    valued = matmul(normed_one, value_proj).astype(jnp.bfloat16)
    all_keys, all_values = (
        lax.all_gather(key_rows.reshape(local_rows, model_width), "narrow", axis=0, tiled=True),
        lax.all_gather(valued, "narrow", axis=0, tiled=True),
    )
    all_keys = all_keys.reshape(row_length, head_count, HEAD_DIM)
    all_values = all_values.reshape(row_length, head_count, HEAD_DIM)
    block_rows = min(local_rows, 512)
    blocks = local_rows // block_rows
    query_blocks = query_rows.reshape(blocks, block_rows, head_count, HEAD_DIM)
    doc_blocks = query_doc.reshape(blocks, block_rows)
    index_blocks = query_index.reshape(blocks, block_rows)

    def allowed_for(doc_rows, index_rows):
        return (doc_rows[:, None] == key_doc[None, :]) & (key_index[None, :] <= index_rows[:, None])

    def forward_block(map_item):
        return attend_block(
            map_item[0], all_keys, all_values, allowed_for(map_item[1], map_item[2])
        )

    attended, logsum = lax.map(forward_block, (query_blocks, doc_blocks, index_blocks))
    attended = attended.reshape(local_rows, model_width)
    hidden = inputs + matmul(attended, output_proj)
    normed, unit_two, scale_two = norm_forward(hidden, ffn_scale)
    normed_two = normed.astype(jnp.bfloat16)
    logits = matmul(normed_two, router_proj)
    experts = router_proj.shape[1]
    pick_table = (routes[:, :, None] == jnp.arange(experts, dtype=jnp.int32)[None, None, :]).astype(
        jnp.float32
    )
    chosen = jnp.sum(pick_table * logits[:, None, :], axis=2)
    gate_probs = jax.nn.softmax(chosen, axis=1)
    keep_float = keep.astype(jnp.float32)
    mixing = gate_probs * keep_float
    common_gate_vals, common_upper_vals, common_act = expert_forward(
        normed_two, common_gate, common_upper
    )
    shared_out = matmul(common_act, common_down)
    pair_expert = routes.reshape(-1)
    pair_total = pair_expert.shape[0]
    onehot = (pair_expert[:, None] == jnp.arange(experts, dtype=jnp.int32)[None, :]).astype(
        jnp.int32
    )
    earlier = jnp.cumsum(onehot, axis=0) - onehot
    slot_place = jnp.sum(earlier * onehot, axis=1)
    slot_index = pair_expert * capacity + slot_place
    slot_total = experts * capacity
    source = (
        jnp.full((slot_total,), -1, jnp.int32)
        .at[slot_index]
        .set(jnp.arange(pair_total, dtype=jnp.int32))
    )
    filled = source >= 0
    pair_index = jnp.maximum(source, 0)

    def fill_slots(in_rows, row_index):
        taken = jnp.take(in_rows, row_index, axis=0)
        return jnp.where(filled[:, None], taken, jnp.zeros((), in_rows.dtype)).reshape(
            experts, capacity, model_width
        )

    received = lax.all_to_all(
        fill_slots(normed_two, pair_index // TOPK), "wide", split_axis=0, concat_axis=0, tiled=True
    )
    expert_in = lax.all_gather(received, "narrow", axis=0, tiled=True).reshape(-1, model_width)
    routed_gate_vals, routed_upper_vals, routed_act = expert_forward(
        expert_in, routed_gate, routed_upper
    )
    partial_value = matmul(routed_act, routed_down)
    expert_out = lax.psum_scatter(partial_value, "narrow", scatter_dimension=0, tiled=True)
    returned = lax.all_to_all(
        expert_out.astype(jnp.bfloat16).reshape(wide_size, capacity, model_width),
        "wide",
        split_axis=0,
        concat_axis=0,
        tiled=True,
    )
    pair_out = (
        jnp.take(returned.reshape(slot_total, model_width), slot_index, axis=0)
        .astype(jnp.float32)
        .reshape(local_rows, TOPK, model_width)
    )
    routed = jnp.sum(mixing[:, :, None] * pair_out, axis=1)
    output = (hidden + shared_out + routed).astype(jnp.bfloat16)
    grad_output = cotangent.astype(jnp.float32)
    grad_pairs = (
        (mixing[:, :, None] * grad_output[:, None, :])
        .astype(jnp.bfloat16)
        .reshape(pair_total, model_width)
    )
    grad_mixing = jnp.sum(pair_out * grad_output[:, None, :], axis=2)
    grad_received = lax.all_to_all(
        fill_slots(grad_pairs, pair_index), "wide", split_axis=0, concat_axis=0, tiled=True
    )
    grad_expert_out = lax.all_gather(grad_received, "narrow", axis=0, tiled=True).reshape(
        -1, model_width
    )
    grad_expert_in, grad_rgate, grad_rupper, grad_rdown = expert_backward(
        expert_in,
        grad_expert_out,
        routed_gate_vals,
        routed_upper_vals,
        routed_act,
        routed_gate,
        routed_upper,
        routed_down,
    )
    grad_slot_rows = lax.psum_scatter(grad_expert_in, "narrow", scatter_dimension=0, tiled=True)
    expert_grads = (grad_rgate, grad_rupper, grad_rdown)
    grad_back = lax.all_to_all(
        grad_slot_rows.astype(jnp.bfloat16).reshape(wide_size, capacity, model_width),
        "wide",
        split_axis=0,
        concat_axis=0,
        tiled=True,
    )
    grad_pair_rows = jnp.take(
        grad_back.reshape(slot_total, model_width), slot_index, axis=0
    ).astype(jnp.float32)
    grad_normed = jnp.sum(grad_pair_rows.reshape(local_rows, TOPK, model_width), axis=1)
    grad_gates = grad_mixing * keep_float
    grad_chosen = gate_probs * (
        grad_gates - jnp.sum(gate_probs * grad_gates, axis=1, keepdims=True)
    )
    grad_logits = jnp.sum(pick_table * grad_chosen[:, :, None], axis=1).astype(jnp.bfloat16)
    grad_router = matmul_left(normed_two, grad_logits)
    grad_normed = grad_normed + matmul_right(grad_logits, router_proj)
    grad_common_in, grad_cgate, grad_cupper, grad_cdown = expert_backward(
        normed_two,
        cotangent,
        common_gate_vals,
        common_upper_vals,
        common_act,
        common_gate,
        common_upper,
        common_down,
    )
    grad_normed = grad_normed + grad_common_in
    grad_hidden_norm, grad_ffn = norm_backward(grad_normed, unit_two, scale_two, ffn_scale)
    grad_hidden = grad_output + grad_hidden_norm
    grad_branch = grad_hidden.astype(jnp.bfloat16)
    grad_output_proj = matmul_left(attended, grad_branch)
    grad_attended = (
        matmul_right(grad_branch, output_proj)
        .astype(jnp.bfloat16)
        .reshape(blocks, block_rows, head_count, HEAD_DIM)
    )

    def backward_block(running, map_item):
        grad_queries, grad_keys, grad_values = attend_back(
            map_item[0],
            all_keys,
            all_values,
            allowed_for(map_item[1], map_item[2]),
            map_item[3],
            map_item[4],
        )
        return ((running[0] + grad_keys, running[1] + grad_values), grad_queries)

    empty_keys = jnp.zeros((row_length, head_count, HEAD_DIM), jnp.float32)
    sums_kv, grad_query_rows = lax.scan(
        backward_block,
        (empty_keys, empty_keys),
        (query_blocks, doc_blocks, index_blocks, logsum, grad_attended),
    )
    grad_key_own, grad_value_own = (
        lax.psum_scatter(
            sums_kv[0].reshape(row_length, model_width).astype(jnp.bfloat16),
            "narrow",
            scatter_dimension=0,
            tiled=True,
        ).astype(jnp.float32),
        lax.psum_scatter(
            sums_kv[1].reshape(row_length, model_width).astype(jnp.bfloat16),
            "narrow",
            scatter_dimension=0,
            tiled=True,
        ).astype(jnp.float32),
    )
    grad_query_rows = rotate(
        grad_query_rows.reshape(head_shape) * HEAD_DIM ** (-0.5), cosine, -sine_table
    )
    grad_query_rows = grad_query_rows.reshape(local_rows, model_width).astype(jnp.bfloat16)
    grad_key_rows = (
        rotate(grad_key_own.reshape(head_shape), cosine, -sine_table)
        .reshape(local_rows, model_width)
        .astype(jnp.bfloat16)
    )
    grad_value_rows = grad_value_own.astype(jnp.bfloat16)
    grad_query_proj = matmul_left(normed_one, grad_query_rows)
    grad_key_proj = matmul_left(normed_one, grad_key_rows)
    grad_value_proj = matmul_left(normed_one, grad_value_rows)
    grad_normed_one = (
        matmul_right(grad_query_rows, query_proj)
        + matmul_right(grad_key_rows, key_proj)
        + matmul_right(grad_value_rows, value_proj)
    )
    grad_input_norm, grad_attn = norm_backward(grad_normed_one, unit_one, scale_one, attn_scale)
    grad_tokens = grad_hidden + grad_input_norm
    halves = (
        lax.psum_scatter(
            grad_attn.astype(jnp.bfloat16), "narrow", scatter_dimension=0, tiled=True
        ).astype(jnp.float32),
        lax.psum_scatter(
            grad_query_proj.astype(jnp.bfloat16), "narrow", scatter_dimension=0, tiled=True
        ).astype(jnp.float32),
        lax.psum_scatter(
            grad_key_proj.astype(jnp.bfloat16), "narrow", scatter_dimension=0, tiled=True
        ).astype(jnp.float32),
        lax.psum_scatter(
            grad_value_proj.astype(jnp.bfloat16), "narrow", scatter_dimension=0, tiled=True
        ).astype(jnp.float32),
        lax.psum_scatter(
            grad_output_proj.astype(jnp.bfloat16), "narrow", scatter_dimension=0, tiled=True
        ).astype(jnp.float32),
        lax.psum_scatter(
            grad_ffn.astype(jnp.bfloat16), "narrow", scatter_dimension=0, tiled=True
        ).astype(jnp.float32),
        lax.psum_scatter(
            grad_router.astype(jnp.bfloat16), "narrow", scatter_dimension=0, tiled=True
        ).astype(jnp.float32),
        lax.psum_scatter(
            grad_cgate.astype(jnp.bfloat16), "narrow", scatter_dimension=0, tiled=True
        ).astype(jnp.float32),
        lax.psum_scatter(
            grad_cupper.astype(jnp.bfloat16), "narrow", scatter_dimension=0, tiled=True
        ).astype(jnp.float32),
        lax.psum_scatter(
            grad_cdown.astype(jnp.bfloat16), "narrow", scatter_dimension=0, tiled=True
        ).astype(jnp.float32),
    )
    owned = lax.psum(
        (
            halves[0],
            halves[1],
            halves[2],
            halves[3],
            halves[4],
            halves[5],
            halves[6],
            halves[7],
            halves[8],
            halves[9],
        ),
        "wide",
    )
    return (
        output,
        grad_tokens,
        owned[0],
        owned[1],
        owned[2],
        owned[3],
        owned[4],
        owned[5],
        owned[6],
        owned[7],
        owned[8],
        owned[9],
        expert_grads[0][None],
        expert_grads[1][None],
        expert_grads[2][None],
    )


def tokens_path(
    tokens,
    cotangent,
    lengths,
    routes,
    keep,
    attn_gain,
    w_query,
    w_key,
    w_value,
    w_out,
    ffn_gain,
    w_router,
    shared_gate,
    shared_up,
    shared_down,
    expert_gate,
    expert_up,
    expert_down,
):
    core = lax.axis_index("narrow")
    place = lax.axis_index("wide")
    wide_size = lax.axis_size("wide")
    levels = wide_size // 4
    local_rows, width = tokens.shape
    row_length = 2 * local_rows
    part = width // 2
    heads = part // HEAD_DIM
    hidden_part = expert_gate.shape[2]
    stored = shared_gate.shape[1] // 2
    slice_width = -(-stored // (16 * wide_size)) * 16
    slices = stored // slice_width
    experts = w_router.shape[1]

    def swap(value):
        return lax.ppermute(value, "narrow", [(0, 1), (1, 0)])

    def other_rows(value):
        return jnp.concatenate([value[local_rows:], value[:local_rows]], axis=0)

    def in_order(mine, theirs, axis):
        return jnp.where(
            core == 0,
            jnp.concatenate([mine, theirs], axis=axis),
            jnp.concatenate([theirs, mine], axis=axis),
        )

    def columns(value, which, size):
        return lax.dynamic_slice_in_dim(value, which * size, size, axis=1)

    picks = (routes[:, :, None] == jnp.arange(experts, dtype=jnp.int32)[None, None, :]).astype(
        jnp.int32
    )
    marks = jnp.sum(picks * (1 + keep)[:, :, None], axis=1).astype(F32)

    first_unit = place * slice_width
    holds = place < slices

    def shared_slice(value, which, axis):
        begin = which * stored + first_unit
        taken = lax.dynamic_slice_in_dim(value, begin, slice_width, axis)
        return jnp.where(holds, taken, jnp.zeros((), value.dtype))

    gate_mine, up_mine = shared_slice(shared_gate, core, 1), shared_slice(shared_up, core, 1)
    gate_send, up_send = shared_slice(shared_gate, 1 - core, 1), shared_slice(shared_up, 1 - core, 1)
    down_slice = shared_slice(shared_down, 0, 0)
    gains = jnp.stack([attn_gain, ffn_gain])
    sent = swap(jnp.concatenate([gate_send, up_send, w_router], axis=1))
    gains = in_order(gains, swap(gains), 1).astype(F32)
    attn_scale, ffn_scale = gains[0], gains[1]
    dense = in_order(jnp.concatenate([gate_mine, up_mine, w_router], axis=1), sent, 0)
    gate_slice = dense[:, :slice_width]
    up_slice = dense[:, slice_width : 2 * slice_width]
    router = dense[:, 2 * slice_width :]

    row_tokens = jnp.concatenate([tokens, swap(tokens)], axis=0).astype(F32)
    normed, unit_one, scale_one = norm_forward(row_tokens, attn_scale)
    normed_one = columns(normed.astype(BF16), core, part)
    projections = [w_query, w_key, w_value]
    keep_side = jnp.concatenate([columns(w, core, part) for w in projections], axis=1)
    send_side = jnp.concatenate([columns(w, 1 - core, part) for w in projections], axis=1)
    arrived = swap(matmul(normed_one, send_side).astype(BF16))
    qkv = matmul(normed_one, keep_side) + other_rows(arrived).astype(F32)
    index = jnp.arange(local_rows, dtype=jnp.int32)
    index = jnp.concatenate([core * local_rows + index, (1 - core) * local_rows + index])
    docs, positions = doc_layout(index, lengths[0])
    allowed = (docs[:, None] == docs[None, :]) & (index[None, :] <= index[:, None])
    cosine, sine_table = rotary_angles(positions)
    head_shape = (row_length, heads, HEAD_DIM)
    query_rows = rotate(qkv[:, :part].reshape(head_shape), cosine, sine_table)
    query_rows = (query_rows * HEAD_DIM ** (-0.5)).astype(BF16)
    key_rows = rotate(qkv[:, part : 2 * part].reshape(head_shape), cosine, sine_table).astype(BF16)
    value_rows = qkv[:, 2 * part :].astype(BF16).reshape(head_shape)
    attended, logsum = attend_block(query_rows, key_rows, value_rows, allowed)
    attended = attended.reshape(row_length, part)
    branch = matmul(attended, w_out)
    arrived = swap(branch[local_rows:].astype(BF16))
    inputs = row_tokens[:local_rows]
    hidden = inputs + branch[:local_rows] + arrived.astype(F32)
    normed, unit_two, scale_two = norm_forward(hidden, ffn_scale)
    normed_two = normed.astype(BF16)

    used = hidden_part + slice_width
    full = -(-(used + experts) // 128) * 128

    def pad(value, size, axis):
        extra = list(value.shape)
        extra[axis] = size - value.shape[axis]
        return jnp.concatenate([value, jnp.zeros(extra, value.dtype)], axis=axis)

    gate_all = pad(jnp.concatenate([expert_gate[0], gate_slice, router], axis=1), full, 1)
    up_all = pad(jnp.concatenate([expert_up[0], up_slice], axis=1), full, 1)
    down_all = pad(jnp.concatenate([expert_down[0], down_slice], axis=0), full, 0)
    (_, _, _, grad_rows, expert_out, grad_mix, *expert_grads, shared_part) = experts_rows(
        normed_two,
        cotangent,
        marks.T,
        jnp.concatenate([gate_all, up_all], axis=1),
        down_all,
        hidden_part,
        used,
        levels,
        1,
    )
    grad_mix = lax.all_to_all(
        grad_mix.reshape(wide_size, 2, local_rows), "wide", split_axis=0, concat_axis=0, tiled=True
    )
    pick_core = jnp.where(core == 0, grad_mix[:, 0], grad_mix[:, 1])
    send_core = jnp.where(core == 0, grad_mix[:, 1], grad_mix[:, 0])
    grad_mix = (pick_core + swap(send_core)).T
    block_shape = (2 * wide_size, local_rows, width)
    grad_rows, expert_out = scatter_wide(
        [grad_rows.reshape(block_shape), expert_out.reshape(block_shape)], levels, True, 2
    )
    output = (hidden + expert_out.astype(F32)).astype(BF16)
    grad_expert_gate, grad_expert_up, grad_expert_down = expert_grads
    shared_t, shared_down_grad = shared_part[: 2 * slice_width], shared_part[2 * slice_width :]
    theirs = swap(columns(shared_t, 1 - core, part))
    shared_t = columns(shared_t, core, part)

    def side_by_side(value):
        return jnp.concatenate([value[:slice_width], value[slice_width:]], axis=1)

    shared_block = jnp.concatenate(
        [in_order(side_by_side(shared_t), side_by_side(theirs), 0), shared_down_grad], axis=0
    )
    (shared_all,) = gather_wide([shared_block], levels, False, 4)
    grad_shared_gate, grad_shared_up, grad_shared_down = shared_grads(
        shared_all, slices, part, stored
    )

    marks = marks.astype(F32)
    routed = marks > 0.0
    logits = matmul(normed_two, router)
    masked = jnp.where(routed, logits, MASKED)
    weights = jnp.where(routed, jnp.exp(masked - jnp.max(masked, axis=1, keepdims=True)), 0.0)
    gates = weights / jnp.sum(weights, axis=1, keepdims=True)
    grad_gates = jnp.where(marks > 1.5, grad_mix, 0.0)
    grad_logits = gates * (grad_gates - jnp.sum(gates * grad_gates, axis=1, keepdims=True))
    grad_logits = grad_logits.astype(BF16)
    grad_router = matmul_left(normed_two, grad_logits)
    grad_normed = grad_rows.astype(F32) + matmul_right(grad_logits, router)
    grad_hidden_norm, grad_ffn = norm_backward(grad_normed, unit_two, scale_two, ffn_scale)
    grad_hidden = cotangent.astype(F32) + grad_hidden_norm
    grad_branch = grad_hidden.astype(BF16)
    row_branch = jnp.concatenate([grad_branch, swap(grad_branch)], axis=0)

    grad_w_out = matmul_left(attended, row_branch)
    grad_attended = matmul_right(row_branch, w_out).astype(BF16).reshape(head_shape)
    grad_queries, grad_keys, grad_values = attend_back(
        query_rows, key_rows, value_rows, allowed, logsum, grad_attended
    )
    grad_queries = rotate(grad_queries * HEAD_DIM ** (-0.5), cosine, -sine_table)
    grad_keys = rotate(grad_keys, cosine, -sine_table)
    mine = jnp.stack([grad_queries, grad_keys, grad_values]).reshape(3, row_length, part)
    mine = mine.astype(BF16)
    theirs = swap(mine)
    theirs = jnp.concatenate([theirs[:, local_rows:], theirs[:, :local_rows]], axis=1)
    grad_qkv = in_order(mine, theirs, 2)
    grad_dense = jnp.stack(
        [matmul_left(normed_one, grad_qkv[k]) for k in range(3)] + [grad_w_out]
    ).astype(BF16)
    grad_part = sum(matmul_right(grad_qkv[k], projections[k]) for k in range(3))
    grad_normed_one = in_order(
        grad_part[:local_rows], swap(grad_part[local_rows:].astype(BF16)).astype(F32), 1
    )
    grad_input_norm, grad_attn = norm_backward(
        grad_normed_one, unit_one[:local_rows], scale_one[:local_rows], attn_scale
    )
    grad_tokens = grad_hidden + grad_input_norm

    small = jnp.concatenate([grad_attn[:, None], grad_ffn[:, None], grad_router], axis=1)
    small_mine = lax.dynamic_slice_in_dim(small, core * part, part, 0)
    small_send = lax.dynamic_slice_in_dim(small, (1 - core) * part, part, 0)
    small = (small_mine + swap(small_send)).astype(BF16)
    size = small.size
    extra_rows = -(-size // (width * 16)) * 16
    flat = jnp.concatenate([small.reshape(-1), jnp.zeros((extra_rows * width - size,), BF16)])
    sum_rows = 4 * part // wide_size
    (summed,) = scatter_wide([grad_dense.reshape(wide_size, sum_rows, width)], levels, False, 5)
    everything, flat = gather_wide([summed, flat.reshape(extra_rows, width)], levels, False, 6)
    owned = everything.reshape(4, part, width)
    flat = flat.astype(F32).reshape(wide_size, -1)
    small = jnp.sum(flat[:, :size], axis=0).reshape(part, 2 + experts)
    return (
        output,
        grad_tokens,
        small[:, 0],
        owned[0].astype(F32),
        owned[1].astype(F32),
        owned[2].astype(F32),
        owned[3].astype(F32),
        small[:, 1],
        small[:, 2:],
        grad_shared_gate,
        grad_shared_up,
        grad_shared_down,
        grad_expert_gate[None],
        grad_expert_up[None],
        grad_expert_down[None],
    )


def per_device(*arrays):
    tokens = arrays[0]
    gathered = lax.axis_size("wide") * lax.axis_size("narrow") * tokens.size * 2
    fits = gathered <= 12 * 1024 * 1024
    return (tokens_path if fits else slots_path)(*arrays)


def solution(mesh):
    in_specs = (
        P(("wide", "narrow"), None),
        P(("wide", "narrow"), None),
        P("wide", None),
        P(("wide", "narrow"), None),
        P(("wide", "narrow"), None),
        P("narrow"),
        P("narrow", None),
        P("narrow", None),
        P("narrow", None),
        P("narrow", None),
        P("narrow"),
        P("narrow", None),
        P("narrow", None),
        P("narrow", None),
        P("narrow", None),
        P("wide", None, "narrow"),
        P("wide", None, "narrow"),
        P("wide", "narrow", None),
    )
    out_specs = (
        P(("wide", "narrow"), None),
        P(("wide", "narrow"), None),
        P("narrow"),
        P("narrow", None),
        P("narrow", None),
        P("narrow", None),
        P("narrow", None),
        P("narrow"),
        P("narrow", None),
        P("narrow", None),
        P("narrow", None),
        P("narrow", None),
        P("wide", None, "narrow"),
        P("wide", None, "narrow"),
        P("wide", "narrow", None),
    )
    return jax.shard_map(
        per_device, mesh=mesh, in_specs=in_specs, out_specs=out_specs, check_vma=False
    )
```

```python
import functools
import math

import jax
import jax.numpy as jnp
from jax import lax
from jax.experimental import pallas as pl
from jax.experimental.pallas import tpu as pltpu
from jax.sharding import PartitionSpec as P

HEAD_DIM = 128
TOPK = 7


EPS = 1e-06
MASKED = -1e30


def matmul(left, right):
    return jnp.dot(left, right, preferred_element_type=jnp.float32)


def matmul_left(left, right):
    return lax.dot_general(
        left, right, (((0,), (0,)), ((), ())), preferred_element_type=jnp.float32
    )


def matmul_right(left, right):
    return lax.dot_general(
        left, right, (((1,), (1,)), ((), ())), preferred_element_type=jnp.float32
    )


def doc_layout(positions, doc_lens):
    doc_ends = jnp.cumsum(doc_lens)
    passed = (positions[:, None] >= doc_ends[None, :]).astype(jnp.int32)
    doc_ids = jnp.sum(passed, axis=1)
    return (doc_ids, positions - jnp.sum(passed * doc_lens[None, :], axis=1))


def rotary_angles(positions):
    half_dim = HEAD_DIM // 2
    inverse = jnp.exp(
        jnp.arange(half_dim, dtype=jnp.float32) * (-2.0 * math.log(10000.0) / HEAD_DIM)
    )
    angles = positions.astype(jnp.float32)[:, None] * inverse[None, :]
    return (jnp.cos(angles), jnp.sin(angles))


def rotate(values, cosine, sine_table):
    half_dim = values.shape[-1] // 2
    lower_half = values[..., :half_dim]
    upper_half = values[..., half_dim:]
    cos_b = cosine[:, None, :]
    sin_b = sine_table[:, None, :]
    return jnp.concatenate(
        [lower_half * cos_b - upper_half * sin_b, upper_half * cos_b + lower_half * sin_b], axis=-1
    )


def norm_forward(values, gain_vec):
    row_scale = lax.rsqrt(jnp.mean(values * values, axis=-1, keepdims=True) + EPS)
    unit_rows = values * row_scale
    return (unit_rows * gain_vec, unit_rows, row_scale)


def norm_backward(grad_rows, unit_rows, row_scale, gain_vec):
    scaled = grad_rows * gain_vec
    grad_gain = jnp.sum(grad_rows * unit_rows, axis=0)
    grad_input = row_scale * (
        scaled - unit_rows * jnp.mean(scaled * unit_rows, axis=-1, keepdims=True)
    )
    return (grad_input, grad_gain)


def silu_parts(gate_vals):
    sigmoid_vals = jax.nn.sigmoid(gate_vals)
    return (gate_vals * sigmoid_vals, sigmoid_vals * (1.0 + gate_vals * (1.0 - sigmoid_vals)))


def expert_forward(in_rows, gate_mat, upper_mat):
    gate_vals = matmul(in_rows, gate_mat)
    upper = matmul(in_rows, upper_mat)
    act_vals, unused = silu_parts(gate_vals)
    return (gate_vals, upper, (act_vals * upper).astype(jnp.bfloat16))


def expert_backward(in_rows, grad_rows, gate_vals, upper, active, gate_mat, upper_mat, down_mat):
    grad_act = matmul_right(grad_rows, down_mat)
    act_vals, slope_vals = silu_parts(gate_vals)
    grad_gate = (grad_act * upper * slope_vals).astype(jnp.bfloat16)
    grad_upper = (grad_act * act_vals).astype(jnp.bfloat16)
    grad_down_mat = matmul_left(active, grad_rows)
    grad_gate_mat = matmul_left(in_rows, grad_gate)
    grad_upper_mat = matmul_left(in_rows, grad_upper)
    grad_input = matmul_right(grad_gate, gate_mat) + matmul_right(grad_upper, upper_mat)
    return (grad_input, grad_gate_mat, grad_upper_mat, grad_down_mat)


def attend_block(queries, keys_all, values_all, allowed):
    scores = jnp.einsum("qhd,khd->hqk", queries, keys_all, preferred_element_type=jnp.float32)
    masked = jnp.where(allowed[None], scores, MASKED)
    row_max = jnp.max(masked, axis=-1, keepdims=True)
    weights = jnp.exp(masked - row_max)
    row_total = jnp.sum(weights, axis=-1, keepdims=True)
    prob_rows = (weights / row_total).astype(jnp.bfloat16)
    attended = jnp.einsum("hqk,khd->qhd", prob_rows, values_all, preferred_element_type=jnp.float32)
    return (attended.astype(jnp.bfloat16), (row_max + jnp.log(row_total))[..., 0])


def attend_back(queries, keys_all, values_all, allowed, logsum, grad_attended):
    scores = jnp.einsum("qhd,khd->hqk", queries, keys_all, preferred_element_type=jnp.float32)
    masked = jnp.where(allowed[None], scores, MASKED)
    prob_rows = jnp.exp(masked - logsum[..., None])
    grad_probs = jnp.einsum(
        "qhd,khd->hqk", grad_attended, values_all, preferred_element_type=jnp.float32
    )
    row_delta = jnp.sum(prob_rows * grad_probs, axis=-1, keepdims=True)
    grad_scores = (prob_rows * (grad_probs - row_delta)).astype(jnp.bfloat16)
    grad_queries = jnp.einsum(
        "hqk,khd->qhd", grad_scores, keys_all, preferred_element_type=jnp.float32
    )
    grad_keys = jnp.einsum("hqk,qhd->khd", grad_scores, queries, preferred_element_type=jnp.float32)
    grad_values = jnp.einsum(
        "hqk,qhd->khd",
        prob_rows.astype(jnp.bfloat16),
        grad_attended,
        preferred_element_type=jnp.float32,
    )
    return (grad_queries, grad_keys, grad_values)


MESH_ID = pl.DeviceIdType.MESH
BF16 = jnp.bfloat16
F32 = jnp.float32


class Place:
    def __init__(self, levels):
        self.levels = levels
        wide = lax.axis_index("wide")
        self.core = lax.axis_index("narrow")
        self.level = wide // 4
        self.spot = lax.rem(wide, 4)
        self.across = self.spot + 1 - 2 * lax.rem(self.spot, 2)
        self.along = lax.rem(self.spot + 2, 4)
        self.corner = 3 - self.spot
        self.has_up = self.level < levels - 1
        self.has_down = self.level > 0

    def choose(self, values):
        result = jnp.int32(values[0])
        for k in range(1, self.levels):
            result = jnp.where(self.level == k, values[k], result)
        return result

    def device(self, level, spot, core=None):
        return {"wide": level * 4 + spot, "narrow": self.core if core is None else core}

    def enter(self, sibling):
        barrier = pltpu.get_barrier_semaphore()

        def greet(device):
            pl.semaphore_signal(barrier, inc=1, device_id=device, device_id_type=MESH_ID)

        greet(self.device(self.level, self.across))
        greet(self.device(self.level, self.along))
        if sibling:
            greet(self.device(self.level, self.spot, 1 - self.core))

        @pl.when(self.has_up)
        def _():
            greet(self.device(self.level + 1, self.spot))

        @pl.when(self.has_down)
        def _():
            greet(self.device(self.level - 1, self.spot))

        both = jnp.where(self.has_up, 1, 0) + jnp.where(self.has_down, 1, 0)
        pl.semaphore_wait(barrier, both + (3 if sibling else 2))


def remote(src, dst, send, recv, device):
    return pltpu.make_async_remote_copy(
        src_ref=src,
        dst_ref=dst,
        send_sem=send,
        recv_sem=recv,
        device_id=device,
        device_id_type=MESH_ID,
    )


class Gather:
    NAMES = ("up", "dn", "x", "y", "cx", "cy", "rz", "rx", "ry", "rcx", "rcy")

    def __init__(self, at, sibling, pairs, sems, keeps_own=True):
        self.at, self.sibling, self.pairs, self.keeps_own = at, sibling, pairs, keeps_own
        self.own_sem = sems[0]
        self.sems = dict(zip(self.NAMES, sems[1:12]))
        self.send_n, self.recv_n = sems[12:]
        self.order = self.visits()

    @staticmethod
    def scratch(levels, arrays):
        dma = pltpu.SemaphoreType.DMA
        return (
            [dma((arrays,))]
            + [dma((arrays, levels))] * 11
            + [dma((arrays, levels * 4))] * 2
        )

    def visits(self):
        at = self.at
        table = [
            sorted(range(at.levels), key=lambda lev: (abs(lev - here), lev))
            for here in range(at.levels)
        ]
        return [at.choose([row[k] for row in table]) for k in range(at.levels)]

    def block(self, n, lev, sp, core=None):
        x_ref, ref = self.pairs[n][:2]
        if self.sibling:
            return ref.at[(lev * 4 + sp) * 2 + (self.at.core if core is None else core)]
        if len(self.pairs[n]) == 3:
            return ref.at[lev * 4 + sp].at[pl.ds(self.pairs[n][2], x_ref.shape[0])]
        return ref.at[lev * 4 + sp]

    def each(self, send, recv, lev, sp, device, part=None, own=False):
        copies = []
        for n, (x_ref, *_) in enumerate(self.pairs):
            dst = self.block(n, lev, sp)
            src = x_ref if own else dst
            if part is not None:
                half = x_ref.shape[0] // 2
                src = src.at[pl.ds(part * half, half)]
                dst = dst.at[pl.ds(part * half, half)]
            copies.append(
                remote(src, dst, self.sems[send].at[n, lev], self.sems[recv].at[n, lev], device)
            )
        return copies

    def up(self, lev, own=False):
        at = self.at
        return self.each("up", "rz", lev, at.spot, at.device(at.level + 1, at.spot), own=own)

    def down(self, lev, own=False):
        at = self.at
        return self.each("dn", "rz", lev, at.spot, at.device(at.level - 1, at.spot), own=own)

    def over_x(self, lev, sp, own=False):
        at = self.at
        return self.each("x", "rx", lev, sp, at.device(at.level, at.across), own=own)

    def over_y(self, lev, sp, own=False):
        at = self.at
        return self.each("y", "ry", lev, sp, at.device(at.level, at.along), own=own)

    def corner_y(self, lev, sp):
        at = self.at
        return self.each("cy", "rcy", lev, sp, at.device(at.level, at.along), part=0)

    def corner_x(self, lev, sp):
        at = self.at
        return self.each("cx", "rcx", lev, sp, at.device(at.level, at.across), part=1)

    def near(self, lev, sp, core=None, own=False):
        at = self.at
        copies = []
        for n, (x_ref, *_) in enumerate(self.pairs):
            dst = self.block(n, lev, sp, core)
            sems = self.send_n.at[n, lev * 4 + sp], self.recv_n.at[n, lev * 4 + sp]
            device = at.device(at.level, at.spot, 1 - at.core)
            copies.append(remote(x_ref if own else dst, dst, *sems, device))
        return copies

    def own_copies(self):
        at = self.at
        return [
            pltpu.make_async_copy(x_ref, self.block(n, at.level, at.spot), self.own_sem.at[n])
            for n, (x_ref, *_) in enumerate(self.pairs)
        ]

    def take_own(self):
        for copy in self.own_copies():
            copy.wait()

    def begin(self):
        at = self.at
        pl.when(at.has_up)(lambda: start(self.up(at.level, own=True)))
        pl.when(at.has_down)(lambda: start(self.down(at.level, own=True)))
        start(self.over_x(at.level, at.spot, own=True))
        start(self.over_y(at.level, at.spot, own=True))
        if self.sibling:
            start(self.near(at.level, at.spot, own=True))
        if self.keeps_own:
            start(self.own_copies())

    def take_column(self, lev):
        at = self.at
        arrived(self.up(lev))
        pl.when((lev < at.level) & at.has_up)(lambda: start(self.up(lev)))
        pl.when((lev > at.level) & at.has_down)(lambda: start(self.down(lev)))
        start(self.over_x(lev, at.spot))
        start(self.over_y(lev, at.spot))
        if self.sibling:
            start(self.near(lev, at.spot))

    def take_x(self, lev):
        at = self.at
        arrived(self.over_x(lev, at.across))
        start(self.corner_y(lev, at.across))
        if self.sibling:
            start(self.near(lev, at.across))

    def take_y(self, lev):
        at = self.at
        arrived(self.over_y(lev, at.along))
        start(self.corner_x(lev, at.along))
        if self.sibling:
            start(self.near(lev, at.along))

    def take_corner(self, lev):
        at = self.at
        arrived(self.corner_y(lev, at.corner))
        arrived(self.corner_x(lev, at.corner))
        if self.sibling:
            start(self.near(lev, at.corner))

    def take_near(self, lev, sp):
        arrived(self.near(lev, sp, 1 - self.at.core))

    def steps(self):
        levels, steps = self.at.levels, []
        for s in range(1, levels + 2):
            if s < levels:
                steps.append(lambda lev=self.order[s]: self.take_column(lev))
            if s - 1 < levels:
                steps.append(lambda lev=self.order[s - 1]: self.take_x(lev))
                steps.append(lambda lev=self.order[s - 1]: self.take_y(lev))
            if s >= 2:
                steps.append(lambda lev=self.order[s - 2]: self.take_corner(lev))
        return steps

    def finish(self, near=True):
        at = self.at
        if near:
            self.take_own()
        for lev in range(at.levels):
            pl.when(at.has_up & (lev <= at.level))(lambda lev=lev: sent(self.up(lev)))
            pl.when(at.has_down & (lev >= at.level))(lambda lev=lev: sent(self.down(lev)))
            sent(self.over_x(lev, at.spot))
            sent(self.over_y(lev, at.spot))
            sent(self.corner_y(lev, at.across))
            sent(self.corner_x(lev, at.along))
            if self.sibling:
                for sp in range(4):
                    sent(self.near(lev, sp))
                    if near:
                        self.take_near(lev, sp)


def start(copies):
    for copy in copies:
        copy.start()


def arrived(copies):
    for copy in copies:
        copy.wait_recv()


def sent(copies):
    for copy in copies:
        copy.wait_send()


def dot_nn(left, right):
    return lax.dot_general(left, right, (((1,), (0,)), ((), ())), preferred_element_type=F32)


def dot_tn(left, right):
    return lax.dot_general(left, right, (((0,), (0,)), ((), ())), preferred_element_type=F32)


def dot_nt(left, right):
    return lax.dot_general(left, right, (((1,), (1,)), ((), ())), preferred_element_type=F32)


def experts_kernel(
    levels, sizes, x_ref, g_ref, m_ref, eg_ref, eu_ref, ed_ref, small_ref, sd_ref,
    rows_ref, grads_ref, marks_ref, back_ref, out_ref, gm_ref, dgate_ref, dup_ref, ddown_ref, shared_ref,
    x_buf, g_buf, mark_buf, cu_buf, g_val, mixed_buf, act_buf, back_buf, out_buf, gm_buf, mark_t,
    in_sem, out_sem, gm_val, gw_ref, gd_ref, gate_ref, down_ref, w_sem, *sems,
):
    hidden, used, full = sizes
    at = Place(levels)
    at.enter(True)
    gather = Gather(at, True, [(x_ref, rows_ref), (g_ref, grads_ref), (m_ref, marks_ref)], sems, False)
    gather.begin()
    size, experts = used - hidden, m_ref.shape[0]
    pieces = [
        (eg_ref, gate_ref, 0, hidden),
        (eu_ref, gate_ref, full, hidden),
        (small_ref.at[pl.ds(0, size)], gate_ref, hidden, size),
        (small_ref.at[pl.ds(size, size)], gate_ref, full + hidden, size),
        (small_ref.at[pl.ds(2 * size, experts)], gate_ref, used, experts),
        (ed_ref, down_ref, 0, hidden),
        (sd_ref, down_ref, hidden, size),
    ]
    weights = [
        pltpu.make_async_copy(src, dst.at[pl.ds(row, count)], w_sem.at[n])
        for n, (src, dst, row, count) in enumerate(pieces)
    ]
    start(weights)
    for ref, row, end in ((gate_ref, used + experts, full), (gate_ref, full + used, 2 * full), (down_ref, used, full)):
        if end > row:
            ref[row:end, :] = jnp.zeros((end - row, ref.shape[1]), BF16)
    place = at.level * 4 + at.spot
    units = 4 * levels
    plan = [(0, 0)]
    for s in range(1, levels + 2):
        if s < levels:
            plan.append((s, 0))
        if s - 1 < levels:
            plan += [(s - 1, 1), (s - 1, 2)]
        if s >= 2:
            plan.append((s - 2, 3))
    rows = x_ref.shape[0]
    batch = 2 * rows

    def pick(k, values):
        result = jnp.int32(0) + values[0]
        for j in range(1, len(values)):
            result = jnp.where(k == j, values[j], result)
        return result

    def unit(k):
        visit = pick(k, [v for v, _ in plan])
        kind = pick(k, [t for _, t in plan])
        lev = pick(visit, gather.order)
        sp = pick(kind, [at.spot, at.across, at.along, at.corner])
        return lev, sp, kind

    def loads(k, first):
        slot = lax.rem(k, 4)
        blocks = pl.ds(first, 2)
        return [
            pltpu.make_async_copy(rows_ref.at[blocks], x_buf.at[slot], in_sem.at[slot, 0]),
            pltpu.make_async_copy(grads_ref.at[blocks], g_buf.at[slot], in_sem.at[slot, 1]),
            pltpu.make_async_copy(marks_ref.at[blocks], mark_buf.at[slot], in_sem.at[slot, 2]),
        ]

    def stores(k, first):
        slot = lax.rem(k, 2)
        rng = pl.ds(pl.multiple_of(first * rows, batch), batch)
        pairs = [(back_buf, back_ref), (out_buf, out_ref)]
        return [
            pltpu.make_async_copy(buf.at[slot], ref.at[rng], out_sem.at[slot, n])
            for n, (buf, ref) in enumerate(pairs)
        ]

    def serve(k):
        lev, sp, kind = unit(k)
        pl.when(kind == 0)(lambda: gather.take_column(lev))
        pl.when(kind == 1)(lambda: gather.take_x(lev))
        pl.when(kind == 2)(lambda: gather.take_y(lev))
        pl.when(kind == 3)(lambda: gather.take_corner(lev))

    def fetch(k):
        lev, sp, _ = unit(k)
        gather.take_near(lev, sp)
        start(loads(k, (lev * 4 + sp) * 2))

    def fetch_own():
        gather.take_near(at.level, at.spot)
        theirs = 1 - at.core
        triples = [(x_ref, rows_ref, x_buf), (g_ref, grads_ref, g_buf), (m_ref, marks_ref, mark_buf)]
        for n, (own, gathered, buf) in enumerate(triples):
            sem = in_sem.at[0, n]
            other = gathered.at[place * 2 + theirs]
            pltpu.make_async_copy(own, buf.at[0, at.core], sem).start()
            pltpu.make_async_copy(other, buf.at[0, theirs], sem).start()

    def lanes(n):
        return lax.broadcasted_iota(jnp.int32, (batch, 128), 1) + n * 128

    def mixing():
        tail = full // 128 - 1
        mark = mark_t[...]
        masked = jnp.where(mark > 0.5, cu_buf[:, full - 128 : full], MASKED)
        top = jnp.max(masked, axis=1, keepdims=True)
        weight = jnp.where(mark > 0.5, jnp.exp(masked - top), 0.0)
        mine = jnp.where((lanes(tail) == used + place) & (mark > 1.5), weight, 0.0)
        return jnp.sum(mine, axis=1, keepdims=True) / jnp.sum(weight, axis=1, keepdims=True)

    def elementwise(odd):
        mix = jnp.broadcast_to(mixing(), (batch, 128))
        total = jnp.zeros((batch, 128), F32)
        for n in range(full // 128):
            cols = slice(n * 128, (n + 1) * 128)
            up_cols = slice(full + n * 128, full + (n + 1) * 128)
            gate, upper, back = cu_buf[:, cols], cu_buf[:, up_cols], g_val[:, cols]
            whole = (n + 1) * 128 <= hidden
            scale = mix
            if not whole:
                scale = jnp.where(lanes(n) < hidden, mix, jnp.where(lanes(n) < used, 1.0, 0.0))
            sig = jax.nn.sigmoid(gate)
            act = gate * sig
            active = act * upper
            grad_act = scale * back
            slope = sig * (1.0 + gate * (1.0 - sig))
            mixed_buf[odd, :, cols] = (scale * active).astype(BF16)
            act_buf[odd, :, cols] = (grad_act * upper * slope).astype(BF16)
            act_buf[odd, :, up_cols] = (grad_act * act).astype(BF16)
            term = active * back
            total = total + (term if whole else jnp.where(lanes(n) < hidden, term, 0.0))
        gm_buf[...] = total

    def forward(k):
        lev, sp, _ = unit(k)
        first = (lev * 4 + sp) * 2
        slot = lax.rem(k, 4)
        for copy in loads(k, first):
            copy.wait()
        x = x_buf[slot].reshape(batch, -1)
        cu_buf[...] = dot_nt(x, gate_ref[...])
        g_val[...] = dot_nt(g_buf[slot].reshape(batch, -1), down_ref[...])
        for n in range(2):
            marks = mark_buf[slot, n]
            above = jnp.zeros((used - (full - 128), 128), F32)
            below = jnp.zeros((full - used - marks.shape[0], 128), F32)
            mark_t[pl.ds(n * rows, rows), :] = jnp.transpose(jnp.concatenate([above, marks, below], axis=0))
        elementwise(lax.rem(k, 2))

    def backward(k):
        lev, sp, _ = unit(k)
        first = (lev * 4 + sp) * 2
        slot = lax.rem(k, 2)

        @pl.when(k >= 2)
        def _():
            for copy in stores(k, 0):
                copy.wait()

        back_buf[slot] = dot_nn(act_buf[slot], gate_ref[...]).astype(BF16)
        out_buf[slot] = dot_nn(mixed_buf[slot], down_ref[...]).astype(BF16)
        for n in range(2):
            gm = jnp.transpose(gm_buf[pl.ds(n * rows, rows), :])
            gm_val[pl.ds(first + n, 1), :] = jnp.sum(gm, axis=0, keepdims=True)
        start(stores(k, first))

        both = pl.ds(lax.rem(k, 4) - 1, 2)

        def gate_grad(m, carry):
            part = pl.ds(pl.multiple_of(m * 256, 256), 256)
            left = act_buf[:, :, part].reshape(2 * batch, 256)
            gw_ref[part, :] += dot_tn(left, x_buf[both].reshape(2 * batch, -1))
            return carry

        def down_grad(m, carry):
            part = pl.ds(pl.multiple_of(m * 256, 256), 256)
            left = mixed_buf[:, :, part].reshape(2 * batch, 256)
            gd_ref[part, :] += dot_tn(left, g_buf[both].reshape(2 * batch, -1))
            return carry

        @pl.when(slot == 1)
        def _():
            lax.fori_loop(0, gw_ref.shape[0] // 256, gate_grad, 0)
            lax.fori_loop(0, full // 256, down_grad, 0)

    gw_ref[...] = jnp.zeros_like(gw_ref)
    gd_ref[...] = jnp.zeros_like(gd_ref)
    fetch_own()
    for copy in weights:
        copy.wait()

    def loop(k, carry):
        pl.when((k > 0) & (k + 1 < units))(lambda: serve(k + 1))
        forward(k)
        pl.when(k == 0)(lambda: serve(1))
        pl.when(k + 1 < units)(lambda: fetch(k + 1))
        backward(k)
        return carry

    lax.fori_loop(0, units, loop, 0)
    gm_ref[...] = gm_val[...]
    finals = [
        pltpu.make_async_copy(src.at[pl.ds(row, hidden)], dst, w_sem.at[n])
        for n, (src, row, dst) in enumerate(
            ((gw_ref, 0, dgate_ref), (gw_ref, full, dup_ref), (gd_ref, 0, ddown_ref))
        )
    ]
    start(finals)
    for n, (ref, row) in enumerate(((gw_ref, hidden), (gw_ref, full + hidden), (gd_ref, hidden))):
        shared_ref[n * size : (n + 1) * size, :] = ref[row : row + size, :].astype(BF16)
    for copy in finals:
        copy.wait()
    for k in (0, 1):
        for copy in stores(k, 0):
            copy.wait()
    gather.finish(near=False)


def experts_rows(x, grads, marks, weights, hidden, used, full, levels, collective_id):
    rows, width = x.shape
    blocks = 8 * levels
    total = blocks * rows
    dma = pltpu.SemaphoreType.DMA
    vmem = pltpu.VMEM
    anywhere = pl.BlockSpec(memory_space=pl.ANY)
    inside = pl.BlockSpec(memory_space=vmem)
    shape = jax.ShapeDtypeStruct
    batch = 2 * rows
    return pl.pallas_call(
        functools.partial(experts_kernel, levels, (hidden, used, full)),
        out_shape=[
            shape((blocks, rows, width), BF16),
            shape((blocks, rows, width), BF16),
            shape((blocks, *marks.shape), F32),
            shape((total, width), BF16),
            shape((total, width), BF16),
            shape((blocks, rows), F32),
            shape((hidden, width), F32),
            shape((hidden, width), F32),
            shape((hidden, width), F32),
            shape((3 * (used - hidden), width), BF16),
        ],
        in_specs=[anywhere] * 8,
        out_specs=[anywhere] * 5 + [inside] + [anywhere] * 3 + [inside],
        scratch_shapes=[
            vmem((4, 2, rows, width), BF16),
            vmem((4, 2, rows, width), BF16),
            vmem((4, 2, *marks.shape), F32),
            vmem((batch, 2 * full), F32),
            vmem((batch, full), F32),
            vmem((2, batch, full), BF16),
            vmem((2, batch, 2 * full), BF16),
            vmem((2, batch, width), BF16),
            vmem((2, batch, width), BF16),
            vmem((batch, 128), F32),
            vmem((batch, 128), F32),
            dma((4, 3)),
            dma((2, 2)),
            vmem((blocks, rows), F32),
            vmem((2 * full, width), F32),
            vmem((full, width), F32),
            vmem((2 * full, width), BF16),
            vmem((full, width), BF16),
            dma((7,)),
        ]
        + Gather.scratch(levels, 3),
        compiler_params=pltpu.CompilerParams(
            collective_id=collective_id,
            has_side_effects=True,
            vmem_limit_bytes=56 * 1024 * 1024,
        ),
    )(x, grads, marks, *weights)


def shared_kernel(slices, x_ref, gate_ref, up_ref, down_ref, gate_buf, up_buf, down_buf, sem):
    part, units = gate_ref.shape
    stored = units // 2
    size = stored // slices
    copies = []
    for n in range(slices):
        for c in range(2):
            rows = pl.ds(c * stored + n * size, size)
            src = x_ref.at[n, pl.ds(c * size, size)]
            for buf, lanes in ((gate_buf, pl.ds(0, part)), (up_buf, pl.ds(part, part))):
                copies.append(pltpu.make_async_copy(src.at[:, lanes], buf.at[rows], sem.at[len(copies)]))
        src, dst = x_ref.at[n, pl.ds(2 * size, size)], down_buf.at[pl.ds(n * size, size)]
        copies.append(pltpu.make_async_copy(src, dst, sem.at[len(copies)]))
    start(copies)
    for copy in copies:
        copy.wait()
    down_ref[...] = down_buf[...].astype(F32)
    for buf, ref in ((gate_buf, gate_ref), (up_buf, up_ref)):
        for n in range(units // 128):
            rows = pl.ds(n * 128, 128)
            ref[:, rows] = jnp.transpose(buf[rows, :].astype(F32))


def shared_grads(gathered, slices, part, stored):
    width = gathered.shape[2]
    vmem = pltpu.VMEM
    inside = pl.BlockSpec(memory_space=vmem)
    shape = jax.ShapeDtypeStruct
    return pl.pallas_call(
        functools.partial(shared_kernel, slices),
        out_shape=[
            shape((part, 2 * stored), F32),
            shape((part, 2 * stored), F32),
            shape((stored, width), F32),
        ],
        in_specs=[pl.BlockSpec(memory_space=pl.ANY)],
        out_specs=[inside] * 3,
        scratch_shapes=[
            vmem((2 * stored, part), BF16),
            vmem((2 * stored, part), BF16),
            vmem((stored, width), BF16),
            pltpu.SemaphoreType.DMA((5 * slices,)),
        ],
        compiler_params=pltpu.CompilerParams(vmem_limit_bytes=32 * 1024 * 1024),
    )(gathered)


def destinations(levels):
    return [
        sorted(range(levels), key=lambda to: (-abs(to - here), -to)) for here in range(levels)
    ]


def add_rows(write, sources, rows):
    step = 16

    def body(k, carry):
        r = pl.ds(pl.multiple_of(k * step, step), step)
        total = sources[0](r)
        for source in sources[1:]:
            total = total + source(r)
        write(r, total)
        return carry

    lax.fori_loop(0, rows // step, body, 0)


def reads(ref):
    return lambda r: ref[r, :].astype(F32)


def writes(ref):
    def write(r, total):
        ref[r, :] = total.astype(ref.dtype)

    return write


class Scatter:
    def __init__(self, at, sibling, x_ref, out_ref, refs, row=None):
        self.at, self.sibling, self.x_ref, self.out_ref = at, sibling, x_ref, out_ref
        self.row = row
        self.acc, self.near, self.hx, self.hy, self.fx, self.fy = refs[:6]
        self.out_buf, self.za, self.zb = refs[6:9]
        self.own_sem, self.send_n, self.recv_n = refs[9:12]
        self.send = dict(zip(("hx", "hy", "fx", "fy", "up", "dn"), refs[12:18]))
        self.recv = dict(zip(("hx", "hy", "fx", "fy", "za", "zb"), refs[18:24]))
        self.rows = out_ref.shape[0]
        table = destinations(at.levels)
        self.order = [at.choose([row[s] for row in table]) for s in range(at.levels)]

    SCRATCH = 24

    @staticmethod
    def scratch(levels, sibling, rows, width):
        dma, vmem = pltpu.SemaphoreType.DMA, pltpu.VMEM
        blocks = levels * 4
        return (
            [
                vmem((blocks, rows, width), BF16),
                vmem((blocks if sibling else 1, rows, width), BF16),
                vmem((levels, rows // 2, width), BF16),
                vmem((levels, rows // 2, width), BF16),
            ]
            + [vmem((levels, rows, width), BF16)] * 5
            + [dma((blocks,))] * 3
            + [dma((levels,))] * 12
        )

    def own(self, lev, sp):
        b = lev * 4 + sp
        src = self.x_ref.at[b * 2 + self.at.core if self.sibling else b]
        if self.row is not None:
            src = src.at[pl.ds(self.row, self.rows)]
        return pltpu.make_async_copy(src, self.acc.at[b], self.own_sem.at[b])

    def to_sibling(self, lev, sp):
        at, b = self.at, lev * 4 + sp
        sems = self.send_n.at[b], self.recv_n.at[b]
        src = self.x_ref.at[b * 2 + 1 - at.core]
        return remote(src, self.near.at[b], *sems, at.device(at.level, at.spot, 1 - at.core))

    def side(self, name, src, dst, lev, spot):
        sems = self.send[name].at[lev], self.recv[name].at[lev]
        return remote(src, dst, *sems, self.at.device(self.at.level, spot))

    def half_y(self, lev):
        src = self.acc.at[lev * 4 + self.at.corner].at[pl.ds(0, self.rows // 2)]
        return self.side("hy", src, self.hy.at[lev], lev, self.at.along)

    def half_x(self, lev):
        src = self.acc.at[lev * 4 + self.at.corner].at[pl.ds(self.rows // 2, self.rows // 2)]
        return self.side("hx", src, self.hx.at[lev], lev, self.at.across)

    def full_x(self, lev):
        return self.side("fx", self.acc.at[lev * 4 + self.at.across], self.fx.at[lev], lev, self.at.across)

    def full_y(self, lev):
        return self.side("fy", self.acc.at[lev * 4 + self.at.along], self.fy.at[lev], lev, self.at.along)

    def go_up(self, lev):
        sems = self.send["up"].at[lev], self.recv["zb"].at[lev]
        device = self.at.device(self.at.level + 1, self.at.spot)
        return remote(self.out_buf.at[lev], self.zb.at[lev], *sems, device)

    def go_down(self, lev):
        sems = self.send["dn"].at[lev], self.recv["za"].at[lev]
        device = self.at.device(self.at.level - 1, self.at.spot)
        return remote(self.out_buf.at[lev], self.za.at[lev], *sems, device)

    def spots(self):
        return self.at.corner, self.at.across, self.at.along, self.at.spot

    def begin(self):
        for lev in self.order:
            for sp in self.spots():
                if self.sibling:
                    self.to_sibling(lev, sp).start()
                self.own(lev, sp).start()

    def local(self, lev):
        for n, sp in enumerate(self.spots()):
            ref = self.acc.at[lev * 4 + sp]
            self.own(lev, sp).wait()
            if self.sibling:
                self.to_sibling(lev, sp).wait_recv()
                add_rows(writes(ref), [reads(ref), reads(self.near.at[lev * 4 + sp])], self.rows)
            if n == 0:
                self.half_y(lev).start()
                self.half_x(lev).start()

    def halves(self, lev):
        half = self.rows // 2
        self.half_y(lev).wait_recv()
        ref = self.acc.at[lev * 4 + self.at.across].at[pl.ds(0, half)]
        add_rows(writes(ref), [reads(ref), reads(self.hy.at[lev])], half)
        self.full_x(lev).start()
        self.half_x(lev).wait_recv()
        ref = self.acc.at[lev * 4 + self.at.along].at[pl.ds(half, half)]
        add_rows(writes(ref), [reads(ref), reads(self.hx.at[lev])], half)
        self.full_y(lev).start()

    def column(self, lev):
        at, rows, level = self.at, self.rows, self.at.level
        self.full_x(lev).wait_recv()
        self.full_y(lev).wait_recv()
        own = [reads(self.acc.at[lev * 4 + at.spot]), reads(self.fx.at[lev]), reads(self.fy.at[lev])]
        above, below = reads(self.za.at[lev]), reads(self.zb.at[lev])
        passed = writes(self.out_buf.at[lev])
        final = writes(self.out_ref)

        def send(has, arrival, term, departure):
            @pl.when(has)
            def _():
                arrival(lev).wait_recv()
                add_rows(passed, [*own, term], rows)

            pl.when(jnp.logical_not(has))(lambda: add_rows(passed, own, rows))
            departure(lev).start()

        pl.when(lev < level)(lambda: send(at.has_up, self.go_down, above, self.go_down))
        pl.when(lev > level)(lambda: send(at.has_down, self.go_up, below, self.go_up))

        @pl.when(lev == level)
        def _():
            pl.when(at.has_up)(lambda: self.go_down(lev).wait_recv())
            pl.when(at.has_down)(lambda: self.go_up(lev).wait_recv())
            both = at.has_up & at.has_down
            pl.when(both)(lambda: add_rows(final, [*own, above, below], rows))
            pl.when(jnp.logical_not(at.has_down))(lambda: add_rows(final, [*own, above], rows))
            pl.when(jnp.logical_not(at.has_up))(lambda: add_rows(final, [*own, below], rows))

    def steps(self):
        levels, steps = self.at.levels, []
        for s in range(levels + 2):
            if s < levels:
                steps.append(lambda lev=self.order[s]: self.local(lev))
            if 0 <= s - 1 < levels:
                steps.append(lambda lev=self.order[s - 1]: self.halves(lev))
            if s >= 2:
                steps.append(lambda lev=self.order[s - 2]: self.column(lev))
        return steps

    def finish(self):
        for lev in range(self.at.levels):
            if self.sibling:
                for sp in range(4):
                    self.to_sibling(lev, sp).wait_send()
            sent([self.half_y(lev), self.half_x(lev), self.full_x(lev), self.full_y(lev)])
            pl.when(lev < self.at.level)(lambda lev=lev: self.go_down(lev).wait_send())
            pl.when(lev > self.at.level)(lambda lev=lev: self.go_up(lev).wait_send())


def dense_kernel(levels, spans, x_ref, flat_ref, all_ref, flat_all_ref, *refs):
    at = Place(levels)
    at.enter(False)
    sums, refs = refs[:2], refs[2:]
    size = Scatter.SCRATCH
    scatters = [
        Scatter(at, False, x_ref, sums[n], refs[n * size : (n + 1) * size], spans[n][0]) for n in range(2)
    ]
    refs = refs[2 * size :]
    pairs = [[(sums[n], all_ref, spans[n][0])] for n in range(2)]
    pairs[1].append((flat_ref, flat_all_ref))
    gathers = []
    for n in range(2):
        gathers.append(Gather(at, False, pairs[n], refs[n * 14 : (n + 1) * 14]))
    for task in scatters:
        task.begin()
    steps = []
    for n, lag in enumerate((0, 7)):
        begin = len(scatters[n].steps()) + lag
        steps += [(s + lag, n, step) for s, step in enumerate(scatters[n].steps())]
        steps.append((begin - 0.5, n, gathers[n].begin))
        steps += [(begin + s, 2 + n, step) for s, step in enumerate(gathers[n].steps())]
    for _, _, step in sorted(steps, key=lambda entry: entry[:2]):
        step()
    for task in [*scatters, *gathers]:
        task.finish()


def sum_dense(x, flat, levels, collective_id):
    blocks, rows, width = x.shape
    first = -(-rows // 64) * 32
    spans = [(0, first), (first, rows - first)]
    vmem, anywhere = pltpu.VMEM, pl.BlockSpec(memory_space=pl.ANY)
    shape = jax.ShapeDtypeStruct
    return pl.pallas_call(
        functools.partial(dense_kernel, levels, spans),
        out_shape=[shape(x.shape, BF16), shape((blocks, *flat.shape), BF16)],
        in_specs=[anywhere, anywhere],
        out_specs=[anywhere, anywhere],
        scratch_shapes=[vmem((n, width), BF16) for _, n in spans]
        + Scatter.scratch(levels, False, spans[0][1], width)
        + Scatter.scratch(levels, False, spans[1][1], width)
        + Gather.scratch(levels, 1)
        + Gather.scratch(levels, 2),
        compiler_params=pltpu.CompilerParams(
            collective_id=collective_id,
            has_side_effects=True,
            vmem_limit_bytes=60 * 1024 * 1024,
        ),
    )(x, flat)


def exchange_kernel(
    levels, back_ref, out_ref, part_ref, rows_ref, sum_ref, all_ref, block, send_s, recv_s, own_s, *refs
):
    at = Place(levels)
    at.enter(True)
    size = Scatter.SCRATCH
    first = Scatter(at, True, back_ref, rows_ref, refs[:size])
    second = Scatter(at, True, out_ref, sum_ref, refs[size : 2 * size])
    gather = Gather(at, False, [(block, all_ref)], refs[2 * size :])
    units, half = part_ref.shape[0] // 3, part_ref.shape[1] // 2
    mine = pl.ds(pl.multiple_of(at.core * units, units), units)
    own, theirs, sends = [], [], []
    for n in range(2):
        rows, lanes = pl.ds(n * units, units), pl.ds(n * half, half)

        def side(core):
            return part_ref.at[rows, pl.ds(pl.multiple_of(core * half, 128), half)]

        own.append(pltpu.make_async_copy(side(at.core), block.at[mine, lanes], own_s.at[n]))
        device = at.device(at.level, at.spot, 1 - at.core)
        sems = send_s.at[n], recv_s.at[n]
        sends.append(remote(side(1 - at.core), block.at[mine, lanes], *sems, device))
    down = pl.ds(2 * units, units)
    own.append(pltpu.make_async_copy(part_ref.at[down], block.at[down], own_s.at[2]))
    start(sends)
    start(own)
    first.begin()
    second.begin()
    for copy in own:
        copy.wait()
    arrived(sends)
    gather.begin()
    steps = [(s, 0, step) for s, step in enumerate(first.steps())]
    steps += [(s + 7, 1, step) for s, step in enumerate(second.steps())]
    steps += [(s + 2, 2, step) for s, step in enumerate(gather.steps())]
    for _, _, step in sorted(steps, key=lambda entry: entry[:2]):
        step()
    sent(sends)
    first.finish()
    second.finish()
    gather.finish()


def exchange_wide(back, out, part, levels, collective_id):
    rows, width = back.shape[1:]
    dma = pltpu.SemaphoreType.DMA
    anywhere, inside = pl.BlockSpec(memory_space=pl.ANY), pl.BlockSpec(memory_space=pltpu.VMEM)
    shape = jax.ShapeDtypeStruct
    return pl.pallas_call(
        functools.partial(exchange_kernel, levels),
        out_shape=[
            shape((rows, width), BF16),
            shape((rows, width), BF16),
            shape((levels * 4, *part.shape), BF16),
        ],
        in_specs=[anywhere, anywhere, inside],
        out_specs=[inside, inside, anywhere],
        scratch_shapes=[pltpu.VMEM(part.shape, BF16), dma((2,)), dma((2,)), dma((3,))]
        + Scatter.scratch(levels, True, rows, width) * 2
        + Gather.scratch(levels, 1),
        compiler_params=pltpu.CompilerParams(
            collective_id=collective_id,
            has_side_effects=True,
            vmem_limit_bytes=60 * 1024 * 1024,
        ),
        cost_estimate=pl.CostEstimate(
            flops=40 * 10**9, bytes_accessed=200 * 10**6, transcendentals=0
        ),
    )(back, out, part)


def slots_path(
    tokens,
    cotangent,
    lengths,
    routes,
    keep,
    attn_gain,
    w_query,
    w_key,
    w_value,
    w_out,
    ffn_gain,
    w_router,
    shared_gate,
    shared_up,
    shared_down,
    expert_gate,
    expert_up,
    expert_down,
):
    narrow_size = lax.axis_size("narrow")
    narrow_index = lax.axis_index("narrow")
    wide_size = lax.axis_size("wide")
    local_rows = tokens.shape[0]
    model_width = tokens.shape[1]
    head_count = model_width // HEAD_DIM
    row_length = local_rows * narrow_size
    capacity = 8 * (3 * local_rows * TOPK // (16 * wide_size) + 1)
    gathered = (
        lax.all_gather(attn_gain, "narrow", axis=0, tiled=True),
        lax.all_gather(w_query, "narrow", axis=0, tiled=True),
        lax.all_gather(w_key, "narrow", axis=0, tiled=True),
        lax.all_gather(w_value, "narrow", axis=0, tiled=True),
        lax.all_gather(w_out, "narrow", axis=0, tiled=True),
        lax.all_gather(ffn_gain, "narrow", axis=0, tiled=True),
        lax.all_gather(w_router, "narrow", axis=0, tiled=True),
        lax.all_gather(shared_gate, "narrow", axis=0, tiled=True),
        lax.all_gather(shared_up, "narrow", axis=0, tiled=True),
        lax.all_gather(shared_down, "narrow", axis=0, tiled=True),
    )
    attn_scale = gathered[0].astype(jnp.float32)
    query_proj = gathered[1]
    key_proj = gathered[2]
    value_proj = gathered[3]
    output_proj = gathered[4]
    ffn_scale = gathered[5].astype(jnp.float32)
    router_proj = gathered[6]
    common_gate = gathered[7]
    common_upper = gathered[8]
    common_down = gathered[9]
    expert_mats = (expert_gate, expert_up, expert_down)
    routed_gate = expert_mats[0][0]
    routed_upper = expert_mats[1][0]
    routed_down = expert_mats[2][0]
    doc_lens = lengths[0]
    key_index = jnp.arange(row_length, dtype=jnp.int32)
    key_doc, unused = doc_layout(key_index, doc_lens)
    query_index = narrow_index * local_rows + jnp.arange(local_rows, dtype=jnp.int32)
    query_doc, query_pos = doc_layout(query_index, doc_lens)
    cosine, sine_table = rotary_angles(query_pos)
    inputs = tokens.astype(jnp.float32)
    normed, unit_one, scale_one = norm_forward(inputs, attn_scale)
    normed_one = normed.astype(jnp.bfloat16)
    head_shape = (local_rows, head_count, HEAD_DIM)
    query_rows = rotate(matmul(normed_one, query_proj).reshape(head_shape), cosine, sine_table)
    query_rows = (query_rows * HEAD_DIM ** (-0.5)).astype(jnp.bfloat16)
    key_rows = rotate(matmul(normed_one, key_proj).reshape(head_shape), cosine, sine_table).astype(
        jnp.bfloat16
    )
    valued = matmul(normed_one, value_proj).astype(jnp.bfloat16)
    all_keys, all_values = (
        lax.all_gather(key_rows.reshape(local_rows, model_width), "narrow", axis=0, tiled=True),
        lax.all_gather(valued, "narrow", axis=0, tiled=True),
    )
    all_keys = all_keys.reshape(row_length, head_count, HEAD_DIM)
    all_values = all_values.reshape(row_length, head_count, HEAD_DIM)
    block_rows = min(local_rows, 512)
    blocks = local_rows // block_rows
    query_blocks = query_rows.reshape(blocks, block_rows, head_count, HEAD_DIM)
    doc_blocks = query_doc.reshape(blocks, block_rows)
    index_blocks = query_index.reshape(blocks, block_rows)

    def allowed_for(doc_rows, index_rows):
        return (doc_rows[:, None] == key_doc[None, :]) & (key_index[None, :] <= index_rows[:, None])

    def forward_block(map_item):
        return attend_block(
            map_item[0], all_keys, all_values, allowed_for(map_item[1], map_item[2])
        )

    attended, logsum = lax.map(forward_block, (query_blocks, doc_blocks, index_blocks))
    attended = attended.reshape(local_rows, model_width)
    hidden = inputs + matmul(attended, output_proj)
    normed, unit_two, scale_two = norm_forward(hidden, ffn_scale)
    normed_two = normed.astype(jnp.bfloat16)
    logits = matmul(normed_two, router_proj)
    experts = router_proj.shape[1]
    pick_table = (routes[:, :, None] == jnp.arange(experts, dtype=jnp.int32)[None, None, :]).astype(
        jnp.float32
    )
    chosen = jnp.sum(pick_table * logits[:, None, :], axis=2)
    gate_probs = jax.nn.softmax(chosen, axis=1)
    keep_float = keep.astype(jnp.float32)
    mixing = gate_probs * keep_float
    common_gate_vals, common_upper_vals, common_act = expert_forward(
        normed_two, common_gate, common_upper
    )
    shared_out = matmul(common_act, common_down)
    pair_expert = routes.reshape(-1)
    pair_total = pair_expert.shape[0]
    onehot = (pair_expert[:, None] == jnp.arange(experts, dtype=jnp.int32)[None, :]).astype(
        jnp.int32
    )
    earlier = jnp.cumsum(onehot, axis=0) - onehot
    slot_place = jnp.sum(earlier * onehot, axis=1)
    slot_index = pair_expert * capacity + slot_place
    slot_total = experts * capacity
    source = (
        jnp.full((slot_total,), -1, jnp.int32)
        .at[slot_index]
        .set(jnp.arange(pair_total, dtype=jnp.int32))
    )
    filled = source >= 0
    pair_index = jnp.maximum(source, 0)

    def fill_slots(in_rows, row_index):
        taken = jnp.take(in_rows, row_index, axis=0)
        return jnp.where(filled[:, None], taken, jnp.zeros((), in_rows.dtype)).reshape(
            experts, capacity, model_width
        )

    received = lax.all_to_all(
        fill_slots(normed_two, pair_index // TOPK), "wide", split_axis=0, concat_axis=0, tiled=True
    )
    expert_in = lax.all_gather(received, "narrow", axis=0, tiled=True).reshape(-1, model_width)
    routed_gate_vals, routed_upper_vals, routed_act = expert_forward(
        expert_in, routed_gate, routed_upper
    )
    partial_value = matmul(routed_act, routed_down)
    expert_out = lax.psum_scatter(partial_value, "narrow", scatter_dimension=0, tiled=True)
    returned = lax.all_to_all(
        expert_out.astype(jnp.bfloat16).reshape(wide_size, capacity, model_width),
        "wide",
        split_axis=0,
        concat_axis=0,
        tiled=True,
    )
    pair_out = (
        jnp.take(returned.reshape(slot_total, model_width), slot_index, axis=0)
        .astype(jnp.float32)
        .reshape(local_rows, TOPK, model_width)
    )
    routed = jnp.sum(mixing[:, :, None] * pair_out, axis=1)
    output = (hidden + shared_out + routed).astype(jnp.bfloat16)
    grad_output = cotangent.astype(jnp.float32)
    grad_pairs = (
        (mixing[:, :, None] * grad_output[:, None, :])
        .astype(jnp.bfloat16)
        .reshape(pair_total, model_width)
    )
    grad_mixing = jnp.sum(pair_out * grad_output[:, None, :], axis=2)
    grad_received = lax.all_to_all(
        fill_slots(grad_pairs, pair_index), "wide", split_axis=0, concat_axis=0, tiled=True
    )
    grad_expert_out = lax.all_gather(grad_received, "narrow", axis=0, tiled=True).reshape(
        -1, model_width
    )
    grad_expert_in, grad_rgate, grad_rupper, grad_rdown = expert_backward(
        expert_in,
        grad_expert_out,
        routed_gate_vals,
        routed_upper_vals,
        routed_act,
        routed_gate,
        routed_upper,
        routed_down,
    )
    grad_slot_rows = lax.psum_scatter(grad_expert_in, "narrow", scatter_dimension=0, tiled=True)
    expert_grads = (grad_rgate, grad_rupper, grad_rdown)
    grad_back = lax.all_to_all(
        grad_slot_rows.astype(jnp.bfloat16).reshape(wide_size, capacity, model_width),
        "wide",
        split_axis=0,
        concat_axis=0,
        tiled=True,
    )
    grad_pair_rows = jnp.take(
        grad_back.reshape(slot_total, model_width), slot_index, axis=0
    ).astype(jnp.float32)
    grad_normed = jnp.sum(grad_pair_rows.reshape(local_rows, TOPK, model_width), axis=1)
    grad_gates = grad_mixing * keep_float
    grad_chosen = gate_probs * (
        grad_gates - jnp.sum(gate_probs * grad_gates, axis=1, keepdims=True)
    )
    grad_logits = jnp.sum(pick_table * grad_chosen[:, :, None], axis=1).astype(jnp.bfloat16)
    grad_router = matmul_left(normed_two, grad_logits)
    grad_normed = grad_normed + matmul_right(grad_logits, router_proj)
    grad_common_in, grad_cgate, grad_cupper, grad_cdown = expert_backward(
        normed_two,
        cotangent,
        common_gate_vals,
        common_upper_vals,
        common_act,
        common_gate,
        common_upper,
        common_down,
    )
    grad_normed = grad_normed + grad_common_in
    grad_hidden_norm, grad_ffn = norm_backward(grad_normed, unit_two, scale_two, ffn_scale)
    grad_hidden = grad_output + grad_hidden_norm
    grad_branch = grad_hidden.astype(jnp.bfloat16)
    grad_output_proj = matmul_left(attended, grad_branch)
    grad_attended = (
        matmul_right(grad_branch, output_proj)
        .astype(jnp.bfloat16)
        .reshape(blocks, block_rows, head_count, HEAD_DIM)
    )

    def backward_block(running, map_item):
        grad_queries, grad_keys, grad_values = attend_back(
            map_item[0],
            all_keys,
            all_values,
            allowed_for(map_item[1], map_item[2]),
            map_item[3],
            map_item[4],
        )
        return ((running[0] + grad_keys, running[1] + grad_values), grad_queries)

    empty_keys = jnp.zeros((row_length, head_count, HEAD_DIM), jnp.float32)
    sums_kv, grad_query_rows = lax.scan(
        backward_block,
        (empty_keys, empty_keys),
        (query_blocks, doc_blocks, index_blocks, logsum, grad_attended),
    )
    grad_key_own, grad_value_own = (
        lax.psum_scatter(
            sums_kv[0].reshape(row_length, model_width).astype(jnp.bfloat16),
            "narrow",
            scatter_dimension=0,
            tiled=True,
        ).astype(jnp.float32),
        lax.psum_scatter(
            sums_kv[1].reshape(row_length, model_width).astype(jnp.bfloat16),
            "narrow",
            scatter_dimension=0,
            tiled=True,
        ).astype(jnp.float32),
    )
    grad_query_rows = rotate(
        grad_query_rows.reshape(head_shape) * HEAD_DIM ** (-0.5), cosine, -sine_table
    )
    grad_query_rows = grad_query_rows.reshape(local_rows, model_width).astype(jnp.bfloat16)
    grad_key_rows = (
        rotate(grad_key_own.reshape(head_shape), cosine, -sine_table)
        .reshape(local_rows, model_width)
        .astype(jnp.bfloat16)
    )
    grad_value_rows = grad_value_own.astype(jnp.bfloat16)
    grad_query_proj = matmul_left(normed_one, grad_query_rows)
    grad_key_proj = matmul_left(normed_one, grad_key_rows)
    grad_value_proj = matmul_left(normed_one, grad_value_rows)
    grad_normed_one = (
        matmul_right(grad_query_rows, query_proj)
        + matmul_right(grad_key_rows, key_proj)
        + matmul_right(grad_value_rows, value_proj)
    )
    grad_input_norm, grad_attn = norm_backward(grad_normed_one, unit_one, scale_one, attn_scale)
    grad_tokens = grad_hidden + grad_input_norm
    halves = (
        lax.psum_scatter(
            grad_attn.astype(jnp.bfloat16), "narrow", scatter_dimension=0, tiled=True
        ).astype(jnp.float32),
        lax.psum_scatter(
            grad_query_proj.astype(jnp.bfloat16), "narrow", scatter_dimension=0, tiled=True
        ).astype(jnp.float32),
        lax.psum_scatter(
            grad_key_proj.astype(jnp.bfloat16), "narrow", scatter_dimension=0, tiled=True
        ).astype(jnp.float32),
        lax.psum_scatter(
            grad_value_proj.astype(jnp.bfloat16), "narrow", scatter_dimension=0, tiled=True
        ).astype(jnp.float32),
        lax.psum_scatter(
            grad_output_proj.astype(jnp.bfloat16), "narrow", scatter_dimension=0, tiled=True
        ).astype(jnp.float32),
        lax.psum_scatter(
            grad_ffn.astype(jnp.bfloat16), "narrow", scatter_dimension=0, tiled=True
        ).astype(jnp.float32),
        lax.psum_scatter(
            grad_router.astype(jnp.bfloat16), "narrow", scatter_dimension=0, tiled=True
        ).astype(jnp.float32),
        lax.psum_scatter(
            grad_cgate.astype(jnp.bfloat16), "narrow", scatter_dimension=0, tiled=True
        ).astype(jnp.float32),
        lax.psum_scatter(
            grad_cupper.astype(jnp.bfloat16), "narrow", scatter_dimension=0, tiled=True
        ).astype(jnp.float32),
        lax.psum_scatter(
            grad_cdown.astype(jnp.bfloat16), "narrow", scatter_dimension=0, tiled=True
        ).astype(jnp.float32),
    )
    owned = lax.psum(
        (
            halves[0],
            halves[1],
            halves[2],
            halves[3],
            halves[4],
            halves[5],
            halves[6],
            halves[7],
            halves[8],
            halves[9],
        ),
        "wide",
    )
    return (
        output,
        grad_tokens,
        owned[0],
        owned[1],
        owned[2],
        owned[3],
        owned[4],
        owned[5],
        owned[6],
        owned[7],
        owned[8],
        owned[9],
        expert_grads[0][None],
        expert_grads[1][None],
        expert_grads[2][None],
    )


def tokens_path(
    tokens,
    cotangent,
    lengths,
    routes,
    keep,
    attn_gain,
    w_query,
    w_key,
    w_value,
    w_out,
    ffn_gain,
    w_router,
    shared_gate,
    shared_up,
    shared_down,
    expert_gate,
    expert_up,
    expert_down,
):
    core = lax.axis_index("narrow")
    place = lax.axis_index("wide")
    wide_size = lax.axis_size("wide")
    levels = wide_size // 4
    local_rows, width = tokens.shape
    row_length = 2 * local_rows
    part = width // 2
    heads = part // HEAD_DIM
    hidden_part = expert_gate.shape[2]
    stored = shared_gate.shape[1] // 2
    slice_width = -(-stored // (16 * wide_size)) * 16
    slices = stored // slice_width
    experts = w_router.shape[1]

    def swap(value):
        return lax.ppermute(value, "narrow", [(0, 1), (1, 0)])

    def other_rows(value):
        return jnp.concatenate([value[local_rows:], value[:local_rows]], axis=0)

    def in_order(mine, theirs, axis):
        return jnp.where(
            core == 0,
            jnp.concatenate([mine, theirs], axis=axis),
            jnp.concatenate([theirs, mine], axis=axis),
        )

    def columns(value, which, size):
        return lax.dynamic_slice_in_dim(value, which * size, size, axis=1)

    picks = (routes[:, :, None] == jnp.arange(experts, dtype=jnp.int32)[None, None, :]).astype(
        jnp.int32
    )
    marks = jnp.sum(picks * (1 + keep)[:, :, None], axis=1).astype(F32)

    first_unit = place * slice_width
    holds = place < slices

    def shared_slice(value, which, axis):
        begin = which * stored + first_unit
        taken = lax.dynamic_slice_in_dim(value, begin, slice_width, axis)
        return jnp.where(holds, taken, jnp.zeros((), value.dtype))

    gate_mine, up_mine = shared_slice(shared_gate, core, 1), shared_slice(shared_up, core, 1)
    gate_send, up_send = shared_slice(shared_gate, 1 - core, 1), shared_slice(shared_up, 1 - core, 1)
    down_slice = shared_slice(shared_down, 0, 0)
    gains = jnp.stack([attn_gain, ffn_gain])
    sent = swap(jnp.concatenate([gate_send.T, up_send.T, w_router.T], axis=0))
    gains = in_order(gains, swap(gains), 1).astype(F32)
    attn_scale, ffn_scale = gains[0], gains[1]
    dense = in_order(jnp.concatenate([gate_mine.T, up_mine.T, w_router.T], axis=0), sent, 1)
    router = dense[2 * slice_width :]

    row_tokens = jnp.concatenate([tokens, swap(tokens)], axis=0).astype(F32)
    normed, unit_one, scale_one = norm_forward(row_tokens, attn_scale)
    normed_one = columns(normed.astype(BF16), core, part)
    projections = [w_query, w_key, w_value]
    keep_side = jnp.concatenate([columns(w, core, part) for w in projections], axis=1)
    send_side = jnp.concatenate([columns(w, 1 - core, part) for w in projections], axis=1)
    arrived = swap(matmul(normed_one, send_side).astype(BF16))
    qkv = matmul(normed_one, keep_side) + other_rows(arrived).astype(F32)
    index = jnp.arange(local_rows, dtype=jnp.int32)
    index = jnp.concatenate([core * local_rows + index, (1 - core) * local_rows + index])
    docs, positions = doc_layout(index, lengths[0])
    allowed = (docs[:, None] == docs[None, :]) & (index[None, :] <= index[:, None])
    cosine, sine_table = rotary_angles(positions)
    head_shape = (row_length, heads, HEAD_DIM)
    query_rows = rotate(qkv[:, :part].reshape(head_shape), cosine, sine_table)
    query_rows = (query_rows * HEAD_DIM ** (-0.5)).astype(BF16)
    key_rows = rotate(qkv[:, part : 2 * part].reshape(head_shape), cosine, sine_table).astype(BF16)
    value_rows = qkv[:, 2 * part :].astype(BF16).reshape(head_shape)
    attended, logsum = attend_block(query_rows, key_rows, value_rows, allowed)
    attended = attended.reshape(row_length, part)
    branch = matmul(attended, w_out)
    arrived = swap(branch[local_rows:].astype(BF16))
    inputs = row_tokens[:local_rows]
    hidden = inputs + branch[:local_rows] + arrived.astype(F32)
    normed, unit_two, scale_two = norm_forward(hidden, ffn_scale)
    normed_two = normed.astype(BF16)

    used = hidden_part + slice_width
    full = -(-(used + experts) // 128) * 128

    (_, _, _, grad_rows, expert_out, grad_mix, *expert_grads, shared_part) = experts_rows(
        normed_two,
        cotangent,
        marks.T,
        [expert_gate[0].T, expert_up[0].T, expert_down[0], dense, down_slice],
        hidden_part,
        used,
        full,
        levels,
        1,
    )
    grad_mix = lax.all_to_all(
        grad_mix.reshape(wide_size, 2, local_rows), "wide", split_axis=0, concat_axis=0, tiled=True
    )
    pick_core = jnp.where(core == 0, grad_mix[:, 0], grad_mix[:, 1])
    send_core = jnp.where(core == 0, grad_mix[:, 1], grad_mix[:, 0])
    grad_mix = (pick_core + swap(send_core)).T
    block_shape = (2 * wide_size, local_rows, width)
    grad_rows, expert_out, shared_all = exchange_wide(
        grad_rows.reshape(block_shape), expert_out.reshape(block_shape), shared_part, levels, 2
    )
    output = (hidden + expert_out.astype(F32)).astype(BF16)
    grad_expert_gate, grad_expert_up, grad_expert_down = expert_grads
    grad_shared_gate, grad_shared_up, grad_shared_down = shared_grads(
        shared_all, slices, part, stored
    )

    marks = marks.astype(F32)
    routed = marks > 0.0
    logits = matmul_right(normed_two, router)
    masked = jnp.where(routed, logits, MASKED)
    weights = jnp.where(routed, jnp.exp(masked - jnp.max(masked, axis=1, keepdims=True)), 0.0)
    gates = weights / jnp.sum(weights, axis=1, keepdims=True)
    grad_gates = jnp.where(marks > 1.5, grad_mix, 0.0)
    grad_logits = gates * (grad_gates - jnp.sum(gates * grad_gates, axis=1, keepdims=True))
    grad_logits = grad_logits.astype(BF16)
    grad_router = matmul_left(normed_two, grad_logits)
    grad_normed = grad_rows.astype(F32) + matmul(grad_logits, router)
    grad_hidden_norm, grad_ffn = norm_backward(grad_normed, unit_two, scale_two, ffn_scale)
    grad_hidden = cotangent.astype(F32) + grad_hidden_norm
    grad_branch = grad_hidden.astype(BF16)
    row_branch = jnp.concatenate([grad_branch, swap(grad_branch)], axis=0)

    grad_w_out = matmul_left(attended, row_branch)
    grad_attended = matmul_right(row_branch, w_out).astype(BF16).reshape(head_shape)
    grad_queries, grad_keys, grad_values = attend_back(
        query_rows, key_rows, value_rows, allowed, logsum, grad_attended
    )
    grad_queries = rotate(grad_queries * HEAD_DIM ** (-0.5), cosine, -sine_table)
    grad_keys = rotate(grad_keys, cosine, -sine_table)
    mine = jnp.stack([grad_queries, grad_keys, grad_values]).reshape(3, row_length, part)
    mine = mine.astype(BF16)
    theirs = swap(mine)
    theirs = jnp.concatenate([theirs[:, local_rows:], theirs[:, :local_rows]], axis=1)
    grad_qkv = in_order(mine, theirs, 2)
    grad_dense = jnp.stack(
        [matmul_left(normed_one, grad_qkv[k]) for k in range(3)] + [grad_w_out]
    ).astype(BF16)
    grad_part = sum(matmul_right(grad_qkv[k], projections[k]) for k in range(3))
    grad_normed_one = in_order(
        grad_part[:local_rows], swap(grad_part[local_rows:].astype(BF16)).astype(F32), 1
    )
    grad_input_norm, grad_attn = norm_backward(
        grad_normed_one, unit_one[:local_rows], scale_one[:local_rows], attn_scale
    )
    grad_tokens = grad_hidden + grad_input_norm

    small = jnp.concatenate([grad_attn[:, None], grad_ffn[:, None], grad_router], axis=1)
    small_mine = lax.dynamic_slice_in_dim(small, core * part, part, 0)
    small_send = lax.dynamic_slice_in_dim(small, (1 - core) * part, part, 0)
    small = (small_mine + swap(small_send)).astype(BF16)
    size = small.size
    extra_rows = -(-size // (width * 16)) * 16
    flat = jnp.concatenate([small.reshape(-1), jnp.zeros((extra_rows * width - size,), BF16)])
    sum_rows = 4 * part // wide_size
    everything, flat = sum_dense(
        grad_dense.reshape(wide_size, sum_rows, width), flat.reshape(extra_rows, width), levels, 3
    )
    owned = everything.reshape(4, part, width)
    flat = flat.astype(F32).reshape(wide_size, -1)
    small = jnp.sum(flat[:, :size], axis=0).reshape(part, 2 + experts)
    return (
        output,
        grad_tokens,
        small[:, 0],
        owned[0].astype(F32),
        owned[1].astype(F32),
        owned[2].astype(F32),
        owned[3].astype(F32),
        small[:, 1],
        small[:, 2:],
        grad_shared_gate,
        grad_shared_up,
        grad_shared_down,
        grad_expert_gate.T[None],
        grad_expert_up.T[None],
        grad_expert_down[None],
    )


def per_device(*arrays):
    tokens = arrays[0]
    gathered = lax.axis_size("wide") * lax.axis_size("narrow") * tokens.size * 2
    fits = gathered <= 12 * 1024 * 1024
    return (tokens_path if fits else slots_path)(*arrays)


def solution(mesh):
    in_specs = (
        P(("wide", "narrow"), None),
        P(("wide", "narrow"), None),
        P("wide", None),
        P(("wide", "narrow"), None),
        P(("wide", "narrow"), None),
        P("narrow"),
        P("narrow", None),
        P("narrow", None),
        P("narrow", None),
        P("narrow", None),
        P("narrow"),
        P("narrow", None),
        P("narrow", None),
        P("narrow", None),
        P("narrow", None),
        P("wide", None, "narrow"),
        P("wide", None, "narrow"),
        P("wide", "narrow", None),
    )
    out_specs = (
        P(("wide", "narrow"), None),
        P(("wide", "narrow"), None),
        P("narrow"),
        P("narrow", None),
        P("narrow", None),
        P("narrow", None),
        P("narrow", None),
        P("narrow"),
        P("narrow", None),
        P("narrow", None),
        P("narrow", None),
        P("narrow", None),
        P("wide", None, "narrow"),
        P("wide", None, "narrow"),
        P("wide", "narrow", None),
    )
    return jax.shard_map(
        per_device, mesh=mesh, in_specs=in_specs, out_specs=out_specs, check_vma=False
    )
```

```python
import functools
import math

import jax
import jax.numpy as jnp
from jax import lax
from jax.experimental import pallas as pl
from jax.experimental.pallas import tpu as pltpu
from jax.sharding import PartitionSpec as P

HEAD_DIM = 128
TOPK = 7


EPS = 1e-06
MASKED = -1e30


def matmul(left, right):
    return jnp.dot(left, right, preferred_element_type=jnp.float32)


def matmul_left(left, right):
    return lax.dot_general(
        left, right, (((0,), (0,)), ((), ())), preferred_element_type=jnp.float32
    )


def matmul_right(left, right):
    return lax.dot_general(
        left, right, (((1,), (1,)), ((), ())), preferred_element_type=jnp.float32
    )


def doc_layout(positions, doc_lens):
    doc_ends = jnp.cumsum(doc_lens)
    passed = (positions[:, None] >= doc_ends[None, :]).astype(jnp.int32)
    doc_ids = jnp.sum(passed, axis=1)
    return (doc_ids, positions - jnp.sum(passed * doc_lens[None, :], axis=1))


def rotary_angles(positions):
    half_dim = HEAD_DIM // 2
    inverse = jnp.exp(
        jnp.arange(half_dim, dtype=jnp.float32) * (-2.0 * math.log(10000.0) / HEAD_DIM)
    )
    angles = positions.astype(jnp.float32)[:, None] * inverse[None, :]
    return (jnp.cos(angles), jnp.sin(angles))


def rotate(values, cosine, sine_table):
    half_dim = values.shape[-1] // 2
    lower_half = values[..., :half_dim]
    upper_half = values[..., half_dim:]
    cos_b = cosine[:, None, :]
    sin_b = sine_table[:, None, :]
    return jnp.concatenate(
        [lower_half * cos_b - upper_half * sin_b, upper_half * cos_b + lower_half * sin_b], axis=-1
    )


def norm_forward(values, gain_vec):
    row_scale = lax.rsqrt(jnp.mean(values * values, axis=-1, keepdims=True) + EPS)
    unit_rows = values * row_scale
    return (unit_rows * gain_vec, unit_rows, row_scale)


def norm_backward(grad_rows, unit_rows, row_scale, gain_vec):
    scaled = grad_rows * gain_vec
    grad_gain = jnp.sum(grad_rows * unit_rows, axis=0)
    grad_input = row_scale * (
        scaled - unit_rows * jnp.mean(scaled * unit_rows, axis=-1, keepdims=True)
    )
    return (grad_input, grad_gain)


def silu_parts(gate_vals):
    sigmoid_vals = jax.nn.sigmoid(gate_vals)
    return (gate_vals * sigmoid_vals, sigmoid_vals * (1.0 + gate_vals * (1.0 - sigmoid_vals)))


def expert_forward(in_rows, gate_mat, upper_mat):
    gate_vals = matmul(in_rows, gate_mat)
    upper = matmul(in_rows, upper_mat)
    act_vals, unused = silu_parts(gate_vals)
    return (gate_vals, upper, (act_vals * upper).astype(jnp.bfloat16))


def expert_backward(in_rows, grad_rows, gate_vals, upper, active, gate_mat, upper_mat, down_mat):
    grad_act = matmul_right(grad_rows, down_mat)
    act_vals, slope_vals = silu_parts(gate_vals)
    grad_gate = (grad_act * upper * slope_vals).astype(jnp.bfloat16)
    grad_upper = (grad_act * act_vals).astype(jnp.bfloat16)
    grad_down_mat = matmul_left(active, grad_rows)
    grad_gate_mat = matmul_left(in_rows, grad_gate)
    grad_upper_mat = matmul_left(in_rows, grad_upper)
    grad_input = matmul_right(grad_gate, gate_mat) + matmul_right(grad_upper, upper_mat)
    return (grad_input, grad_gate_mat, grad_upper_mat, grad_down_mat)


def attend_block(queries, keys_all, values_all, allowed):
    scores = jnp.einsum("qhd,khd->hqk", queries, keys_all, preferred_element_type=jnp.float32)
    masked = jnp.where(allowed[None], scores, MASKED)
    row_max = jnp.max(masked, axis=-1, keepdims=True)
    weights = jnp.exp(masked - row_max)
    row_total = jnp.sum(weights, axis=-1, keepdims=True)
    prob_rows = (weights / row_total).astype(jnp.bfloat16)
    attended = jnp.einsum("hqk,khd->qhd", prob_rows, values_all, preferred_element_type=jnp.float32)
    return (attended.astype(jnp.bfloat16), (row_max + jnp.log(row_total))[..., 0])


def attend_back(queries, keys_all, values_all, allowed, logsum, grad_attended):
    scores = jnp.einsum("qhd,khd->hqk", queries, keys_all, preferred_element_type=jnp.float32)
    masked = jnp.where(allowed[None], scores, MASKED)
    prob_rows = jnp.exp(masked - logsum[..., None])
    grad_probs = jnp.einsum(
        "qhd,khd->hqk", grad_attended, values_all, preferred_element_type=jnp.float32
    )
    row_delta = jnp.sum(prob_rows * grad_probs, axis=-1, keepdims=True)
    grad_scores = (prob_rows * (grad_probs - row_delta)).astype(jnp.bfloat16)
    grad_queries = jnp.einsum(
        "hqk,khd->qhd", grad_scores, keys_all, preferred_element_type=jnp.float32
    )
    grad_keys = jnp.einsum("hqk,qhd->khd", grad_scores, queries, preferred_element_type=jnp.float32)
    grad_values = jnp.einsum(
        "hqk,qhd->khd",
        prob_rows.astype(jnp.bfloat16),
        grad_attended,
        preferred_element_type=jnp.float32,
    )
    return (grad_queries, grad_keys, grad_values)


MESH_ID = pl.DeviceIdType.MESH
BF16 = jnp.bfloat16
F32 = jnp.float32


class Place:
    def __init__(self, levels):
        self.levels = levels
        wide = lax.axis_index("wide")
        self.core = lax.axis_index("narrow")
        self.level = wide // 4
        self.spot = lax.rem(wide, 4)
        self.across = self.spot + 1 - 2 * lax.rem(self.spot, 2)
        self.along = lax.rem(self.spot + 2, 4)
        self.corner = 3 - self.spot
        self.has_up = self.level < levels - 1
        self.has_down = self.level > 0

    def choose(self, values):
        result = jnp.int32(values[0])
        for k in range(1, self.levels):
            result = jnp.where(self.level == k, values[k], result)
        return result

    def device(self, level, spot, core=None):
        return {"wide": level * 4 + spot, "narrow": self.core if core is None else core}

    def enter(self, sibling):
        barrier = pltpu.get_barrier_semaphore()

        def greet(device):
            pl.semaphore_signal(barrier, inc=1, device_id=device, device_id_type=MESH_ID)

        greet(self.device(self.level, self.across))
        greet(self.device(self.level, self.along))
        if sibling:
            greet(self.device(self.level, self.spot, 1 - self.core))

        @pl.when(self.has_up)
        def _():
            greet(self.device(self.level + 1, self.spot))

        @pl.when(self.has_down)
        def _():
            greet(self.device(self.level - 1, self.spot))

        both = jnp.where(self.has_up, 1, 0) + jnp.where(self.has_down, 1, 0)
        pl.semaphore_wait(barrier, both + (3 if sibling else 2))


def remote(src, dst, send, recv, device):
    return pltpu.make_async_remote_copy(
        src_ref=src,
        dst_ref=dst,
        send_sem=send,
        recv_sem=recv,
        device_id=device,
        device_id_type=MESH_ID,
    )


class Gather:
    NAMES = ("up", "dn", "x", "y", "cx", "cy", "rz", "rx", "ry", "rcx", "rcy")

    def __init__(self, at, sibling, pairs, sems, keeps_own=True):
        self.at, self.sibling, self.pairs, self.keeps_own = at, sibling, pairs, keeps_own
        self.own_sem = sems[0]
        self.sems = dict(zip(self.NAMES, sems[1:12]))
        self.send_n, self.recv_n = sems[12:]
        self.order = self.visits()

    @staticmethod
    def scratch(levels, arrays):
        dma = pltpu.SemaphoreType.DMA
        return (
            [dma((arrays,))]
            + [dma((arrays, levels))] * 11
            + [dma((arrays, levels * 4))] * 2
        )

    def visits(self):
        at = self.at
        table = [
            sorted(range(at.levels), key=lambda lev: (abs(lev - here), lev))
            for here in range(at.levels)
        ]
        return [at.choose([row[k] for row in table]) for k in range(at.levels)]

    def block(self, n, lev, sp, core=None):
        x_ref, ref = self.pairs[n][:2]
        if self.sibling:
            return ref.at[(lev * 4 + sp) * 2 + (self.at.core if core is None else core)]
        if len(self.pairs[n]) == 3:
            return ref.at[lev * 4 + sp].at[pl.ds(self.pairs[n][2], x_ref.shape[0])]
        return ref.at[lev * 4 + sp]

    def each(self, send, recv, lev, sp, device, part=None, own=False):
        copies = []
        for n, (x_ref, *_) in enumerate(self.pairs):
            dst = self.block(n, lev, sp)
            src = x_ref if own else dst
            if part is not None:
                half = x_ref.shape[0] // 2
                src = src.at[pl.ds(part * half, half)]
                dst = dst.at[pl.ds(part * half, half)]
            copies.append(
                remote(src, dst, self.sems[send].at[n, lev], self.sems[recv].at[n, lev], device)
            )
        return copies

    def up(self, lev, own=False):
        at = self.at
        return self.each("up", "rz", lev, at.spot, at.device(at.level + 1, at.spot), own=own)

    def down(self, lev, own=False):
        at = self.at
        return self.each("dn", "rz", lev, at.spot, at.device(at.level - 1, at.spot), own=own)

    def over_x(self, lev, sp, own=False):
        at = self.at
        return self.each("x", "rx", lev, sp, at.device(at.level, at.across), own=own)

    def over_y(self, lev, sp, own=False):
        at = self.at
        return self.each("y", "ry", lev, sp, at.device(at.level, at.along), own=own)

    def corner_y(self, lev, sp):
        at = self.at
        return self.each("cy", "rcy", lev, sp, at.device(at.level, at.along), part=0)

    def corner_x(self, lev, sp):
        at = self.at
        return self.each("cx", "rcx", lev, sp, at.device(at.level, at.across), part=1)

    def near(self, lev, sp, core=None, own=False):
        at = self.at
        copies = []
        for n, (x_ref, *_) in enumerate(self.pairs):
            dst = self.block(n, lev, sp, core)
            sems = self.send_n.at[n, lev * 4 + sp], self.recv_n.at[n, lev * 4 + sp]
            device = at.device(at.level, at.spot, 1 - at.core)
            copies.append(remote(x_ref if own else dst, dst, *sems, device))
        return copies

    def own_copies(self):
        at = self.at
        return [
            pltpu.make_async_copy(x_ref, self.block(n, at.level, at.spot), self.own_sem.at[n])
            for n, (x_ref, *_) in enumerate(self.pairs)
        ]

    def take_own(self):
        for copy in self.own_copies():
            copy.wait()

    def begin(self):
        at = self.at
        pl.when(at.has_up)(lambda: start(self.up(at.level, own=True)))
        pl.when(at.has_down)(lambda: start(self.down(at.level, own=True)))
        start(self.over_x(at.level, at.spot, own=True))
        start(self.over_y(at.level, at.spot, own=True))
        if self.sibling:
            start(self.near(at.level, at.spot, own=True))
        if self.keeps_own:
            start(self.own_copies())

    def take_column(self, lev):
        at = self.at
        arrived(self.up(lev))
        pl.when((lev < at.level) & at.has_up)(lambda: start(self.up(lev)))
        pl.when((lev > at.level) & at.has_down)(lambda: start(self.down(lev)))
        start(self.over_x(lev, at.spot))
        start(self.over_y(lev, at.spot))
        if self.sibling:
            start(self.near(lev, at.spot))

    def take_x(self, lev):
        at = self.at
        arrived(self.over_x(lev, at.across))
        start(self.corner_y(lev, at.across))
        if self.sibling:
            start(self.near(lev, at.across))

    def take_y(self, lev):
        at = self.at
        arrived(self.over_y(lev, at.along))
        start(self.corner_x(lev, at.along))
        if self.sibling:
            start(self.near(lev, at.along))

    def take_corner(self, lev):
        at = self.at
        arrived(self.corner_y(lev, at.corner))
        arrived(self.corner_x(lev, at.corner))
        if self.sibling:
            start(self.near(lev, at.corner))

    def take_near(self, lev, sp):
        arrived(self.near(lev, sp, 1 - self.at.core))

    def steps(self):
        levels, steps = self.at.levels, []
        for s in range(1, levels + 2):
            if s < levels:
                steps.append(lambda lev=self.order[s]: self.take_column(lev))
            if s - 1 < levels:
                steps.append(lambda lev=self.order[s - 1]: self.take_x(lev))
                steps.append(lambda lev=self.order[s - 1]: self.take_y(lev))
            if s >= 2:
                steps.append(lambda lev=self.order[s - 2]: self.take_corner(lev))
        return steps

    def finish(self, near=True):
        at = self.at
        if near:
            self.take_own()
        for lev in range(at.levels):
            pl.when(at.has_up & (lev <= at.level))(lambda lev=lev: sent(self.up(lev)))
            pl.when(at.has_down & (lev >= at.level))(lambda lev=lev: sent(self.down(lev)))
            sent(self.over_x(lev, at.spot))
            sent(self.over_y(lev, at.spot))
            sent(self.corner_y(lev, at.across))
            sent(self.corner_x(lev, at.along))
            if self.sibling:
                for sp in range(4):
                    sent(self.near(lev, sp))
                    if near:
                        self.take_near(lev, sp)


def start(copies):
    for copy in copies:
        copy.start()


def arrived(copies):
    for copy in copies:
        copy.wait_recv()


def sent(copies):
    for copy in copies:
        copy.wait_send()


def dot_nn(left, right):
    return lax.dot_general(left, right, (((1,), (0,)), ((), ())), preferred_element_type=F32)


def dot_tn(left, right):
    return lax.dot_general(left, right, (((0,), (0,)), ((), ())), preferred_element_type=F32)


def dot_nt(left, right):
    return lax.dot_general(left, right, (((1,), (1,)), ((), ())), preferred_element_type=F32)


def experts_kernel(
    levels, sizes, x_ref, g_ref, m_ref, eg_ref, eu_ref, ed_ref, small_ref, sd_ref,
    rows_ref, grads_ref, marks_ref, back_ref, out_ref, gm_ref, dgate_ref, dup_ref, ddown_ref, shared_ref,
    x_buf, g_buf, mark_buf, cu_buf, g_val, mixed_buf, act_buf, back_buf, out_buf, gm_buf, mark_t,
    in_sem, out_sem, gm_val, gw_ref, gd_ref, gate_ref, down_ref, w_sem, *sems,
):
    hidden, used, full = sizes
    at = Place(levels)
    at.enter(True)
    gather = Gather(at, True, [(x_ref, rows_ref), (g_ref, grads_ref), (m_ref, marks_ref)], sems, False)
    gather.begin()
    size, experts = used - hidden, m_ref.shape[0]
    pieces = [
        (eg_ref, gate_ref, 0, hidden),
        (eu_ref, gate_ref, full, hidden),
        (small_ref.at[pl.ds(0, size)], gate_ref, hidden, size),
        (small_ref.at[pl.ds(size, size)], gate_ref, full + hidden, size),
        (small_ref.at[pl.ds(2 * size, experts)], gate_ref, used, experts),
        (ed_ref, down_ref, 0, hidden),
        (sd_ref, down_ref, hidden, size),
    ]
    weights = [
        pltpu.make_async_copy(src, dst.at[pl.ds(row, count)], w_sem.at[n])
        for n, (src, dst, row, count) in enumerate(pieces)
    ]
    start(weights)
    for ref, row, end in ((gate_ref, used + experts, full), (gate_ref, full + used, 2 * full), (down_ref, used, full)):
        if end > row:
            ref[row:end, :] = jnp.zeros((end - row, ref.shape[1]), BF16)
    place = at.level * 4 + at.spot
    units = 4 * levels
    plan = [(0, 0)]
    for s in range(1, levels + 2):
        if s < levels:
            plan.append((s, 0))
        if s - 1 < levels:
            plan += [(s - 1, 1), (s - 1, 2)]
        if s >= 2:
            plan.append((s - 2, 3))
    rows = x_ref.shape[0]
    batch = 2 * rows

    def pick(k, values):
        result = jnp.int32(0) + values[0]
        for j in range(1, len(values)):
            result = jnp.where(k == j, values[j], result)
        return result

    def unit(k):
        visit = pick(k, [v for v, _ in plan])
        kind = pick(k, [t for _, t in plan])
        lev = pick(visit, gather.order)
        sp = pick(kind, [at.spot, at.across, at.along, at.corner])
        return lev, sp, kind

    def loads(k, first):
        slot = lax.rem(k, 4)
        blocks = pl.ds(first, 2)
        return [
            pltpu.make_async_copy(rows_ref.at[blocks], x_buf.at[slot], in_sem.at[slot, 0]),
            pltpu.make_async_copy(grads_ref.at[blocks], g_buf.at[slot], in_sem.at[slot, 1]),
            pltpu.make_async_copy(marks_ref.at[blocks], mark_buf.at[slot], in_sem.at[slot, 2]),
        ]

    def stores(k, first):
        slot = lax.rem(k, 2)
        rng = pl.ds(pl.multiple_of(first * rows, batch), batch)
        pairs = [(back_buf, back_ref), (out_buf, out_ref)]
        return [
            pltpu.make_async_copy(buf.at[slot], ref.at[rng], out_sem.at[slot, n])
            for n, (buf, ref) in enumerate(pairs)
        ]

    def serve(k):
        lev, sp, kind = unit(k)
        pl.when(kind == 0)(lambda: gather.take_column(lev))
        pl.when(kind == 1)(lambda: gather.take_x(lev))
        pl.when(kind == 2)(lambda: gather.take_y(lev))
        pl.when(kind == 3)(lambda: gather.take_corner(lev))

    def fetch(k):
        lev, sp, _ = unit(k)
        gather.take_near(lev, sp)
        start(loads(k, (lev * 4 + sp) * 2))

    def fetch_own():
        gather.take_near(at.level, at.spot)
        theirs = 1 - at.core
        triples = [(x_ref, rows_ref, x_buf), (g_ref, grads_ref, g_buf), (m_ref, marks_ref, mark_buf)]
        for n, (own, gathered, buf) in enumerate(triples):
            sem = in_sem.at[0, n]
            other = gathered.at[place * 2 + theirs]
            pltpu.make_async_copy(own, buf.at[0, at.core], sem).start()
            pltpu.make_async_copy(other, buf.at[0, theirs], sem).start()

    def lanes(n):
        return lax.broadcasted_iota(jnp.int32, (batch, 128), 1) + n * 128

    def mixing():
        tail = full // 128 - 1
        mark = mark_t[...]
        masked = jnp.where(mark > 0.5, cu_buf[:, full - 128 : full], MASKED)
        top = jnp.max(masked, axis=1, keepdims=True)
        weight = jnp.where(mark > 0.5, jnp.exp(masked - top), 0.0)
        mine = jnp.where((lanes(tail) == used + place) & (mark > 1.5), weight, 0.0)
        return jnp.sum(mine, axis=1, keepdims=True) / jnp.sum(weight, axis=1, keepdims=True)

    def elementwise(odd):
        mix = jnp.broadcast_to(mixing(), (batch, 128))
        total = jnp.zeros((batch, 128), F32)
        for n in range(full // 128):
            cols = slice(n * 128, (n + 1) * 128)
            up_cols = slice(full + n * 128, full + (n + 1) * 128)
            gate, upper, back = cu_buf[:, cols], cu_buf[:, up_cols], g_val[:, cols]
            whole = (n + 1) * 128 <= hidden
            scale = mix
            if not whole:
                scale = jnp.where(lanes(n) < hidden, mix, jnp.where(lanes(n) < used, 1.0, 0.0))
            sig = jax.nn.sigmoid(gate)
            act = gate * sig
            active = act * upper
            grad_act = scale * back
            slope = sig * (1.0 + gate * (1.0 - sig))
            mixed_buf[odd, :, cols] = (scale * active).astype(BF16)
            act_buf[odd, :, cols] = (grad_act * upper * slope).astype(BF16)
            act_buf[odd, :, up_cols] = (grad_act * act).astype(BF16)
            term = active * back
            total = total + (term if whole else jnp.where(lanes(n) < hidden, term, 0.0))
        gm_buf[...] = total

    def forward(k):
        lev, sp, _ = unit(k)
        first = (lev * 4 + sp) * 2
        slot = lax.rem(k, 4)
        for copy in loads(k, first):
            copy.wait()
        x = x_buf[slot].reshape(batch, -1)
        cu_buf[...] = dot_nt(x, gate_ref[...])
        g_val[...] = dot_nt(g_buf[slot].reshape(batch, -1), down_ref[...])
        for n in range(2):
            marks = mark_buf[slot, n]
            above = jnp.zeros((used - (full - 128), 128), F32)
            below = jnp.zeros((full - used - marks.shape[0], 128), F32)
            mark_t[pl.ds(n * rows, rows), :] = jnp.transpose(jnp.concatenate([above, marks, below], axis=0))
        elementwise(lax.rem(k, 2))

    def backward(k):
        lev, sp, _ = unit(k)
        first = (lev * 4 + sp) * 2
        slot = lax.rem(k, 2)

        @pl.when(k >= 2)
        def _():
            for copy in stores(k, 0):
                copy.wait()

        back_buf[slot] = dot_nn(act_buf[slot], gate_ref[...]).astype(BF16)
        out_buf[slot] = dot_nn(mixed_buf[slot], down_ref[...]).astype(BF16)
        for n in range(2):
            gm = jnp.transpose(gm_buf[pl.ds(n * rows, rows), :])
            gm_val[pl.ds(first + n, 1), :] = jnp.sum(gm, axis=0, keepdims=True)
        start(stores(k, first))

        both = pl.ds(lax.rem(k, 4) - 1, 2)

        def gate_grad(m, carry):
            part = pl.ds(pl.multiple_of(m * 256, 256), 256)
            left = act_buf[:, :, part].reshape(2 * batch, 256)
            gw_ref[part, :] += dot_tn(left, x_buf[both].reshape(2 * batch, -1))
            return carry

        def down_grad(m, carry):
            part = pl.ds(pl.multiple_of(m * 256, 256), 256)
            left = mixed_buf[:, :, part].reshape(2 * batch, 256)
            gd_ref[part, :] += dot_tn(left, g_buf[both].reshape(2 * batch, -1))
            return carry

        @pl.when(slot == 1)
        def _():
            lax.fori_loop(0, gw_ref.shape[0] // 256, gate_grad, 0)
            lax.fori_loop(0, full // 256, down_grad, 0)

    gw_ref[...] = jnp.zeros_like(gw_ref)
    gd_ref[...] = jnp.zeros_like(gd_ref)
    fetch_own()
    for copy in weights:
        copy.wait()

    def loop(k, carry):
        pl.when((k > 0) & (k + 1 < units))(lambda: serve(k + 1))
        forward(k)
        pl.when(k == 0)(lambda: serve(1))
        pl.when(k + 1 < units)(lambda: fetch(k + 1))
        backward(k)
        return carry

    lax.fori_loop(0, units, loop, 0)
    gm_ref[...] = gm_val[...]
    finals = [
        pltpu.make_async_copy(src.at[pl.ds(row, hidden)], dst, w_sem.at[n])
        for n, (src, row, dst) in enumerate(
            ((gw_ref, 0, dgate_ref), (gw_ref, full, dup_ref), (gd_ref, 0, ddown_ref))
        )
    ]
    start(finals)
    for n, (ref, row) in enumerate(((gw_ref, hidden), (gw_ref, full + hidden), (gd_ref, hidden))):
        shared_ref[n * size : (n + 1) * size, :] = ref[row : row + size, :].astype(BF16)
    for copy in finals:
        copy.wait()
    for k in (0, 1):
        for copy in stores(k, 0):
            copy.wait()
    gather.finish(near=False)


def experts_rows(x, grads, marks, weights, hidden, used, full, levels, collective_id):
    rows, width = x.shape
    blocks = 8 * levels
    total = blocks * rows
    dma = pltpu.SemaphoreType.DMA
    vmem = pltpu.VMEM
    anywhere = pl.BlockSpec(memory_space=pl.ANY)
    inside = pl.BlockSpec(memory_space=vmem)
    shape = jax.ShapeDtypeStruct
    batch = 2 * rows
    return pl.pallas_call(
        functools.partial(experts_kernel, levels, (hidden, used, full)),
        out_shape=[
            shape((blocks, rows, width), BF16),
            shape((blocks, rows, width), BF16),
            shape((blocks, *marks.shape), F32),
            shape((total, width), BF16),
            shape((total, width), BF16),
            shape((blocks, rows), F32),
            shape((hidden, width), F32),
            shape((hidden, width), F32),
            shape((hidden, width), F32),
            shape((3 * (used - hidden), width), BF16),
        ],
        in_specs=[anywhere] * 8,
        out_specs=[anywhere] * 5 + [inside] + [anywhere] * 3 + [inside],
        scratch_shapes=[
            vmem((4, 2, rows, width), BF16),
            vmem((4, 2, rows, width), BF16),
            vmem((4, 2, *marks.shape), F32),
            vmem((batch, 2 * full), F32),
            vmem((batch, full), F32),
            vmem((2, batch, full), BF16),
            vmem((2, batch, 2 * full), BF16),
            vmem((2, batch, width), BF16),
            vmem((2, batch, width), BF16),
            vmem((batch, 128), F32),
            vmem((batch, 128), F32),
            dma((4, 3)),
            dma((2, 2)),
            vmem((blocks, rows), F32),
            vmem((2 * full, width), F32),
            vmem((full, width), F32),
            vmem((2 * full, width), BF16),
            vmem((full, width), BF16),
            dma((7,)),
        ]
        + Gather.scratch(levels, 3),
        compiler_params=pltpu.CompilerParams(
            collective_id=collective_id,
            has_side_effects=True,
            vmem_limit_bytes=56 * 1024 * 1024,
        ),
    )(x, grads, marks, *weights)


def shared_kernel(slices, x_ref, gate_ref, up_ref, down_ref, gate_buf, up_buf, down_buf, sem):
    part, units = gate_ref.shape
    stored = units // 2
    size = stored // slices
    copies = []
    for n in range(slices):
        for c in range(2):
            rows = pl.ds(c * stored + n * size, size)
            src = x_ref.at[n, pl.ds(c * size, size)]
            for buf, lanes in ((gate_buf, pl.ds(0, part)), (up_buf, pl.ds(part, part))):
                copies.append(pltpu.make_async_copy(src.at[:, lanes], buf.at[rows], sem.at[len(copies)]))
        src, dst = x_ref.at[n, pl.ds(2 * size, size)], down_buf.at[pl.ds(n * size, size)]
        copies.append(pltpu.make_async_copy(src, dst, sem.at[len(copies)]))
    start(copies)
    for copy in copies:
        copy.wait()
    down_ref[...] = down_buf[...].astype(F32)
    for buf, ref in ((gate_buf, gate_ref), (up_buf, up_ref)):
        for n in range(units // 128):
            rows = pl.ds(n * 128, 128)
            ref[:, rows] = jnp.transpose(buf[rows, :].astype(F32))


def shared_grads(gathered, slices, part, stored):
    width = gathered.shape[2]
    vmem = pltpu.VMEM
    inside = pl.BlockSpec(memory_space=vmem)
    shape = jax.ShapeDtypeStruct
    return pl.pallas_call(
        functools.partial(shared_kernel, slices),
        out_shape=[
            shape((part, 2 * stored), F32),
            shape((part, 2 * stored), F32),
            shape((stored, width), F32),
        ],
        in_specs=[pl.BlockSpec(memory_space=pl.ANY)],
        out_specs=[inside] * 3,
        scratch_shapes=[
            vmem((2 * stored, part), BF16),
            vmem((2 * stored, part), BF16),
            vmem((stored, width), BF16),
            pltpu.SemaphoreType.DMA((5 * slices,)),
        ],
        compiler_params=pltpu.CompilerParams(vmem_limit_bytes=32 * 1024 * 1024),
    )(gathered)


def destinations(levels):
    return [
        sorted(range(levels), key=lambda to: (-abs(to - here), -to)) for here in range(levels)
    ]


def add_rows(write, sources, rows):
    step = 16

    def body(k, carry):
        r = pl.ds(pl.multiple_of(k * step, step), step)
        total = sources[0](r)
        for source in sources[1:]:
            total = total + source(r)
        write(r, total)
        return carry

    lax.fori_loop(0, rows // step, body, 0)


def reads(ref):
    return lambda r: ref[r, :].astype(F32)


def writes(ref):
    def write(r, total):
        ref[r, :] = total.astype(ref.dtype)

    return write


class Scatter:
    def __init__(self, at, sibling, x_ref, out_ref, refs, row=None):
        self.at, self.sibling, self.x_ref, self.out_ref = at, sibling, x_ref, out_ref
        self.row = row
        self.acc, self.near, self.hx, self.hy, self.fx, self.fy = refs[:6]
        self.out_buf, self.za, self.zb = refs[6:9]
        self.own_sem, self.send_n, self.recv_n = refs[9:12]
        self.send = dict(zip(("hx", "hy", "fx", "fy", "up", "dn"), refs[12:18]))
        self.recv = dict(zip(("hx", "hy", "fx", "fy", "za", "zb"), refs[18:24]))
        self.rows = out_ref.shape[0]
        table = destinations(at.levels)
        self.order = [at.choose([row[s] for row in table]) for s in range(at.levels)]

    SCRATCH = 24

    @staticmethod
    def scratch(levels, sibling, rows, width):
        dma, vmem = pltpu.SemaphoreType.DMA, pltpu.VMEM
        blocks = levels * 4
        return (
            [
                vmem((blocks, rows, width), BF16),
                vmem((blocks if sibling else 1, rows, width), BF16),
                vmem((levels, rows // 2, width), BF16),
                vmem((levels, rows // 2, width), BF16),
            ]
            + [vmem((levels, rows, width), BF16)] * 5
            + [dma((blocks,))] * 3
            + [dma((levels,))] * 12
        )

    def own(self, lev, sp):
        b = lev * 4 + sp
        src = self.x_ref.at[b * 2 + self.at.core if self.sibling else b]
        if self.row is not None:
            src = src.at[pl.ds(self.row, self.rows)]
        return pltpu.make_async_copy(src, self.acc.at[b], self.own_sem.at[b])

    def to_sibling(self, lev, sp):
        at, b = self.at, lev * 4 + sp
        sems = self.send_n.at[b], self.recv_n.at[b]
        src = self.x_ref.at[b * 2 + 1 - at.core]
        return remote(src, self.near.at[b], *sems, at.device(at.level, at.spot, 1 - at.core))

    def side(self, name, src, dst, lev, spot):
        sems = self.send[name].at[lev], self.recv[name].at[lev]
        return remote(src, dst, *sems, self.at.device(self.at.level, spot))

    def half_y(self, lev):
        src = self.acc.at[lev * 4 + self.at.corner].at[pl.ds(0, self.rows // 2)]
        return self.side("hy", src, self.hy.at[lev], lev, self.at.along)

    def half_x(self, lev):
        src = self.acc.at[lev * 4 + self.at.corner].at[pl.ds(self.rows // 2, self.rows // 2)]
        return self.side("hx", src, self.hx.at[lev], lev, self.at.across)

    def full_x(self, lev):
        return self.side("fx", self.acc.at[lev * 4 + self.at.across], self.fx.at[lev], lev, self.at.across)

    def full_y(self, lev):
        return self.side("fy", self.acc.at[lev * 4 + self.at.along], self.fy.at[lev], lev, self.at.along)

    def go_up(self, lev):
        sems = self.send["up"].at[lev], self.recv["zb"].at[lev]
        device = self.at.device(self.at.level + 1, self.at.spot)
        return remote(self.out_buf.at[lev], self.zb.at[lev], *sems, device)

    def go_down(self, lev):
        sems = self.send["dn"].at[lev], self.recv["za"].at[lev]
        device = self.at.device(self.at.level - 1, self.at.spot)
        return remote(self.out_buf.at[lev], self.za.at[lev], *sems, device)

    def spots(self):
        return self.at.corner, self.at.across, self.at.along, self.at.spot

    def begin(self):
        for lev in self.order:
            for sp in self.spots():
                if self.sibling:
                    self.to_sibling(lev, sp).start()
                self.own(lev, sp).start()

    def local(self, lev):
        for n, sp in enumerate(self.spots()):
            ref = self.acc.at[lev * 4 + sp]
            self.own(lev, sp).wait()
            if self.sibling:
                self.to_sibling(lev, sp).wait_recv()
                add_rows(writes(ref), [reads(ref), reads(self.near.at[lev * 4 + sp])], self.rows)
            if n == 0:
                self.half_y(lev).start()
                self.half_x(lev).start()

    def halves(self, lev):
        half = self.rows // 2
        self.half_y(lev).wait_recv()
        ref = self.acc.at[lev * 4 + self.at.across].at[pl.ds(0, half)]
        add_rows(writes(ref), [reads(ref), reads(self.hy.at[lev])], half)
        self.full_x(lev).start()
        self.half_x(lev).wait_recv()
        ref = self.acc.at[lev * 4 + self.at.along].at[pl.ds(half, half)]
        add_rows(writes(ref), [reads(ref), reads(self.hx.at[lev])], half)
        self.full_y(lev).start()

    def column(self, lev):
        at, rows, level = self.at, self.rows, self.at.level
        self.full_x(lev).wait_recv()
        self.full_y(lev).wait_recv()
        own = [reads(self.acc.at[lev * 4 + at.spot]), reads(self.fx.at[lev]), reads(self.fy.at[lev])]
        above, below = reads(self.za.at[lev]), reads(self.zb.at[lev])
        passed = writes(self.out_buf.at[lev])
        final = writes(self.out_ref)

        def send(has, arrival, term, departure):
            @pl.when(has)
            def _():
                arrival(lev).wait_recv()
                add_rows(passed, [*own, term], rows)

            pl.when(jnp.logical_not(has))(lambda: add_rows(passed, own, rows))
            departure(lev).start()

        pl.when(lev < level)(lambda: send(at.has_up, self.go_down, above, self.go_down))
        pl.when(lev > level)(lambda: send(at.has_down, self.go_up, below, self.go_up))

        @pl.when(lev == level)
        def _():
            pl.when(at.has_up)(lambda: self.go_down(lev).wait_recv())
            pl.when(at.has_down)(lambda: self.go_up(lev).wait_recv())
            both = at.has_up & at.has_down
            pl.when(both)(lambda: add_rows(final, [*own, above, below], rows))
            pl.when(jnp.logical_not(at.has_down))(lambda: add_rows(final, [*own, above], rows))
            pl.when(jnp.logical_not(at.has_up))(lambda: add_rows(final, [*own, below], rows))

    def steps(self):
        levels, steps = self.at.levels, []
        for s in range(levels + 2):
            if s < levels:
                steps.append(lambda lev=self.order[s]: self.local(lev))
            if 0 <= s - 1 < levels:
                steps.append(lambda lev=self.order[s - 1]: self.halves(lev))
            if s >= 2:
                steps.append(lambda lev=self.order[s - 2]: self.column(lev))
        return steps

    def finish(self):
        for lev in range(self.at.levels):
            if self.sibling:
                for sp in range(4):
                    self.to_sibling(lev, sp).wait_send()
            sent([self.half_y(lev), self.half_x(lev), self.full_x(lev), self.full_y(lev)])
            pl.when(lev < self.at.level)(lambda lev=lev: self.go_down(lev).wait_send())
            pl.when(lev > self.at.level)(lambda lev=lev: self.go_up(lev).wait_send())


def dense_kernel(levels, spans, x_ref, flat_ref, all_ref, flat_all_ref, *refs):
    at = Place(levels)
    at.enter(False)
    sums, refs = refs[:2], refs[2:]
    size = Scatter.SCRATCH
    scatters = [
        Scatter(at, False, x_ref, sums[n], refs[n * size : (n + 1) * size], spans[n][0]) for n in range(2)
    ]
    refs = refs[2 * size :]
    pairs = [[(sums[n], all_ref, spans[n][0])] for n in range(2)]
    pairs[1].append((flat_ref, flat_all_ref))
    gathers = []
    for n in range(2):
        gathers.append(Gather(at, False, pairs[n], refs[n * 14 : (n + 1) * 14]))
    for task in scatters:
        task.begin()
    steps = []
    for n, lag in enumerate((0, 7)):
        begin = len(scatters[n].steps()) + lag
        steps += [(s + lag, n, step) for s, step in enumerate(scatters[n].steps())]
        steps.append((begin - 0.5, n, gathers[n].begin))
        steps += [(begin + s, 2 + n, step) for s, step in enumerate(gathers[n].steps())]
    for _, _, step in sorted(steps, key=lambda entry: entry[:2]):
        step()
    for task in [*scatters, *gathers]:
        task.finish()


def sum_dense(x, flat, levels, collective_id):
    blocks, rows, width = x.shape
    first = -(-rows // 64) * 32
    spans = [(0, first), (first, rows - first)]
    vmem, anywhere = pltpu.VMEM, pl.BlockSpec(memory_space=pl.ANY)
    shape = jax.ShapeDtypeStruct
    return pl.pallas_call(
        functools.partial(dense_kernel, levels, spans),
        out_shape=[shape(x.shape, BF16), shape((blocks, *flat.shape), BF16)],
        in_specs=[anywhere, anywhere],
        out_specs=[anywhere, anywhere],
        scratch_shapes=[vmem((n, width), BF16) for _, n in spans]
        + Scatter.scratch(levels, False, spans[0][1], width)
        + Scatter.scratch(levels, False, spans[1][1], width)
        + Gather.scratch(levels, 1)
        + Gather.scratch(levels, 2),
        compiler_params=pltpu.CompilerParams(
            collective_id=collective_id,
            has_side_effects=True,
            vmem_limit_bytes=60 * 1024 * 1024,
        ),
    )(x, flat)


def exchange_kernel(
    levels, back_ref, out_ref, part_ref, rows_ref, sum_ref, all_ref, block, send_s, recv_s, own_s, *refs
):
    at = Place(levels)
    at.enter(True)
    size = Scatter.SCRATCH
    first = Scatter(at, True, back_ref, rows_ref, refs[:size])
    second = Scatter(at, True, out_ref, sum_ref, refs[size : 2 * size])
    gather = Gather(at, False, [(block, all_ref)], refs[2 * size :])
    units, half = part_ref.shape[0] // 3, part_ref.shape[1] // 2
    mine = pl.ds(pl.multiple_of(at.core * units, units), units)
    own, theirs, sends = [], [], []
    for n in range(2):
        rows, lanes = pl.ds(n * units, units), pl.ds(n * half, half)

        def side(core):
            return part_ref.at[rows, pl.ds(pl.multiple_of(core * half, 128), half)]

        own.append(pltpu.make_async_copy(side(at.core), block.at[mine, lanes], own_s.at[n]))
        device = at.device(at.level, at.spot, 1 - at.core)
        sems = send_s.at[n], recv_s.at[n]
        sends.append(remote(side(1 - at.core), block.at[mine, lanes], *sems, device))
    down = pl.ds(2 * units, units)
    own.append(pltpu.make_async_copy(part_ref.at[down], block.at[down], own_s.at[2]))
    start(sends)
    start(own)
    first.begin()
    second.begin()
    for copy in own:
        copy.wait()
    arrived(sends)
    gather.begin()
    steps = [(s, 0, step) for s, step in enumerate(first.steps())]
    steps += [(s + 7, 1, step) for s, step in enumerate(second.steps())]
    steps += [(s + 2, 2, step) for s, step in enumerate(gather.steps())]
    for _, _, step in sorted(steps, key=lambda entry: entry[:2]):
        step()
    sent(sends)
    first.finish()
    second.finish()
    gather.finish()


def exchange_wide(back, out, part, levels, collective_id):
    rows, width = back.shape[1:]
    dma = pltpu.SemaphoreType.DMA
    anywhere, inside = pl.BlockSpec(memory_space=pl.ANY), pl.BlockSpec(memory_space=pltpu.VMEM)
    shape = jax.ShapeDtypeStruct
    return pl.pallas_call(
        functools.partial(exchange_kernel, levels),
        out_shape=[
            shape((rows, width), BF16),
            shape((rows, width), BF16),
            shape((levels * 4, *part.shape), BF16),
        ],
        in_specs=[anywhere, anywhere, inside],
        out_specs=[inside, inside, anywhere],
        scratch_shapes=[pltpu.VMEM(part.shape, BF16), dma((2,)), dma((2,)), dma((3,))]
        + Scatter.scratch(levels, True, rows, width) * 2
        + Gather.scratch(levels, 1),
        compiler_params=pltpu.CompilerParams(
            collective_id=collective_id,
            has_side_effects=True,
            vmem_limit_bytes=60 * 1024 * 1024,
        ),
        cost_estimate=pl.CostEstimate(
            flops=40 * 10**9, bytes_accessed=200 * 10**6, transcendentals=0
        ),
    )(back, out, part)


def local_call(kernel, outs, scratch, *args):
    inside = pl.BlockSpec(memory_space=pltpu.VMEM)
    return pl.pallas_call(
        kernel,
        out_shape=[jax.ShapeDtypeStruct(s, d) for s, d in outs],
        in_specs=[inside] * len(args),
        out_specs=[inside] * len(outs),
        scratch_shapes=[pltpu.VMEM(s, d) for s, d in scratch],
        compiler_params=pltpu.CompilerParams(vmem_limit_bytes=48 * 1024 * 1024),
    )(*args)


def half_lanes(which, size):
    return pl.ds(pl.multiple_of(which * size, 128), size)


def project_kernel(mine_ref, theirs_ref, scale_ref, q_ref, k_ref, v_ref, n_ref, keep_ref, send_ref, buf):
    core = lax.axis_index("narrow")
    rows = mine_ref.shape[0]
    part = n_ref.shape[1]
    for n, ref in enumerate((mine_ref, theirs_ref)):
        x = ref[...].astype(F32)
        r = lax.rsqrt(jnp.mean(x * x, axis=1, keepdims=True) + EPS)
        buf[n * rows : (n + 1) * rows, :] = (x * r * scale_ref[...]).astype(BF16)
    normed = buf[:, half_lanes(core, part)]
    n_ref[...] = normed
    for n, ref in enumerate((q_ref, k_ref, v_ref)):
        cols = slice(n * part, (n + 1) * part)
        send_ref[:, cols] = dot_nn(normed, ref[:, half_lanes(1 - core, part)]).astype(BF16)
        keep_ref[:, cols] = dot_nn(normed, ref[:, half_lanes(core, part)])


def probabilities(q, k, allowed):
    scores = jnp.where(allowed, dot_nt(q, k), MASKED)
    weights = jnp.exp(scores - jnp.max(scores, axis=1, keepdims=True))
    return weights / jnp.sum(weights, axis=1, keepdims=True)


def turn(values, cosine, sine_table):
    return values * cosine + pltpu.roll(values, HEAD_DIM // 2, 1) * sine_table


def attend_kernel(
    keep_ref, got_ref, cos_ref, sin_ref, mask_ref, out_w_ref,
    q_ref, k_ref, v_ref, o_ref, branch_ref, send_ref,
):
    rows, part = q_ref.shape
    half = rows // 2
    allowed = mask_ref[...] > 0.5
    cosine, sine_table = cos_ref[...], sin_ref[...]

    def full(cols):
        got = jnp.concatenate([got_ref[half:, cols], got_ref[:half, cols]], axis=0)
        return keep_ref[:, cols] + got.astype(F32)

    for h in range(part // HEAD_DIM):
        cols = slice(h * HEAD_DIM, (h + 1) * HEAD_DIM)
        q = full(slice(cols.start, cols.stop))
        k = full(slice(part + cols.start, part + cols.stop))
        v = full(slice(2 * part + cols.start, 2 * part + cols.stop)).astype(BF16)
        q = (turn(q, cosine, sine_table) * HEAD_DIM ** (-0.5)).astype(BF16)
        k = turn(k, cosine, sine_table).astype(BF16)
        q_ref[:, cols] = q
        k_ref[:, cols] = k
        v_ref[:, cols] = v
        o_ref[:, cols] = dot_nn(probabilities(q, k, allowed).astype(BF16), v).astype(BF16)
    send_ref[...] = dot_nn(o_ref[half:, :], out_w_ref[...]).astype(BF16)
    branch_ref[...] = dot_nn(o_ref[:half, :], out_w_ref[...])


def attend_back_kernel(
    branch_ref, their_ref, q_ref, k_ref, v_ref, o_ref, cos_ref, sin_ref, mask_ref, out_w_ref,
    grad_w_ref, mine_ref, row_buf, grad_buf,
):
    rows, part = q_ref.shape
    half = rows // 2
    allowed = mask_ref[...] > 0.5
    cosine, sine_table = cos_ref[...], -sin_ref[...]
    row_buf[:half, :] = branch_ref[...]
    row_buf[half:, :] = their_ref[...]
    grad_buf[...] = dot_nt(row_buf[...], out_w_ref[...]).astype(BF16)
    for h in range(part // HEAD_DIM):
        cols = slice(h * HEAD_DIM, (h + 1) * HEAD_DIM)
        q, k, v, grad = q_ref[:, cols], k_ref[:, cols], v_ref[:, cols], grad_buf[:, cols]
        probs = probabilities(q, k, allowed)
        grad_probs = dot_nt(grad, v)
        delta = jnp.sum(probs * grad_probs, axis=1, keepdims=True)
        grad_scores = (probs * (grad_probs - delta)).astype(BF16)
        grad_q = dot_nn(grad_scores, k) * HEAD_DIM ** (-0.5)
        mine_ref[0, :, cols] = turn(grad_q, cosine, sine_table).astype(BF16)
        mine_ref[1, :, cols] = turn(dot_tn(grad_scores, q), cosine, sine_table).astype(BF16)
        mine_ref[2, :, cols] = dot_tn(probs.astype(BF16), grad).astype(BF16)
    grad_w_ref[...] = dot_tn(o_ref[...], row_buf[...]).astype(BF16)


def dense_back_kernel(
    mine_ref, their_ref, n_ref, grad_w_ref, q_ref, k_ref, v_ref, dense_ref, part_ref, send_ref, buf
):
    core = lax.axis_index("narrow")
    rows, part = n_ref.shape
    half = rows // 2
    total = None
    for n, ref in enumerate((q_ref, k_ref, v_ref)):
        buf[n, :, half_lanes(core, part)] = mine_ref[n]
        buf[n, :half, half_lanes(1 - core, part)] = their_ref[n, half:, :]
        buf[n, half:, half_lanes(1 - core, part)] = their_ref[n, :half, :]
        term = dot_nt(buf[n], ref[...])
        total = term if total is None else total + term
        dense_ref[n] = dot_tn(n_ref[...], buf[n]).astype(BF16)
    dense_ref[3] = grad_w_ref[...]
    part_ref[...] = total[:half]
    send_ref[...] = total[half:].astype(BF16)


def slots_path(
    tokens,
    cotangent,
    lengths,
    routes,
    keep,
    attn_gain,
    w_query,
    w_key,
    w_value,
    w_out,
    ffn_gain,
    w_router,
    shared_gate,
    shared_up,
    shared_down,
    expert_gate,
    expert_up,
    expert_down,
):
    narrow_size = lax.axis_size("narrow")
    narrow_index = lax.axis_index("narrow")
    wide_size = lax.axis_size("wide")
    local_rows = tokens.shape[0]
    model_width = tokens.shape[1]
    head_count = model_width // HEAD_DIM
    row_length = local_rows * narrow_size
    capacity = 8 * (3 * local_rows * TOPK // (16 * wide_size) + 1)
    gathered = (
        lax.all_gather(attn_gain, "narrow", axis=0, tiled=True),
        lax.all_gather(w_query, "narrow", axis=0, tiled=True),
        lax.all_gather(w_key, "narrow", axis=0, tiled=True),
        lax.all_gather(w_value, "narrow", axis=0, tiled=True),
        lax.all_gather(w_out, "narrow", axis=0, tiled=True),
        lax.all_gather(ffn_gain, "narrow", axis=0, tiled=True),
        lax.all_gather(w_router, "narrow", axis=0, tiled=True),
        lax.all_gather(shared_gate, "narrow", axis=0, tiled=True),
        lax.all_gather(shared_up, "narrow", axis=0, tiled=True),
        lax.all_gather(shared_down, "narrow", axis=0, tiled=True),
    )
    attn_scale = gathered[0].astype(jnp.float32)
    query_proj = gathered[1]
    key_proj = gathered[2]
    value_proj = gathered[3]
    output_proj = gathered[4]
    ffn_scale = gathered[5].astype(jnp.float32)
    router_proj = gathered[6]
    common_gate = gathered[7]
    common_upper = gathered[8]
    common_down = gathered[9]
    expert_mats = (expert_gate, expert_up, expert_down)
    routed_gate = expert_mats[0][0]
    routed_upper = expert_mats[1][0]
    routed_down = expert_mats[2][0]
    doc_lens = lengths[0]
    key_index = jnp.arange(row_length, dtype=jnp.int32)
    key_doc, unused = doc_layout(key_index, doc_lens)
    query_index = narrow_index * local_rows + jnp.arange(local_rows, dtype=jnp.int32)
    query_doc, query_pos = doc_layout(query_index, doc_lens)
    cosine, sine_table = rotary_angles(query_pos)
    inputs = tokens.astype(jnp.float32)
    normed, unit_one, scale_one = norm_forward(inputs, attn_scale)
    normed_one = normed.astype(jnp.bfloat16)
    head_shape = (local_rows, head_count, HEAD_DIM)
    query_rows = rotate(matmul(normed_one, query_proj).reshape(head_shape), cosine, sine_table)
    query_rows = (query_rows * HEAD_DIM ** (-0.5)).astype(jnp.bfloat16)
    key_rows = rotate(matmul(normed_one, key_proj).reshape(head_shape), cosine, sine_table).astype(
        jnp.bfloat16
    )
    valued = matmul(normed_one, value_proj).astype(jnp.bfloat16)
    all_keys, all_values = (
        lax.all_gather(key_rows.reshape(local_rows, model_width), "narrow", axis=0, tiled=True),
        lax.all_gather(valued, "narrow", axis=0, tiled=True),
    )
    all_keys = all_keys.reshape(row_length, head_count, HEAD_DIM)
    all_values = all_values.reshape(row_length, head_count, HEAD_DIM)
    block_rows = min(local_rows, 512)
    blocks = local_rows // block_rows
    query_blocks = query_rows.reshape(blocks, block_rows, head_count, HEAD_DIM)
    doc_blocks = query_doc.reshape(blocks, block_rows)
    index_blocks = query_index.reshape(blocks, block_rows)

    def allowed_for(doc_rows, index_rows):
        return (doc_rows[:, None] == key_doc[None, :]) & (key_index[None, :] <= index_rows[:, None])

    def forward_block(map_item):
        return attend_block(
            map_item[0], all_keys, all_values, allowed_for(map_item[1], map_item[2])
        )

    attended, logsum = lax.map(forward_block, (query_blocks, doc_blocks, index_blocks))
    attended = attended.reshape(local_rows, model_width)
    hidden = inputs + matmul(attended, output_proj)
    normed, unit_two, scale_two = norm_forward(hidden, ffn_scale)
    normed_two = normed.astype(jnp.bfloat16)
    logits = matmul(normed_two, router_proj)
    experts = router_proj.shape[1]
    pick_table = (routes[:, :, None] == jnp.arange(experts, dtype=jnp.int32)[None, None, :]).astype(
        jnp.float32
    )
    chosen = jnp.sum(pick_table * logits[:, None, :], axis=2)
    gate_probs = jax.nn.softmax(chosen, axis=1)
    keep_float = keep.astype(jnp.float32)
    mixing = gate_probs * keep_float
    common_gate_vals, common_upper_vals, common_act = expert_forward(
        normed_two, common_gate, common_upper
    )
    shared_out = matmul(common_act, common_down)
    pair_expert = routes.reshape(-1)
    pair_total = pair_expert.shape[0]
    onehot = (pair_expert[:, None] == jnp.arange(experts, dtype=jnp.int32)[None, :]).astype(
        jnp.int32
    )
    earlier = jnp.cumsum(onehot, axis=0) - onehot
    slot_place = jnp.sum(earlier * onehot, axis=1)
    slot_index = pair_expert * capacity + slot_place
    slot_total = experts * capacity
    source = (
        jnp.full((slot_total,), -1, jnp.int32)
        .at[slot_index]
        .set(jnp.arange(pair_total, dtype=jnp.int32))
    )
    filled = source >= 0
    pair_index = jnp.maximum(source, 0)

    def fill_slots(in_rows, row_index):
        taken = jnp.take(in_rows, row_index, axis=0)
        return jnp.where(filled[:, None], taken, jnp.zeros((), in_rows.dtype)).reshape(
            experts, capacity, model_width
        )

    received = lax.all_to_all(
        fill_slots(normed_two, pair_index // TOPK), "wide", split_axis=0, concat_axis=0, tiled=True
    )
    expert_in = lax.all_gather(received, "narrow", axis=0, tiled=True).reshape(-1, model_width)
    routed_gate_vals, routed_upper_vals, routed_act = expert_forward(
        expert_in, routed_gate, routed_upper
    )
    partial_value = matmul(routed_act, routed_down)
    expert_out = lax.psum_scatter(partial_value, "narrow", scatter_dimension=0, tiled=True)
    returned = lax.all_to_all(
        expert_out.astype(jnp.bfloat16).reshape(wide_size, capacity, model_width),
        "wide",
        split_axis=0,
        concat_axis=0,
        tiled=True,
    )
    pair_out = (
        jnp.take(returned.reshape(slot_total, model_width), slot_index, axis=0)
        .astype(jnp.float32)
        .reshape(local_rows, TOPK, model_width)
    )
    routed = jnp.sum(mixing[:, :, None] * pair_out, axis=1)
    output = (hidden + shared_out + routed).astype(jnp.bfloat16)
    grad_output = cotangent.astype(jnp.float32)
    grad_pairs = (
        (mixing[:, :, None] * grad_output[:, None, :])
        .astype(jnp.bfloat16)
        .reshape(pair_total, model_width)
    )
    grad_mixing = jnp.sum(pair_out * grad_output[:, None, :], axis=2)
    grad_received = lax.all_to_all(
        fill_slots(grad_pairs, pair_index), "wide", split_axis=0, concat_axis=0, tiled=True
    )
    grad_expert_out = lax.all_gather(grad_received, "narrow", axis=0, tiled=True).reshape(
        -1, model_width
    )
    grad_expert_in, grad_rgate, grad_rupper, grad_rdown = expert_backward(
        expert_in,
        grad_expert_out,
        routed_gate_vals,
        routed_upper_vals,
        routed_act,
        routed_gate,
        routed_upper,
        routed_down,
    )
    grad_slot_rows = lax.psum_scatter(grad_expert_in, "narrow", scatter_dimension=0, tiled=True)
    expert_grads = (grad_rgate, grad_rupper, grad_rdown)
    grad_back = lax.all_to_all(
        grad_slot_rows.astype(jnp.bfloat16).reshape(wide_size, capacity, model_width),
        "wide",
        split_axis=0,
        concat_axis=0,
        tiled=True,
    )
    grad_pair_rows = jnp.take(
        grad_back.reshape(slot_total, model_width), slot_index, axis=0
    ).astype(jnp.float32)
    grad_normed = jnp.sum(grad_pair_rows.reshape(local_rows, TOPK, model_width), axis=1)
    grad_gates = grad_mixing * keep_float
    grad_chosen = gate_probs * (
        grad_gates - jnp.sum(gate_probs * grad_gates, axis=1, keepdims=True)
    )
    grad_logits = jnp.sum(pick_table * grad_chosen[:, :, None], axis=1).astype(jnp.bfloat16)
    grad_router = matmul_left(normed_two, grad_logits)
    grad_normed = grad_normed + matmul_right(grad_logits, router_proj)
    grad_common_in, grad_cgate, grad_cupper, grad_cdown = expert_backward(
        normed_two,
        cotangent,
        common_gate_vals,
        common_upper_vals,
        common_act,
        common_gate,
        common_upper,
        common_down,
    )
    grad_normed = grad_normed + grad_common_in
    grad_hidden_norm, grad_ffn = norm_backward(grad_normed, unit_two, scale_two, ffn_scale)
    grad_hidden = grad_output + grad_hidden_norm
    grad_branch = grad_hidden.astype(jnp.bfloat16)
    grad_output_proj = matmul_left(attended, grad_branch)
    grad_attended = (
        matmul_right(grad_branch, output_proj)
        .astype(jnp.bfloat16)
        .reshape(blocks, block_rows, head_count, HEAD_DIM)
    )

    def backward_block(running, map_item):
        grad_queries, grad_keys, grad_values = attend_back(
            map_item[0],
            all_keys,
            all_values,
            allowed_for(map_item[1], map_item[2]),
            map_item[3],
            map_item[4],
        )
        return ((running[0] + grad_keys, running[1] + grad_values), grad_queries)

    empty_keys = jnp.zeros((row_length, head_count, HEAD_DIM), jnp.float32)
    sums_kv, grad_query_rows = lax.scan(
        backward_block,
        (empty_keys, empty_keys),
        (query_blocks, doc_blocks, index_blocks, logsum, grad_attended),
    )
    grad_key_own, grad_value_own = (
        lax.psum_scatter(
            sums_kv[0].reshape(row_length, model_width).astype(jnp.bfloat16),
            "narrow",
            scatter_dimension=0,
            tiled=True,
        ).astype(jnp.float32),
        lax.psum_scatter(
            sums_kv[1].reshape(row_length, model_width).astype(jnp.bfloat16),
            "narrow",
            scatter_dimension=0,
            tiled=True,
        ).astype(jnp.float32),
    )
    grad_query_rows = rotate(
        grad_query_rows.reshape(head_shape) * HEAD_DIM ** (-0.5), cosine, -sine_table
    )
    grad_query_rows = grad_query_rows.reshape(local_rows, model_width).astype(jnp.bfloat16)
    grad_key_rows = (
        rotate(grad_key_own.reshape(head_shape), cosine, -sine_table)
        .reshape(local_rows, model_width)
        .astype(jnp.bfloat16)
    )
    grad_value_rows = grad_value_own.astype(jnp.bfloat16)
    grad_query_proj = matmul_left(normed_one, grad_query_rows)
    grad_key_proj = matmul_left(normed_one, grad_key_rows)
    grad_value_proj = matmul_left(normed_one, grad_value_rows)
    grad_normed_one = (
        matmul_right(grad_query_rows, query_proj)
        + matmul_right(grad_key_rows, key_proj)
        + matmul_right(grad_value_rows, value_proj)
    )
    grad_input_norm, grad_attn = norm_backward(grad_normed_one, unit_one, scale_one, attn_scale)
    grad_tokens = grad_hidden + grad_input_norm
    halves = (
        lax.psum_scatter(
            grad_attn.astype(jnp.bfloat16), "narrow", scatter_dimension=0, tiled=True
        ).astype(jnp.float32),
        lax.psum_scatter(
            grad_query_proj.astype(jnp.bfloat16), "narrow", scatter_dimension=0, tiled=True
        ).astype(jnp.float32),
        lax.psum_scatter(
            grad_key_proj.astype(jnp.bfloat16), "narrow", scatter_dimension=0, tiled=True
        ).astype(jnp.float32),
        lax.psum_scatter(
            grad_value_proj.astype(jnp.bfloat16), "narrow", scatter_dimension=0, tiled=True
        ).astype(jnp.float32),
        lax.psum_scatter(
            grad_output_proj.astype(jnp.bfloat16), "narrow", scatter_dimension=0, tiled=True
        ).astype(jnp.float32),
        lax.psum_scatter(
            grad_ffn.astype(jnp.bfloat16), "narrow", scatter_dimension=0, tiled=True
        ).astype(jnp.float32),
        lax.psum_scatter(
            grad_router.astype(jnp.bfloat16), "narrow", scatter_dimension=0, tiled=True
        ).astype(jnp.float32),
        lax.psum_scatter(
            grad_cgate.astype(jnp.bfloat16), "narrow", scatter_dimension=0, tiled=True
        ).astype(jnp.float32),
        lax.psum_scatter(
            grad_cupper.astype(jnp.bfloat16), "narrow", scatter_dimension=0, tiled=True
        ).astype(jnp.float32),
        lax.psum_scatter(
            grad_cdown.astype(jnp.bfloat16), "narrow", scatter_dimension=0, tiled=True
        ).astype(jnp.float32),
    )
    owned = lax.psum(
        (
            halves[0],
            halves[1],
            halves[2],
            halves[3],
            halves[4],
            halves[5],
            halves[6],
            halves[7],
            halves[8],
            halves[9],
        ),
        "wide",
    )
    return (
        output,
        grad_tokens,
        owned[0],
        owned[1],
        owned[2],
        owned[3],
        owned[4],
        owned[5],
        owned[6],
        owned[7],
        owned[8],
        owned[9],
        expert_grads[0][None],
        expert_grads[1][None],
        expert_grads[2][None],
    )


def tokens_path(
    tokens,
    cotangent,
    lengths,
    routes,
    keep,
    attn_gain,
    w_query,
    w_key,
    w_value,
    w_out,
    ffn_gain,
    w_router,
    shared_gate,
    shared_up,
    shared_down,
    expert_gate,
    expert_up,
    expert_down,
):
    core = lax.axis_index("narrow")
    place = lax.axis_index("wide")
    wide_size = lax.axis_size("wide")
    levels = wide_size // 4
    local_rows, width = tokens.shape
    row_length = 2 * local_rows
    part = width // 2
    hidden_part = expert_gate.shape[2]
    stored = shared_gate.shape[1] // 2
    slice_width = -(-stored // (16 * wide_size)) * 16
    slices = stored // slice_width
    experts = w_router.shape[1]

    def swap(value):
        return lax.ppermute(value, "narrow", [(0, 1), (1, 0)])

    def in_order(mine, theirs, axis):
        return jnp.where(
            core == 0,
            jnp.concatenate([mine, theirs], axis=axis),
            jnp.concatenate([theirs, mine], axis=axis),
        )

    picks = (routes[:, :, None] == jnp.arange(experts, dtype=jnp.int32)[None, None, :]).astype(
        jnp.int32
    )
    marks = jnp.sum(picks * (1 + keep)[:, :, None], axis=1).astype(F32)

    first_unit = place * slice_width
    holds = place < slices

    def shared_slice(value, which, axis):
        begin = which * stored + first_unit
        taken = lax.dynamic_slice_in_dim(value, begin, slice_width, axis)
        return jnp.where(holds, taken, jnp.zeros((), value.dtype))

    gate_mine, up_mine = shared_slice(shared_gate, core, 1), shared_slice(shared_up, core, 1)
    gate_send, up_send = shared_slice(shared_gate, 1 - core, 1), shared_slice(shared_up, 1 - core, 1)
    down_slice = shared_slice(shared_down, 0, 0)
    gains = jnp.stack([attn_gain, ffn_gain])
    sent = swap(jnp.concatenate([gate_send.T, up_send.T, w_router.T], axis=0))
    gains = in_order(gains, swap(gains), 1).astype(F32)
    attn_scale, ffn_scale = gains[0], gains[1]
    dense = in_order(jnp.concatenate([gate_mine.T, up_mine.T, w_router.T], axis=0), sent, 1)
    router = dense[2 * slice_width :]

    inputs = tokens.astype(F32)
    square, wide_rows = (row_length, part), (local_rows, width)
    projections = [w_query, w_key, w_value]
    normed_one, qkv, sent = local_call(
        project_kernel,
        [(square, BF16), ((row_length, 3 * part), F32), ((row_length, 3 * part), BF16)],
        [((row_length, width), BF16)],
        tokens,
        swap(tokens),
        attn_scale[None, :],
        *projections,
    )
    index = jnp.arange(local_rows, dtype=jnp.int32)
    index = jnp.concatenate([core * local_rows + index, (1 - core) * local_rows + index])
    docs, positions = doc_layout(index, lengths[0])
    allowed = (docs[:, None] == docs[None, :]) & (index[None, :] <= index[:, None])
    cosine, sine_table = rotary_angles(positions)
    tables = [
        jnp.concatenate([cosine, cosine], axis=1),
        jnp.concatenate([-sine_table, sine_table], axis=1),
        allowed.astype(F32),
    ]
    *attention, branch, sent = local_call(
        attend_kernel,
        [(square, BF16)] * 4 + [(wide_rows, F32), (wide_rows, BF16)],
        [],
        qkv,
        swap(sent),
        *tables,
        w_out,
    )
    hidden = inputs + branch + swap(sent).astype(F32)
    normed, unit_two, scale_two = norm_forward(hidden, ffn_scale)
    normed_two = normed.astype(BF16)

    used = hidden_part + slice_width
    full = -(-(used + experts) // 128) * 128

    (_, _, _, grad_rows, expert_out, grad_mix, *expert_grads, shared_part) = experts_rows(
        normed_two,
        cotangent,
        marks.T,
        [expert_gate[0].T, expert_up[0].T, expert_down[0], dense, down_slice],
        hidden_part,
        used,
        full,
        levels,
        1,
    )
    grad_mix = lax.all_to_all(
        grad_mix.reshape(wide_size, 2, local_rows), "wide", split_axis=0, concat_axis=0, tiled=True
    )
    pick_core = jnp.where(core == 0, grad_mix[:, 0], grad_mix[:, 1])
    send_core = jnp.where(core == 0, grad_mix[:, 1], grad_mix[:, 0])
    grad_mix = (pick_core + swap(send_core)).T
    block_shape = (2 * wide_size, local_rows, width)
    grad_rows, expert_out, shared_all = exchange_wide(
        grad_rows.reshape(block_shape), expert_out.reshape(block_shape), shared_part, levels, 2
    )
    output = (hidden + expert_out.astype(F32)).astype(BF16)
    grad_expert_gate, grad_expert_up, grad_expert_down = expert_grads
    grad_shared_gate, grad_shared_up, grad_shared_down = shared_grads(
        shared_all, slices, part, stored
    )

    marks = marks.astype(F32)
    routed = marks > 0.0
    logits = matmul_right(normed_two, router)
    masked = jnp.where(routed, logits, MASKED)
    weights = jnp.where(routed, jnp.exp(masked - jnp.max(masked, axis=1, keepdims=True)), 0.0)
    gates = weights / jnp.sum(weights, axis=1, keepdims=True)
    grad_gates = jnp.where(marks > 1.5, grad_mix, 0.0)
    grad_logits = gates * (grad_gates - jnp.sum(gates * grad_gates, axis=1, keepdims=True))
    grad_logits = grad_logits.astype(BF16)
    grad_router = matmul_left(normed_two, grad_logits)
    grad_normed = grad_rows.astype(F32) + matmul(grad_logits, router)
    grad_hidden_norm, grad_ffn = norm_backward(grad_normed, unit_two, scale_two, ffn_scale)
    grad_hidden = cotangent.astype(F32) + grad_hidden_norm
    grad_branch = grad_hidden.astype(BF16)

    grad_w_out, mine = local_call(
        attend_back_kernel,
        [((part, width), BF16), ((3, *square), BF16)],
        [((row_length, width), BF16), (square, BF16)],
        grad_branch,
        swap(grad_branch),
        *attention,
        *tables,
        w_out,
    )
    grad_dense, grad_part, sent = local_call(
        dense_back_kernel,
        [((4, part, width), BF16), ((local_rows, part), F32), ((local_rows, part), BF16)],
        [((3, row_length, width), BF16)],
        mine,
        swap(mine),
        normed_one,
        grad_w_out,
        *projections,
    )
    grad_normed_one = in_order(grad_part, swap(sent).astype(F32), 1)
    _, unit_one, scale_one = norm_forward(inputs, attn_scale)
    grad_input_norm, grad_attn = norm_backward(grad_normed_one, unit_one, scale_one, attn_scale)
    grad_tokens = grad_hidden + grad_input_norm

    small = jnp.concatenate([grad_attn[:, None], grad_ffn[:, None], grad_router], axis=1)
    small_mine = lax.dynamic_slice_in_dim(small, core * part, part, 0)
    small_send = lax.dynamic_slice_in_dim(small, (1 - core) * part, part, 0)
    small = (small_mine + swap(small_send)).astype(BF16)
    size = small.size
    extra_rows = -(-size // (width * 16)) * 16
    flat = jnp.concatenate([small.reshape(-1), jnp.zeros((extra_rows * width - size,), BF16)])
    sum_rows = 4 * part // wide_size
    everything, flat = sum_dense(
        grad_dense.reshape(wide_size, sum_rows, width), flat.reshape(extra_rows, width), levels, 3
    )
    owned = everything.reshape(4, part, width)
    flat = flat.astype(F32).reshape(wide_size, -1)
    small = jnp.sum(flat[:, :size], axis=0).reshape(part, 2 + experts)
    return (
        output,
        grad_tokens,
        small[:, 0],
        owned[0].astype(F32),
        owned[1].astype(F32),
        owned[2].astype(F32),
        owned[3].astype(F32),
        small[:, 1],
        small[:, 2:],
        grad_shared_gate,
        grad_shared_up,
        grad_shared_down,
        grad_expert_gate.T[None],
        grad_expert_up.T[None],
        grad_expert_down[None],
    )


def per_device(*arrays):
    tokens = arrays[0]
    gathered = lax.axis_size("wide") * lax.axis_size("narrow") * tokens.size * 2
    fits = gathered <= 12 * 1024 * 1024
    return (tokens_path if fits else slots_path)(*arrays)


def solution(mesh):
    in_specs = (
        P(("wide", "narrow"), None),
        P(("wide", "narrow"), None),
        P("wide", None),
        P(("wide", "narrow"), None),
        P(("wide", "narrow"), None),
        P("narrow"),
        P("narrow", None),
        P("narrow", None),
        P("narrow", None),
        P("narrow", None),
        P("narrow"),
        P("narrow", None),
        P("narrow", None),
        P("narrow", None),
        P("narrow", None),
        P("wide", None, "narrow"),
        P("wide", None, "narrow"),
        P("wide", "narrow", None),
    )
    out_specs = (
        P(("wide", "narrow"), None),
        P(("wide", "narrow"), None),
        P("narrow"),
        P("narrow", None),
        P("narrow", None),
        P("narrow", None),
        P("narrow", None),
        P("narrow"),
        P("narrow", None),
        P("narrow", None),
        P("narrow", None),
        P("narrow", None),
        P("wide", None, "narrow"),
        P("wide", None, "narrow"),
        P("wide", "narrow", None),
    )
    return jax.shard_map(
        per_device, mesh=mesh, in_specs=in_specs, out_specs=out_specs, check_vma=False
    )
```

```python
import functools
import math

import jax
import jax.numpy as jnp
from jax import lax
from jax.experimental import pallas as pl
from jax.experimental.pallas import tpu as pltpu
from jax.sharding import PartitionSpec as P

HEAD_DIM = 128
TOPK = 7


EPS = 1e-06
MASKED = -1e30


def matmul(left, right):
    return jnp.dot(left, right, preferred_element_type=jnp.float32)


def matmul_left(left, right):
    return lax.dot_general(
        left, right, (((0,), (0,)), ((), ())), preferred_element_type=jnp.float32
    )


def matmul_right(left, right):
    return lax.dot_general(
        left, right, (((1,), (1,)), ((), ())), preferred_element_type=jnp.float32
    )


def doc_layout(positions, doc_lens):
    doc_ends = jnp.cumsum(doc_lens)
    passed = (positions[:, None] >= doc_ends[None, :]).astype(jnp.int32)
    doc_ids = jnp.sum(passed, axis=1)
    return (doc_ids, positions - jnp.sum(passed * doc_lens[None, :], axis=1))


def rotary_angles(positions):
    half_dim = HEAD_DIM // 2
    inverse = jnp.exp(
        jnp.arange(half_dim, dtype=jnp.float32) * (-2.0 * math.log(10000.0) / HEAD_DIM)
    )
    angles = positions.astype(jnp.float32)[:, None] * inverse[None, :]
    return (jnp.cos(angles), jnp.sin(angles))


def rotate(values, cosine, sine_table):
    half_dim = values.shape[-1] // 2
    lower_half = values[..., :half_dim]
    upper_half = values[..., half_dim:]
    cos_b = cosine[:, None, :]
    sin_b = sine_table[:, None, :]
    return jnp.concatenate(
        [lower_half * cos_b - upper_half * sin_b, upper_half * cos_b + lower_half * sin_b], axis=-1
    )


def norm_forward(values, gain_vec):
    row_scale = lax.rsqrt(jnp.mean(values * values, axis=-1, keepdims=True) + EPS)
    unit_rows = values * row_scale
    return (unit_rows * gain_vec, unit_rows, row_scale)


def norm_backward(grad_rows, unit_rows, row_scale, gain_vec):
    scaled = grad_rows * gain_vec
    grad_gain = jnp.sum(grad_rows * unit_rows, axis=0)
    grad_input = row_scale * (
        scaled - unit_rows * jnp.mean(scaled * unit_rows, axis=-1, keepdims=True)
    )
    return (grad_input, grad_gain)


def silu_parts(gate_vals):
    sigmoid_vals = jax.nn.sigmoid(gate_vals)
    return (gate_vals * sigmoid_vals, sigmoid_vals * (1.0 + gate_vals * (1.0 - sigmoid_vals)))


def expert_forward(in_rows, gate_mat, upper_mat):
    gate_vals = matmul(in_rows, gate_mat)
    upper = matmul(in_rows, upper_mat)
    act_vals, unused = silu_parts(gate_vals)
    return (gate_vals, upper, (act_vals * upper).astype(jnp.bfloat16))


def expert_backward(in_rows, grad_rows, gate_vals, upper, active, gate_mat, upper_mat, down_mat):
    grad_act = matmul_right(grad_rows, down_mat)
    act_vals, slope_vals = silu_parts(gate_vals)
    grad_gate = (grad_act * upper * slope_vals).astype(jnp.bfloat16)
    grad_upper = (grad_act * act_vals).astype(jnp.bfloat16)
    grad_down_mat = matmul_left(active, grad_rows)
    grad_gate_mat = matmul_left(in_rows, grad_gate)
    grad_upper_mat = matmul_left(in_rows, grad_upper)
    grad_input = matmul_right(grad_gate, gate_mat) + matmul_right(grad_upper, upper_mat)
    return (grad_input, grad_gate_mat, grad_upper_mat, grad_down_mat)


def attend_block(queries, keys_all, values_all, allowed):
    scores = jnp.einsum("qhd,khd->hqk", queries, keys_all, preferred_element_type=jnp.float32)
    masked = jnp.where(allowed[None], scores, MASKED)
    row_max = jnp.max(masked, axis=-1, keepdims=True)
    weights = jnp.exp(masked - row_max)
    row_total = jnp.sum(weights, axis=-1, keepdims=True)
    prob_rows = (weights / row_total).astype(jnp.bfloat16)
    attended = jnp.einsum("hqk,khd->qhd", prob_rows, values_all, preferred_element_type=jnp.float32)
    return (attended.astype(jnp.bfloat16), (row_max + jnp.log(row_total))[..., 0])


def attend_back(queries, keys_all, values_all, allowed, logsum, grad_attended):
    scores = jnp.einsum("qhd,khd->hqk", queries, keys_all, preferred_element_type=jnp.float32)
    masked = jnp.where(allowed[None], scores, MASKED)
    prob_rows = jnp.exp(masked - logsum[..., None])
    grad_probs = jnp.einsum(
        "qhd,khd->hqk", grad_attended, values_all, preferred_element_type=jnp.float32
    )
    row_delta = jnp.sum(prob_rows * grad_probs, axis=-1, keepdims=True)
    grad_scores = (prob_rows * (grad_probs - row_delta)).astype(jnp.bfloat16)
    grad_queries = jnp.einsum(
        "hqk,khd->qhd", grad_scores, keys_all, preferred_element_type=jnp.float32
    )
    grad_keys = jnp.einsum("hqk,qhd->khd", grad_scores, queries, preferred_element_type=jnp.float32)
    grad_values = jnp.einsum(
        "hqk,qhd->khd",
        prob_rows.astype(jnp.bfloat16),
        grad_attended,
        preferred_element_type=jnp.float32,
    )
    return (grad_queries, grad_keys, grad_values)


MESH_ID = pl.DeviceIdType.MESH
BF16 = jnp.bfloat16
F32 = jnp.float32


class Place:
    def __init__(self, levels):
        self.levels = levels
        wide = lax.axis_index("wide")
        self.core = lax.axis_index("narrow")
        self.level = wide // 4
        self.spot = lax.rem(wide, 4)
        self.across = self.spot + 1 - 2 * lax.rem(self.spot, 2)
        self.along = lax.rem(self.spot + 2, 4)
        self.corner = 3 - self.spot
        self.has_up = self.level < levels - 1
        self.has_down = self.level > 0

    def choose(self, values):
        result = jnp.int32(values[0])
        for k in range(1, self.levels):
            result = jnp.where(self.level == k, values[k], result)
        return result

    def device(self, level, spot, core=None):
        return {"wide": level * 4 + spot, "narrow": self.core if core is None else core}

    def enter(self, sibling):
        barrier = pltpu.get_barrier_semaphore()

        def greet(device):
            pl.semaphore_signal(barrier, inc=1, device_id=device, device_id_type=MESH_ID)

        greet(self.device(self.level, self.across))
        greet(self.device(self.level, self.along))
        if sibling:
            greet(self.device(self.level, self.spot, 1 - self.core))

        @pl.when(self.has_up)
        def _():
            greet(self.device(self.level + 1, self.spot))

        @pl.when(self.has_down)
        def _():
            greet(self.device(self.level - 1, self.spot))

        both = jnp.where(self.has_up, 1, 0) + jnp.where(self.has_down, 1, 0)
        pl.semaphore_wait(barrier, both + (3 if sibling else 2))


def remote(src, dst, send, recv, device):
    return pltpu.make_async_remote_copy(
        src_ref=src,
        dst_ref=dst,
        send_sem=send,
        recv_sem=recv,
        device_id=device,
        device_id_type=MESH_ID,
    )


class Gather:
    NAMES = ("up", "dn", "x", "y", "cx", "cy", "rz", "rx", "ry", "rcx", "rcy")

    def __init__(self, at, sibling, pairs, sems, keeps_own=True):
        self.at, self.sibling, self.pairs, self.keeps_own = at, sibling, pairs, keeps_own
        self.own_sem = sems[0]
        self.sems = dict(zip(self.NAMES, sems[1:12]))
        self.send_n, self.recv_n = sems[12:]
        self.order = self.visits()

    @staticmethod
    def scratch(levels, arrays):
        dma = pltpu.SemaphoreType.DMA
        return (
            [dma((arrays,))]
            + [dma((arrays, levels))] * 11
            + [dma((arrays, levels * 4))] * 2
        )

    def visits(self):
        at = self.at
        table = [
            sorted(range(at.levels), key=lambda lev: (abs(lev - here), lev))
            for here in range(at.levels)
        ]
        return [at.choose([row[k] for row in table]) for k in range(at.levels)]

    def block(self, n, lev, sp, core=None):
        x_ref, ref = self.pairs[n][:2]
        if self.sibling:
            return ref.at[(lev * 4 + sp) * 2 + (self.at.core if core is None else core)]
        if len(self.pairs[n]) == 3:
            return ref.at[lev * 4 + sp].at[pl.ds(self.pairs[n][2], x_ref.shape[0])]
        return ref.at[lev * 4 + sp]

    def each(self, send, recv, lev, sp, device, part=None, own=False):
        copies = []
        for n, (x_ref, *_) in enumerate(self.pairs):
            dst = self.block(n, lev, sp)
            src = x_ref if own else dst
            if part is not None:
                half = x_ref.shape[0] // 2
                src = src.at[pl.ds(part * half, half)]
                dst = dst.at[pl.ds(part * half, half)]
            copies.append(
                remote(src, dst, self.sems[send].at[n, lev], self.sems[recv].at[n, lev], device)
            )
        return copies

    def up(self, lev, own=False):
        at = self.at
        return self.each("up", "rz", lev, at.spot, at.device(at.level + 1, at.spot), own=own)

    def down(self, lev, own=False):
        at = self.at
        return self.each("dn", "rz", lev, at.spot, at.device(at.level - 1, at.spot), own=own)

    def over_x(self, lev, sp, own=False):
        at = self.at
        return self.each("x", "rx", lev, sp, at.device(at.level, at.across), own=own)

    def over_y(self, lev, sp, own=False):
        at = self.at
        return self.each("y", "ry", lev, sp, at.device(at.level, at.along), own=own)

    def corner_y(self, lev, sp):
        at = self.at
        return self.each("cy", "rcy", lev, sp, at.device(at.level, at.along), part=0)

    def corner_x(self, lev, sp):
        at = self.at
        return self.each("cx", "rcx", lev, sp, at.device(at.level, at.across), part=1)

    def near(self, lev, sp, core=None, own=False):
        at = self.at
        copies = []
        for n, (x_ref, *_) in enumerate(self.pairs):
            dst = self.block(n, lev, sp, core)
            sems = self.send_n.at[n, lev * 4 + sp], self.recv_n.at[n, lev * 4 + sp]
            device = at.device(at.level, at.spot, 1 - at.core)
            copies.append(remote(x_ref if own else dst, dst, *sems, device))
        return copies

    def own_copies(self):
        at = self.at
        return [
            pltpu.make_async_copy(x_ref, self.block(n, at.level, at.spot), self.own_sem.at[n])
            for n, (x_ref, *_) in enumerate(self.pairs)
        ]

    def take_own(self):
        for copy in self.own_copies():
            copy.wait()

    def begin(self):
        at = self.at
        pl.when(at.has_up)(lambda: start(self.up(at.level, own=True)))
        pl.when(at.has_down)(lambda: start(self.down(at.level, own=True)))
        start(self.over_x(at.level, at.spot, own=True))
        start(self.over_y(at.level, at.spot, own=True))
        if self.sibling:
            start(self.near(at.level, at.spot, own=True))
        if self.keeps_own:
            start(self.own_copies())

    def take_column(self, lev):
        at = self.at
        arrived(self.up(lev))
        pl.when((lev < at.level) & at.has_up)(lambda: start(self.up(lev)))
        pl.when((lev > at.level) & at.has_down)(lambda: start(self.down(lev)))
        start(self.over_x(lev, at.spot))
        start(self.over_y(lev, at.spot))
        if self.sibling:
            start(self.near(lev, at.spot))

    def take_x(self, lev):
        at = self.at
        arrived(self.over_x(lev, at.across))
        start(self.corner_y(lev, at.across))
        if self.sibling:
            start(self.near(lev, at.across))

    def take_y(self, lev):
        at = self.at
        arrived(self.over_y(lev, at.along))
        start(self.corner_x(lev, at.along))
        if self.sibling:
            start(self.near(lev, at.along))

    def take_corner(self, lev):
        at = self.at
        arrived(self.corner_y(lev, at.corner))
        arrived(self.corner_x(lev, at.corner))
        if self.sibling:
            start(self.near(lev, at.corner))

    def take_near(self, lev, sp):
        arrived(self.near(lev, sp, 1 - self.at.core))

    def steps(self):
        levels, steps = self.at.levels, []
        for s in range(1, levels + 2):
            if s < levels:
                steps.append(lambda lev=self.order[s]: self.take_column(lev))
            if s - 1 < levels:
                steps.append(lambda lev=self.order[s - 1]: self.take_x(lev))
                steps.append(lambda lev=self.order[s - 1]: self.take_y(lev))
            if s >= 2:
                steps.append(lambda lev=self.order[s - 2]: self.take_corner(lev))
        return steps

    def finish(self, near=True):
        at = self.at
        if near:
            self.take_own()
        for lev in range(at.levels):
            pl.when(at.has_up & (lev <= at.level))(lambda lev=lev: sent(self.up(lev)))
            pl.when(at.has_down & (lev >= at.level))(lambda lev=lev: sent(self.down(lev)))
            sent(self.over_x(lev, at.spot))
            sent(self.over_y(lev, at.spot))
            sent(self.corner_y(lev, at.across))
            sent(self.corner_x(lev, at.along))
            if self.sibling:
                for sp in range(4):
                    sent(self.near(lev, sp))
                    if near:
                        self.take_near(lev, sp)


def start(copies):
    for copy in copies:
        copy.start()


def arrived(copies):
    for copy in copies:
        copy.wait_recv()


def sent(copies):
    for copy in copies:
        copy.wait_send()


def dot_nn(left, right):
    return lax.dot_general(left, right, (((1,), (0,)), ((), ())), preferred_element_type=F32)


def dot_tn(left, right):
    return lax.dot_general(left, right, (((0,), (0,)), ((), ())), preferred_element_type=F32)


def dot_nt(left, right):
    return lax.dot_general(left, right, (((1,), (1,)), ((), ())), preferred_element_type=F32)


def experts_kernel(
    levels, sizes, x_ref, g_ref, m_ref, eg_ref, eu_ref, ed_ref, small_ref, sd_ref,
    rows_ref, grads_ref, marks_ref, back_ref, out_ref, gm_ref, dgate_ref, dup_ref, ddown_ref, shared_ref,
    x_buf, g_buf, mark_buf, cu_buf, g_val, mixed_buf, act_buf, back_buf, out_buf, gm_buf, mark_t,
    in_sem, out_sem, gm_val, gw_ref, gd_ref, gate_ref, down_ref, w_sem, *sems,
):
    hidden, used, full = sizes
    at = Place(levels)
    at.enter(True)
    gather = Gather(at, True, [(x_ref, rows_ref), (g_ref, grads_ref), (m_ref, marks_ref)], sems, False)
    gather.begin()
    size, experts = used - hidden, m_ref.shape[0]
    pieces = [
        (eg_ref, gate_ref, 0, hidden),
        (eu_ref, gate_ref, full, hidden),
        (small_ref.at[pl.ds(0, size)], gate_ref, hidden, size),
        (small_ref.at[pl.ds(size, size)], gate_ref, full + hidden, size),
        (small_ref.at[pl.ds(2 * size, experts)], gate_ref, used, experts),
        (ed_ref, down_ref, 0, hidden),
        (sd_ref, down_ref, hidden, size),
    ]
    weights = [
        pltpu.make_async_copy(src, dst.at[pl.ds(row, count)], w_sem.at[n])
        for n, (src, dst, row, count) in enumerate(pieces)
    ]
    start(weights)
    for ref, row, end in ((gate_ref, used + experts, full), (gate_ref, full + used, 2 * full), (down_ref, used, full)):
        if end > row:
            ref[row:end, :] = jnp.zeros((end - row, ref.shape[1]), BF16)
    place = at.level * 4 + at.spot
    units, ahead = 4 * levels, 3
    plan = [(0, 0)]
    for s in range(1, levels + 2):
        if s < levels:
            plan.append((s, 0))
        if s - 1 < levels:
            plan += [(s - 1, 1), (s - 1, 2)]
        if s >= 2:
            plan.append((s - 2, 3))
    rows = x_ref.shape[0]
    batch = 2 * rows

    def pick(k, values):
        result = jnp.int32(0) + values[0]
        for j in range(1, len(values)):
            result = jnp.where(k == j, values[j], result)
        return result

    def unit(k):
        visit = pick(k, [v for v, _ in plan])
        kind = pick(k, [t for _, t in plan])
        lev = pick(visit, gather.order)
        sp = pick(kind, [at.spot, at.across, at.along, at.corner])
        return lev, sp, kind

    def loads(k, first):
        slot = lax.rem(k, 4)
        blocks = pl.ds(first, 2)
        return [
            pltpu.make_async_copy(rows_ref.at[blocks], x_buf.at[slot], in_sem.at[slot, 0]),
            pltpu.make_async_copy(grads_ref.at[blocks], g_buf.at[slot], in_sem.at[slot, 1]),
            pltpu.make_async_copy(marks_ref.at[blocks], mark_buf.at[slot], in_sem.at[slot, 2]),
        ]

    def stores(k, first):
        slot = lax.rem(k, 2)
        rng = pl.ds(pl.multiple_of(first * rows, batch), batch)
        pairs = [(back_buf, back_ref), (out_buf, out_ref)]
        return [
            pltpu.make_async_copy(buf.at[slot], ref.at[rng], out_sem.at[slot, n])
            for n, (buf, ref) in enumerate(pairs)
        ]

    def serve(k):
        lev, sp, kind = unit(k)
        pl.when(kind == 0)(lambda: gather.take_column(lev))
        pl.when(kind == 1)(lambda: gather.take_x(lev))
        pl.when(kind == 2)(lambda: gather.take_y(lev))
        pl.when(kind == 3)(lambda: gather.take_corner(lev))

    def fetch(k):
        lev, sp, _ = unit(k)
        gather.take_near(lev, sp)
        start(loads(k, (lev * 4 + sp) * 2))

    def fetch_own():
        gather.take_near(at.level, at.spot)
        theirs = 1 - at.core
        triples = [(x_ref, rows_ref, x_buf), (g_ref, grads_ref, g_buf), (m_ref, marks_ref, mark_buf)]
        for n, (own, gathered, buf) in enumerate(triples):
            sem = in_sem.at[0, n]
            other = gathered.at[place * 2 + theirs]
            pltpu.make_async_copy(own, buf.at[0, at.core], sem).start()
            pltpu.make_async_copy(other, buf.at[0, theirs], sem).start()

    def lanes(n):
        return lax.broadcasted_iota(jnp.int32, (batch, 128), 1) + n * 128

    def mixing():
        tail = full // 128 - 1
        mark = mark_t[...]
        masked = jnp.where(mark > 0.5, cu_buf[:, full - 128 : full], MASKED)
        top = jnp.max(masked, axis=1, keepdims=True)
        weight = jnp.where(mark > 0.5, jnp.exp(masked - top), 0.0)
        mine = jnp.where((lanes(tail) == used + place) & (mark > 1.5), weight, 0.0)
        return jnp.sum(mine, axis=1, keepdims=True) / jnp.sum(weight, axis=1, keepdims=True)

    def elementwise(odd):
        mix = jnp.broadcast_to(mixing(), (batch, 128))
        total = jnp.zeros((batch, 128), F32)
        for n in range(full // 128):
            cols = slice(n * 128, (n + 1) * 128)
            up_cols = slice(full + n * 128, full + (n + 1) * 128)
            gate, upper, back = cu_buf[:, cols], cu_buf[:, up_cols], g_val[:, cols]
            whole = (n + 1) * 128 <= hidden
            scale = mix
            if not whole:
                scale = jnp.where(lanes(n) < hidden, mix, jnp.where(lanes(n) < used, 1.0, 0.0))
            sig = jax.nn.sigmoid(gate)
            act = gate * sig
            active = act * upper
            grad_act = scale * back
            slope = sig * (1.0 + gate * (1.0 - sig))
            mixed_buf[odd, :, cols] = (scale * active).astype(BF16)
            act_buf[odd, :, cols] = (grad_act * upper * slope).astype(BF16)
            act_buf[odd, :, up_cols] = (grad_act * act).astype(BF16)
            term = active * back
            total = total + (term if whole else jnp.where(lanes(n) < hidden, term, 0.0))
        gm_buf[...] = total

    def forward(k):
        lev, sp, _ = unit(k)
        first = (lev * 4 + sp) * 2
        slot = lax.rem(k, 4)
        for copy in loads(k, first):
            copy.wait()
        x = x_buf[slot].reshape(batch, -1)
        cu_buf[...] = dot_nt(x, gate_ref[...])
        g_val[...] = dot_nt(g_buf[slot].reshape(batch, -1), down_ref[...])
        for n in range(2):
            marks = mark_buf[slot, n]
            above = jnp.zeros((used - (full - 128), 128), F32)
            below = jnp.zeros((full - used - marks.shape[0], 128), F32)
            mark_t[pl.ds(n * rows, rows), :] = jnp.transpose(jnp.concatenate([above, marks, below], axis=0))
        elementwise(lax.rem(k, 2))

    def backward(k):
        lev, sp, _ = unit(k)
        first = (lev * 4 + sp) * 2
        slot = lax.rem(k, 2)

        @pl.when(k >= 2)
        def _():
            for copy in stores(k, 0):
                copy.wait()

        back_buf[slot] = dot_nn(act_buf[slot], gate_ref[...]).astype(BF16)
        out_buf[slot] = dot_nn(mixed_buf[slot], down_ref[...]).astype(BF16)
        for n in range(2):
            gm = jnp.transpose(gm_buf[pl.ds(n * rows, rows), :])
            gm_val[pl.ds(first + n, 1), :] = jnp.sum(gm, axis=0, keepdims=True)
        start(stores(k, first))

        both = pl.ds(lax.rem(k, 4) - 1, 2)

        def gate_grad(m, carry):
            part = pl.ds(pl.multiple_of(m * 256, 256), 256)
            left = act_buf[:, :, part].reshape(2 * batch, 256)
            gw_ref[part, :] += dot_tn(left, x_buf[both].reshape(2 * batch, -1))
            return carry

        def down_grad(m, carry):
            part = pl.ds(pl.multiple_of(m * 256, 256), 256)
            left = mixed_buf[:, :, part].reshape(2 * batch, 256)
            gd_ref[part, :] += dot_tn(left, g_buf[both].reshape(2 * batch, -1))
            return carry

        @pl.when(slot == 1)
        def _():
            lax.fori_loop(0, gw_ref.shape[0] // 256, gate_grad, 0)
            lax.fori_loop(0, full // 256, down_grad, 0)

    gw_ref[...] = jnp.zeros_like(gw_ref)
    gd_ref[...] = jnp.zeros_like(gd_ref)
    fetch_own()
    for copy in weights:
        copy.wait()

    def loop(k, carry):
        pl.when((k > 0) & (k + 1 < units))(lambda: fetch(k + 1))
        forward(k)

        @pl.when(k == 0)
        def _():
            for n in range(1, ahead + 1):
                serve(n)
            fetch(1)

        pl.when((k > 0) & (k + ahead < units))(lambda: serve(k + ahead))
        backward(k)
        return carry

    lax.fori_loop(0, units, loop, 0)
    gm_ref[...] = gm_val[...]
    finals = [
        pltpu.make_async_copy(src.at[pl.ds(row, hidden)], dst, w_sem.at[n])
        for n, (src, row, dst) in enumerate(
            ((gw_ref, 0, dgate_ref), (gw_ref, full, dup_ref), (gd_ref, 0, ddown_ref))
        )
    ]
    start(finals)
    for n, (ref, row) in enumerate(((gw_ref, hidden), (gw_ref, full + hidden), (gd_ref, hidden))):
        shared_ref[n * size : (n + 1) * size, :] = ref[row : row + size, :].astype(BF16)
    for copy in finals:
        copy.wait()
    for k in (0, 1):
        for copy in stores(k, 0):
            copy.wait()
    gather.finish(near=False)


def experts_rows(x, grads, marks, weights, hidden, used, full, levels, collective_id):
    rows, width = x.shape
    blocks = 8 * levels
    total = blocks * rows
    dma = pltpu.SemaphoreType.DMA
    vmem = pltpu.VMEM
    anywhere = pl.BlockSpec(memory_space=pl.ANY)
    inside = pl.BlockSpec(memory_space=vmem)
    shape = jax.ShapeDtypeStruct
    batch = 2 * rows
    return pl.pallas_call(
        functools.partial(experts_kernel, levels, (hidden, used, full)),
        out_shape=[
            shape((blocks, rows, width), BF16),
            shape((blocks, rows, width), BF16),
            shape((blocks, *marks.shape), F32),
            shape((total, width), BF16),
            shape((total, width), BF16),
            shape((blocks, rows), F32),
            shape((hidden, width), F32),
            shape((hidden, width), F32),
            shape((hidden, width), F32),
            shape((3 * (used - hidden), width), BF16),
        ],
        in_specs=[anywhere] * 8,
        out_specs=[anywhere] * 5 + [inside] + [anywhere] * 3 + [inside],
        scratch_shapes=[
            vmem((4, 2, rows, width), BF16),
            vmem((4, 2, rows, width), BF16),
            vmem((4, 2, *marks.shape), F32),
            vmem((batch, 2 * full), F32),
            vmem((batch, full), F32),
            vmem((2, batch, full), BF16),
            vmem((2, batch, 2 * full), BF16),
            vmem((2, batch, width), BF16),
            vmem((2, batch, width), BF16),
            vmem((batch, 128), F32),
            vmem((batch, 128), F32),
            dma((4, 3)),
            dma((2, 2)),
            vmem((blocks, rows), F32),
            vmem((2 * full, width), F32),
            vmem((full, width), F32),
            vmem((2 * full, width), BF16),
            vmem((full, width), BF16),
            dma((7,)),
        ]
        + Gather.scratch(levels, 3),
        compiler_params=pltpu.CompilerParams(
            collective_id=collective_id,
            has_side_effects=True,
            vmem_limit_bytes=56 * 1024 * 1024,
        ),
    )(x, grads, marks, *weights)


def shared_kernel(slices, x_ref, gate_ref, up_ref, down_ref, gate_buf, up_buf, down_buf, sem):
    part, units = gate_ref.shape
    stored = units // 2
    size = stored // slices
    copies = []
    for n in range(slices):
        for c in range(2):
            rows = pl.ds(c * stored + n * size, size)
            src = x_ref.at[n, pl.ds(c * size, size)]
            for buf, lanes in ((gate_buf, pl.ds(0, part)), (up_buf, pl.ds(part, part))):
                copies.append(pltpu.make_async_copy(src.at[:, lanes], buf.at[rows], sem.at[len(copies)]))
        src, dst = x_ref.at[n, pl.ds(2 * size, size)], down_buf.at[pl.ds(n * size, size)]
        copies.append(pltpu.make_async_copy(src, dst, sem.at[len(copies)]))
    start(copies)
    for copy in copies:
        copy.wait()
    down_ref[...] = down_buf[...].astype(F32)
    for buf, ref in ((gate_buf, gate_ref), (up_buf, up_ref)):
        for n in range(units // 128):
            rows = pl.ds(n * 128, 128)
            ref[:, rows] = jnp.transpose(buf[rows, :].astype(F32))


def shared_grads(gathered, slices, part, stored):
    width = gathered.shape[2]
    vmem = pltpu.VMEM
    inside = pl.BlockSpec(memory_space=vmem)
    shape = jax.ShapeDtypeStruct
    return pl.pallas_call(
        functools.partial(shared_kernel, slices),
        out_shape=[
            shape((part, 2 * stored), F32),
            shape((part, 2 * stored), F32),
            shape((stored, width), F32),
        ],
        in_specs=[pl.BlockSpec(memory_space=pl.ANY)],
        out_specs=[inside] * 3,
        scratch_shapes=[
            vmem((2 * stored, part), BF16),
            vmem((2 * stored, part), BF16),
            vmem((stored, width), BF16),
            pltpu.SemaphoreType.DMA((5 * slices,)),
        ],
        compiler_params=pltpu.CompilerParams(vmem_limit_bytes=60 * 1024 * 1024),
    )(gathered)


def destinations(levels):
    return [
        sorted(range(levels), key=lambda to: (-abs(to - here), -to)) for here in range(levels)
    ]


def add_rows(write, sources, rows):
    step = 16

    def body(k, carry):
        r = pl.ds(pl.multiple_of(k * step, step), step)
        total = sources[0](r)
        for source in sources[1:]:
            total = total + source(r)
        write(r, total)
        return carry

    lax.fori_loop(0, rows // step, body, 0)


def reads(ref):
    return lambda r: ref[r, :].astype(F32)


def writes(ref):
    def write(r, total):
        ref[r, :] = total.astype(ref.dtype)

    return write


class Scatter:
    def __init__(self, at, sibling, x_ref, out_ref, refs, row=None):
        self.at, self.sibling, self.x_ref, self.out_ref = at, sibling, x_ref, out_ref
        self.row = row
        self.acc, self.near, self.hx, self.hy, self.fx, self.fy = refs[:6]
        self.out_buf, self.za, self.zb = refs[6:9]
        self.own_sem, self.send_n, self.recv_n = refs[9:12]
        self.send = dict(zip(("hx", "hy", "fx", "fy", "up", "dn"), refs[12:18]))
        self.recv = dict(zip(("hx", "hy", "fx", "fy", "za", "zb"), refs[18:24]))
        self.rows = out_ref.shape[0]
        table = destinations(at.levels)
        self.order = [at.choose([row[s] for row in table]) for s in range(at.levels)]

    SCRATCH = 24

    @staticmethod
    def scratch(levels, sibling, rows, width):
        dma, vmem = pltpu.SemaphoreType.DMA, pltpu.VMEM
        blocks = levels * 4
        return (
            [
                vmem((blocks, rows, width), BF16),
                vmem((blocks if sibling else 1, rows, width), BF16),
                vmem((levels, rows // 2, width), BF16),
                vmem((levels, rows // 2, width), BF16),
            ]
            + [vmem((levels, rows, width), BF16)] * 5
            + [dma((blocks,))] * 3
            + [dma((levels,))] * 12
        )

    def own(self, lev, sp):
        b = lev * 4 + sp
        src = self.x_ref.at[b * 2 + self.at.core if self.sibling else b]
        if self.row is not None:
            src = src.at[pl.ds(self.row, self.rows)]
        return pltpu.make_async_copy(src, self.acc.at[b], self.own_sem.at[b])

    def to_sibling(self, lev, sp):
        at, b = self.at, lev * 4 + sp
        sems = self.send_n.at[b], self.recv_n.at[b]
        src = self.x_ref.at[b * 2 + 1 - at.core]
        return remote(src, self.near.at[b], *sems, at.device(at.level, at.spot, 1 - at.core))

    def side(self, name, src, dst, lev, spot):
        sems = self.send[name].at[lev], self.recv[name].at[lev]
        return remote(src, dst, *sems, self.at.device(self.at.level, spot))

    def half_y(self, lev):
        src = self.acc.at[lev * 4 + self.at.corner].at[pl.ds(0, self.rows // 2)]
        return self.side("hy", src, self.hy.at[lev], lev, self.at.along)

    def half_x(self, lev):
        src = self.acc.at[lev * 4 + self.at.corner].at[pl.ds(self.rows // 2, self.rows // 2)]
        return self.side("hx", src, self.hx.at[lev], lev, self.at.across)

    def full_x(self, lev):
        return self.side("fx", self.acc.at[lev * 4 + self.at.across], self.fx.at[lev], lev, self.at.across)

    def full_y(self, lev):
        return self.side("fy", self.acc.at[lev * 4 + self.at.along], self.fy.at[lev], lev, self.at.along)

    def go_up(self, lev):
        sems = self.send["up"].at[lev], self.recv["zb"].at[lev]
        device = self.at.device(self.at.level + 1, self.at.spot)
        return remote(self.out_buf.at[lev], self.zb.at[lev], *sems, device)

    def go_down(self, lev):
        sems = self.send["dn"].at[lev], self.recv["za"].at[lev]
        device = self.at.device(self.at.level - 1, self.at.spot)
        return remote(self.out_buf.at[lev], self.za.at[lev], *sems, device)

    def spots(self):
        return self.at.corner, self.at.across, self.at.along, self.at.spot

    def begin(self):
        for lev in self.order:
            for sp in self.spots():
                if self.sibling:
                    self.to_sibling(lev, sp).start()
                self.own(lev, sp).start()

    def local(self, lev):
        for n, sp in enumerate(self.spots()):
            ref = self.acc.at[lev * 4 + sp]
            self.own(lev, sp).wait()
            if self.sibling:
                self.to_sibling(lev, sp).wait_recv()
                add_rows(writes(ref), [reads(ref), reads(self.near.at[lev * 4 + sp])], self.rows)
            if n == 0:
                self.half_y(lev).start()
                self.half_x(lev).start()

    def halves(self, lev):
        half = self.rows // 2
        self.half_y(lev).wait_recv()
        ref = self.acc.at[lev * 4 + self.at.across].at[pl.ds(0, half)]
        add_rows(writes(ref), [reads(ref), reads(self.hy.at[lev])], half)
        self.full_x(lev).start()
        self.half_x(lev).wait_recv()
        ref = self.acc.at[lev * 4 + self.at.along].at[pl.ds(half, half)]
        add_rows(writes(ref), [reads(ref), reads(self.hx.at[lev])], half)
        self.full_y(lev).start()

    def column(self, lev):
        at, rows, level = self.at, self.rows, self.at.level
        self.full_x(lev).wait_recv()
        self.full_y(lev).wait_recv()
        own = [reads(self.acc.at[lev * 4 + at.spot]), reads(self.fx.at[lev]), reads(self.fy.at[lev])]
        above, below = reads(self.za.at[lev]), reads(self.zb.at[lev])
        passed = writes(self.out_buf.at[lev])
        final = writes(self.out_ref)

        def send(has, arrival, term, departure):
            @pl.when(has)
            def _():
                arrival(lev).wait_recv()
                add_rows(passed, [*own, term], rows)

            pl.when(jnp.logical_not(has))(lambda: add_rows(passed, own, rows))
            departure(lev).start()

        pl.when(lev < level)(lambda: send(at.has_up, self.go_down, above, self.go_down))
        pl.when(lev > level)(lambda: send(at.has_down, self.go_up, below, self.go_up))

        @pl.when(lev == level)
        def _():
            pl.when(at.has_up)(lambda: self.go_down(lev).wait_recv())
            pl.when(at.has_down)(lambda: self.go_up(lev).wait_recv())
            both = at.has_up & at.has_down
            pl.when(both)(lambda: add_rows(final, [*own, above, below], rows))
            pl.when(jnp.logical_not(at.has_down))(lambda: add_rows(final, [*own, above], rows))
            pl.when(jnp.logical_not(at.has_up))(lambda: add_rows(final, [*own, below], rows))

    def steps(self):
        levels, steps = self.at.levels, []
        for s in range(levels + 2):
            if s < levels:
                steps.append(lambda lev=self.order[s]: self.local(lev))
            if 0 <= s - 1 < levels:
                steps.append(lambda lev=self.order[s - 1]: self.halves(lev))
            if s >= 2:
                steps.append(lambda lev=self.order[s - 2]: self.column(lev))
        return steps

    def finish(self):
        for lev in range(self.at.levels):
            if self.sibling:
                for sp in range(4):
                    self.to_sibling(lev, sp).wait_send()
            sent([self.half_y(lev), self.half_x(lev), self.full_x(lev), self.full_y(lev)])
            pl.when(lev < self.at.level)(lambda lev=lev: self.go_down(lev).wait_send())
            pl.when(lev > self.at.level)(lambda lev=lev: self.go_up(lev).wait_send())


def dense_kernel(levels, spans, x_ref, flat_ref, all_ref, flat_all_ref, *refs):
    at = Place(levels)
    at.enter(False)
    sums, refs = refs[:2], refs[2:]
    size = Scatter.SCRATCH
    scatters = [
        Scatter(at, False, x_ref, sums[n], refs[n * size : (n + 1) * size], spans[n][0]) for n in range(2)
    ]
    refs = refs[2 * size :]
    pairs = [[(sums[n], all_ref, spans[n][0])] for n in range(2)]
    pairs[1].append((flat_ref, flat_all_ref))
    gathers = []
    for n in range(2):
        gathers.append(Gather(at, False, pairs[n], refs[n * 14 : (n + 1) * 14]))
    for task in scatters:
        task.begin()
    steps = []
    for n, lag in enumerate((0, 7)):
        begin = len(scatters[n].steps()) + lag
        steps += [(s + lag, n, step) for s, step in enumerate(scatters[n].steps())]
        steps.append((begin - 0.5, n, gathers[n].begin))
        steps += [(begin + s, 2 + n, step) for s, step in enumerate(gathers[n].steps())]
    for _, _, step in sorted(steps, key=lambda entry: entry[:2]):
        step()
    for task in [*scatters, *gathers]:
        task.finish()


def sum_dense(x, flat, levels, collective_id):
    blocks, rows, width = x.shape
    first = -(-rows // 64) * 32
    spans = [(0, first), (first, rows - first)]
    vmem, anywhere = pltpu.VMEM, pl.BlockSpec(memory_space=pl.ANY)
    shape = jax.ShapeDtypeStruct
    return pl.pallas_call(
        functools.partial(dense_kernel, levels, spans),
        out_shape=[shape(x.shape, BF16), shape((blocks, *flat.shape), BF16)],
        in_specs=[anywhere, anywhere],
        out_specs=[anywhere, anywhere],
        scratch_shapes=[vmem((n, width), BF16) for _, n in spans]
        + Scatter.scratch(levels, False, spans[0][1], width)
        + Scatter.scratch(levels, False, spans[1][1], width)
        + Gather.scratch(levels, 1)
        + Gather.scratch(levels, 2),
        compiler_params=pltpu.CompilerParams(
            collective_id=collective_id,
            has_side_effects=True,
            vmem_limit_bytes=60 * 1024 * 1024,
        ),
    )(x, flat)


def exchange_kernel(
    levels, back_ref, out_ref, part_ref, rows_ref, sum_ref, all_ref, block, send_s, recv_s, own_s, *refs
):
    at = Place(levels)
    at.enter(True)
    size = Scatter.SCRATCH
    first = Scatter(at, True, back_ref, rows_ref, refs[:size])
    second = Scatter(at, True, out_ref, sum_ref, refs[size : 2 * size])
    gather = Gather(at, False, [(block, all_ref)], refs[2 * size :])
    units, half = part_ref.shape[0] // 3, part_ref.shape[1] // 2
    mine = pl.ds(pl.multiple_of(at.core * units, units), units)
    own, theirs, sends = [], [], []
    for n in range(2):
        rows, lanes = pl.ds(n * units, units), pl.ds(n * half, half)

        def side(core):
            return part_ref.at[rows, pl.ds(pl.multiple_of(core * half, 128), half)]

        own.append(pltpu.make_async_copy(side(at.core), block.at[mine, lanes], own_s.at[n]))
        device = at.device(at.level, at.spot, 1 - at.core)
        sems = send_s.at[n], recv_s.at[n]
        sends.append(remote(side(1 - at.core), block.at[mine, lanes], *sems, device))
    down = pl.ds(2 * units, units)
    own.append(pltpu.make_async_copy(part_ref.at[down], block.at[down], own_s.at[2]))
    start(sends)
    start(own)
    first.begin()
    second.begin()
    for copy in own:
        copy.wait()
    arrived(sends)
    gather.begin()
    steps = [(s, 0, step) for s, step in enumerate(first.steps())]
    steps += [(s + 7, 1, step) for s, step in enumerate(second.steps())]
    steps += [(s + 2, 2, step) for s, step in enumerate(gather.steps())]
    for _, _, step in sorted(steps, key=lambda entry: entry[:2]):
        step()
    sent(sends)
    first.finish()
    second.finish()
    gather.finish()


def exchange_wide(back, out, part, levels, collective_id):
    rows, width = back.shape[1:]
    dma = pltpu.SemaphoreType.DMA
    anywhere, inside = pl.BlockSpec(memory_space=pl.ANY), pl.BlockSpec(memory_space=pltpu.VMEM)
    shape = jax.ShapeDtypeStruct
    return pl.pallas_call(
        functools.partial(exchange_kernel, levels),
        out_shape=[
            shape((rows, width), BF16),
            shape((rows, width), BF16),
            shape((levels * 4, *part.shape), BF16),
        ],
        in_specs=[anywhere, anywhere, inside],
        out_specs=[inside, inside, anywhere],
        scratch_shapes=[pltpu.VMEM(part.shape, BF16), dma((2,)), dma((2,)), dma((3,))]
        + Scatter.scratch(levels, True, rows, width) * 2
        + Gather.scratch(levels, 1),
        compiler_params=pltpu.CompilerParams(
            collective_id=collective_id,
            has_side_effects=True,
            vmem_limit_bytes=60 * 1024 * 1024,
        ),
        cost_estimate=pl.CostEstimate(
            flops=40 * 10**9, bytes_accessed=200 * 10**6, transcendentals=0
        ),
    )(back, out, part)


def local_call(kernel, outs, scratch, *args):
    inside = pl.BlockSpec(memory_space=pltpu.VMEM)
    return pl.pallas_call(
        kernel,
        out_shape=[jax.ShapeDtypeStruct(s, d) for s, d in outs],
        in_specs=[inside] * len(args),
        out_specs=[inside] * len(outs),
        scratch_shapes=[pltpu.VMEM(s, d) for s, d in scratch],
        compiler_params=pltpu.CompilerParams(vmem_limit_bytes=48 * 1024 * 1024),
    )(*args)


def half_lanes(which, size):
    return pl.ds(pl.multiple_of(which * size, 128), size)


def project_kernel(mine_ref, theirs_ref, scale_ref, q_ref, k_ref, v_ref, n_ref, keep_ref, send_ref, buf):
    core = lax.axis_index("narrow")
    rows = mine_ref.shape[0]
    part = n_ref.shape[1]
    for n, ref in enumerate((mine_ref, theirs_ref)):
        x = ref[...].astype(F32)
        r = lax.rsqrt(jnp.mean(x * x, axis=1, keepdims=True) + EPS)
        buf[n * rows : (n + 1) * rows, :] = (x * r * scale_ref[...]).astype(BF16)
    normed = buf[:, half_lanes(core, part)]
    n_ref[...] = normed
    for n, ref in enumerate((q_ref, k_ref, v_ref)):
        cols = slice(n * part, (n + 1) * part)
        send_ref[:, cols] = dot_nn(normed, ref[:, half_lanes(1 - core, part)]).astype(BF16)
        keep_ref[:, cols] = dot_nn(normed, ref[:, half_lanes(core, part)])


def probabilities(q, k, allowed):
    scores = jnp.where(allowed, dot_nt(q, k), MASKED)
    weights = jnp.exp(scores - jnp.max(scores, axis=1, keepdims=True))
    return weights / jnp.sum(weights, axis=1, keepdims=True)


def turn(values, cosine, sine_table):
    return values * cosine + pltpu.roll(values, HEAD_DIM // 2, 1) * sine_table


def attend_kernel(
    keep_ref, got_ref, cos_ref, sin_ref, mask_ref, out_w_ref,
    q_ref, k_ref, v_ref, o_ref, branch_ref, send_ref,
):
    rows, part = q_ref.shape
    half = rows // 2
    allowed = mask_ref[...] > 0.5
    cosine, sine_table = cos_ref[...], sin_ref[...]

    def full(cols):
        got = jnp.concatenate([got_ref[half:, cols], got_ref[:half, cols]], axis=0)
        return keep_ref[:, cols] + got.astype(F32)

    for h in range(part // HEAD_DIM):
        cols = slice(h * HEAD_DIM, (h + 1) * HEAD_DIM)
        q = full(slice(cols.start, cols.stop))
        k = full(slice(part + cols.start, part + cols.stop))
        v = full(slice(2 * part + cols.start, 2 * part + cols.stop)).astype(BF16)
        q = (turn(q, cosine, sine_table) * HEAD_DIM ** (-0.5)).astype(BF16)
        k = turn(k, cosine, sine_table).astype(BF16)
        q_ref[:, cols] = q
        k_ref[:, cols] = k
        v_ref[:, cols] = v
        o_ref[:, cols] = dot_nn(probabilities(q, k, allowed).astype(BF16), v).astype(BF16)
    send_ref[...] = dot_nn(o_ref[half:, :], out_w_ref[...]).astype(BF16)
    branch_ref[...] = dot_nn(o_ref[:half, :], out_w_ref[...])


def attend_back_kernel(
    branch_ref, their_ref, q_ref, k_ref, v_ref, o_ref, cos_ref, sin_ref, mask_ref, out_w_ref,
    grad_w_ref, mine_ref, row_buf, grad_buf,
):
    rows, part = q_ref.shape
    half = rows // 2
    allowed = mask_ref[...] > 0.5
    cosine, sine_table = cos_ref[...], -sin_ref[...]
    row_buf[:half, :] = branch_ref[...]
    row_buf[half:, :] = their_ref[...]
    grad_buf[...] = dot_nt(row_buf[...], out_w_ref[...]).astype(BF16)
    for h in range(part // HEAD_DIM):
        cols = slice(h * HEAD_DIM, (h + 1) * HEAD_DIM)
        q, k, v, grad = q_ref[:, cols], k_ref[:, cols], v_ref[:, cols], grad_buf[:, cols]
        probs = probabilities(q, k, allowed)
        grad_probs = dot_nt(grad, v)
        delta = jnp.sum(probs * grad_probs, axis=1, keepdims=True)
        grad_scores = (probs * (grad_probs - delta)).astype(BF16)
        grad_q = dot_nn(grad_scores, k) * HEAD_DIM ** (-0.5)
        mine_ref[0, :, cols] = turn(grad_q, cosine, sine_table).astype(BF16)
        mine_ref[1, :, cols] = turn(dot_tn(grad_scores, q), cosine, sine_table).astype(BF16)
        mine_ref[2, :, cols] = dot_tn(probs.astype(BF16), grad).astype(BF16)
    grad_w_ref[...] = dot_tn(o_ref[...], row_buf[...]).astype(BF16)


def dense_back_kernel(
    mine_ref, their_ref, n_ref, grad_w_ref, q_ref, k_ref, v_ref, dense_ref, part_ref, send_ref, buf
):
    core = lax.axis_index("narrow")
    rows, part = n_ref.shape
    half = rows // 2
    total = None
    for n, ref in enumerate((q_ref, k_ref, v_ref)):
        buf[n, :, half_lanes(core, part)] = mine_ref[n]
        buf[n, :half, half_lanes(1 - core, part)] = their_ref[n, half:, :]
        buf[n, half:, half_lanes(1 - core, part)] = their_ref[n, :half, :]
        term = dot_nt(buf[n], ref[...])
        total = term if total is None else total + term
        dense_ref[n] = dot_tn(n_ref[...], buf[n]).astype(BF16)
    dense_ref[3] = grad_w_ref[...]
    part_ref[...] = total[:half]
    send_ref[...] = total[half:].astype(BF16)


def widen_kernel(steps, x_ref, *refs):
    count = (len(refs) - 4) // 2
    step = pl.program_id(0)
    for n in range(count):
        refs[count + n][...] = refs[n][...]
    for n, ref in enumerate(refs[2 * count :]):

        @pl.when(step // steps == n)
        def _(ref=ref):
            ref[...] = x_ref[...].reshape(ref.shape).astype(F32)


def widen(gathered, passed):
    blocks, rows, width = gathered.shape
    each = 2 if blocks % 8 == 0 else 1
    grid, steps = blocks // each, blocks // each // 4
    shape = jax.ShapeDtypeStruct

    def spec(n):
        return pl.BlockSpec((each * rows, width), lambda i: (jnp.clip(i - steps * n, 0, steps - 1), 0))

    copied = [pl.BlockSpec((x.shape[0] // grid, width), lambda i: (i, 0)) for x in passed]
    return pl.pallas_call(
        functools.partial(widen_kernel, steps),
        grid=(grid,),
        out_shape=[shape(x.shape, x.dtype) for x in passed]
        + [shape((blocks // 4 * rows, width), F32)] * 4,
        in_specs=[pl.BlockSpec((each, rows, width), lambda i: (i, 0, 0))] + copied,
        out_specs=copied + [spec(n) for n in range(4)],
        compiler_params=pltpu.CompilerParams(vmem_limit_bytes=60 * 1024 * 1024),
    )(gathered, *passed)


def slots_path(
    tokens,
    cotangent,
    lengths,
    routes,
    keep,
    attn_gain,
    w_query,
    w_key,
    w_value,
    w_out,
    ffn_gain,
    w_router,
    shared_gate,
    shared_up,
    shared_down,
    expert_gate,
    expert_up,
    expert_down,
):
    narrow_size = lax.axis_size("narrow")
    narrow_index = lax.axis_index("narrow")
    wide_size = lax.axis_size("wide")
    local_rows = tokens.shape[0]
    model_width = tokens.shape[1]
    head_count = model_width // HEAD_DIM
    row_length = local_rows * narrow_size
    capacity = 8 * (3 * local_rows * TOPK // (16 * wide_size) + 1)
    gathered = (
        lax.all_gather(attn_gain, "narrow", axis=0, tiled=True),
        lax.all_gather(w_query, "narrow", axis=0, tiled=True),
        lax.all_gather(w_key, "narrow", axis=0, tiled=True),
        lax.all_gather(w_value, "narrow", axis=0, tiled=True),
        lax.all_gather(w_out, "narrow", axis=0, tiled=True),
        lax.all_gather(ffn_gain, "narrow", axis=0, tiled=True),
        lax.all_gather(w_router, "narrow", axis=0, tiled=True),
        lax.all_gather(shared_gate, "narrow", axis=0, tiled=True),
        lax.all_gather(shared_up, "narrow", axis=0, tiled=True),
        lax.all_gather(shared_down, "narrow", axis=0, tiled=True),
    )
    attn_scale = gathered[0].astype(jnp.float32)
    query_proj = gathered[1]
    key_proj = gathered[2]
    value_proj = gathered[3]
    output_proj = gathered[4]
    ffn_scale = gathered[5].astype(jnp.float32)
    router_proj = gathered[6]
    common_gate = gathered[7]
    common_upper = gathered[8]
    common_down = gathered[9]
    expert_mats = (expert_gate, expert_up, expert_down)
    routed_gate = expert_mats[0][0]
    routed_upper = expert_mats[1][0]
    routed_down = expert_mats[2][0]
    doc_lens = lengths[0]
    key_index = jnp.arange(row_length, dtype=jnp.int32)
    key_doc, unused = doc_layout(key_index, doc_lens)
    query_index = narrow_index * local_rows + jnp.arange(local_rows, dtype=jnp.int32)
    query_doc, query_pos = doc_layout(query_index, doc_lens)
    cosine, sine_table = rotary_angles(query_pos)
    inputs = tokens.astype(jnp.float32)
    normed, unit_one, scale_one = norm_forward(inputs, attn_scale)
    normed_one = normed.astype(jnp.bfloat16)
    head_shape = (local_rows, head_count, HEAD_DIM)
    query_rows = rotate(matmul(normed_one, query_proj).reshape(head_shape), cosine, sine_table)
    query_rows = (query_rows * HEAD_DIM ** (-0.5)).astype(jnp.bfloat16)
    key_rows = rotate(matmul(normed_one, key_proj).reshape(head_shape), cosine, sine_table).astype(
        jnp.bfloat16
    )
    valued = matmul(normed_one, value_proj).astype(jnp.bfloat16)
    all_keys, all_values = (
        lax.all_gather(key_rows.reshape(local_rows, model_width), "narrow", axis=0, tiled=True),
        lax.all_gather(valued, "narrow", axis=0, tiled=True),
    )
    all_keys = all_keys.reshape(row_length, head_count, HEAD_DIM)
    all_values = all_values.reshape(row_length, head_count, HEAD_DIM)
    block_rows = min(local_rows, 512)
    blocks = local_rows // block_rows
    query_blocks = query_rows.reshape(blocks, block_rows, head_count, HEAD_DIM)
    doc_blocks = query_doc.reshape(blocks, block_rows)
    index_blocks = query_index.reshape(blocks, block_rows)

    def allowed_for(doc_rows, index_rows):
        return (doc_rows[:, None] == key_doc[None, :]) & (key_index[None, :] <= index_rows[:, None])

    def forward_block(map_item):
        return attend_block(
            map_item[0], all_keys, all_values, allowed_for(map_item[1], map_item[2])
        )

    attended, logsum = lax.map(forward_block, (query_blocks, doc_blocks, index_blocks))
    attended = attended.reshape(local_rows, model_width)
    hidden = inputs + matmul(attended, output_proj)
    normed, unit_two, scale_two = norm_forward(hidden, ffn_scale)
    normed_two = normed.astype(jnp.bfloat16)
    logits = matmul(normed_two, router_proj)
    experts = router_proj.shape[1]
    pick_table = (routes[:, :, None] == jnp.arange(experts, dtype=jnp.int32)[None, None, :]).astype(
        jnp.float32
    )
    chosen = jnp.sum(pick_table * logits[:, None, :], axis=2)
    gate_probs = jax.nn.softmax(chosen, axis=1)
    keep_float = keep.astype(jnp.float32)
    mixing = gate_probs * keep_float
    common_gate_vals, common_upper_vals, common_act = expert_forward(
        normed_two, common_gate, common_upper
    )
    shared_out = matmul(common_act, common_down)
    pair_expert = routes.reshape(-1)
    pair_total = pair_expert.shape[0]
    onehot = (pair_expert[:, None] == jnp.arange(experts, dtype=jnp.int32)[None, :]).astype(
        jnp.int32
    )
    earlier = jnp.cumsum(onehot, axis=0) - onehot
    slot_place = jnp.sum(earlier * onehot, axis=1)
    slot_index = pair_expert * capacity + slot_place
    slot_total = experts * capacity
    source = (
        jnp.full((slot_total,), -1, jnp.int32)
        .at[slot_index]
        .set(jnp.arange(pair_total, dtype=jnp.int32))
    )
    filled = source >= 0
    pair_index = jnp.maximum(source, 0)

    def fill_slots(in_rows, row_index):
        taken = jnp.take(in_rows, row_index, axis=0)
        return jnp.where(filled[:, None], taken, jnp.zeros((), in_rows.dtype)).reshape(
            experts, capacity, model_width
        )

    received = lax.all_to_all(
        fill_slots(normed_two, pair_index // TOPK), "wide", split_axis=0, concat_axis=0, tiled=True
    )
    expert_in = lax.all_gather(received, "narrow", axis=0, tiled=True).reshape(-1, model_width)
    routed_gate_vals, routed_upper_vals, routed_act = expert_forward(
        expert_in, routed_gate, routed_upper
    )
    partial_value = matmul(routed_act, routed_down)
    expert_out = lax.psum_scatter(partial_value, "narrow", scatter_dimension=0, tiled=True)
    returned = lax.all_to_all(
        expert_out.astype(jnp.bfloat16).reshape(wide_size, capacity, model_width),
        "wide",
        split_axis=0,
        concat_axis=0,
        tiled=True,
    )
    pair_out = (
        jnp.take(returned.reshape(slot_total, model_width), slot_index, axis=0)
        .astype(jnp.float32)
        .reshape(local_rows, TOPK, model_width)
    )
    routed = jnp.sum(mixing[:, :, None] * pair_out, axis=1)
    output = (hidden + shared_out + routed).astype(jnp.bfloat16)
    grad_output = cotangent.astype(jnp.float32)
    grad_pairs = (
        (mixing[:, :, None] * grad_output[:, None, :])
        .astype(jnp.bfloat16)
        .reshape(pair_total, model_width)
    )
    grad_mixing = jnp.sum(pair_out * grad_output[:, None, :], axis=2)
    grad_received = lax.all_to_all(
        fill_slots(grad_pairs, pair_index), "wide", split_axis=0, concat_axis=0, tiled=True
    )
    grad_expert_out = lax.all_gather(grad_received, "narrow", axis=0, tiled=True).reshape(
        -1, model_width
    )
    grad_expert_in, grad_rgate, grad_rupper, grad_rdown = expert_backward(
        expert_in,
        grad_expert_out,
        routed_gate_vals,
        routed_upper_vals,
        routed_act,
        routed_gate,
        routed_upper,
        routed_down,
    )
    grad_slot_rows = lax.psum_scatter(grad_expert_in, "narrow", scatter_dimension=0, tiled=True)
    expert_grads = (grad_rgate, grad_rupper, grad_rdown)
    grad_back = lax.all_to_all(
        grad_slot_rows.astype(jnp.bfloat16).reshape(wide_size, capacity, model_width),
        "wide",
        split_axis=0,
        concat_axis=0,
        tiled=True,
    )
    grad_pair_rows = jnp.take(
        grad_back.reshape(slot_total, model_width), slot_index, axis=0
    ).astype(jnp.float32)
    grad_normed = jnp.sum(grad_pair_rows.reshape(local_rows, TOPK, model_width), axis=1)
    grad_gates = grad_mixing * keep_float
    grad_chosen = gate_probs * (
        grad_gates - jnp.sum(gate_probs * grad_gates, axis=1, keepdims=True)
    )
    grad_logits = jnp.sum(pick_table * grad_chosen[:, :, None], axis=1).astype(jnp.bfloat16)
    grad_router = matmul_left(normed_two, grad_logits)
    grad_normed = grad_normed + matmul_right(grad_logits, router_proj)
    grad_common_in, grad_cgate, grad_cupper, grad_cdown = expert_backward(
        normed_two,
        cotangent,
        common_gate_vals,
        common_upper_vals,
        common_act,
        common_gate,
        common_upper,
        common_down,
    )
    grad_normed = grad_normed + grad_common_in
    grad_hidden_norm, grad_ffn = norm_backward(grad_normed, unit_two, scale_two, ffn_scale)
    grad_hidden = grad_output + grad_hidden_norm
    grad_branch = grad_hidden.astype(jnp.bfloat16)
    grad_output_proj = matmul_left(attended, grad_branch)
    grad_attended = (
        matmul_right(grad_branch, output_proj)
        .astype(jnp.bfloat16)
        .reshape(blocks, block_rows, head_count, HEAD_DIM)
    )

    def backward_block(running, map_item):
        grad_queries, grad_keys, grad_values = attend_back(
            map_item[0],
            all_keys,
            all_values,
            allowed_for(map_item[1], map_item[2]),
            map_item[3],
            map_item[4],
        )
        return ((running[0] + grad_keys, running[1] + grad_values), grad_queries)

    empty_keys = jnp.zeros((row_length, head_count, HEAD_DIM), jnp.float32)
    sums_kv, grad_query_rows = lax.scan(
        backward_block,
        (empty_keys, empty_keys),
        (query_blocks, doc_blocks, index_blocks, logsum, grad_attended),
    )
    grad_key_own, grad_value_own = (
        lax.psum_scatter(
            sums_kv[0].reshape(row_length, model_width).astype(jnp.bfloat16),
            "narrow",
            scatter_dimension=0,
            tiled=True,
        ).astype(jnp.float32),
        lax.psum_scatter(
            sums_kv[1].reshape(row_length, model_width).astype(jnp.bfloat16),
            "narrow",
            scatter_dimension=0,
            tiled=True,
        ).astype(jnp.float32),
    )
    grad_query_rows = rotate(
        grad_query_rows.reshape(head_shape) * HEAD_DIM ** (-0.5), cosine, -sine_table
    )
    grad_query_rows = grad_query_rows.reshape(local_rows, model_width).astype(jnp.bfloat16)
    grad_key_rows = (
        rotate(grad_key_own.reshape(head_shape), cosine, -sine_table)
        .reshape(local_rows, model_width)
        .astype(jnp.bfloat16)
    )
    grad_value_rows = grad_value_own.astype(jnp.bfloat16)
    grad_query_proj = matmul_left(normed_one, grad_query_rows)
    grad_key_proj = matmul_left(normed_one, grad_key_rows)
    grad_value_proj = matmul_left(normed_one, grad_value_rows)
    grad_normed_one = (
        matmul_right(grad_query_rows, query_proj)
        + matmul_right(grad_key_rows, key_proj)
        + matmul_right(grad_value_rows, value_proj)
    )
    grad_input_norm, grad_attn = norm_backward(grad_normed_one, unit_one, scale_one, attn_scale)
    grad_tokens = grad_hidden + grad_input_norm
    halves = (
        lax.psum_scatter(
            grad_attn.astype(jnp.bfloat16), "narrow", scatter_dimension=0, tiled=True
        ).astype(jnp.float32),
        lax.psum_scatter(
            grad_query_proj.astype(jnp.bfloat16), "narrow", scatter_dimension=0, tiled=True
        ).astype(jnp.float32),
        lax.psum_scatter(
            grad_key_proj.astype(jnp.bfloat16), "narrow", scatter_dimension=0, tiled=True
        ).astype(jnp.float32),
        lax.psum_scatter(
            grad_value_proj.astype(jnp.bfloat16), "narrow", scatter_dimension=0, tiled=True
        ).astype(jnp.float32),
        lax.psum_scatter(
            grad_output_proj.astype(jnp.bfloat16), "narrow", scatter_dimension=0, tiled=True
        ).astype(jnp.float32),
        lax.psum_scatter(
            grad_ffn.astype(jnp.bfloat16), "narrow", scatter_dimension=0, tiled=True
        ).astype(jnp.float32),
        lax.psum_scatter(
            grad_router.astype(jnp.bfloat16), "narrow", scatter_dimension=0, tiled=True
        ).astype(jnp.float32),
        lax.psum_scatter(
            grad_cgate.astype(jnp.bfloat16), "narrow", scatter_dimension=0, tiled=True
        ).astype(jnp.float32),
        lax.psum_scatter(
            grad_cupper.astype(jnp.bfloat16), "narrow", scatter_dimension=0, tiled=True
        ).astype(jnp.float32),
        lax.psum_scatter(
            grad_cdown.astype(jnp.bfloat16), "narrow", scatter_dimension=0, tiled=True
        ).astype(jnp.float32),
    )
    owned = lax.psum(
        (
            halves[0],
            halves[1],
            halves[2],
            halves[3],
            halves[4],
            halves[5],
            halves[6],
            halves[7],
            halves[8],
            halves[9],
        ),
        "wide",
    )
    return (
        output,
        grad_tokens,
        owned[0],
        owned[1],
        owned[2],
        owned[3],
        owned[4],
        owned[5],
        owned[6],
        owned[7],
        owned[8],
        owned[9],
        expert_grads[0][None],
        expert_grads[1][None],
        expert_grads[2][None],
    )


def tokens_path(
    tokens,
    cotangent,
    lengths,
    routes,
    keep,
    attn_gain,
    w_query,
    w_key,
    w_value,
    w_out,
    ffn_gain,
    w_router,
    shared_gate,
    shared_up,
    shared_down,
    expert_gate,
    expert_up,
    expert_down,
):
    core = lax.axis_index("narrow")
    place = lax.axis_index("wide")
    wide_size = lax.axis_size("wide")
    levels = wide_size // 4
    local_rows, width = tokens.shape
    row_length = 2 * local_rows
    part = width // 2
    hidden_part = expert_gate.shape[2]
    stored = shared_gate.shape[1] // 2
    slice_width = -(-stored // (16 * wide_size)) * 16
    slices = stored // slice_width
    experts = w_router.shape[1]

    def swap(value):
        return lax.ppermute(value, "narrow", [(0, 1), (1, 0)])

    def in_order(mine, theirs, axis):
        return jnp.where(
            core == 0,
            jnp.concatenate([mine, theirs], axis=axis),
            jnp.concatenate([theirs, mine], axis=axis),
        )

    picks = (routes[:, :, None] == jnp.arange(experts, dtype=jnp.int32)[None, None, :]).astype(
        jnp.int32
    )
    marks = jnp.sum(picks * (1 + keep)[:, :, None], axis=1).astype(F32)

    first_unit = place * slice_width
    holds = place < slices

    def shared_slice(value, which, axis):
        begin = which * stored + first_unit
        taken = lax.dynamic_slice_in_dim(value, begin, slice_width, axis)
        return jnp.where(holds, taken, jnp.zeros((), value.dtype))

    gate_mine, up_mine = shared_slice(shared_gate, core, 1), shared_slice(shared_up, core, 1)
    gate_send, up_send = shared_slice(shared_gate, 1 - core, 1), shared_slice(shared_up, 1 - core, 1)
    down_slice = shared_slice(shared_down, 0, 0)
    gains = jnp.stack([attn_gain, ffn_gain])
    sent = swap(jnp.concatenate([gate_send.T, up_send.T, w_router.T], axis=0))
    gains = in_order(gains, swap(gains), 1).astype(F32)
    attn_scale, ffn_scale = gains[0], gains[1]
    dense = in_order(jnp.concatenate([gate_mine.T, up_mine.T, w_router.T], axis=0), sent, 1)
    router = dense[2 * slice_width :]

    inputs = tokens.astype(F32)
    square, wide_rows = (row_length, part), (local_rows, width)
    projections = [w_query, w_key, w_value]
    normed_one, qkv, sent = local_call(
        project_kernel,
        [(square, BF16), ((row_length, 3 * part), F32), ((row_length, 3 * part), BF16)],
        [((row_length, width), BF16)],
        tokens,
        swap(tokens),
        attn_scale[None, :],
        *projections,
    )
    index = jnp.arange(local_rows, dtype=jnp.int32)
    index = jnp.concatenate([core * local_rows + index, (1 - core) * local_rows + index])
    docs, positions = doc_layout(index, lengths[0])
    allowed = (docs[:, None] == docs[None, :]) & (index[None, :] <= index[:, None])
    cosine, sine_table = rotary_angles(positions)
    tables = [
        jnp.concatenate([cosine, cosine], axis=1),
        jnp.concatenate([-sine_table, sine_table], axis=1),
        allowed.astype(F32),
    ]
    *attention, branch, sent = local_call(
        attend_kernel,
        [(square, BF16)] * 4 + [(wide_rows, F32), (wide_rows, BF16)],
        [],
        qkv,
        swap(sent),
        *tables,
        w_out,
    )
    hidden = inputs + branch + swap(sent).astype(F32)
    normed, unit_two, scale_two = norm_forward(hidden, ffn_scale)
    normed_two = normed.astype(BF16)

    used = hidden_part + slice_width
    full = -(-(used + experts) // 128) * 128

    (_, _, _, grad_rows, expert_out, grad_mix, *expert_grads, shared_part) = experts_rows(
        normed_two,
        cotangent,
        marks.T,
        [expert_gate[0].T, expert_up[0].T, expert_down[0], dense, down_slice],
        hidden_part,
        used,
        full,
        levels,
        1,
    )
    grad_mix = lax.all_to_all(
        grad_mix.reshape(wide_size, 2, local_rows), "wide", split_axis=0, concat_axis=0, tiled=True
    )
    pick_core = jnp.where(core == 0, grad_mix[:, 0], grad_mix[:, 1])
    send_core = jnp.where(core == 0, grad_mix[:, 1], grad_mix[:, 0])
    grad_mix = (pick_core + swap(send_core)).T
    block_shape = (2 * wide_size, local_rows, width)
    grad_rows, expert_out, shared_all = exchange_wide(
        grad_rows.reshape(block_shape), expert_out.reshape(block_shape), shared_part, levels, 2
    )
    output = (hidden + expert_out.astype(F32)).astype(BF16)
    grad_shared_gate, grad_shared_up, grad_shared_down = shared_grads(
        shared_all, slices, part, stored
    )

    marks = marks.astype(F32)
    routed = marks > 0.0
    logits = matmul_right(normed_two, router)
    masked = jnp.where(routed, logits, MASKED)
    weights = jnp.where(routed, jnp.exp(masked - jnp.max(masked, axis=1, keepdims=True)), 0.0)
    gates = weights / jnp.sum(weights, axis=1, keepdims=True)
    grad_gates = jnp.where(marks > 1.5, grad_mix, 0.0)
    grad_logits = gates * (grad_gates - jnp.sum(gates * grad_gates, axis=1, keepdims=True))
    grad_logits = grad_logits.astype(BF16)
    grad_router = matmul_left(normed_two, grad_logits)
    grad_normed = grad_rows.astype(F32) + matmul(grad_logits, router)
    grad_hidden_norm, grad_ffn = norm_backward(grad_normed, unit_two, scale_two, ffn_scale)
    grad_hidden = cotangent.astype(F32) + grad_hidden_norm
    grad_branch = grad_hidden.astype(BF16)

    grad_w_out, mine = local_call(
        attend_back_kernel,
        [((part, width), BF16), ((3, *square), BF16)],
        [((row_length, width), BF16), (square, BF16)],
        grad_branch,
        swap(grad_branch),
        *attention,
        *tables,
        w_out,
    )
    grad_dense, grad_part, sent = local_call(
        dense_back_kernel,
        [((4, part, width), BF16), ((local_rows, part), F32), ((local_rows, part), BF16)],
        [((3, row_length, width), BF16)],
        mine,
        swap(mine),
        normed_one,
        grad_w_out,
        *projections,
    )
    grad_normed_one = in_order(grad_part, swap(sent).astype(F32), 1)
    _, unit_one, scale_one = norm_forward(inputs, attn_scale)
    grad_input_norm, grad_attn = norm_backward(grad_normed_one, unit_one, scale_one, attn_scale)
    grad_tokens = grad_hidden + grad_input_norm

    small = jnp.concatenate([grad_attn[:, None], grad_ffn[:, None], grad_router], axis=1)
    small_mine = lax.dynamic_slice_in_dim(small, core * part, part, 0)
    small_send = lax.dynamic_slice_in_dim(small, (1 - core) * part, part, 0)
    small = (small_mine + swap(small_send)).astype(BF16)
    size = small.size
    extra_rows = -(-size // (width * 16)) * 16
    flat = jnp.concatenate([small.reshape(-1), jnp.zeros((extra_rows * width - size,), BF16)])
    sum_rows = 4 * part // wide_size
    everything, flat = sum_dense(
        grad_dense.reshape(wide_size, sum_rows, width), flat.reshape(extra_rows, width), levels, 3
    )
    *expert_grads, grad_query, grad_key, grad_value, grad_out = widen(everything, expert_grads)
    grad_expert_gate, grad_expert_up, grad_expert_down = expert_grads
    flat = flat.astype(F32).reshape(wide_size, -1)
    small = jnp.sum(flat[:, :size], axis=0).reshape(part, 2 + experts)
    return (
        output,
        grad_tokens,
        small[:, 0],
        grad_query,
        grad_key,
        grad_value,
        grad_out,
        small[:, 1],
        small[:, 2:],
        grad_shared_gate,
        grad_shared_up,
        grad_shared_down,
        grad_expert_gate.T[None],
        grad_expert_up.T[None],
        grad_expert_down[None],
    )


def per_device(*arrays):
    tokens = arrays[0]
    gathered = lax.axis_size("wide") * lax.axis_size("narrow") * tokens.size * 2
    fits = gathered <= 12 * 1024 * 1024
    return (tokens_path if fits else slots_path)(*arrays)


def solution(mesh):
    in_specs = (
        P(("wide", "narrow"), None),
        P(("wide", "narrow"), None),
        P("wide", None),
        P(("wide", "narrow"), None),
        P(("wide", "narrow"), None),
        P("narrow"),
        P("narrow", None),
        P("narrow", None),
        P("narrow", None),
        P("narrow", None),
        P("narrow"),
        P("narrow", None),
        P("narrow", None),
        P("narrow", None),
        P("narrow", None),
        P("wide", None, "narrow"),
        P("wide", None, "narrow"),
        P("wide", "narrow", None),
    )
    out_specs = (
        P(("wide", "narrow"), None),
        P(("wide", "narrow"), None),
        P("narrow"),
        P("narrow", None),
        P("narrow", None),
        P("narrow", None),
        P("narrow", None),
        P("narrow"),
        P("narrow", None),
        P("narrow", None),
        P("narrow", None),
        P("narrow", None),
        P("wide", None, "narrow"),
        P("wide", None, "narrow"),
        P("wide", "narrow", None),
    )
    return jax.shard_map(
        per_device, mesh=mesh, in_specs=in_specs, out_specs=out_specs, check_vma=False
    )
```

```python
import functools
import math

import jax
import jax.numpy as jnp
from jax import lax
from jax.experimental import pallas as pl
from jax.experimental.pallas import tpu as pltpu
from jax.sharding import PartitionSpec as P

HEAD_DIM = 128
TOPK = 7


EPS = 1e-06
MASKED = -1e30


def matmul(left, right):
    return jnp.dot(left, right, preferred_element_type=jnp.float32)


def matmul_left(left, right):
    return lax.dot_general(
        left, right, (((0,), (0,)), ((), ())), preferred_element_type=jnp.float32
    )


def matmul_right(left, right):
    return lax.dot_general(
        left, right, (((1,), (1,)), ((), ())), preferred_element_type=jnp.float32
    )


def doc_layout(positions, doc_lens):
    doc_ends = jnp.cumsum(doc_lens)
    passed = (positions[:, None] >= doc_ends[None, :]).astype(jnp.int32)
    doc_ids = jnp.sum(passed, axis=1)
    return (doc_ids, positions - jnp.sum(passed * doc_lens[None, :], axis=1))


def rotary_angles(positions):
    half_dim = HEAD_DIM // 2
    inverse = jnp.exp(
        jnp.arange(half_dim, dtype=jnp.float32) * (-2.0 * math.log(10000.0) / HEAD_DIM)
    )
    angles = positions.astype(jnp.float32)[:, None] * inverse[None, :]
    return (jnp.cos(angles), jnp.sin(angles))


def rotate(values, cosine, sine_table):
    half_dim = values.shape[-1] // 2
    lower_half = values[..., :half_dim]
    upper_half = values[..., half_dim:]
    cos_b = cosine[:, None, :]
    sin_b = sine_table[:, None, :]
    return jnp.concatenate(
        [lower_half * cos_b - upper_half * sin_b, upper_half * cos_b + lower_half * sin_b], axis=-1
    )


def norm_forward(values, gain_vec):
    row_scale = lax.rsqrt(jnp.mean(values * values, axis=-1, keepdims=True) + EPS)
    unit_rows = values * row_scale
    return (unit_rows * gain_vec, unit_rows, row_scale)


def norm_backward(grad_rows, unit_rows, row_scale, gain_vec):
    scaled = grad_rows * gain_vec
    grad_gain = jnp.sum(grad_rows * unit_rows, axis=0)
    grad_input = row_scale * (
        scaled - unit_rows * jnp.mean(scaled * unit_rows, axis=-1, keepdims=True)
    )
    return (grad_input, grad_gain)


def silu_parts(gate_vals):
    sigmoid_vals = jax.nn.sigmoid(gate_vals)
    return (gate_vals * sigmoid_vals, sigmoid_vals * (1.0 + gate_vals * (1.0 - sigmoid_vals)))


def expert_forward(in_rows, gate_mat, upper_mat):
    gate_vals = matmul(in_rows, gate_mat)
    upper = matmul(in_rows, upper_mat)
    act_vals, unused = silu_parts(gate_vals)
    return (gate_vals, upper, (act_vals * upper).astype(jnp.bfloat16))


def expert_backward(in_rows, grad_rows, gate_vals, upper, active, gate_mat, upper_mat, down_mat):
    grad_act = matmul_right(grad_rows, down_mat)
    act_vals, slope_vals = silu_parts(gate_vals)
    grad_gate = (grad_act * upper * slope_vals).astype(jnp.bfloat16)
    grad_upper = (grad_act * act_vals).astype(jnp.bfloat16)
    grad_down_mat = matmul_left(active, grad_rows)
    grad_gate_mat = matmul_left(in_rows, grad_gate)
    grad_upper_mat = matmul_left(in_rows, grad_upper)
    grad_input = matmul_right(grad_gate, gate_mat) + matmul_right(grad_upper, upper_mat)
    return (grad_input, grad_gate_mat, grad_upper_mat, grad_down_mat)


def attend_block(queries, keys_all, values_all, allowed):
    scores = jnp.einsum("qhd,khd->hqk", queries, keys_all, preferred_element_type=jnp.float32)
    masked = jnp.where(allowed[None], scores, MASKED)
    row_max = jnp.max(masked, axis=-1, keepdims=True)
    weights = jnp.exp(masked - row_max)
    row_total = jnp.sum(weights, axis=-1, keepdims=True)
    prob_rows = (weights / row_total).astype(jnp.bfloat16)
    attended = jnp.einsum("hqk,khd->qhd", prob_rows, values_all, preferred_element_type=jnp.float32)
    return (attended.astype(jnp.bfloat16), (row_max + jnp.log(row_total))[..., 0])


def attend_back(queries, keys_all, values_all, allowed, logsum, grad_attended):
    scores = jnp.einsum("qhd,khd->hqk", queries, keys_all, preferred_element_type=jnp.float32)
    masked = jnp.where(allowed[None], scores, MASKED)
    prob_rows = jnp.exp(masked - logsum[..., None])
    grad_probs = jnp.einsum(
        "qhd,khd->hqk", grad_attended, values_all, preferred_element_type=jnp.float32
    )
    row_delta = jnp.sum(prob_rows * grad_probs, axis=-1, keepdims=True)
    grad_scores = (prob_rows * (grad_probs - row_delta)).astype(jnp.bfloat16)
    grad_queries = jnp.einsum(
        "hqk,khd->qhd", grad_scores, keys_all, preferred_element_type=jnp.float32
    )
    grad_keys = jnp.einsum("hqk,qhd->khd", grad_scores, queries, preferred_element_type=jnp.float32)
    grad_values = jnp.einsum(
        "hqk,qhd->khd",
        prob_rows.astype(jnp.bfloat16),
        grad_attended,
        preferred_element_type=jnp.float32,
    )
    return (grad_queries, grad_keys, grad_values)


MESH_ID = pl.DeviceIdType.MESH
BF16 = jnp.bfloat16
F32 = jnp.float32


class Place:
    def __init__(self, levels):
        self.levels = levels
        wide = lax.axis_index("wide")
        self.core = lax.axis_index("narrow")
        self.level = wide // 4
        self.spot = lax.rem(wide, 4)
        self.across = self.spot + 1 - 2 * lax.rem(self.spot, 2)
        self.along = lax.rem(self.spot + 2, 4)
        self.corner = 3 - self.spot
        self.has_up = self.level < levels - 1
        self.has_down = self.level > 0

    def choose(self, values):
        result = jnp.int32(values[0])
        for k in range(1, self.levels):
            result = jnp.where(self.level == k, values[k], result)
        return result

    def device(self, level, spot, core=None):
        return {"wide": level * 4 + spot, "narrow": self.core if core is None else core}

    def enter(self, sibling):
        barrier = pltpu.get_barrier_semaphore()

        def greet(device):
            pl.semaphore_signal(barrier, inc=1, device_id=device, device_id_type=MESH_ID)

        greet(self.device(self.level, self.across))
        greet(self.device(self.level, self.along))
        if sibling:
            greet(self.device(self.level, self.spot, 1 - self.core))

        @pl.when(self.has_up)
        def _():
            greet(self.device(self.level + 1, self.spot))

        @pl.when(self.has_down)
        def _():
            greet(self.device(self.level - 1, self.spot))

        both = jnp.where(self.has_up, 1, 0) + jnp.where(self.has_down, 1, 0)
        pl.semaphore_wait(barrier, both + (3 if sibling else 2))


def remote(src, dst, send, recv, device):
    return pltpu.make_async_remote_copy(
        src_ref=src,
        dst_ref=dst,
        send_sem=send,
        recv_sem=recv,
        device_id=device,
        device_id_type=MESH_ID,
    )


class Gather:
    NAMES = ("up", "dn", "x", "y", "cx", "cy", "rz", "rx", "ry", "rcx", "rcy")

    def __init__(self, at, sibling, pairs, sems, keeps_own=True):
        self.at, self.sibling, self.pairs, self.keeps_own = at, sibling, pairs, keeps_own
        self.own_sem = sems[0]
        self.sems = dict(zip(self.NAMES, sems[1:12]))
        self.send_n, self.recv_n = sems[12:]
        self.order = self.visits()

    @staticmethod
    def scratch(levels, arrays):
        dma = pltpu.SemaphoreType.DMA
        return (
            [dma((arrays,))]
            + [dma((arrays, levels))] * 11
            + [dma((arrays, levels * 4))] * 2
        )

    def visits(self):
        at = self.at
        table = [
            sorted(range(at.levels), key=lambda lev: (abs(lev - here), lev))
            for here in range(at.levels)
        ]
        return [at.choose([row[k] for row in table]) for k in range(at.levels)]

    def block(self, n, lev, sp, core=None):
        x_ref, ref = self.pairs[n][:2]
        if self.sibling:
            return ref.at[(lev * 4 + sp) * 2 + (self.at.core if core is None else core)]
        if len(self.pairs[n]) == 3:
            return ref.at[lev * 4 + sp].at[pl.ds(self.pairs[n][2], x_ref.shape[0])]
        return ref.at[lev * 4 + sp]

    def each(self, send, recv, lev, sp, device, part=None, own=False):
        copies = []
        for n, (x_ref, *_) in enumerate(self.pairs):
            dst = self.block(n, lev, sp)
            src = x_ref if own else dst
            if part is not None:
                half = x_ref.shape[0] // 2
                src = src.at[pl.ds(part * half, half)]
                dst = dst.at[pl.ds(part * half, half)]
            copies.append(
                remote(src, dst, self.sems[send].at[n, lev], self.sems[recv].at[n, lev], device)
            )
        return copies

    def up(self, lev, own=False):
        at = self.at
        return self.each("up", "rz", lev, at.spot, at.device(at.level + 1, at.spot), own=own)

    def down(self, lev, own=False):
        at = self.at
        return self.each("dn", "rz", lev, at.spot, at.device(at.level - 1, at.spot), own=own)

    def over_x(self, lev, sp, own=False):
        at = self.at
        return self.each("x", "rx", lev, sp, at.device(at.level, at.across), own=own)

    def over_y(self, lev, sp, own=False):
        at = self.at
        return self.each("y", "ry", lev, sp, at.device(at.level, at.along), own=own)

    def corner_y(self, lev, sp):
        at = self.at
        return self.each("cy", "rcy", lev, sp, at.device(at.level, at.along), part=0)

    def corner_x(self, lev, sp):
        at = self.at
        return self.each("cx", "rcx", lev, sp, at.device(at.level, at.across), part=1)

    def near(self, lev, sp, core=None, own=False):
        at = self.at
        copies = []
        for n, (x_ref, *_) in enumerate(self.pairs):
            dst = self.block(n, lev, sp, core)
            sems = self.send_n.at[n, lev * 4 + sp], self.recv_n.at[n, lev * 4 + sp]
            device = at.device(at.level, at.spot, 1 - at.core)
            copies.append(remote(x_ref if own else dst, dst, *sems, device))
        return copies

    def own_copies(self):
        at = self.at
        return [
            pltpu.make_async_copy(x_ref, self.block(n, at.level, at.spot), self.own_sem.at[n])
            for n, (x_ref, *_) in enumerate(self.pairs)
        ]

    def take_own(self):
        for copy in self.own_copies():
            copy.wait()

    def begin(self):
        at = self.at
        pl.when(at.has_up)(lambda: start(self.up(at.level, own=True)))
        pl.when(at.has_down)(lambda: start(self.down(at.level, own=True)))
        start(self.over_x(at.level, at.spot, own=True))
        start(self.over_y(at.level, at.spot, own=True))
        if self.sibling:
            start(self.near(at.level, at.spot, own=True))
        if self.keeps_own:
            start(self.own_copies())

    def take_column(self, lev):
        at = self.at
        arrived(self.up(lev))
        pl.when((lev < at.level) & at.has_up)(lambda: start(self.up(lev)))
        pl.when((lev > at.level) & at.has_down)(lambda: start(self.down(lev)))
        start(self.over_x(lev, at.spot))
        start(self.over_y(lev, at.spot))
        if self.sibling:
            start(self.near(lev, at.spot))

    def take_x(self, lev):
        at = self.at
        arrived(self.over_x(lev, at.across))
        start(self.corner_y(lev, at.across))
        if self.sibling:
            start(self.near(lev, at.across))

    def take_y(self, lev):
        at = self.at
        arrived(self.over_y(lev, at.along))
        start(self.corner_x(lev, at.along))
        if self.sibling:
            start(self.near(lev, at.along))

    def take_corner(self, lev):
        at = self.at
        arrived(self.corner_y(lev, at.corner))
        arrived(self.corner_x(lev, at.corner))
        if self.sibling:
            start(self.near(lev, at.corner))

    def take_near(self, lev, sp):
        arrived(self.near(lev, sp, 1 - self.at.core))

    def steps(self):
        levels, steps = self.at.levels, []
        for s in range(1, levels + 2):
            if s < levels:
                steps.append(lambda lev=self.order[s]: self.take_column(lev))
            if s - 1 < levels:
                steps.append(lambda lev=self.order[s - 1]: self.take_x(lev))
                steps.append(lambda lev=self.order[s - 1]: self.take_y(lev))
            if s >= 2:
                steps.append(lambda lev=self.order[s - 2]: self.take_corner(lev))
        return steps

    def finish(self, near=True):
        at = self.at
        if near:
            self.take_own()
        for lev in range(at.levels):
            pl.when(at.has_up & (lev <= at.level))(lambda lev=lev: sent(self.up(lev)))
            pl.when(at.has_down & (lev >= at.level))(lambda lev=lev: sent(self.down(lev)))
            sent(self.over_x(lev, at.spot))
            sent(self.over_y(lev, at.spot))
            sent(self.corner_y(lev, at.across))
            sent(self.corner_x(lev, at.along))
            if self.sibling:
                for sp in range(4):
                    sent(self.near(lev, sp))
                    if near:
                        self.take_near(lev, sp)


def start(copies):
    for copy in copies:
        copy.start()


def arrived(copies):
    for copy in copies:
        copy.wait_recv()


def sent(copies):
    for copy in copies:
        copy.wait_send()


def dot_nn(left, right):
    return lax.dot_general(left, right, (((1,), (0,)), ((), ())), preferred_element_type=F32)


def dot_tn(left, right):
    return lax.dot_general(left, right, (((0,), (0,)), ((), ())), preferred_element_type=F32)


def dot_nt(left, right):
    return lax.dot_general(left, right, (((1,), (1,)), ((), ())), preferred_element_type=F32)


def experts_kernel(
    levels, sizes, x_ref, g_ref, m_ref, eg_ref, eu_ref, ed_ref, small_ref, sd_ref,
    rows_ref, grads_ref, marks_ref, back_ref, out_ref, gm_ref, dgate_ref, dup_ref, ddown_ref, shared_ref,
    x_buf, g_buf, mark_buf, cu_buf, g_val, mixed_buf, act_buf, back_buf, out_buf, gm_buf, mark_t,
    in_sem, out_sem, gm_val, gw_ref, gd_ref, gate_ref, down_ref, w_sem, *sems,
):
    hidden, used, full = sizes
    at = Place(levels)
    at.enter(True)
    gather = Gather(at, True, [(x_ref, rows_ref), (g_ref, grads_ref), (m_ref, marks_ref)], sems, False)
    gather.begin()
    size, experts = used - hidden, m_ref.shape[0]
    pieces = [
        (eg_ref, gate_ref, 0, hidden),
        (eu_ref, gate_ref, full, hidden),
        (small_ref.at[pl.ds(0, size)], gate_ref, hidden, size),
        (small_ref.at[pl.ds(size, size)], gate_ref, full + hidden, size),
        (small_ref.at[pl.ds(2 * size, experts)], gate_ref, used, experts),
        (ed_ref, down_ref, 0, hidden),
        (sd_ref, down_ref, hidden, size),
    ]
    weights = [
        pltpu.make_async_copy(src, dst.at[pl.ds(row, count)], w_sem.at[n])
        for n, (src, dst, row, count) in enumerate(pieces)
    ]
    start(weights)
    for ref, row, end in ((gate_ref, used + experts, full), (gate_ref, full + used, 2 * full), (down_ref, used, full)):
        if end > row:
            ref[row:end, :] = jnp.zeros((end - row, ref.shape[1]), BF16)
    place = at.level * 4 + at.spot
    units, ahead = 4 * levels, 3
    plan = [(0, 0)]
    for s in range(1, levels + 2):
        if s < levels:
            plan.append((s, 0))
        if s - 1 < levels:
            plan += [(s - 1, 1), (s - 1, 2)]
        if s >= 2:
            plan.append((s - 2, 3))
    rows = x_ref.shape[0]
    batch = 2 * rows

    def pick(k, values):
        result = jnp.int32(0) + values[0]
        for j in range(1, len(values)):
            result = jnp.where(k == j, values[j], result)
        return result

    def unit(k):
        visit = pick(k, [v for v, _ in plan])
        kind = pick(k, [t for _, t in plan])
        lev = pick(visit, gather.order)
        sp = pick(kind, [at.spot, at.across, at.along, at.corner])
        return lev, sp, kind

    def loads(k, first):
        slot = lax.rem(k, 4)
        blocks = pl.ds(first, 2)
        return [
            pltpu.make_async_copy(rows_ref.at[blocks], x_buf.at[slot], in_sem.at[slot, 0]),
            pltpu.make_async_copy(grads_ref.at[blocks], g_buf.at[slot], in_sem.at[slot, 1]),
            pltpu.make_async_copy(marks_ref.at[blocks], mark_buf.at[slot], in_sem.at[slot, 2]),
        ]

    def stores(k, first):
        slot = lax.rem(k, 2)
        rng = pl.ds(pl.multiple_of(first * rows, batch), batch)
        pairs = [(back_buf, back_ref), (out_buf, out_ref)]
        return [
            pltpu.make_async_copy(buf.at[slot], ref.at[rng], out_sem.at[slot, n])
            for n, (buf, ref) in enumerate(pairs)
        ]

    def serve(k):
        lev, sp, kind = unit(k)
        pl.when(kind == 0)(lambda: gather.take_column(lev))
        pl.when(kind == 1)(lambda: gather.take_x(lev))
        pl.when(kind == 2)(lambda: gather.take_y(lev))
        pl.when(kind == 3)(lambda: gather.take_corner(lev))

    def fetch(k):
        lev, sp, _ = unit(k)
        gather.take_near(lev, sp)
        start(loads(k, (lev * 4 + sp) * 2))

    def fetch_own():
        gather.take_near(at.level, at.spot)
        theirs = 1 - at.core
        triples = [(x_ref, rows_ref, x_buf), (g_ref, grads_ref, g_buf), (m_ref, marks_ref, mark_buf)]
        for n, (own, gathered, buf) in enumerate(triples):
            sem = in_sem.at[0, n]
            other = gathered.at[place * 2 + theirs]
            pltpu.make_async_copy(own, buf.at[0, at.core], sem).start()
            pltpu.make_async_copy(other, buf.at[0, theirs], sem).start()

    def lanes(n):
        return lax.broadcasted_iota(jnp.int32, (batch, 128), 1) + n * 128

    def mixing():
        tail = full // 128 - 1
        mark = mark_t[...]
        masked = jnp.where(mark > 0.5, cu_buf[:, full - 128 : full], MASKED)
        top = jnp.max(masked, axis=1, keepdims=True)
        weight = jnp.where(mark > 0.5, jnp.exp(masked - top), 0.0)
        mine = jnp.where((lanes(tail) == used + place) & (mark > 1.5), weight, 0.0)
        return jnp.sum(mine, axis=1, keepdims=True) / jnp.sum(weight, axis=1, keepdims=True)

    def elementwise(odd):
        mix = jnp.broadcast_to(mixing(), (batch, 128))
        total = jnp.zeros((batch, 128), F32)
        for n in range(full // 128):
            cols = slice(n * 128, (n + 1) * 128)
            up_cols = slice(full + n * 128, full + (n + 1) * 128)
            gate, upper, back = cu_buf[:, cols], cu_buf[:, up_cols], g_val[:, cols]
            whole = (n + 1) * 128 <= hidden
            scale = mix
            if not whole:
                scale = jnp.where(lanes(n) < hidden, mix, jnp.where(lanes(n) < used, 1.0, 0.0))
            sig = jax.nn.sigmoid(gate)
            act = gate * sig
            active = act * upper
            grad_act = scale * back
            slope = sig * (1.0 + gate * (1.0 - sig))
            mixed_buf[odd, :, cols] = (scale * active).astype(BF16)
            act_buf[odd, :, cols] = (grad_act * upper * slope).astype(BF16)
            act_buf[odd, :, up_cols] = (grad_act * act).astype(BF16)
            term = active * back
            total = total + (term if whole else jnp.where(lanes(n) < hidden, term, 0.0))
        gm_buf[...] = total

    def forward(k):
        lev, sp, _ = unit(k)
        first = (lev * 4 + sp) * 2
        slot = lax.rem(k, 4)
        for copy in loads(k, first):
            copy.wait()
        x = x_buf[slot].reshape(batch, -1)
        cu_buf[...] = dot_nt(x, gate_ref[...])
        g_val[...] = dot_nt(g_buf[slot].reshape(batch, -1), down_ref[...])
        for n in range(2):
            marks = mark_buf[slot, n]
            above = jnp.zeros((used - (full - 128), 128), F32)
            below = jnp.zeros((full - used - marks.shape[0], 128), F32)
            mark_t[pl.ds(n * rows, rows), :] = jnp.transpose(jnp.concatenate([above, marks, below], axis=0))
        elementwise(lax.rem(k, 2))

    def backward(k):
        lev, sp, _ = unit(k)
        first = (lev * 4 + sp) * 2
        slot = lax.rem(k, 2)

        @pl.when(k >= 2)
        def _():
            for copy in stores(k, 0):
                copy.wait()

        back_buf[slot] = dot_nn(act_buf[slot], gate_ref[...]).astype(BF16)
        out_buf[slot] = dot_nn(mixed_buf[slot], down_ref[...]).astype(BF16)
        for n in range(2):
            gm = jnp.transpose(gm_buf[pl.ds(n * rows, rows), :])
            gm_val[pl.ds(first + n, 1), :] = jnp.sum(gm, axis=0, keepdims=True)
        start(stores(k, first))

        both = pl.ds(lax.rem(k, 4) - 1, 2)

        def gate_grad(m, carry):
            part = pl.ds(pl.multiple_of(m * 256, 256), 256)
            left = act_buf[:, :, part].reshape(2 * batch, 256)
            gw_ref[part, :] += dot_tn(left, x_buf[both].reshape(2 * batch, -1))
            return carry

        def down_grad(m, carry):
            part = pl.ds(pl.multiple_of(m * 256, 256), 256)
            left = mixed_buf[:, :, part].reshape(2 * batch, 256)
            gd_ref[part, :] += dot_tn(left, g_buf[both].reshape(2 * batch, -1))
            return carry

        @pl.when(slot == 1)
        def _():
            lax.fori_loop(0, gw_ref.shape[0] // 256, gate_grad, 0)
            lax.fori_loop(0, full // 256, down_grad, 0)

    gw_ref[...] = jnp.zeros_like(gw_ref)
    gd_ref[...] = jnp.zeros_like(gd_ref)
    fetch_own()
    for copy in weights:
        copy.wait()

    def loop(k, carry):
        pl.when((k > 0) & (k + 1 < units))(lambda: fetch(k + 1))
        forward(k)

        @pl.when(k == 0)
        def _():
            for n in range(1, ahead + 1):
                serve(n)
            fetch(1)

        pl.when((k > 0) & (k + ahead < units))(lambda: serve(k + ahead))
        backward(k)
        return carry

    lax.fori_loop(0, units, loop, 0)
    gm_ref[...] = gm_val[...]
    finals = [
        pltpu.make_async_copy(src.at[pl.ds(row, hidden)], dst, w_sem.at[n])
        for n, (src, row, dst) in enumerate(
            ((gw_ref, 0, dgate_ref), (gw_ref, full, dup_ref), (gd_ref, 0, ddown_ref))
        )
    ]
    start(finals)
    for n, (ref, row) in enumerate(((gw_ref, hidden), (gw_ref, full + hidden), (gd_ref, hidden))):
        shared_ref[n * size : (n + 1) * size, :] = ref[row : row + size, :].astype(BF16)
    for copy in finals:
        copy.wait()
    for k in (0, 1):
        for copy in stores(k, 0):
            copy.wait()
    gather.finish(near=False)


def experts_rows(x, grads, marks, weights, hidden, used, full, levels, collective_id):
    rows, width = x.shape
    blocks = 8 * levels
    total = blocks * rows
    dma = pltpu.SemaphoreType.DMA
    vmem = pltpu.VMEM
    anywhere = pl.BlockSpec(memory_space=pl.ANY)
    inside = pl.BlockSpec(memory_space=vmem)
    shape = jax.ShapeDtypeStruct
    batch = 2 * rows
    return pl.pallas_call(
        functools.partial(experts_kernel, levels, (hidden, used, full)),
        out_shape=[
            shape((blocks, rows, width), BF16),
            shape((blocks, rows, width), BF16),
            shape((blocks, *marks.shape), F32),
            shape((total, width), BF16),
            shape((total, width), BF16),
            shape((blocks, rows), F32),
            shape((hidden, width), F32),
            shape((hidden, width), F32),
            shape((hidden, width), F32),
            shape((3 * (used - hidden), width), BF16),
        ],
        in_specs=[anywhere] * 8,
        out_specs=[anywhere] * 5 + [inside] + [anywhere] * 3 + [inside],
        scratch_shapes=[
            vmem((4, 2, rows, width), BF16),
            vmem((4, 2, rows, width), BF16),
            vmem((4, 2, *marks.shape), F32),
            vmem((batch, 2 * full), F32),
            vmem((batch, full), F32),
            vmem((2, batch, full), BF16),
            vmem((2, batch, 2 * full), BF16),
            vmem((2, batch, width), BF16),
            vmem((2, batch, width), BF16),
            vmem((batch, 128), F32),
            vmem((batch, 128), F32),
            dma((4, 3)),
            dma((2, 2)),
            vmem((blocks, rows), F32),
            vmem((2 * full, width), F32),
            vmem((full, width), F32),
            vmem((2 * full, width), BF16),
            vmem((full, width), BF16),
            dma((7,)),
        ]
        + Gather.scratch(levels, 3),
        compiler_params=pltpu.CompilerParams(
            collective_id=collective_id,
            has_side_effects=True,
            vmem_limit_bytes=56 * 1024 * 1024,
        ),
    )(x, grads, marks, *weights)


def shared_kernel(slices, x_ref, gate_ref, up_ref, down_ref, gate_buf, up_buf, down_buf, sem):
    part, units = gate_ref.shape
    stored = units // 2
    size = stored // slices
    copies = []
    for n in range(slices):
        for c in range(2):
            rows = pl.ds(c * stored + n * size, size)
            src = x_ref.at[n, pl.ds(c * size, size)]
            for buf, lanes in ((gate_buf, pl.ds(0, part)), (up_buf, pl.ds(part, part))):
                copies.append(pltpu.make_async_copy(src.at[:, lanes], buf.at[rows], sem.at[len(copies)]))
        src, dst = x_ref.at[n, pl.ds(2 * size, size)], down_buf.at[pl.ds(n * size, size)]
        copies.append(pltpu.make_async_copy(src, dst, sem.at[len(copies)]))
    start(copies)
    for copy in copies:
        copy.wait()
    down_ref[...] = down_buf[...].astype(F32)
    for buf, ref in ((gate_buf, gate_ref), (up_buf, up_ref)):
        for n in range(units // 128):
            rows = pl.ds(n * 128, 128)
            ref[:, rows] = jnp.transpose(buf[rows, :].astype(F32))


def shared_grads(gathered, slices, part, stored):
    width = gathered.shape[2]
    vmem = pltpu.VMEM
    inside = pl.BlockSpec(memory_space=vmem)
    shape = jax.ShapeDtypeStruct
    return pl.pallas_call(
        functools.partial(shared_kernel, slices),
        out_shape=[
            shape((part, 2 * stored), F32),
            shape((part, 2 * stored), F32),
            shape((stored, width), F32),
        ],
        in_specs=[pl.BlockSpec(memory_space=pl.ANY)],
        out_specs=[inside] * 3,
        scratch_shapes=[
            vmem((2 * stored, part), BF16),
            vmem((2 * stored, part), BF16),
            vmem((stored, width), BF16),
            pltpu.SemaphoreType.DMA((5 * slices,)),
        ],
        compiler_params=pltpu.CompilerParams(vmem_limit_bytes=60 * 1024 * 1024),
    )(gathered)


def destinations(levels):
    return [
        sorted(range(levels), key=lambda to: (-abs(to - here), -to)) for here in range(levels)
    ]


def add_rows(write, sources, rows):
    step = 16

    def body(k, carry):
        r = pl.ds(pl.multiple_of(k * step, step), step)
        total = sources[0](r)
        for source in sources[1:]:
            total = total + source(r)
        write(r, total)
        return carry

    lax.fori_loop(0, rows // step, body, 0)


def reads(ref):
    return lambda r: ref[r, :].astype(F32)


def writes(ref):
    def write(r, total):
        ref[r, :] = total.astype(ref.dtype)

    return write


class Scatter:
    def __init__(self, at, sibling, x_ref, out_ref, refs, row=None):
        self.at, self.sibling, self.x_ref, self.out_ref = at, sibling, x_ref, out_ref
        self.row = row
        self.acc, self.near, self.hx, self.hy, self.fx, self.fy = refs[:6]
        self.out_buf, self.za, self.zb = refs[6:9]
        self.own_sem, self.send_n, self.recv_n = refs[9:12]
        self.send = dict(zip(("hx", "hy", "fx", "fy", "up", "dn"), refs[12:18]))
        self.recv = dict(zip(("hx", "hy", "fx", "fy", "za", "zb"), refs[18:24]))
        self.rows = out_ref.shape[0]
        table = destinations(at.levels)
        self.order = [at.choose([row[s] for row in table]) for s in range(at.levels)]

    SCRATCH = 24

    @staticmethod
    def scratch(levels, sibling, rows, width):
        dma, vmem = pltpu.SemaphoreType.DMA, pltpu.VMEM
        blocks = levels * 4
        return (
            [
                vmem((blocks, rows, width), BF16),
                vmem((blocks if sibling else 1, rows, width), BF16),
                vmem((levels, rows // 2, width), BF16),
                vmem((levels, rows // 2, width), BF16),
            ]
            + [vmem((levels, rows, width), BF16)] * 5
            + [dma((blocks,))] * 3
            + [dma((levels,))] * 12
        )

    def own(self, lev, sp):
        b = lev * 4 + sp
        src = self.x_ref.at[b * 2 + self.at.core if self.sibling else b]
        if self.row is not None:
            src = src.at[pl.ds(self.row, self.rows)]
        return pltpu.make_async_copy(src, self.acc.at[b], self.own_sem.at[b])

    def to_sibling(self, lev, sp):
        at, b = self.at, lev * 4 + sp
        sems = self.send_n.at[b], self.recv_n.at[b]
        src = self.x_ref.at[b * 2 + 1 - at.core]
        return remote(src, self.near.at[b], *sems, at.device(at.level, at.spot, 1 - at.core))

    def side(self, name, src, dst, lev, spot):
        sems = self.send[name].at[lev], self.recv[name].at[lev]
        return remote(src, dst, *sems, self.at.device(self.at.level, spot))

    def half_y(self, lev):
        src = self.acc.at[lev * 4 + self.at.corner].at[pl.ds(0, self.rows // 2)]
        return self.side("hy", src, self.hy.at[lev], lev, self.at.along)

    def half_x(self, lev):
        src = self.acc.at[lev * 4 + self.at.corner].at[pl.ds(self.rows // 2, self.rows // 2)]
        return self.side("hx", src, self.hx.at[lev], lev, self.at.across)

    def full_x(self, lev):
        return self.side("fx", self.acc.at[lev * 4 + self.at.across], self.fx.at[lev], lev, self.at.across)

    def full_y(self, lev):
        return self.side("fy", self.acc.at[lev * 4 + self.at.along], self.fy.at[lev], lev, self.at.along)

    def go_up(self, lev):
        sems = self.send["up"].at[lev], self.recv["zb"].at[lev]
        device = self.at.device(self.at.level + 1, self.at.spot)
        return remote(self.out_buf.at[lev], self.zb.at[lev], *sems, device)

    def go_down(self, lev):
        sems = self.send["dn"].at[lev], self.recv["za"].at[lev]
        device = self.at.device(self.at.level - 1, self.at.spot)
        return remote(self.out_buf.at[lev], self.za.at[lev], *sems, device)

    def spots(self):
        return self.at.corner, self.at.across, self.at.along, self.at.spot

    def begin(self):
        for lev in self.order:
            for sp in self.spots():
                if self.sibling:
                    self.to_sibling(lev, sp).start()
                self.own(lev, sp).start()

    def local(self, lev):
        for n, sp in enumerate(self.spots()):
            ref = self.acc.at[lev * 4 + sp]
            self.own(lev, sp).wait()
            if self.sibling:
                self.to_sibling(lev, sp).wait_recv()
                add_rows(writes(ref), [reads(ref), reads(self.near.at[lev * 4 + sp])], self.rows)
            if n == 0:
                self.half_y(lev).start()
                self.half_x(lev).start()

    def halves(self, lev):
        half = self.rows // 2
        self.half_y(lev).wait_recv()
        ref = self.acc.at[lev * 4 + self.at.across].at[pl.ds(0, half)]
        add_rows(writes(ref), [reads(ref), reads(self.hy.at[lev])], half)
        self.full_x(lev).start()
        self.half_x(lev).wait_recv()
        ref = self.acc.at[lev * 4 + self.at.along].at[pl.ds(half, half)]
        add_rows(writes(ref), [reads(ref), reads(self.hx.at[lev])], half)
        self.full_y(lev).start()

    def column(self, lev):
        at, rows, level = self.at, self.rows, self.at.level
        self.full_x(lev).wait_recv()
        self.full_y(lev).wait_recv()
        own = [reads(self.acc.at[lev * 4 + at.spot]), reads(self.fx.at[lev]), reads(self.fy.at[lev])]
        above, below = reads(self.za.at[lev]), reads(self.zb.at[lev])
        passed = writes(self.out_buf.at[lev])
        final = writes(self.out_ref)

        def send(has, arrival, term, departure):
            @pl.when(has)
            def _():
                arrival(lev).wait_recv()
                add_rows(passed, [*own, term], rows)

            pl.when(jnp.logical_not(has))(lambda: add_rows(passed, own, rows))
            departure(lev).start()

        pl.when(lev < level)(lambda: send(at.has_up, self.go_down, above, self.go_down))
        pl.when(lev > level)(lambda: send(at.has_down, self.go_up, below, self.go_up))

        @pl.when(lev == level)
        def _():
            pl.when(at.has_up)(lambda: self.go_down(lev).wait_recv())
            pl.when(at.has_down)(lambda: self.go_up(lev).wait_recv())
            both = at.has_up & at.has_down
            pl.when(both)(lambda: add_rows(final, [*own, above, below], rows))
            pl.when(jnp.logical_not(at.has_down))(lambda: add_rows(final, [*own, above], rows))
            pl.when(jnp.logical_not(at.has_up))(lambda: add_rows(final, [*own, below], rows))

    def steps(self):
        levels, steps = self.at.levels, []
        for s in range(levels + 2):
            if s < levels:
                steps.append(lambda lev=self.order[s]: self.local(lev))
            if 0 <= s - 1 < levels:
                steps.append(lambda lev=self.order[s - 1]: self.halves(lev))
            if s >= 2:
                steps.append(lambda lev=self.order[s - 2]: self.column(lev))
        return steps

    def finish(self):
        for lev in range(self.at.levels):
            if self.sibling:
                for sp in range(4):
                    self.to_sibling(lev, sp).wait_send()
            sent([self.half_y(lev), self.half_x(lev), self.full_x(lev), self.full_y(lev)])
            pl.when(lev < self.at.level)(lambda lev=lev: self.go_down(lev).wait_send())
            pl.when(lev > self.at.level)(lambda lev=lev: self.go_up(lev).wait_send())


def dense_kernel(levels, spans, x_ref, flat_ref, all_ref, flat_all_ref, *refs):
    at = Place(levels)
    at.enter(False)
    sums, refs = refs[:2], refs[2:]
    size = Scatter.SCRATCH
    scatters = [
        Scatter(at, False, x_ref, sums[n], refs[n * size : (n + 1) * size], spans[n][0]) for n in range(2)
    ]
    refs = refs[2 * size :]
    pairs = [[(sums[n], all_ref, spans[n][0])] for n in range(2)]
    pairs[1].append((flat_ref, flat_all_ref))
    gathers = []
    for n in range(2):
        gathers.append(Gather(at, False, pairs[n], refs[n * 14 : (n + 1) * 14]))
    for task in scatters:
        task.begin()
    steps = []
    for n, lag in enumerate((0, 5.5)):
        begin = len(scatters[n].steps()) + lag
        steps += [(s + lag, n, step) for s, step in enumerate(scatters[n].steps())]
        steps.append((begin - 0.5, n, gathers[n].begin))
        steps += [(begin + s, 2 + n, step) for s, step in enumerate(gathers[n].steps())]
    for _, _, step in sorted(steps, key=lambda entry: entry[:2]):
        step()
    for task in [*scatters, *gathers]:
        task.finish()


def sum_dense(x, flat, levels, collective_id):
    blocks, rows, width = x.shape
    first = -(-rows // 64) * 32
    spans = [(0, first), (first, rows - first)]
    vmem, anywhere = pltpu.VMEM, pl.BlockSpec(memory_space=pl.ANY)
    shape = jax.ShapeDtypeStruct
    return pl.pallas_call(
        functools.partial(dense_kernel, levels, spans),
        out_shape=[shape(x.shape, BF16), shape((blocks, *flat.shape), BF16)],
        in_specs=[anywhere, anywhere],
        out_specs=[anywhere, anywhere],
        scratch_shapes=[vmem((n, width), BF16) for _, n in spans]
        + Scatter.scratch(levels, False, spans[0][1], width)
        + Scatter.scratch(levels, False, spans[1][1], width)
        + Gather.scratch(levels, 1)
        + Gather.scratch(levels, 2),
        compiler_params=pltpu.CompilerParams(
            collective_id=collective_id,
            has_side_effects=True,
            vmem_limit_bytes=60 * 1024 * 1024,
        ),
    )(x, flat)


def exchange_kernel(
    levels, back_ref, out_ref, part_ref, rows_ref, sum_ref, all_ref, block, send_s, recv_s, own_s, *refs
):
    at = Place(levels)
    at.enter(True)
    size = Scatter.SCRATCH
    first = Scatter(at, True, back_ref, rows_ref, refs[:size])
    second = Scatter(at, True, out_ref, sum_ref, refs[size : 2 * size])
    gather = Gather(at, False, [(block, all_ref)], refs[2 * size :])
    units, half = part_ref.shape[0] // 3, part_ref.shape[1] // 2
    mine = pl.ds(pl.multiple_of(at.core * units, units), units)
    own, theirs, sends = [], [], []
    for n in range(2):
        rows, lanes = pl.ds(n * units, units), pl.ds(n * half, half)

        def side(core):
            return part_ref.at[rows, pl.ds(pl.multiple_of(core * half, 128), half)]

        own.append(pltpu.make_async_copy(side(at.core), block.at[mine, lanes], own_s.at[n]))
        device = at.device(at.level, at.spot, 1 - at.core)
        sems = send_s.at[n], recv_s.at[n]
        sends.append(remote(side(1 - at.core), block.at[mine, lanes], *sems, device))
    down = pl.ds(2 * units, units)
    own.append(pltpu.make_async_copy(part_ref.at[down], block.at[down], own_s.at[2]))
    start(sends)
    start(own)
    first.begin()
    second.begin()
    for copy in own:
        copy.wait()
    arrived(sends)
    gather.begin()
    steps = [(s, 0, step) for s, step in enumerate(first.steps())]
    steps += [(s + 7, 1, step) for s, step in enumerate(second.steps())]
    steps += [(s + 8, 2, step) for s, step in enumerate(gather.steps())]
    for _, _, step in sorted(steps, key=lambda entry: entry[:2]):
        step()
    sent(sends)
    first.finish()
    second.finish()
    gather.finish()


def exchange_wide(back, out, part, levels, collective_id):
    rows, width = back.shape[1:]
    dma = pltpu.SemaphoreType.DMA
    anywhere, inside = pl.BlockSpec(memory_space=pl.ANY), pl.BlockSpec(memory_space=pltpu.VMEM)
    shape = jax.ShapeDtypeStruct
    return pl.pallas_call(
        functools.partial(exchange_kernel, levels),
        out_shape=[
            shape((rows, width), BF16),
            shape((rows, width), BF16),
            shape((levels * 4, *part.shape), BF16),
        ],
        in_specs=[anywhere, anywhere, inside],
        out_specs=[inside, inside, anywhere],
        scratch_shapes=[pltpu.VMEM(part.shape, BF16), dma((2,)), dma((2,)), dma((3,))]
        + Scatter.scratch(levels, True, rows, width) * 2
        + Gather.scratch(levels, 1),
        compiler_params=pltpu.CompilerParams(
            collective_id=collective_id,
            has_side_effects=True,
            vmem_limit_bytes=60 * 1024 * 1024,
        ),
        cost_estimate=pl.CostEstimate(
            flops=40 * 10**9, bytes_accessed=200 * 10**6, transcendentals=0
        ),
    )(back, out, part)


def local_call(kernel, outs, scratch, *args):
    inside = pl.BlockSpec(memory_space=pltpu.VMEM)
    return pl.pallas_call(
        kernel,
        out_shape=[jax.ShapeDtypeStruct(s, d) for s, d in outs],
        in_specs=[inside] * len(args),
        out_specs=[inside] * len(outs),
        scratch_shapes=[pltpu.VMEM(s, d) for s, d in scratch],
        compiler_params=pltpu.CompilerParams(vmem_limit_bytes=48 * 1024 * 1024),
    )(*args)


def half_lanes(which, size):
    return pl.ds(pl.multiple_of(which * size, 128), size)


def project_kernel(mine_ref, theirs_ref, scale_ref, q_ref, k_ref, v_ref, n_ref, keep_ref, send_ref, buf):
    core = lax.axis_index("narrow")
    rows = mine_ref.shape[0]
    part = n_ref.shape[1]
    for n, ref in enumerate((mine_ref, theirs_ref)):
        x = ref[...].astype(F32)
        r = lax.rsqrt(jnp.mean(x * x, axis=1, keepdims=True) + EPS)
        buf[n * rows : (n + 1) * rows, :] = (x * r * scale_ref[...]).astype(BF16)
    normed = buf[:, half_lanes(core, part)]
    n_ref[...] = normed
    for n, ref in enumerate((q_ref, k_ref, v_ref)):
        cols = slice(n * part, (n + 1) * part)
        send_ref[:, cols] = dot_nn(normed, ref[:, half_lanes(1 - core, part)]).astype(BF16)
        keep_ref[:, cols] = dot_nn(normed, ref[:, half_lanes(core, part)])


def probabilities(q, k, allowed):
    scores = jnp.where(allowed, dot_nt(q, k), MASKED)
    weights = jnp.exp(scores - jnp.max(scores, axis=1, keepdims=True))
    return weights / jnp.sum(weights, axis=1, keepdims=True)


def turn(values, cosine, sine_table):
    return values * cosine + pltpu.roll(values, HEAD_DIM // 2, 1) * sine_table


def attend_kernel(
    keep_ref, got_ref, cos_ref, sin_ref, mask_ref, out_w_ref,
    q_ref, k_ref, v_ref, o_ref, branch_ref, send_ref,
):
    rows, part = q_ref.shape
    half = rows // 2
    allowed = mask_ref[...] > 0.5
    cosine, sine_table = cos_ref[...], sin_ref[...]

    def full(cols):
        got = jnp.concatenate([got_ref[half:, cols], got_ref[:half, cols]], axis=0)
        return keep_ref[:, cols] + got.astype(F32)

    for h in range(part // HEAD_DIM):
        cols = slice(h * HEAD_DIM, (h + 1) * HEAD_DIM)
        q = full(slice(cols.start, cols.stop))
        k = full(slice(part + cols.start, part + cols.stop))
        v = full(slice(2 * part + cols.start, 2 * part + cols.stop)).astype(BF16)
        q = (turn(q, cosine, sine_table) * HEAD_DIM ** (-0.5)).astype(BF16)
        k = turn(k, cosine, sine_table).astype(BF16)
        q_ref[:, cols] = q
        k_ref[:, cols] = k
        v_ref[:, cols] = v
        o_ref[:, cols] = dot_nn(probabilities(q, k, allowed).astype(BF16), v).astype(BF16)
    send_ref[...] = dot_nn(o_ref[half:, :], out_w_ref[...]).astype(BF16)
    branch_ref[...] = dot_nn(o_ref[:half, :], out_w_ref[...])


def attend_back_kernel(
    branch_ref, their_ref, q_ref, k_ref, v_ref, o_ref, cos_ref, sin_ref, mask_ref, out_w_ref,
    grad_w_ref, mine_ref, row_buf, grad_buf,
):
    rows, part = q_ref.shape
    half = rows // 2
    allowed = mask_ref[...] > 0.5
    cosine, sine_table = cos_ref[...], -sin_ref[...]
    row_buf[:half, :] = branch_ref[...]
    row_buf[half:, :] = their_ref[...]
    grad_buf[...] = dot_nt(row_buf[...], out_w_ref[...]).astype(BF16)
    for h in range(part // HEAD_DIM):
        cols = slice(h * HEAD_DIM, (h + 1) * HEAD_DIM)
        q, k, v, grad = q_ref[:, cols], k_ref[:, cols], v_ref[:, cols], grad_buf[:, cols]
        probs = probabilities(q, k, allowed)
        grad_probs = dot_nt(grad, v)
        delta = jnp.sum(probs * grad_probs, axis=1, keepdims=True)
        grad_scores = (probs * (grad_probs - delta)).astype(BF16)
        grad_q = dot_nn(grad_scores, k) * HEAD_DIM ** (-0.5)
        mine_ref[0, :, cols] = turn(grad_q, cosine, sine_table).astype(BF16)
        mine_ref[1, :, cols] = turn(dot_tn(grad_scores, q), cosine, sine_table).astype(BF16)
        mine_ref[2, :, cols] = dot_tn(probs.astype(BF16), grad).astype(BF16)
    grad_w_ref[...] = dot_tn(o_ref[...], row_buf[...]).astype(BF16)


def dense_back_kernel(
    mine_ref, their_ref, n_ref, grad_w_ref, q_ref, k_ref, v_ref, dense_ref, part_ref, send_ref, buf
):
    core = lax.axis_index("narrow")
    rows, part = n_ref.shape
    half = rows // 2
    total = None
    for n, ref in enumerate((q_ref, k_ref, v_ref)):
        buf[n, :, half_lanes(core, part)] = mine_ref[n]
        buf[n, :half, half_lanes(1 - core, part)] = their_ref[n, half:, :]
        buf[n, half:, half_lanes(1 - core, part)] = their_ref[n, :half, :]
        term = dot_nt(buf[n], ref[...])
        total = term if total is None else total + term
        dense_ref[n] = dot_tn(n_ref[...], buf[n]).astype(BF16)
    dense_ref[3] = grad_w_ref[...]
    part_ref[...] = total[:half]
    send_ref[...] = total[half:].astype(BF16)


def widen_kernel(steps, x_ref, *refs):
    count = (len(refs) - 4) // 2
    step = pl.program_id(0)
    for n in range(count):
        refs[count + n][...] = refs[n][...]
    for n, ref in enumerate(refs[2 * count :]):

        @pl.when(step // steps == n)
        def _(ref=ref):
            ref[...] = x_ref[...].reshape(ref.shape).astype(F32)


def widen(gathered, passed):
    blocks, rows, width = gathered.shape
    each = 2 if blocks % 8 == 0 else 1
    grid, steps = blocks // each, blocks // each // 4
    shape = jax.ShapeDtypeStruct

    def spec(n):
        return pl.BlockSpec((each * rows, width), lambda i: (jnp.clip(i - steps * n, 0, steps - 1), 0))

    copied = [pl.BlockSpec((x.shape[0] // grid, width), lambda i: (i, 0)) for x in passed]
    return pl.pallas_call(
        functools.partial(widen_kernel, steps),
        grid=(grid,),
        out_shape=[shape(x.shape, x.dtype) for x in passed]
        + [shape((blocks // 4 * rows, width), F32)] * 4,
        in_specs=[pl.BlockSpec((each, rows, width), lambda i: (i, 0, 0))] + copied,
        out_specs=copied + [spec(n) for n in range(4)],
        compiler_params=pltpu.CompilerParams(vmem_limit_bytes=60 * 1024 * 1024),
    )(gathered, *passed)


def slots_path(
    tokens,
    cotangent,
    lengths,
    routes,
    keep,
    attn_gain,
    w_query,
    w_key,
    w_value,
    w_out,
    ffn_gain,
    w_router,
    shared_gate,
    shared_up,
    shared_down,
    expert_gate,
    expert_up,
    expert_down,
):
    narrow_size = lax.axis_size("narrow")
    narrow_index = lax.axis_index("narrow")
    wide_size = lax.axis_size("wide")
    local_rows = tokens.shape[0]
    model_width = tokens.shape[1]
    head_count = model_width // HEAD_DIM
    row_length = local_rows * narrow_size
    capacity = 8 * (3 * local_rows * TOPK // (16 * wide_size) + 1)
    gathered = (
        lax.all_gather(attn_gain, "narrow", axis=0, tiled=True),
        lax.all_gather(w_query, "narrow", axis=0, tiled=True),
        lax.all_gather(w_key, "narrow", axis=0, tiled=True),
        lax.all_gather(w_value, "narrow", axis=0, tiled=True),
        lax.all_gather(w_out, "narrow", axis=0, tiled=True),
        lax.all_gather(ffn_gain, "narrow", axis=0, tiled=True),
        lax.all_gather(w_router, "narrow", axis=0, tiled=True),
        lax.all_gather(shared_gate, "narrow", axis=0, tiled=True),
        lax.all_gather(shared_up, "narrow", axis=0, tiled=True),
        lax.all_gather(shared_down, "narrow", axis=0, tiled=True),
    )
    attn_scale = gathered[0].astype(jnp.float32)
    query_proj = gathered[1]
    key_proj = gathered[2]
    value_proj = gathered[3]
    output_proj = gathered[4]
    ffn_scale = gathered[5].astype(jnp.float32)
    router_proj = gathered[6]
    common_gate = gathered[7]
    common_upper = gathered[8]
    common_down = gathered[9]
    expert_mats = (expert_gate, expert_up, expert_down)
    routed_gate = expert_mats[0][0]
    routed_upper = expert_mats[1][0]
    routed_down = expert_mats[2][0]
    doc_lens = lengths[0]
    key_index = jnp.arange(row_length, dtype=jnp.int32)
    key_doc, unused = doc_layout(key_index, doc_lens)
    query_index = narrow_index * local_rows + jnp.arange(local_rows, dtype=jnp.int32)
    query_doc, query_pos = doc_layout(query_index, doc_lens)
    cosine, sine_table = rotary_angles(query_pos)
    inputs = tokens.astype(jnp.float32)
    normed, unit_one, scale_one = norm_forward(inputs, attn_scale)
    normed_one = normed.astype(jnp.bfloat16)
    head_shape = (local_rows, head_count, HEAD_DIM)
    query_rows = rotate(matmul(normed_one, query_proj).reshape(head_shape), cosine, sine_table)
    query_rows = (query_rows * HEAD_DIM ** (-0.5)).astype(jnp.bfloat16)
    key_rows = rotate(matmul(normed_one, key_proj).reshape(head_shape), cosine, sine_table).astype(
        jnp.bfloat16
    )
    valued = matmul(normed_one, value_proj).astype(jnp.bfloat16)
    all_keys, all_values = (
        lax.all_gather(key_rows.reshape(local_rows, model_width), "narrow", axis=0, tiled=True),
        lax.all_gather(valued, "narrow", axis=0, tiled=True),
    )
    all_keys = all_keys.reshape(row_length, head_count, HEAD_DIM)
    all_values = all_values.reshape(row_length, head_count, HEAD_DIM)
    block_rows = min(local_rows, 512)
    blocks = local_rows // block_rows
    query_blocks = query_rows.reshape(blocks, block_rows, head_count, HEAD_DIM)
    doc_blocks = query_doc.reshape(blocks, block_rows)
    index_blocks = query_index.reshape(blocks, block_rows)

    def allowed_for(doc_rows, index_rows):
        return (doc_rows[:, None] == key_doc[None, :]) & (key_index[None, :] <= index_rows[:, None])

    def forward_block(map_item):
        return attend_block(
            map_item[0], all_keys, all_values, allowed_for(map_item[1], map_item[2])
        )

    attended, logsum = lax.map(forward_block, (query_blocks, doc_blocks, index_blocks))
    attended = attended.reshape(local_rows, model_width)
    hidden = inputs + matmul(attended, output_proj)
    normed, unit_two, scale_two = norm_forward(hidden, ffn_scale)
    normed_two = normed.astype(jnp.bfloat16)
    logits = matmul(normed_two, router_proj)
    experts = router_proj.shape[1]
    pick_table = (routes[:, :, None] == jnp.arange(experts, dtype=jnp.int32)[None, None, :]).astype(
        jnp.float32
    )
    chosen = jnp.sum(pick_table * logits[:, None, :], axis=2)
    gate_probs = jax.nn.softmax(chosen, axis=1)
    keep_float = keep.astype(jnp.float32)
    mixing = gate_probs * keep_float
    common_gate_vals, common_upper_vals, common_act = expert_forward(
        normed_two, common_gate, common_upper
    )
    shared_out = matmul(common_act, common_down)
    pair_expert = routes.reshape(-1)
    pair_total = pair_expert.shape[0]
    onehot = (pair_expert[:, None] == jnp.arange(experts, dtype=jnp.int32)[None, :]).astype(
        jnp.int32
    )
    earlier = jnp.cumsum(onehot, axis=0) - onehot
    slot_place = jnp.sum(earlier * onehot, axis=1)
    slot_index = pair_expert * capacity + slot_place
    slot_total = experts * capacity
    source = (
        jnp.full((slot_total,), -1, jnp.int32)
        .at[slot_index]
        .set(jnp.arange(pair_total, dtype=jnp.int32))
    )
    filled = source >= 0
    pair_index = jnp.maximum(source, 0)

    def fill_slots(in_rows, row_index):
        taken = jnp.take(in_rows, row_index, axis=0)
        return jnp.where(filled[:, None], taken, jnp.zeros((), in_rows.dtype)).reshape(
            experts, capacity, model_width
        )

    received = lax.all_to_all(
        fill_slots(normed_two, pair_index // TOPK), "wide", split_axis=0, concat_axis=0, tiled=True
    )
    expert_in = lax.all_gather(received, "narrow", axis=0, tiled=True).reshape(-1, model_width)
    routed_gate_vals, routed_upper_vals, routed_act = expert_forward(
        expert_in, routed_gate, routed_upper
    )
    partial_value = matmul(routed_act, routed_down)
    expert_out = lax.psum_scatter(partial_value, "narrow", scatter_dimension=0, tiled=True)
    returned = lax.all_to_all(
        expert_out.astype(jnp.bfloat16).reshape(wide_size, capacity, model_width),
        "wide",
        split_axis=0,
        concat_axis=0,
        tiled=True,
    )
    pair_out = (
        jnp.take(returned.reshape(slot_total, model_width), slot_index, axis=0)
        .astype(jnp.float32)
        .reshape(local_rows, TOPK, model_width)
    )
    routed = jnp.sum(mixing[:, :, None] * pair_out, axis=1)
    output = (hidden + shared_out + routed).astype(jnp.bfloat16)
    grad_output = cotangent.astype(jnp.float32)
    grad_pairs = (
        (mixing[:, :, None] * grad_output[:, None, :])
        .astype(jnp.bfloat16)
        .reshape(pair_total, model_width)
    )
    grad_mixing = jnp.sum(pair_out * grad_output[:, None, :], axis=2)
    grad_received = lax.all_to_all(
        fill_slots(grad_pairs, pair_index), "wide", split_axis=0, concat_axis=0, tiled=True
    )
    grad_expert_out = lax.all_gather(grad_received, "narrow", axis=0, tiled=True).reshape(
        -1, model_width
    )
    grad_expert_in, grad_rgate, grad_rupper, grad_rdown = expert_backward(
        expert_in,
        grad_expert_out,
        routed_gate_vals,
        routed_upper_vals,
        routed_act,
        routed_gate,
        routed_upper,
        routed_down,
    )
    grad_slot_rows = lax.psum_scatter(grad_expert_in, "narrow", scatter_dimension=0, tiled=True)
    expert_grads = (grad_rgate, grad_rupper, grad_rdown)
    grad_back = lax.all_to_all(
        grad_slot_rows.astype(jnp.bfloat16).reshape(wide_size, capacity, model_width),
        "wide",
        split_axis=0,
        concat_axis=0,
        tiled=True,
    )
    grad_pair_rows = jnp.take(
        grad_back.reshape(slot_total, model_width), slot_index, axis=0
    ).astype(jnp.float32)
    grad_normed = jnp.sum(grad_pair_rows.reshape(local_rows, TOPK, model_width), axis=1)
    grad_gates = grad_mixing * keep_float
    grad_chosen = gate_probs * (
        grad_gates - jnp.sum(gate_probs * grad_gates, axis=1, keepdims=True)
    )
    grad_logits = jnp.sum(pick_table * grad_chosen[:, :, None], axis=1).astype(jnp.bfloat16)
    grad_router = matmul_left(normed_two, grad_logits)
    grad_normed = grad_normed + matmul_right(grad_logits, router_proj)
    grad_common_in, grad_cgate, grad_cupper, grad_cdown = expert_backward(
        normed_two,
        cotangent,
        common_gate_vals,
        common_upper_vals,
        common_act,
        common_gate,
        common_upper,
        common_down,
    )
    grad_normed = grad_normed + grad_common_in
    grad_hidden_norm, grad_ffn = norm_backward(grad_normed, unit_two, scale_two, ffn_scale)
    grad_hidden = grad_output + grad_hidden_norm
    grad_branch = grad_hidden.astype(jnp.bfloat16)
    grad_output_proj = matmul_left(attended, grad_branch)
    grad_attended = (
        matmul_right(grad_branch, output_proj)
        .astype(jnp.bfloat16)
        .reshape(blocks, block_rows, head_count, HEAD_DIM)
    )

    def backward_block(running, map_item):
        grad_queries, grad_keys, grad_values = attend_back(
            map_item[0],
            all_keys,
            all_values,
            allowed_for(map_item[1], map_item[2]),
            map_item[3],
            map_item[4],
        )
        return ((running[0] + grad_keys, running[1] + grad_values), grad_queries)

    empty_keys = jnp.zeros((row_length, head_count, HEAD_DIM), jnp.float32)
    sums_kv, grad_query_rows = lax.scan(
        backward_block,
        (empty_keys, empty_keys),
        (query_blocks, doc_blocks, index_blocks, logsum, grad_attended),
    )
    grad_key_own, grad_value_own = (
        lax.psum_scatter(
            sums_kv[0].reshape(row_length, model_width).astype(jnp.bfloat16),
            "narrow",
            scatter_dimension=0,
            tiled=True,
        ).astype(jnp.float32),
        lax.psum_scatter(
            sums_kv[1].reshape(row_length, model_width).astype(jnp.bfloat16),
            "narrow",
            scatter_dimension=0,
            tiled=True,
        ).astype(jnp.float32),
    )
    grad_query_rows = rotate(
        grad_query_rows.reshape(head_shape) * HEAD_DIM ** (-0.5), cosine, -sine_table
    )
    grad_query_rows = grad_query_rows.reshape(local_rows, model_width).astype(jnp.bfloat16)
    grad_key_rows = (
        rotate(grad_key_own.reshape(head_shape), cosine, -sine_table)
        .reshape(local_rows, model_width)
        .astype(jnp.bfloat16)
    )
    grad_value_rows = grad_value_own.astype(jnp.bfloat16)
    grad_query_proj = matmul_left(normed_one, grad_query_rows)
    grad_key_proj = matmul_left(normed_one, grad_key_rows)
    grad_value_proj = matmul_left(normed_one, grad_value_rows)
    grad_normed_one = (
        matmul_right(grad_query_rows, query_proj)
        + matmul_right(grad_key_rows, key_proj)
        + matmul_right(grad_value_rows, value_proj)
    )
    grad_input_norm, grad_attn = norm_backward(grad_normed_one, unit_one, scale_one, attn_scale)
    grad_tokens = grad_hidden + grad_input_norm
    halves = (
        lax.psum_scatter(
            grad_attn.astype(jnp.bfloat16), "narrow", scatter_dimension=0, tiled=True
        ).astype(jnp.float32),
        lax.psum_scatter(
            grad_query_proj.astype(jnp.bfloat16), "narrow", scatter_dimension=0, tiled=True
        ).astype(jnp.float32),
        lax.psum_scatter(
            grad_key_proj.astype(jnp.bfloat16), "narrow", scatter_dimension=0, tiled=True
        ).astype(jnp.float32),
        lax.psum_scatter(
            grad_value_proj.astype(jnp.bfloat16), "narrow", scatter_dimension=0, tiled=True
        ).astype(jnp.float32),
        lax.psum_scatter(
            grad_output_proj.astype(jnp.bfloat16), "narrow", scatter_dimension=0, tiled=True
        ).astype(jnp.float32),
        lax.psum_scatter(
            grad_ffn.astype(jnp.bfloat16), "narrow", scatter_dimension=0, tiled=True
        ).astype(jnp.float32),
        lax.psum_scatter(
            grad_router.astype(jnp.bfloat16), "narrow", scatter_dimension=0, tiled=True
        ).astype(jnp.float32),
        lax.psum_scatter(
            grad_cgate.astype(jnp.bfloat16), "narrow", scatter_dimension=0, tiled=True
        ).astype(jnp.float32),
        lax.psum_scatter(
            grad_cupper.astype(jnp.bfloat16), "narrow", scatter_dimension=0, tiled=True
        ).astype(jnp.float32),
        lax.psum_scatter(
            grad_cdown.astype(jnp.bfloat16), "narrow", scatter_dimension=0, tiled=True
        ).astype(jnp.float32),
    )
    owned = lax.psum(
        (
            halves[0],
            halves[1],
            halves[2],
            halves[3],
            halves[4],
            halves[5],
            halves[6],
            halves[7],
            halves[8],
            halves[9],
        ),
        "wide",
    )
    return (
        output,
        grad_tokens,
        owned[0],
        owned[1],
        owned[2],
        owned[3],
        owned[4],
        owned[5],
        owned[6],
        owned[7],
        owned[8],
        owned[9],
        expert_grads[0][None],
        expert_grads[1][None],
        expert_grads[2][None],
    )


def tokens_path(
    tokens,
    cotangent,
    lengths,
    routes,
    keep,
    attn_gain,
    w_query,
    w_key,
    w_value,
    w_out,
    ffn_gain,
    w_router,
    shared_gate,
    shared_up,
    shared_down,
    expert_gate,
    expert_up,
    expert_down,
):
    core = lax.axis_index("narrow")
    place = lax.axis_index("wide")
    wide_size = lax.axis_size("wide")
    levels = wide_size // 4
    local_rows, width = tokens.shape
    row_length = 2 * local_rows
    part = width // 2
    hidden_part = expert_gate.shape[2]
    stored = shared_gate.shape[1] // 2
    slice_width = -(-stored // (16 * wide_size)) * 16
    slices = stored // slice_width
    experts = w_router.shape[1]

    def swap(value):
        return lax.ppermute(value, "narrow", [(0, 1), (1, 0)])

    def in_order(mine, theirs, axis):
        return jnp.where(
            core == 0,
            jnp.concatenate([mine, theirs], axis=axis),
            jnp.concatenate([theirs, mine], axis=axis),
        )

    picks = (routes[:, :, None] == jnp.arange(experts, dtype=jnp.int32)[None, None, :]).astype(
        jnp.int32
    )
    marks = jnp.sum(picks * (1 + keep)[:, :, None], axis=1).astype(F32)

    first_unit = place * slice_width
    holds = place < slices

    def shared_slice(value, which, axis):
        begin = which * stored + first_unit
        taken = lax.dynamic_slice_in_dim(value, begin, slice_width, axis)
        return jnp.where(holds, taken, jnp.zeros((), value.dtype))

    gate_mine, up_mine = shared_slice(shared_gate, core, 1), shared_slice(shared_up, core, 1)
    gate_send, up_send = shared_slice(shared_gate, 1 - core, 1), shared_slice(shared_up, 1 - core, 1)
    down_slice = shared_slice(shared_down, 0, 0)
    gains = jnp.stack([attn_gain, ffn_gain])
    sent = swap(jnp.concatenate([gate_send.T, up_send.T, w_router.T], axis=0))
    gains = in_order(gains, swap(gains), 1).astype(F32)
    attn_scale, ffn_scale = gains[0], gains[1]
    dense = in_order(jnp.concatenate([gate_mine.T, up_mine.T, w_router.T], axis=0), sent, 1)
    router = dense[2 * slice_width :]

    inputs = tokens.astype(F32)
    square, wide_rows = (row_length, part), (local_rows, width)
    projections = [w_query, w_key, w_value]
    normed_one, qkv, sent = local_call(
        project_kernel,
        [(square, BF16), ((row_length, 3 * part), F32), ((row_length, 3 * part), BF16)],
        [((row_length, width), BF16)],
        tokens,
        swap(tokens),
        attn_scale[None, :],
        *projections,
    )
    index = jnp.arange(local_rows, dtype=jnp.int32)
    index = jnp.concatenate([core * local_rows + index, (1 - core) * local_rows + index])
    docs, positions = doc_layout(index, lengths[0])
    allowed = (docs[:, None] == docs[None, :]) & (index[None, :] <= index[:, None])
    cosine, sine_table = rotary_angles(positions)
    tables = [
        jnp.concatenate([cosine, cosine], axis=1),
        jnp.concatenate([-sine_table, sine_table], axis=1),
        allowed.astype(F32),
    ]
    *attention, branch, sent = local_call(
        attend_kernel,
        [(square, BF16)] * 4 + [(wide_rows, F32), (wide_rows, BF16)],
        [],
        qkv,
        swap(sent),
        *tables,
        w_out,
    )
    hidden = inputs + branch + swap(sent).astype(F32)
    normed, unit_two, scale_two = norm_forward(hidden, ffn_scale)
    normed_two = normed.astype(BF16)

    used = hidden_part + slice_width
    full = -(-(used + experts) // 128) * 128

    (_, _, _, grad_rows, expert_out, grad_mix, *expert_grads, shared_part) = experts_rows(
        normed_two,
        cotangent,
        marks.T,
        [expert_gate[0].T, expert_up[0].T, expert_down[0], dense, down_slice],
        hidden_part,
        used,
        full,
        levels,
        1,
    )
    grad_mix = lax.all_to_all(
        grad_mix.reshape(wide_size, 2, local_rows), "wide", split_axis=0, concat_axis=0, tiled=True
    )
    pick_core = jnp.where(core == 0, grad_mix[:, 0], grad_mix[:, 1])
    send_core = jnp.where(core == 0, grad_mix[:, 1], grad_mix[:, 0])
    grad_mix = (pick_core + swap(send_core)).T
    block_shape = (2 * wide_size, local_rows, width)
    grad_rows, expert_out, shared_all = exchange_wide(
        grad_rows.reshape(block_shape), expert_out.reshape(block_shape), shared_part, levels, 2
    )
    output = (hidden + expert_out.astype(F32)).astype(BF16)
    grad_shared_gate, grad_shared_up, grad_shared_down = shared_grads(
        shared_all, slices, part, stored
    )

    marks = marks.astype(F32)
    routed = marks > 0.0
    logits = matmul_right(normed_two, router)
    masked = jnp.where(routed, logits, MASKED)
    weights = jnp.where(routed, jnp.exp(masked - jnp.max(masked, axis=1, keepdims=True)), 0.0)
    gates = weights / jnp.sum(weights, axis=1, keepdims=True)
    grad_gates = jnp.where(marks > 1.5, grad_mix, 0.0)
    grad_logits = gates * (grad_gates - jnp.sum(gates * grad_gates, axis=1, keepdims=True))
    grad_logits = grad_logits.astype(BF16)
    grad_router = matmul_left(normed_two, grad_logits)
    grad_normed = grad_rows.astype(F32) + matmul(grad_logits, router)
    grad_hidden_norm, grad_ffn = norm_backward(grad_normed, unit_two, scale_two, ffn_scale)
    grad_hidden = cotangent.astype(F32) + grad_hidden_norm
    grad_branch = grad_hidden.astype(BF16)

    grad_w_out, mine = local_call(
        attend_back_kernel,
        [((part, width), BF16), ((3, *square), BF16)],
        [((row_length, width), BF16), (square, BF16)],
        grad_branch,
        swap(grad_branch),
        *attention,
        *tables,
        w_out,
    )
    grad_dense, grad_part, sent = local_call(
        dense_back_kernel,
        [((4, part, width), BF16), ((local_rows, part), F32), ((local_rows, part), BF16)],
        [((3, row_length, width), BF16)],
        mine,
        swap(mine),
        normed_one,
        grad_w_out,
        *projections,
    )
    grad_normed_one = in_order(grad_part, swap(sent).astype(F32), 1)
    _, unit_one, scale_one = norm_forward(inputs, attn_scale)
    grad_input_norm, grad_attn = norm_backward(grad_normed_one, unit_one, scale_one, attn_scale)
    grad_tokens = grad_hidden + grad_input_norm

    small = jnp.concatenate([grad_attn[:, None], grad_ffn[:, None], grad_router], axis=1)
    small_mine = lax.dynamic_slice_in_dim(small, core * part, part, 0)
    small_send = lax.dynamic_slice_in_dim(small, (1 - core) * part, part, 0)
    small = (small_mine + swap(small_send)).astype(BF16)
    size = small.size
    extra_rows = -(-size // (width * 16)) * 16
    flat = jnp.concatenate([small.reshape(-1), jnp.zeros((extra_rows * width - size,), BF16)])
    sum_rows = 4 * part // wide_size
    everything, flat = sum_dense(
        grad_dense.reshape(wide_size, sum_rows, width), flat.reshape(extra_rows, width), levels, 3
    )
    *expert_grads, grad_query, grad_key, grad_value, grad_out = widen(everything, expert_grads)
    grad_expert_gate, grad_expert_up, grad_expert_down = expert_grads
    flat = flat.astype(F32).reshape(wide_size, -1)
    small = jnp.sum(flat[:, :size], axis=0).reshape(part, 2 + experts)
    return (
        output,
        grad_tokens,
        small[:, 0],
        grad_query,
        grad_key,
        grad_value,
        grad_out,
        small[:, 1],
        small[:, 2:],
        grad_shared_gate,
        grad_shared_up,
        grad_shared_down,
        grad_expert_gate.T[None],
        grad_expert_up.T[None],
        grad_expert_down[None],
    )


def per_device(*arrays):
    tokens = arrays[0]
    gathered = lax.axis_size("wide") * lax.axis_size("narrow") * tokens.size * 2
    fits = gathered <= 12 * 1024 * 1024
    return (tokens_path if fits else slots_path)(*arrays)


def solution(mesh):
    in_specs = (
        P(("wide", "narrow"), None),
        P(("wide", "narrow"), None),
        P("wide", None),
        P(("wide", "narrow"), None),
        P(("wide", "narrow"), None),
        P("narrow"),
        P("narrow", None),
        P("narrow", None),
        P("narrow", None),
        P("narrow", None),
        P("narrow"),
        P("narrow", None),
        P("narrow", None),
        P("narrow", None),
        P("narrow", None),
        P("wide", None, "narrow"),
        P("wide", None, "narrow"),
        P("wide", "narrow", None),
    )
    out_specs = (
        P(("wide", "narrow"), None),
        P(("wide", "narrow"), None),
        P("narrow"),
        P("narrow", None),
        P("narrow", None),
        P("narrow", None),
        P("narrow", None),
        P("narrow"),
        P("narrow", None),
        P("narrow", None),
        P("narrow", None),
        P("narrow", None),
        P("wide", None, "narrow"),
        P("wide", None, "narrow"),
        P("wide", "narrow", None),
    )
    return jax.shard_map(
        per_device, mesh=mesh, in_specs=in_specs, out_specs=out_specs, check_vma=False
    )
```
